32 devices in a mesh: seq: 8 (over y, x, core), row: 4 (over z).
Axes of the slice: x: 2, y: 2, z: 4, core: 2. Of those that a mesh axis runs over, the one named last changes fastest.
Arguments:
- tokens: bfloat16 [12, 1024, 1024], P('row', 'seq'), may hold values from -6 to 6
- segments: int32 [12, 1024], P('row'), may hold values from 0 to 1023, as said below
- routes: int32 [12, 1024, 8], P('row', 'seq'), may hold values from 0 to 15, all different within a row
- cotangent: bfloat16 [12, 1024, 1024], P('row', 'seq'), may hold values from -6 to 6
- norm_attn: bfloat16 [1024], P(('seq', 'row')), may hold values from 0.5 to 1.5
- w_query: bfloat16 [1024, 1024], P(('seq', 'row')), may hold values from -0.1875 to 0.1875
- w_key: bfloat16 [1024, 512], P(('seq', 'row')), may hold values from -0.1875 to 0.1875
- w_value: bfloat16 [1024, 512], P(('seq', 'row')), may hold values from -0.1875 to 0.1875
- w_out: bfloat16 [1024, 1024], P(('seq', 'row')), may hold values from -3 to 3
- norm_ffn: bfloat16 [1024], P(('seq', 'row')), may hold values from 0.5 to 1.5
- w_router: bfloat16 [1024, 16], P(('seq', 'row')), may hold values from -0.09375 to 0.09375
- w_gate: bfloat16 [16, 1024, 512], P(None, ('seq', 'row')), may hold values from -0.1875 to 0.1875
- w_up: bfloat16 [16, 1024, 512], P(None, ('seq', 'row')), may hold values from -0.1875 to 0.1875
- w_down: bfloat16 [16, 512, 1024], P(None, ('seq', 'row')), may hold values from -1 to 1
Outputs:
- block_out: bfloat16 [12, 1024, 1024], P('row', 'seq')
- grad_input: bfloat16 [12, 1024, 1024], P('row', 'seq')
- grad_norm_attn: float32 [1024], P(('seq', 'row'))
- grad_w_query: float32 [1024, 1024], P(('seq', 'row'))
- grad_w_key: float32 [1024, 512], P(('seq', 'row'))
- grad_w_value: float32 [1024, 512], P(('seq', 'row'))
- grad_w_out: float32 [1024, 1024], P(('seq', 'row'))
- grad_norm_ffn: float32 [1024], P(('seq', 'row'))
- grad_w_router: float32 [1024, 16], P(('seq', 'row'))
- grad_w_gate: float32 [16, 1024, 512], P(None, ('seq', 'row'))
- grad_w_up: float32 [16, 1024, 512], P(None, ('seq', 'row'))
- grad_w_down: float32 [16, 512, 1024], P(None, ('seq', 'row'))
The draws below stay inside these ranges and needn't reach their ends.
Inputs may be any that keep to these rules, and one draw needn't show every extreme that they name: `segments`: along each row the numbers never fall; the first position holds 0 and the last 1023; in every row one segment covers all positions from some position under 128 to some position at 896 or later. `routes`: the 8 entries of one position are different experts; the same expert is named at many positions of a row.
All inputs are finite; a program needn't handle non-finite values.
Results may differ from the reference program's by a relative error of at most 0.015.
Values may be sent and summed in bfloat16 or wider, within the bound.
A program may use at most 384 MiB of HBM per device.

```python
import jax
import jax.numpy as jnp
from jax import lax

D = 1024
F = 512
H = 16
KVH = 8
TOPK = 8
HD = 64
E = 16
TOK_DEV = 128
KBLOCK = 512
LENGTH = 1024
ROWS = 12


def draw_segments(key, part):
    key_start, key_end, key_breaks = jax.random.split(key, 3)
    opening = jax.random.randint(key_start, (ROWS, 1), 1, TOK_DEV)
    closing = jax.random.randint(key_end, (ROWS, 1), LENGTH - TOK_DEV + 1, LENGTH)
    breaks = jax.random.randint(key_breaks, (ROWS, LENGTH), 0, 16) == 0
    places = jnp.arange(LENGTH, dtype=jnp.int32)[None, :]
    inside = (places > opening) & (places < closing)
    edges = (places == opening) | (places == closing)
    starts = jnp.where(inside, False, breaks | edges) & (places > 0)
    numbers = jnp.cumsum(starts.astype(jnp.int32), axis=1)
    final_count = numbers[:, LENGTH - 1:LENGTH]
    return numbers * (LENGTH - 1) // final_count


def levels(own_key, shape, pieces, low, largest):
    level = 1.0
    for dim, blocks in pieces:
        draws = jax.random.uniform(jax.random.fold_in(jax.random.fold_in(own_key, 6), dim), (blocks,), jnp.float32, low / len(pieces), largest / len(pieces))
        level = level * jnp.repeat(jnp.exp(draws), shape[dim] // blocks).reshape((-1,) + (1,) * (len(shape) - 1 - dim))
    return level


def different_ones(own_key, rows, count, top, lift):
    sequence = jax.random.permutation(jax.random.fold_in(own_key, 1), count)
    favour = sequence
    for power in range(3):
        favour = favour * favour // count
    favour = favour * lift // count
    chance = jax.random.randint(jax.random.fold_in(own_key, 2), (rows, count), 0, 4096) + favour
    fixed_rows = jax.random.permutation(jax.random.fold_in(own_key, 3), rows)[jnp.arange(count) % rows]
    chance = jnp.where(jnp.arange(rows)[:, None] == fixed_rows[None, :], 1 << 14, chance)
    merit = chance * count + jnp.arange(count)
    return lax.top_k(merit.astype(jnp.int32), top)[1].astype(jnp.int32)


def centred(own_key, dims, spread, limit, cuts=(), kind=jnp.bfloat16):
    loudness = levels(own_key, dims, cuts, -0.22, 0.18) if cuts else 1.0
    drawn = jax.random.normal(own_key, dims, jnp.float32) * spread * loudness
    return jnp.minimum(jnp.maximum(drawn, -limit), limit).astype(kind)


def setup_inputs(seed: int = 0) -> dict:
    seeds = jax.random.split(jax.random.key(seed), 15)
    return {
        "tokens": centred(seeds[0], (ROWS, LENGTH, D), 1.0, 6.0, ((0, 4), (1, 8))),
        "segments": draw_segments(jax.random.fold_in(seeds[14], 71), 0),
        "routes": different_ones(seeds[2], ROWS * LENGTH, E, TOPK, 8192).reshape((ROWS, LENGTH, TOPK)),
        "cotangent": centred(seeds[3], (ROWS, LENGTH, D), 1.0, 6.0, ((0, 4), (1, 8))),
        "norm_attn": jnp.clip(1.0 + 0.1 * jax.random.normal(seeds[4], (D,), jnp.float32), 0.5, 1.5).astype(jnp.bfloat16),
        "w_query": centred(seeds[5], (D, H * HD), D ** -0.5, 0.1875, ((0, 32),)),
        "w_key": centred(seeds[6], (D, KVH * HD), D ** -0.5, 0.1875, ((0, 32),)),
        "w_value": centred(seeds[7], (D, KVH * HD), D ** -0.5, 0.1875, ((0, 32),)),
        "w_out": centred(seeds[8], (H * HD, D), (max(H * HD // 256, 1)) ** -0.5, 3.0, ((0, 32),)),
        "norm_ffn": jnp.clip(1.0 + 0.1 * jax.random.normal(seeds[9], (D,), jnp.float32), 0.5, 1.5).astype(jnp.bfloat16),
        "w_router": centred(seeds[10], (D, E), (4 * D) ** -0.5, 0.09375, ((0, 32),)),
        "w_gate": centred(seeds[11], (E, D, F), D ** -0.5, 0.1875, ((1, 32),)),
        "w_up": centred(seeds[12], (E, D, F), D ** -0.5, 0.1875, ((1, 32),)),
        "w_down": centred(seeds[13], (E, F, D), (F // 16) ** -0.5, 1.0, ((1, 32),)),
    }


EPS = 1e-05
BASE = 10000.0

@jax.custom_vjp
def low(v):
    return lax.optimization_barrier(v.astype(jnp.bfloat16)).astype(jnp.float32)

@jax.custom_vjp
def low_back(v):
    return v

def low_keep(v):
    return (low(v), None)

def low_pass(kept, grad):
    return (grad,)

def back_keep(v):
    return (v, None)

def back_low(kept, grad):
    return (low(grad),)
low.defvjp(low_keep, low_pass)
low_back.defvjp(back_keep, back_low)

def highest(left_side, right_side):
    return jnp.dot(left_side, right_side, precision=lax.Precision.HIGHEST)

def rms_scale(row_values, gain):
    inverse = lax.rsqrt(lax.optimization_barrier(jnp.mean(row_values * row_values, axis=-1, keepdims=True)) + EPS)
    return row_values * inverse * gain

def rotary(row_values, heads, offset, direction):
    positions = row_values.shape[-2]
    head_width = row_values.shape[-1] // heads
    halfway = head_width // 2
    places = (offset + jnp.arange(positions)).astype(jnp.float32)
    frequency = BASE ** (-2.0 * jnp.arange(halfway).astype(jnp.float32) / head_width)
    angles = places[:, None] * frequency[None, :]
    cosine = jnp.cos(angles)[:, None, :]
    sine_part = direction * jnp.sin(angles)[:, None, :]
    halves = row_values.reshape(row_values.shape[:-1] + (heads, head_width))
    leading = halves[..., :halfway]
    trailing = halves[..., halfway:]
    turned = jnp.concatenate([leading * cosine - trailing * sine_part, trailing * cosine + leading * sine_part], axis=-1)
    return turned.reshape(row_values.shape)

def attention(queries, keys, values, segment_row):
    seq_length = queries.shape[0]
    block_size = min(KBLOCK, seq_length)
    block_count = seq_length // block_size
    groups = H // KVH
    keys_heads = keys.reshape(seq_length, KVH, HD)
    values_heads = values.reshape(seq_length, KVH, HD)
    key_places = jnp.arange(seq_length)

    def one_block(item):
        query_block, block_start = item
        query_places = block_start + jnp.arange(block_size)
        query_ids = lax.dynamic_slice_in_dim(segment_row, block_start, block_size)
        allowed = (key_places[None, :] <= query_places[:, None]) & (segment_row[None, :] == query_ids[:, None])
        grouped = query_block.reshape(block_size, KVH, groups, HD)
        scores = low_back(jnp.einsum('qkgd,tkd->kgqt', grouped, keys_heads, precision=lax.Precision.HIGHEST) * HD ** (-0.5))
        scores = jnp.where(allowed[None, None], scores, -jnp.inf)
        probability = low(jnp.exp(scores - jax.nn.logsumexp(scores, axis=-1, keepdims=True)))
        context = jnp.einsum('kgqt,tkd->qkgd', probability, values_heads, precision=lax.Precision.HIGHEST)
        return context.reshape(block_size, H * HD)
    starts = (jnp.arange(block_count) * block_size).astype(jnp.int32)
    blocks_out = lax.map(jax.checkpoint(one_block), (queries.reshape(block_count, block_size, H * HD), starts))
    return blocks_out.reshape(seq_length, H * HD)

def layer_row(inputs, segment_row, route_row, weight_set):
    norm_attn, w_query, w_key, w_value, w_out, norm_ffn, w_router, w_gate, w_up, w_down = weight_set
    normed = low(rms_scale(inputs, norm_attn))
    queries = low(rotary(low_back(highest(normed, w_query)), H, 0, 1.0))
    keys = low(rotary(low_back(highest(normed, w_key)), KVH, 0, 1.0))
    values = low(low_back(highest(normed, w_value)))
    context = low(low_back(attention(queries, keys, values, segment_row)))
    mixed = inputs + low_back(highest(context, w_out))
    normed_ffn = low(rms_scale(mixed, norm_ffn))
    logits = low_back(highest(normed_ffn, w_router))
    chosen = jnp.any(route_row[:, :, None] == jnp.arange(E)[None, None, :], axis=1)
    gates = jax.nn.softmax(jnp.where(chosen, logits, -jnp.inf), axis=-1)
    gate_act = low_back(jnp.einsum('td,edf->etf', normed_ffn, w_gate, precision=lax.Precision.HIGHEST))
    up_act = low_back(jnp.einsum('td,edf->etf', normed_ffn, w_up, precision=lax.Precision.HIGHEST))
    hidden = low(jax.nn.silu(gate_act) * up_act)
    expert_out = low_back(jnp.einsum('etf,efd->etd', hidden, w_down, precision=lax.Precision.HIGHEST))
    return mixed + jnp.einsum('te,etd->td', gates, expert_out, precision=lax.Precision.HIGHEST)

def reference(tokens, segments, routes, cotangent, norm_attn, w_query, w_key, w_value, w_out, norm_ffn, w_router, w_gate, w_up, w_down):
    params = tuple((item.astype(jnp.float32) for item in (norm_attn, w_query, w_key, w_value, w_out, norm_ffn, w_router, w_gate, w_up, w_down)))

    def row_step(carry, row_items):
        row_tokens, segment_row, route_row, row_cotangent = row_items

        def forward(inputs, weight_set):
            return layer_row(inputs, segment_row, route_row, weight_set)
        output, pull = jax.vjp(forward, row_tokens.astype(jnp.float32), params)
        grad_inputs, grad_weights = pull(row_cotangent.astype(jnp.float32))
        carry = jax.tree.map(lambda summed, added: summed + added, carry, grad_weights)
        return (carry, (output.astype(jnp.bfloat16), grad_inputs.astype(jnp.bfloat16)))
    zeros = tuple((jnp.zeros(item.shape, jnp.float32) for item in params))
    sums, (outputs, grads_in) = lax.scan(row_step, zeros, (tokens, segments, routes, cotangent))
    return (outputs, grads_in, sums[0], sums[1], sums[2], sums[3], sums[4], sums[5], sums[6], sums[7], sums[8], sums[9])
```

```python
import functools

import jax
import jax.numpy as jnp
from jax import lax
from jax.experimental import pallas as pl
from jax.experimental.pallas import tpu as pltpu
from jax.sharding import PartitionSpec as P

H = 16
KVH = 8
TOPK = 8
HD = 64
E = 16
UNIT = 8
LANES = 128
QBLOCK = 256

EPS = 1e-05
BASE = 10000.0
NEGATIVE = -1e30
F32 = jnp.float32
BF16 = jnp.bfloat16
VMEM_LIMIT = 60 * 1024 * 1024


def dot_nn(left, right):
    return lax.dot_general(left, right, (((1,), (0,)), ((), ())), preferred_element_type=F32)


def dot_nt(left, right):
    return lax.dot_general(left, right, (((1,), (1,)), ((), ())), preferred_element_type=F32)


def params(**kw):
    return pltpu.CompilerParams(vmem_limit_bytes=VMEM_LIMIT, **kw)


def cost(flops, nbytes):
    return pl.CostEstimate(flops=int(flops), bytes_accessed=int(nbytes), transcendentals=0)


def lane_iota(shape):
    return lax.broadcasted_iota(jnp.int32, shape, len(shape) - 1)


def turn(u, cosine, sine):
    low_half = lane_iota(u.shape) % HD < HD // 2
    partner = jnp.where(
        low_half, pltpu.roll(u, LANES - HD // 2, u.ndim - 1), pltpu.roll(u, HD // 2, u.ndim - 1)
    )
    return u * cosine + partner * sine


def project_kernel(tok_ref, gain_ref, w_ref, cos_ref, sin_ref, normed_ref, q_ref, kv_ref):
    count = q_ref.shape[1]
    width = w_ref.shape[0]
    x = tok_ref[...].reshape(count, width).astype(F32)
    inverse = lax.rsqrt(jnp.mean(x * x, axis=-1, keepdims=True) + EPS)
    normed = (x * inverse * gain_ref[...]).astype(BF16)
    normed_ref[...] = normed.reshape(normed_ref.shape)
    raw = dot_nn(normed, w_ref[...])
    cosine, sine = cos_ref[...], sin_ref[...]
    q = turn(raw[:, :LANES], cosine[:, :LANES], sine[:, :LANES]).astype(BF16)
    q_ref[0] = (q.astype(F32) * HD**-0.5).astype(BF16)
    kv_ref[0] = turn(raw[:, LANES:], cosine[:, LANES:], sine[:, LANES:]).astype(BF16)


def pair_keys(kv):
    kv = kv.astype(F32)
    rolled = pltpu.roll(kv, HD, 1)
    low = lane_iota(kv.shape) < HD
    return jnp.where(low, kv, rolled), jnp.where(low, rolled, kv)


def bias_block(seg_col, seg_row, q_places, first, length):
    key_places = lax.broadcasted_iota(jnp.int32, (length, q_places.shape[1]), 0)
    allowed = (seg_col[:length] == seg_row) & (key_places <= q_places)
    return jnp.where(allowed, 0.0, NEGATIVE)


def attention_kernel(skip, q_ref, kv_ref, segq_ref, segk_ref, place_ref, ctx_ref, lse_ref):
    length = kv_ref.shape[1]
    queries = q_ref.shape[1]
    kk, vv = pair_keys(kv_ref[0])
    v_t = vv.T.astype(BF16)[:HD]
    kk = kk.astype(BF16)
    seg_col = jnp.broadcast_to(segk_ref[0], (8, length)).T[:, :1]
    for block in range(queries // QBLOCK):
        here = slice(block * QBLOCK, (block + 1) * QBLOCK)
        keys = (block + 1) * QBLOCK if skip else length
        bias = bias_block(seg_col, segq_ref[0][:, here], place_ref[:, here], 0, keys)
        q = q_ref[0, here, :]
        low = lane_iota(q.shape) < HD
        parts = []
        for head in range(2):
            mine = jnp.where(low == (head == 0), q, jnp.zeros_like(q))
            scores = dot_nt(kk[:keys], mine) + bias
            top = jnp.max(scores, axis=0, keepdims=True)
            weight = jnp.exp(scores - top)
            total = jnp.sum(weight, axis=0, keepdims=True)
            prob = (weight * (1.0 / total)).astype(BF16)
            parts.append(dot_nn(v_t[:, :keys], prob))
            lse_ref[0, head : head + 1, here] = top + jnp.log(total)
        ctx = jnp.concatenate(parts, axis=0).T.astype(BF16)
        per = QBLOCK // LANES
        ctx_ref[block * per : (block + 1) * per, 0] = ctx.reshape(per, LANES, LANES)


def attention_back_kernel(
    skip, q_ref, kv_ref, segq_ref, segk_ref, place_ref, lse_ref, do_ref, cosq_ref, sinq_ref,
    coskv_ref, sinkv_ref, gq_ref, gkv_ref, dk_acc, dv_acc,
):
    length = kv_ref.shape[1]
    queries = q_ref.shape[1]
    kk, vv = pair_keys(kv_ref[0])
    k_t = kk.T.astype(BF16)[:HD]
    kk = kk.astype(BF16)
    vv = vv.astype(BF16)
    seg_col = jnp.broadcast_to(segk_ref[0], (8, length)).T[:, :1]
    dk_acc[...] = jnp.zeros_like(dk_acc)
    dv_acc[...] = jnp.zeros_like(dv_acc)
    per = QBLOCK // LANES
    for block in range(queries // QBLOCK):
        here = slice(block * QBLOCK, (block + 1) * QBLOCK)
        keys = (block + 1) * QBLOCK if skip else length
        bias = bias_block(seg_col, segq_ref[0][:, here], place_ref[:, here], 0, keys)
        q = q_ref[0, here, :]
        do = do_ref[block * per : (block + 1) * per, 0].reshape(QBLOCK, LANES)
        low = lane_iota(q.shape) < HD
        parts = []
        for head in range(2):
            pick = low == (head == 0)
            mine = jnp.where(pick, q, jnp.zeros_like(q))
            mine_do = jnp.where(pick, do, jnp.zeros_like(do))
            scores = dot_nt(kk[:keys], mine) + bias
            weight = jnp.exp(scores - lse_ref[0, head : head + 1, here])
            product = dot_nt(vv[:keys], mine_do)
            delta = jnp.sum(weight * product, axis=0, keepdims=True)
            grad_scores = (weight * (product - delta)).astype(BF16)
            dv_acc[:keys] += dot_nn(weight.astype(BF16), mine_do)
            dk_acc[:keys] += dot_nn(grad_scores, mine)
            parts.append(dot_nn(k_t[:, :keys], grad_scores))
        dq = jnp.concatenate(parts, axis=0).T * HD**-0.5
        dq = turn(dq, cosq_ref[here, :], -sinq_ref[here, :]).astype(BF16)
        gq_ref[block * per : (block + 1) * per, 0] = dq.reshape(per, LANES, LANES)
    dk = dk_acc[...]
    dv = dv_acc[...]
    dk = dk + pltpu.roll(dk, HD, 1)
    dv = dv + pltpu.roll(dv, HD, 1)
    gkv = jnp.where(lane_iota(dk.shape) < HD, dk, dv)
    gkv = turn(gkv, coskv_ref[...], -sinkv_ref[...]).astype(BF16)
    gkv_ref[...] = gkv.reshape(gkv_ref.shape)


def mix_kernel(ctx_ref, w_ref, tok_ref, gain_ref, mixed_ref, normed_ref, ctx_out):
    count, width = tok_ref.shape
    for b in range(UNIT):
        ctx_out[:, b * LANES : (b + 1) * LANES] = ctx_ref[b].reshape(count, LANES)
    mixed = tok_ref[...].astype(F32) + dot_nn(ctx_out[...], w_ref[...])
    mixed_ref[...] = mixed
    inverse = lax.rsqrt(jnp.mean(mixed * mixed, axis=-1, keepdims=True) + EPS)
    normed_ref[...] = (mixed * inverse * gain_ref[...]).astype(BF16)


def soft_gates(normed, router, chosen):
    logits = jnp.where(chosen > 0, dot_nn(normed, router), NEGATIVE)
    top = jnp.max(logits, axis=-1, keepdims=True)
    weight = jnp.where(chosen > 0, jnp.exp(logits - top), 0.0)
    return weight / jnp.sum(weight, axis=-1, keepdims=True)


def expert_kernel(
    first, gid_ref, x_ref, dz_ref, wr_ref, wg_ref, wu_ref, wd_ref, *rest,
):
    if first:
        (out_ref, dx_ref, gg_ref, dwg_ref, dwu_ref, dwd_ref,
         x_t, gates, oacc, dxacc, ggacc, ag, au, ad) = rest
    else:
        (oin_ref, dxin_ref, ggin_ref, out_ref, dx_ref, gg_ref, dwg_ref, dwu_ref, dwd_ref,
         x_t, gates, oacc, dxacc, ggacc, ag, au, ad) = rest
    e, t = pl.program_id(0), pl.program_id(1)
    last_e, last_t = pl.num_programs(0) - 1, pl.num_programs(1) - 1
    width = x_ref.shape[1]
    x = x_ref[...]
    dz = dz_ref[:, :width]

    @pl.when(e == 0)
    def _():
        x_t[t] = x.T
        gates[t] = soft_gates(x, wr_ref[...], dz_ref[:, width:].astype(F32))
        if first:
            oacc[t] = jnp.zeros_like(oacc[t])
            dxacc[t] = jnp.zeros_like(dxacc[t])
            ggacc[t] = jnp.zeros_like(ggacc[t])
        else:
            oacc[t] = oin_ref[...]
            dxacc[t] = dxin_ref[...]
            ggacc[t] = ggin_ref[...]

    mine = lane_iota(gates.shape[1:]) == gid_ref[e]
    gate = jnp.sum(jnp.where(mine, gates[t], 0.0), axis=1, keepdims=True)
    gate_act = dot_nn(x, wg_ref[0])
    up_act = dot_nn(x, wu_ref[0])
    back = dot_nt(dz, wd_ref[0])
    sig = 1.0 / (1.0 + jnp.exp(-gate_act))
    silu = gate_act * sig
    hidden = silu * up_act
    ggacc[t] += jnp.where(mine, jnp.sum(hidden * back, axis=1, keepdims=True), 0.0)
    grad_hidden = back * gate
    grad_gate = (grad_hidden * up_act * (sig * (1.0 + gate_act * (1.0 - sig)))).astype(BF16)
    grad_up = (grad_hidden * silu).astype(BF16)
    gated = (hidden * gate).astype(BF16)
    oacc[t] += dot_nn(gated, wd_ref[0])
    dxacc[t] += dot_nt(grad_gate, wg_ref[0]) + dot_nt(grad_up, wu_ref[0])
    x_turned = x_t[t]
    term_gate = dot_nn(x_turned, grad_gate)
    term_up = dot_nn(x_turned, grad_up)
    term_down = dot_nn(gated.T, dz)

    @pl.when(t == 0)
    def _():
        ag[...] = term_gate
        au[...] = term_up
        ad[...] = term_down

    @pl.when(t > 0)
    def _():
        ag[...] += term_gate
        au[...] += term_up
        ad[...] += term_down

    @pl.when(t == last_t)
    def _():
        dwg_ref[0] = ag[...].astype(BF16)
        dwu_ref[0] = au[...].astype(BF16)
        dwd_ref[0] = ad[...].astype(BF16)

    @pl.when(e == last_e)
    def _():
        out_ref[...] = oacc[t].astype(out_ref.dtype)
        dx_ref[...] = dxacc[t].astype(dx_ref.dtype)
        gg_ref[...] = ggacc[t]


def run_experts(gids, x, dz, router, wg, wu, wd, carried):
    tokens, width = x.shape
    count, _, hidden = wg.shape
    tile = tokens // 4
    tiles = tokens // tile
    first = carried is None
    kind = F32 if first else BF16

    def whole(e, t):
        return (0, 0)

    def by_token(e, t):
        return (t, 0)

    def by_expert(e, t):
        return (e, 0, 0)

    def at_end(e, t):
        return (jnp.where(e == count - 1, t, 0), 0)

    def at_start(e, t):
        return (jnp.where(e == 0, t, tiles - 1), 0)

    in_specs = [
        pl.BlockSpec(memory_space=pltpu.SMEM),
        pl.BlockSpec((tile, width), by_token),
        pl.BlockSpec((tile, width + LANES), by_token),
        pl.BlockSpec((width, LANES), whole),
        pl.BlockSpec((1, width, hidden), by_expert),
        pl.BlockSpec((1, width, hidden), by_expert),
        pl.BlockSpec((1, hidden, width), by_expert),
    ]
    args = [gids, x, dz, router, wg, wu, wd]
    if not first:
        in_specs += [
            pl.BlockSpec((tile, width), at_start),
            pl.BlockSpec((tile, width), at_start),
            pl.BlockSpec((tile, LANES), at_start),
        ]
        args += list(carried)
    return pl.pallas_call(
        functools.partial(expert_kernel, first),
        grid=(count, tiles),
        in_specs=in_specs,
        out_specs=[
            pl.BlockSpec((tile, width), at_end),
            pl.BlockSpec((tile, width), at_end),
            pl.BlockSpec((tile, LANES), at_end),
            pl.BlockSpec((1, width, hidden), by_expert),
            pl.BlockSpec((1, width, hidden), by_expert),
            pl.BlockSpec((1, hidden, width), by_expert),
        ],
        out_shape=[
            jax.ShapeDtypeStruct((tokens, width), kind),
            jax.ShapeDtypeStruct((tokens, width), kind),
            jax.ShapeDtypeStruct((tokens, LANES), F32),
            jax.ShapeDtypeStruct((count, width, hidden), BF16),
            jax.ShapeDtypeStruct((count, width, hidden), BF16),
            jax.ShapeDtypeStruct((count, hidden, width), BF16),
        ],
        scratch_shapes=[
            pltpu.VMEM((tiles, width, tile), BF16),
            pltpu.VMEM((tiles, tile, LANES), F32),
            pltpu.VMEM((tiles, tile, width), F32),
            pltpu.VMEM((tiles, tile, width), F32),
            pltpu.VMEM((tiles, tile, LANES), F32),
            pltpu.VMEM((width, hidden), F32),
            pltpu.VMEM((width, hidden), F32),
            pltpu.VMEM((hidden, width), F32),
        ],
        compiler_params=params(),
        cost_estimate=cost(18.0 * tokens * width * hidden * count, 4e7),
    )(*args)


def back_kernel(
    p0, p1, p2, p3, g0, g1, g2, g3, mixed_ref, normed_ref, dz_ref, gain_ref, wr_ref, w_ref,
    gmixed_ref, gbranch_ref, glog_ref, gctx_ref,
):
    count, width = mixed_ref.shape
    dz_all = dz_ref[...]
    dz = dz_all[:, :width].astype(F32)
    gates = soft_gates(normed_ref[...], wr_ref[...], dz_all[:, width:].astype(F32))
    grad_gates = g0[...] + g1[...] + g2[...] + g3[...]
    centre = jnp.sum(gates * grad_gates, axis=-1, keepdims=True)
    glog = (gates * (grad_gates - centre)).astype(BF16)
    glog_ref[...] = glog
    dy = p0[...].astype(F32) + p1[...].astype(F32) + p2[...].astype(F32) + p3[...].astype(F32)
    dy = dy + dot_nt(glog, wr_ref[...])
    v = mixed_ref[...]
    inverse = lax.rsqrt(jnp.mean(v * v, axis=-1, keepdims=True) + EPS)
    scaled = dy * gain_ref[...]
    mean = jnp.mean(scaled * v, axis=-1, keepdims=True)
    gmixed = dz + scaled * inverse - v * (inverse * inverse * inverse * mean)
    gmixed_ref[...] = gmixed
    gbranch = gmixed.astype(BF16)
    gbranch_ref[...] = gbranch
    gctx = dot_nt(gbranch, w_ref[...]).astype(BF16)
    for b in range(UNIT):
        gctx_ref[b] = gctx[:, b * LANES : (b + 1) * LANES].reshape(gctx_ref.shape[1:])


def input_kernel(graw_ref, w_ref, tok_ref, gain_ref, gmixed_ref, gin_ref, acc):
    b = pl.program_id(0)
    count, width = tok_ref.shape
    term = dot_nt(graw_ref[0].reshape(count, 2 * LANES), w_ref[0])

    @pl.when(b == 0)
    def _():
        acc[...] = term

    @pl.when(b > 0)
    def _():
        acc[...] += term

    @pl.when(b == pl.num_programs(0) - 1)
    def _():
        v = tok_ref[...].astype(F32)
        inverse = lax.rsqrt(jnp.mean(v * v, axis=-1, keepdims=True) + EPS)
        scaled = acc[...] * gain_ref[...]
        mean = jnp.mean(scaled * v, axis=-1, keepdims=True)
        grad = gmixed_ref[...] + scaled * inverse - v * (inverse * inverse * inverse * mean)
        gin_ref[...] = grad.astype(BF16)


def shards(
    copies, tokens, segments, routes, cotangent, norm_attn, w_query, w_key, w_value, w_out, norm_ffn,
    w_router, w_gate, w_up, w_down, rows,
):
    micro, local_len, width = tokens.shape
    length = segments.shape[1]
    count = micro * local_len
    unit_len = UNIT * local_len
    part = w_query.shape[0]
    hidden = w_gate.shape[2]
    seq_size = copies * UNIT
    seq = lax.axis_index("seq")
    row = lax.axis_index("row")
    unit = seq // UNIT
    me = seq % UNIT
    unit_groups = None
    copy_groups = None
    if copies > 1:
        unit_groups = [[a * UNIT + b for b in range(UNIT)] for a in range(copies)]
        copy_groups = [[a * UNIT + b for a in range(copies)] for b in range(UNIT)]

    def exchange(x):
        return lax.all_to_all(x, "seq", 0, 0, tiled=True, axis_index_groups=unit_groups)

    def flip(x, k):
        return lax.ppermute(x, "seq", [(s, s ^ k) for s in range(seq_size)])

    def gather_rows(x, axis):
        x = lax.all_gather(x, "row", axis=axis, tiled=True)
        if copies > 1:
            x = lax.all_gather(x, "seq", axis=axis - 1, tiled=True, axis_index_groups=copy_groups)
        return x

    def reduce_rows(x, axis):
        own = lax.dynamic_index_in_dim(x, row, axis, False).astype(F32)
        for k in range(1, rows):
            sent = lax.dynamic_index_in_dim(x, (row + k) % rows, axis, False)
            own = own + lax.ppermute(
                sent, "row", [(i, (i + k) % rows) for i in range(rows)]
            ).astype(F32)
        if copies > 1:
            own = lax.psum_scatter(
                own.astype(BF16), "seq", scatter_dimension=axis - 2, axis_index_groups=copy_groups
            ).astype(F32)
        else:
            own = lax.squeeze(own, (axis - 2,))
        return own

    flat_tokens = tokens.reshape(count, width)

    head_part = jnp.concatenate(
        [
            w_query.reshape(part, UNIT, 2 * HD),
            w_key.reshape(part, UNIT, HD),
            w_value.reshape(part, UNIT, HD),
        ],
        axis=2,
    ).transpose(1, 0, 2)
    small = jnp.concatenate(
        [
            norm_attn[:, None],
            norm_ffn[:, None],
            w_router,
            jnp.zeros((part, LANES - 2 - E), BF16),
        ],
        axis=1,
    )
    small = lax.all_gather(small, ("seq", "row"), axis=0, tiled=True)
    gain_attn = small[:, 0].astype(F32)[None]
    gain_ffn = small[:, 1].astype(F32)[None]
    router = jnp.concatenate([small[:, 2 : 2 + E], jnp.zeros((width, LANES - E), BF16)], axis=1)
    w_head = gather_rows(exchange(head_part), 1).reshape(width, 4 * HD)

    def gather_expert(w):
        piece = w.reshape((UNIT, E // UNIT) + w.shape[1:])
        piece = exchange(piece).transpose(1, 0, 2, 3)
        return gather_rows(piece, 2).reshape(E // UNIT, -1, w.shape[2])

    own_weights = tuple(gather_expert(w) for w in (w_gate, w_up, w_down))
    sib_weights = tuple(flip(w, 1) for w in own_weights)

    same = [flat_tokens] + [flip(flat_tokens, k) for k in (2, 4, 6)]
    stacked = jnp.stack(same)
    other = flip(stacked, 1)
    tok_all = jnp.zeros((UNIT, count, width), BF16)
    for i in range(4):
        tok_all = lax.dynamic_update_index_in_dim(tok_all, stacked[i], me ^ (2 * i), 0)
        tok_all = lax.dynamic_update_index_in_dim(tok_all, other[i], me ^ 1 ^ (2 * i), 0)
    tok_all = tok_all.reshape(UNIT, micro, local_len, width)

    frequency = BASE ** (-2.0 * jnp.arange(HD // 2).astype(F32) / HD)
    places = unit * unit_len + jnp.arange(unit_len, dtype=jnp.int32)
    angles = places.astype(F32)[:, None] * frequency[None, :]
    cos_one = jnp.concatenate([jnp.cos(angles)] * 2, axis=1)
    sin_one = jnp.concatenate([-jnp.sin(angles), jnp.sin(angles)], axis=1)
    cosine = jnp.concatenate([cos_one] * 3 + [jnp.ones_like(cos_one)], axis=1)
    sine = jnp.concatenate([sin_one] * 3 + [jnp.zeros_like(sin_one)], axis=1)

    def by_row4(m):
        return (0, m, 0, 0)

    def by_row3(m):
        return (m, 0, 0)

    def fixed(*_):
        return (0, 0)

    normed_all, q_all, kv_own = pl.pallas_call(
        project_kernel,
        grid=(micro,),
        in_specs=[
            pl.BlockSpec((UNIT, 1, local_len, width), by_row4),
            pl.BlockSpec((1, width), fixed),
            pl.BlockSpec((width, 4 * HD), fixed),
            pl.BlockSpec((unit_len, 4 * HD), fixed),
            pl.BlockSpec((unit_len, 4 * HD), fixed),
        ],
        out_specs=[
            pl.BlockSpec((UNIT, 1, local_len, width), by_row4),
            pl.BlockSpec((1, unit_len, LANES), by_row3),
            pl.BlockSpec((1, unit_len, LANES), by_row3),
        ],
        out_shape=[
            jax.ShapeDtypeStruct((UNIT, micro, local_len, width), BF16),
            jax.ShapeDtypeStruct((micro, unit_len, LANES), BF16),
            jax.ShapeDtypeStruct((micro, unit_len, LANES), BF16),
        ],
        compiler_params=params(),
        cost_estimate=cost(2.0 * UNIT * count * width * 4 * HD, 1.5e7),
    )(tok_all, gain_attn, w_head, cosine, sine)

    kv_all = kv_own
    if copies > 1:
        kv_all = lax.all_gather(kv_own, "seq", axis=1, tiled=True, axis_index_groups=copy_groups)
    seg_keys = segments.astype(F32).reshape(micro, 1, length)
    seg_queries = lax.dynamic_slice_in_dim(seg_keys, unit * unit_len, unit_len, 2)
    skip = copies == 1
    place_row = places[None]
    attention_flops = 4.0 * micro * unit_len * length * 2 * LANES
    attention_specs = [
        pl.BlockSpec((1, unit_len, LANES), by_row3),
        pl.BlockSpec((1, length, LANES), by_row3),
        pl.BlockSpec((1, 1, unit_len), by_row3),
        pl.BlockSpec((1, 1, length), by_row3),
        pl.BlockSpec((1, unit_len), fixed),
    ]
    ctx_heads, lse = pl.pallas_call(
        functools.partial(attention_kernel, skip),
        grid=(micro,),
        in_specs=attention_specs,
        out_specs=[
            pl.BlockSpec((UNIT, 1, local_len, LANES), by_row4),
            pl.BlockSpec((1, 2, unit_len), by_row3),
        ],
        out_shape=[
            jax.ShapeDtypeStruct((UNIT, micro, local_len, LANES), BF16),
            jax.ShapeDtypeStruct((micro, 2, unit_len), F32),
        ],
        compiler_params=params(),
        cost_estimate=cost(attention_flops, 4e6),
    )(q_all, kv_all, seg_queries, seg_keys, place_row)
    ctx_own = exchange(ctx_heads)

    w_out_all = lax.all_gather(w_out, ("seq", "row"), axis=0, tiled=True)
    mixed, normed_ffn, context = pl.pallas_call(
        mix_kernel,
        out_shape=[
            jax.ShapeDtypeStruct((count, width), F32),
            jax.ShapeDtypeStruct((count, width), BF16),
            jax.ShapeDtypeStruct((count, H * HD), BF16),
        ],
        compiler_params=params(),
        cost_estimate=cost(2.0 * count * width * width, 8e6),
    )(ctx_own, w_out_all, flat_tokens, gain_ffn)

    chosen = jnp.any(
        routes.reshape(count, TOPK)[:, :, None] == jnp.arange(LANES, dtype=jnp.int32)[None, None, :],
        axis=1,
    ).astype(BF16)
    dz_own = jnp.concatenate([cotangent.reshape(count, width), chosen], axis=1)
    dz_all = jnp.concatenate([dz_own] + [flip(dz_own, k) for k in (2, 4, 6)], axis=0)
    x_all = jnp.concatenate([normed_ffn] + [flip(normed_ffn, k) for k in (2, 4, 6)], axis=0)

    own_ids = 2 * me + jnp.arange(2, dtype=jnp.int32)
    sib_ids = 2 * (me ^ 1) + jnp.arange(2, dtype=jnp.int32)
    carried = run_experts(sib_ids, x_all, dz_all, router, *sib_weights, None)
    sib_terms = [flip(term, 1) for term in carried[3:]]
    results = run_experts(own_ids, x_all, dz_all, router, *own_weights, carried[:3])
    out_part, dx_part, gg_part = results[:3]
    own_terms = results[3:]

    def give_back(x):
        pieces = x.reshape(4, count, x.shape[1])
        return [pieces[0]] + [flip(pieces[i], 2 * i) for i in (1, 2, 3)]

    dx_pieces = give_back(dx_part)
    gg_pieces = give_back(gg_part)
    gmixed, gbranch, glog, gctx = pl.pallas_call(
        back_kernel,
        out_shape=[
            jax.ShapeDtypeStruct((count, width), F32),
            jax.ShapeDtypeStruct((count, width), BF16),
            jax.ShapeDtypeStruct((count, LANES), BF16),
            jax.ShapeDtypeStruct((UNIT, micro, local_len, LANES), BF16),
        ],
        compiler_params=params(),
        cost_estimate=cost(2.0 * count * width * width, 1.2e7),
    )(*dx_pieces, *gg_pieces, mixed, normed_ffn, dz_own, gain_ffn, router, w_out_all)
    do_heads = exchange(gctx)

    def fixed_q(m):
        return (0, 0)

    def fixed_kv(m):
        return (0, 1)

    if copies > 1:
        key_angles = jnp.arange(length, dtype=jnp.int32).astype(F32)[:, None] * frequency[None, :]
        key_cos = jnp.concatenate([jnp.cos(key_angles)] * 2 + [jnp.ones((length, HD), F32)], axis=1)
        key_sin = jnp.concatenate(
            [-jnp.sin(key_angles), jnp.sin(key_angles), jnp.zeros((length, HD), F32)], axis=1
        )
    else:
        key_cos, key_sin = cosine[:, LANES:], sine[:, LANES:]
    graw_q, graw_kv = pl.pallas_call(
        functools.partial(attention_back_kernel, skip),
        grid=(micro,),
        in_specs=attention_specs
        + [
            pl.BlockSpec((1, 2, unit_len), by_row3),
            pl.BlockSpec((UNIT, 1, local_len, LANES), by_row4),
            pl.BlockSpec((unit_len, LANES), fixed),
            pl.BlockSpec((unit_len, LANES), fixed),
            pl.BlockSpec((length, LANES), fixed),
            pl.BlockSpec((length, LANES), fixed),
        ],
        out_specs=[
            pl.BlockSpec((UNIT, 1, local_len, LANES), by_row4),
            pl.BlockSpec((seq_size, 1, local_len, LANES), by_row4),
        ],
        out_shape=[
            jax.ShapeDtypeStruct((UNIT, micro, local_len, LANES), BF16),
            jax.ShapeDtypeStruct((seq_size, micro, local_len, LANES), BF16),
        ],
        scratch_shapes=[pltpu.VMEM((length, LANES), F32), pltpu.VMEM((length, LANES), F32)],
        compiler_params=params(),
        cost_estimate=cost(2.5 * attention_flops, 8e6),
    )(
        q_all, kv_all, seg_queries, seg_keys, place_row, lse, do_heads,
        cosine[:, :LANES], sine[:, :LANES], key_cos, key_sin,
    )
    if copies > 1:
        graw_kv = lax.psum_scatter(
            graw_kv, "seq", scatter_dimension=0, tiled=True, axis_index_groups=copy_groups
        )
    graw = jnp.concatenate([graw_q, graw_kv], axis=3)
    graw_own = exchange(graw)
    w_heads = lax.all_gather(w_head, "seq", axis=0, axis_index_groups=unit_groups)

    def by_head4(b):
        return (b, 0, 0, 0)

    def by_head3(b):
        return (b, 0, 0)

    grad_input = pl.pallas_call(
        input_kernel,
        grid=(UNIT,),
        in_specs=[
            pl.BlockSpec((1, micro, local_len, 2 * LANES), by_head4),
            pl.BlockSpec((1, width, 2 * LANES), by_head3),
            pl.BlockSpec((count, width), fixed),
            pl.BlockSpec((1, width), fixed),
            pl.BlockSpec((count, width), fixed),
        ],
        out_specs=pl.BlockSpec((count, width), fixed),
        out_shape=jax.ShapeDtypeStruct((count, width), BF16),
        scratch_shapes=[pltpu.VMEM((count, width), F32)],
        compiler_params=params(),
        cost_estimate=cost(2.0 * count * width * 2048, 1e7),
    )(graw_own, w_heads, flat_tokens, gain_attn, gmixed)

    out_pieces = give_back(out_part)
    block_out = mixed
    for piece in out_pieces:
        block_out = block_out + piece.astype(F32)

    def finish_expert(own, sib):
        total = (own.astype(F32) + sib.astype(F32)).astype(BF16)
        lead, rest = total.shape[0], total.shape[2]
        total = total.reshape(lead, copies, UNIT, rows, -1, rest)
        mine = reduce_rows(total, 3).astype(BF16)
        return exchange(mine.transpose(1, 0, 2, 3)).reshape(E, -1, rest).astype(F32)

    grad_gate, grad_up, grad_down = [
        finish_expert(own, sib) for own, sib in zip(own_terms, sib_terms)
    ]
    head_term = jnp.einsum(
        "nd,nh->dh",
        normed_all.reshape(UNIT * count, width),
        graw.reshape(UNIT * count, 2 * LANES),
        preferred_element_type=F32,
    ).astype(BF16)
    head_term = head_term.reshape(copies, UNIT, rows, part, 2 * LANES)
    head_grad = exchange(reduce_rows(head_term, 2).astype(BF16)).astype(F32)
    grad_query = head_grad[:, :, :LANES].transpose(1, 0, 2).reshape(part, H * HD)
    grad_key = head_grad[:, :, LANES : LANES + HD].transpose(1, 0, 2).reshape(part, KVH * HD)
    grad_value = head_grad[:, :, LANES + HD :].transpose(1, 0, 2).reshape(part, KVH * HD)

    out_term = jnp.einsum("nh,nd->hd", context, gbranch, preferred_element_type=F32)
    router_term = jnp.einsum("nd,ne->de", normed_ffn, glog, preferred_element_type=F32)
    term = jnp.concatenate([out_term, router_term], axis=1).astype(BF16)
    term = term.reshape(copies, UNIT, rows, part, width + LANES)
    if copies > 1:
        term = term.transpose(1, 0, 2, 3, 4)
        term = jnp.sum(exchange(term).astype(F32).reshape(UNIT, copies, rows, part, -1), axis=0)
        term = term[:, None].astype(BF16)
    else:
        term = jnp.sum(exchange(term[0]).astype(F32), axis=0)[None, None].astype(BF16)
    term = reduce_rows(term, 2)[0]
    grad_out = term[:, :width]
    grad_router = term[:, width : width + E]

    attn_weights = jnp.concatenate([w_query, w_key, w_value], axis=1).astype(F32)
    attn_grads = jnp.concatenate([grad_query, grad_key, grad_value], axis=1)
    grad_norm_attn = jnp.sum(attn_weights * attn_grads, axis=1) / norm_attn.astype(F32)
    grad_norm_ffn = (
        jnp.sum(w_gate.astype(F32) * grad_gate, axis=(0, 2))
        + jnp.sum(w_up.astype(F32) * grad_up, axis=(0, 2))
        + jnp.sum(w_router.astype(F32) * grad_router, axis=1)
    ) / norm_ffn.astype(F32)
    return (
        block_out.astype(BF16).reshape(tokens.shape),
        grad_input.reshape(tokens.shape),
        grad_norm_attn,
        grad_query,
        grad_key,
        grad_value,
        grad_out,
        grad_norm_ffn,
        grad_router,
        grad_gate,
        grad_up,
        grad_down,
    )


def solution(mesh):
    both = ("seq", "row")
    body = functools.partial(shards, mesh.shape["seq"] // UNIT, rows=mesh.shape["row"])
    return jax.shard_map(
        body,
        mesh=mesh,
        in_specs=(
            P("row", "seq", None),
            P("row", None),
            P("row", "seq", None),
            P("row", "seq", None),
            P(both),
            P(both, None),
            P(both, None),
            P(both, None),
            P(both, None),
            P(both),
            P(both, None),
            P(None, both, None),
            P(None, both, None),
            P(None, both, None),
        ),
        out_specs=(
            P("row", "seq", None),
            P("row", "seq", None),
            P(both),
            P(both, None),
            P(both, None),
            P(both, None),
            P(both, None),
            P(both),
            P(both, None),
            P(None, both, None),
            P(None, both, None),
            P(None, both, None),
        ),
        check_vma=False,
    )
```

```python
import functools

import jax
import jax.numpy as jnp
from jax import lax
from jax.experimental import pallas as pl
from jax.experimental.pallas import tpu as pltpu
from jax.sharding import PartitionSpec as P

H = 16
KVH = 8
TOPK = 8
HD = 64
E = 16
UNIT = 8
LANES = 128
QBLOCK = 256
PIECES = 4
ROWS_IN = 32
ROWS_OUT = 16

EPS = 1e-05
BASE = 10000.0
NEGATIVE = -1e30
F32 = jnp.float32
BF16 = jnp.bfloat16
VMEM_LIMIT = 60 * 1024 * 1024


def dot_nn(left, right):
    return lax.dot_general(left, right, (((1,), (0,)), ((), ())), preferred_element_type=F32)


def dot_nt(left, right):
    return lax.dot_general(left, right, (((1,), (1,)), ((), ())), preferred_element_type=F32)


def params(**kw):
    return pltpu.CompilerParams(vmem_limit_bytes=VMEM_LIMIT, **kw)


def cost(flops, nbytes):
    return pl.CostEstimate(flops=int(flops), bytes_accessed=int(nbytes), transcendentals=0)


def neighbours(seq):
    core = seq % 2
    chip = (seq // 2) % 4
    base = seq - seq % UNIT

    def at(other, same=True):
        return base + 2 * other + (core if same else 1 - core)

    across = chip + 1 - 2 * (chip % 2)
    along = (chip + 2) % 4
    return at(across), at(along), at(3 - chip), at(chip, False)


def greet(targets):
    barrier = pltpu.get_barrier_semaphore()
    for target in targets:
        pl.semaphore_signal(
            barrier, inc=1, device_id=target, device_id_type=pl.DeviceIdType.MESH
        )
    pl.semaphore_wait(barrier, len(targets))


class Pushes:
    def __init__(self, send, recv):
        self.send, self.recv, self.used = send, recv, 0

    def start(self, source, target, device):
        n = self.used
        self.used += 1
        copy = pltpu.make_async_remote_copy(
            src_ref=source,
            dst_ref=target,
            send_sem=self.send.at[n],
            recv_sem=self.recv.at[n],
            device_id=device,
            device_id_type=pl.DeviceIdType.MESH,
        )
        copy.start()
        return copy


class Bounce:
    def __init__(self, source, middle, target, sems):
        self.inward = pltpu.make_async_copy(source, middle, sems.at[0])
        self.outward = pltpu.make_async_copy(middle, target, sems.at[1])
        self.inward.start()

    def turn(self):
        self.inward.wait()
        self.outward.start()

    def wait(self):
        self.outward.wait()


def begin_kernel(
    rows, packed0, packed1, head_ref, wout_ref, mine0, mine1, head_all, wout_all,
    head_mine, own0, own1, own2, send, recv, local,
):
    seq, row = lax.axis_index("seq"), lax.axis_index("row")
    me = seq % UNIT
    base = seq - me
    unit = [(me + k) % UNIT for k in range(1, UNIT)]
    column = [(row + k) % rows for k in range(1, rows)]
    greet([{"seq": base + b} for b in unit] + [{"row": r} for r in column])
    pushes = Pushes(send, recv)
    first = pltpu.make_async_copy(head_ref.at[me], head_mine.at[me], local.at[3, 0])
    first.start()
    heads = [pushes.start(head_ref.at[b], head_mine.at[me], {"seq": base + b}) for b in unit]
    others = [pushes.start(wout_ref, wout_all.at[row], {"row": r}) for r in column]
    for source, target in ((packed0, mine0), (packed1, mine1)):
        others += [pushes.start(source.at[b], target.at[me], {"seq": base + b}) for b in unit]
    own = [
        Bounce(packed0.at[me], own0, mine0.at[me], local.at[0]),
        Bounce(packed1.at[me], own1, mine1.at[me], local.at[1]),
        Bounce(wout_ref, own2, wout_all.at[row], local.at[2]),
    ]
    for copy in own:
        copy.turn()
    first.wait()
    for copy in heads:
        copy.wait_recv()
    last = pltpu.make_async_copy(head_mine, head_all.at[row], local.at[3, 1])
    last.start()
    others += [pushes.start(head_mine, head_all.at[row], {"row": r}) for r in column]
    for copy in heads:
        copy.wait_send()
    for copy in own + [last]:
        copy.wait()
    for copy in others:
        copy.wait()


def begin(rows, packed0, packed1, head_part, w_out):
    any_spec = pl.BlockSpec(memory_space=pl.ANY)
    count = 3 * (UNIT - 1) + 2 * (rows - 1)
    like = jax.ShapeDtypeStruct
    return pl.pallas_call(
        functools.partial(begin_kernel, rows),
        in_specs=[any_spec] * 4,
        out_specs=[any_spec] * 4,
        out_shape=[
            like(packed0.shape, BF16),
            like(packed1.shape, BF16),
            like((rows,) + head_part.shape, BF16),
            like((rows,) + w_out.shape, BF16),
        ],
        scratch_shapes=[
            pltpu.VMEM(head_part.shape, BF16),
            pltpu.VMEM(packed0.shape[1:], BF16),
            pltpu.VMEM(packed0.shape[1:], BF16),
            pltpu.VMEM(w_out.shape, BF16),
            pltpu.SemaphoreType.DMA((count,)),
            pltpu.SemaphoreType.DMA((count,)),
            pltpu.SemaphoreType.DMA((4, 2)),
        ],
        compiler_params=pltpu.CompilerParams(collective_id=0, has_side_effects=True),
        cost_estimate=cost(1, 2e7),
    )(packed0, packed1, head_part, w_out)


def unit_gather_kernel(sources, *refs):
    ins, outs = refs[:sources], refs[sources : 2 * sources]
    middles = refs[2 * sources : 3 * sources]
    send, recv, local = refs[3 * sources :]
    seq = lax.axis_index("seq")
    me = seq % UNIT
    base = seq - me
    across, along, _, twin = neighbours(seq)
    a, b, t = across - base, along - base, twin - base
    d = UNIT - 1 - me + 2 * (me % 2) - 1
    greet([{"seq": across}, {"seq": along}, {"seq": twin}])
    pushes = Pushes(send, recv)
    own, done, stage = [], [], []
    for n, (source, target) in enumerate(zip(ins, outs)):
        half = source.shape[0] // 2
        halves = [pl.ds(0, half), pl.ds(half, half)]
        own.append(Bounce(source, middles[n], target.at[me], local.at[n]))

        def part(device, h, source=source, target=target, halves=halves):
            return pushes.start(
                source.at[halves[h]], target.at[me, halves[h]], {"seq": device}
            )

        xa, yb = part(across, 0), part(along, 1)
        xb, ya = part(across, 1), part(along, 0)
        done.append(pushes.start(source, target.at[me], {"seq": twin}))
        stage.append((target, halves, xa, yb, xb, ya))
    for copy in own:
        copy.turn()
    for target, halves, xa, yb, xb, ya in stage:

        def pass_on(slot, h, device, target=target, halves=halves):
            view = target.at[slot, halves[h]]
            return pushes.start(view, view, {"seq": device})

        xa.wait_recv()
        da = pass_on(a, 0, along)
        done.append(pass_on(a, 0, twin))
        yb.wait_recv()
        db = pass_on(b, 1, across)
        done.append(pass_on(b, 1, twin))
        xb.wait_recv()
        done.append(pass_on(a, 1, twin))
        ya.wait_recv()
        done.append(pass_on(b, 0, twin))
        da.wait_recv()
        done.append(pass_on(d, 0, twin))
        db.wait_recv()
        done.append(pass_on(d, 1, twin))
        for copy in (xa, yb, xb, ya, da, db):
            copy.wait_send()
    for copy in own + done:
        copy.wait()


def unit_gather(sources, collective):
    any_spec = pl.BlockSpec(memory_space=pl.ANY)
    n = len(sources)
    return pl.pallas_call(
        functools.partial(unit_gather_kernel, n),
        in_specs=[any_spec] * n,
        out_specs=[any_spec] * n,
        out_shape=[jax.ShapeDtypeStruct((UNIT,) + x.shape, x.dtype) for x in sources],
        scratch_shapes=[pltpu.VMEM(x.shape, x.dtype) for x in sources]
        + [
            pltpu.SemaphoreType.DMA((13 * n,)),
            pltpu.SemaphoreType.DMA((13 * n,)),
            pltpu.SemaphoreType.DMA((n, 2)),
        ],
        compiler_params=params(collective_id=collective, has_side_effects=True),
        cost_estimate=cost(1, 8e7),
    )(*sources)


def core_gather_kernel(
    source, weights, z0, z1, z2, z3, target, flipped, z_all, middle, z_middle, send, recv, local
):
    across, along, _, twin = neighbours(lax.axis_index("seq"))
    greet([{"seq": across}, {"seq": along}, {"seq": twin}])
    pushes = Pushes(send, recv)
    half = source.shape[0] // 2
    halves = [pl.ds(0, half), pl.ds(half, half)]

    def part(device, slot, h):
        return pushes.start(source.at[halves[h]], target.at[slot, halves[h]], {"seq": device})

    def pass_on(slot, h, device):
        return pushes.start(
            target.at[slot, halves[h]], target.at[3, halves[h]], {"seq": device}
        )

    xa, yb = part(across, 1, 0), part(along, 2, 1)
    xb, ya = part(across, 1, 1), part(along, 2, 0)
    turned = pushes.start(weights, flipped, {"seq": twin})
    own = [Bounce(source, middle, target.at[0], local.at[0])]
    for n, piece in enumerate((z0, z1, z2, z3)):
        own.append(Bounce(piece, z_middle.at[n], z_all.at[n], local.at[n + 1]))
    for copy in own:
        copy.turn()
    xa.wait_recv()
    da = pass_on(1, 0, along)
    yb.wait_recv()
    db = pass_on(2, 1, across)
    for copy in (xb, ya, da, db):
        copy.wait_recv()
    for copy in (xa, yb, xb, ya, da, db):
        copy.wait_send()
    turned.wait()
    for copy in own:
        copy.wait()


def core_gather(source, weights, z_pieces, collective):
    any_spec = pl.BlockSpec(memory_space=pl.ANY)
    like = jax.ShapeDtypeStruct
    return pl.pallas_call(
        core_gather_kernel,
        in_specs=[any_spec] * 6,
        out_specs=[any_spec] * 3,
        out_shape=[
            like((4,) + source.shape, source.dtype),
            like(weights.shape, weights.dtype),
            like((4,) + z_pieces[0].shape, z_pieces[0].dtype),
        ],
        scratch_shapes=[
            pltpu.VMEM(source.shape, source.dtype),
            pltpu.VMEM((4,) + z_pieces[0].shape, z_pieces[0].dtype),
            pltpu.SemaphoreType.DMA((7,)),
            pltpu.SemaphoreType.DMA((7,)),
            pltpu.SemaphoreType.DMA((5, 2)),
        ],
        compiler_params=params(collective_id=collective, has_side_effects=True),
        cost_estimate=cost(1, 8e7),
    )(source, weights, *z_pieces)


def finish_kernel(
    rows, graw_ref, head_ref, out_ref, graw_own, head_fin, out_fin,
    head_col, head_sum, out_sum, out_col, own_raw, send, recv, local,
):
    seq, row = lax.axis_index("seq"), lax.axis_index("row")
    me = seq % UNIT
    base = seq - me
    unit = [(me + k) % UNIT for k in range(1, UNIT)]
    column = [(row + k) % rows for k in range(1, rows)]
    greet([{"seq": base + b} for b in unit] + [{"row": r} for r in column])
    pushes = Pushes(send, recv)
    first = pltpu.make_async_copy(head_ref.at[row], head_col.at[row], local.at[0, 0])
    first.start()
    second = Bounce(graw_ref.at[me], own_raw, graw_own.at[me], local.at[1])
    heads = [pushes.start(head_ref.at[r], head_col.at[row], {"row": r}) for r in column]
    others = [pushes.start(graw_ref.at[b], graw_own.at[me], {"seq": base + b}) for b in unit]
    total = out_ref[0].astype(F32)
    for b in range(1, UNIT):
        total = total + out_ref[b].astype(F32)
    out_sum[...] = total.astype(BF16)
    second.turn()
    third = pltpu.make_async_copy(out_sum.at[row], out_col.at[row], local.at[2, 0])
    third.start()
    outs = [pushes.start(out_sum.at[r], out_col.at[row], {"row": r}) for r in column]
    first.wait()
    for copy in heads:
        copy.wait_recv()
    total = head_col[0].astype(F32)
    for r in range(1, rows):
        total = total + head_col[r].astype(F32)
    head_sum[...] = total.astype(BF16)
    fourth = pltpu.make_async_copy(head_sum.at[me], head_fin.at[me], local.at[3, 0])
    fourth.start()
    others += [pushes.start(head_sum.at[b], head_fin.at[me], {"seq": base + b}) for b in unit]
    third.wait()
    for copy in outs:
        copy.wait_recv()
    total = out_col[0].astype(F32)
    for r in range(1, rows):
        total = total + out_col[r].astype(F32)
    out_fin[...] = total
    for copy in heads + outs:
        copy.wait_send()
    second.wait()
    fourth.wait()
    for copy in others:
        copy.wait()


def finish(rows, graw, head_term, out_term, collective):
    any_spec = pl.BlockSpec(memory_space=pl.ANY)
    vmem_spec = pl.BlockSpec(memory_space=pltpu.VMEM)
    like = jax.ShapeDtypeStruct
    count = 2 * (UNIT - 1) + 2 * (rows - 1)
    return pl.pallas_call(
        functools.partial(finish_kernel, rows),
        in_specs=[any_spec, any_spec, vmem_spec],
        out_specs=[any_spec, any_spec, vmem_spec],
        out_shape=[
            like(graw.shape, BF16),
            like(head_term.shape[1:], BF16),
            like(out_term.shape[2:], F32),
        ],
        scratch_shapes=[
            pltpu.VMEM(head_term.shape, BF16),
            pltpu.VMEM(head_term.shape[1:], BF16),
            pltpu.VMEM(out_term.shape[1:], BF16),
            pltpu.VMEM(out_term.shape[1:], BF16),
            pltpu.VMEM(graw.shape[1:], BF16),
            pltpu.SemaphoreType.DMA((count,)),
            pltpu.SemaphoreType.DMA((count,)),
            pltpu.SemaphoreType.DMA((4, 2)),
        ],
        compiler_params=params(collective_id=collective, has_side_effects=True),
        cost_estimate=cost(1, 4e7),
    )(graw, head_term, out_term)


def give_back_kernel(sources, *refs):
    ins, outs = refs[:sources], refs[sources : 2 * sources]
    send, recv = refs[2 * sources :]
    peers = neighbours(lax.axis_index("seq"))[:3]
    greet([{"seq": peer} for peer in peers])
    pushes = Pushes(send, recv)
    copies = []
    for source, target in zip(ins, outs):
        for n in (2, 0, 1):
            copies.append(pushes.start(source.at[n + 1], target.at[n], {"seq": peers[n]}))
    for copy in copies:
        copy.wait()


def give_back(sources, collective):
    any_spec = pl.BlockSpec(memory_space=pl.ANY)
    n = len(sources)
    return pl.pallas_call(
        functools.partial(give_back_kernel, n),
        in_specs=[any_spec] * n,
        out_specs=[any_spec] * n,
        out_shape=[jax.ShapeDtypeStruct((3,) + x.shape[1:], x.dtype) for x in sources],
        scratch_shapes=[pltpu.SemaphoreType.DMA((3 * n,)), pltpu.SemaphoreType.DMA((3 * n,))],
        compiler_params=pltpu.CompilerParams(collective_id=collective, has_side_effects=True),
        cost_estimate=cost(1, 1e8),
    )(*sources)


def lane_iota(shape):
    return lax.broadcasted_iota(jnp.int32, shape, len(shape) - 1)


def turn(u, cosine, sine):
    low_half = lane_iota(u.shape) % HD < HD // 2
    partner = jnp.where(
        low_half, pltpu.roll(u, LANES - HD // 2, u.ndim - 1), pltpu.roll(u, HD // 2, u.ndim - 1)
    )
    return u * cosine + partner * sine


def project_kernel(tok_ref, gain_ref, w_ref, cos_ref, sin_ref, normed_ref, q_ref, kv_ref):
    count = q_ref.shape[1]
    width = w_ref.shape[0]
    x = tok_ref[...].reshape(count, width).astype(F32)
    inverse = lax.rsqrt(jnp.mean(x * x, axis=-1, keepdims=True) + EPS)
    normed = (x * inverse * gain_ref[...]).astype(BF16)
    normed_ref[...] = normed.reshape(normed_ref.shape)
    raw = dot_nn(normed, w_ref[...])
    cosine, sine = cos_ref[...], sin_ref[...]
    q = turn(raw[:, :LANES], cosine[:, :LANES], sine[:, :LANES]).astype(BF16)
    q_ref[0] = (q.astype(F32) * HD**-0.5).astype(BF16)
    kv_ref[0] = turn(raw[:, LANES:], cosine[:, LANES:], sine[:, LANES:]).astype(BF16)


def pair_keys(kv):
    kv = kv.astype(F32)
    rolled = pltpu.roll(kv, HD, 1)
    low = lane_iota(kv.shape) < HD
    return jnp.where(low, kv, rolled), jnp.where(low, rolled, kv)


def bias_block(seg_col, seg_row, q_places, first, length):
    key_places = lax.broadcasted_iota(jnp.int32, (length, q_places.shape[1]), 0)
    allowed = (seg_col[:length] == seg_row) & (key_places <= q_places)
    return jnp.where(allowed, 0.0, NEGATIVE)


def attention_kernel(skip, q_ref, kv_ref, segq_ref, segk_ref, place_ref, ctx_ref, lse_ref):
    length = kv_ref.shape[1]
    queries = q_ref.shape[1]
    kk, vv = pair_keys(kv_ref[0])
    v_t = vv.T.astype(BF16)[:HD]
    kk = kk.astype(BF16)
    seg_col = jnp.broadcast_to(segk_ref[0], (8, length)).T[:, :1]
    for block in range(queries // QBLOCK):
        here = slice(block * QBLOCK, (block + 1) * QBLOCK)
        keys = (block + 1) * QBLOCK if skip else length
        bias = bias_block(seg_col, segq_ref[0][:, here], place_ref[:, here], 0, keys)
        q = q_ref[0, here, :]
        low = lane_iota(q.shape) < HD
        parts = []
        for head in range(2):
            mine = jnp.where(low == (head == 0), q, jnp.zeros_like(q))
            scores = dot_nt(kk[:keys], mine) + bias
            top = jnp.max(scores, axis=0, keepdims=True)
            weight = jnp.exp(scores - top)
            total = jnp.sum(weight, axis=0, keepdims=True)
            prob = (weight * (1.0 / total)).astype(BF16)
            parts.append(dot_nn(v_t[:, :keys], prob))
            lse_ref[0, head : head + 1, here] = top + jnp.log(total)
        ctx = jnp.concatenate(parts, axis=0).T.astype(BF16)
        per = QBLOCK // LANES
        ctx_ref[block * per : (block + 1) * per, 0] = ctx.reshape(per, LANES, LANES)


def attention_back_kernel(
    skip, q_ref, kv_ref, segq_ref, segk_ref, place_ref, lse_ref, do_ref, cosq_ref, sinq_ref,
    coskv_ref, sinkv_ref, normed_ref, graw_ref, term_ref, dk_acc, dv_acc, term_acc,
):
    length = kv_ref.shape[1]
    queries = q_ref.shape[1]
    kk, vv = pair_keys(kv_ref[0])
    k_t = kk.T.astype(BF16)[:HD]
    kk = kk.astype(BF16)
    vv = vv.astype(BF16)
    seg_col = jnp.broadcast_to(segk_ref[0], (8, length)).T[:, :1]
    dk_acc[...] = jnp.zeros_like(dk_acc)
    dv_acc[...] = jnp.zeros_like(dv_acc)
    per = QBLOCK // LANES
    for block in range(queries // QBLOCK):
        here = slice(block * QBLOCK, (block + 1) * QBLOCK)
        keys = (block + 1) * QBLOCK if skip else length
        bias = bias_block(seg_col, segq_ref[0][:, here], place_ref[:, here], 0, keys)
        q = q_ref[0, here, :]
        do = do_ref[block * per : (block + 1) * per, 0].reshape(QBLOCK, LANES)
        low = lane_iota(q.shape) < HD
        parts = []
        for head in range(2):
            pick = low == (head == 0)
            mine = jnp.where(pick, q, jnp.zeros_like(q))
            mine_do = jnp.where(pick, do, jnp.zeros_like(do))
            scores = dot_nt(kk[:keys], mine) + bias
            weight = jnp.exp(scores - lse_ref[0, head : head + 1, here])
            product = dot_nt(vv[:keys], mine_do)
            delta = jnp.sum(weight * product, axis=0, keepdims=True)
            grad_scores = (weight * (product - delta)).astype(BF16)
            dv_acc[:keys] += dot_nn(weight.astype(BF16), mine_do)
            dk_acc[:keys] += dot_nn(grad_scores, mine)
            parts.append(dot_nn(k_t[:, :keys], grad_scores))
        dq = jnp.concatenate(parts, axis=0).T * HD**-0.5
        dq = turn(dq, cosq_ref[here, :], -sinq_ref[here, :]).astype(BF16)
        graw_ref[block * per : (block + 1) * per, 0, :, :LANES] = dq.reshape(per, LANES, LANES)
    dk = dk_acc[...]
    dv = dv_acc[...]
    dk = dk + pltpu.roll(dk, HD, 1)
    dv = dv + pltpu.roll(dv, HD, 1)
    gkv = jnp.where(lane_iota(dk.shape) < HD, dk, dv)
    gkv = turn(gkv, coskv_ref[...], -sinkv_ref[...]).astype(BF16)
    graw_ref[:, 0, :, LANES:] = gkv.reshape(length // LANES, LANES, LANES)
    if skip:
        normed_t = normed_ref[...].reshape(queries, -1).T
        term = dot_nn(normed_t, graw_ref[...].reshape(queries, 2 * LANES))
        m = pl.program_id(0)

        @pl.when(m == 0)
        def _():
            term_acc[...] = term

        @pl.when(m > 0)
        def _():
            term_acc[...] += term

        @pl.when(m == pl.num_programs(0) - 1)
        def _():
            for b in range(UNIT):
                for r in range(PIECES):
                    at = (b * PIECES + r) * ROWS_IN
                    term_ref[r, b] = term_acc[at : at + ROWS_IN].astype(BF16)


def mix_kernel(ctx_ref, w_ref, tok_ref, gain_ref, mixed_ref, normed_ref, ctx_out):
    count, width = tok_ref.shape
    for b in range(UNIT):
        ctx_out[:, b * LANES : (b + 1) * LANES] = ctx_ref[b].reshape(count, LANES)
    mixed = tok_ref[...].astype(F32) + dot_nn(ctx_out[...], w_ref[...])
    mixed_ref[...] = mixed
    inverse = lax.rsqrt(jnp.mean(mixed * mixed, axis=-1, keepdims=True) + EPS)
    normed_ref[...] = (mixed * inverse * gain_ref[...]).astype(BF16)


def soft_gates(normed, router, chosen):
    logits = jnp.where(chosen > 0, dot_nn(normed, router), NEGATIVE)
    top = jnp.max(logits, axis=-1, keepdims=True)
    weight = jnp.where(chosen > 0, jnp.exp(logits - top), 0.0)
    return weight / jnp.sum(weight, axis=-1, keepdims=True)


def expert_kernel(first, gid_ref, x_ref, dz_ref, wr_ref, w_ref, *rest):
    if first:
        out_ref, dx_ref, gg_ref, dw_ref, wg, wu, wd, ag, au, ad = rest
    else:
        oin_ref, dxin_ref, ggin_ref, out_ref, dx_ref, gg_ref, dw_ref, wg, wu, wd, ag, au, ad = rest
    t = pl.program_id(0)
    last_t = pl.num_programs(0) - 1
    width = x_ref.shape[1]
    half = w_ref.shape[3]
    x = x_ref[...]
    dz = dz_ref[:, :width]

    @pl.when(t == 0)
    def _():
        for r in range(PIECES):
            for b in range(UNIT):
                at = (b * PIECES + r) * ROWS_IN
                low = (b * PIECES + r) * ROWS_OUT
                wg[at : at + ROWS_IN] = w_ref[r, b, :ROWS_IN]
                wu[at : at + ROWS_IN] = w_ref[r, b, ROWS_IN : 2 * ROWS_IN]
                for c in range(2):
                    start = 2 * ROWS_IN + c * ROWS_OUT
                    wd[low : low + ROWS_OUT, c * half : (c + 1) * half] = w_ref[
                        r, b, start : start + ROWS_OUT
                    ]

    gates = soft_gates(x, wr_ref[...], dz_ref[:, width:].astype(F32))
    mine = lane_iota(gates.shape) == gid_ref[0]
    gate = jnp.sum(jnp.where(mine, gates, 0.0), axis=1, keepdims=True)
    gate_act = dot_nn(x, wg[...])
    up_act = dot_nn(x, wu[...])
    back = dot_nt(dz, wd[...])
    sig = 1.0 / (1.0 + jnp.exp(-gate_act))
    silu = gate_act * sig
    hidden = silu * up_act
    ggterm = jnp.where(mine, jnp.sum(hidden * back, axis=1, keepdims=True), 0.0)
    grad_hidden = back * gate
    grad_gate = (grad_hidden * up_act * (sig * (1.0 + gate_act * (1.0 - sig)))).astype(BF16)
    grad_up = (grad_hidden * silu).astype(BF16)
    gated = (hidden * gate).astype(BF16)
    out = dot_nn(gated, wd[...])
    dx = dot_nt(grad_gate, wg[...]) + dot_nt(grad_up, wu[...])
    if first:
        out_ref[...] = out.astype(out_ref.dtype)
        dx_ref[...] = dx.astype(dx_ref.dtype)
        gg_ref[...] = ggterm
    else:
        out_ref[...] = (oin_ref[...] + out).astype(out_ref.dtype)
        dx_ref[...] = (dxin_ref[...] + dx).astype(dx_ref.dtype)
        gg_ref[...] = ggin_ref[...] + ggterm
    x_turned = x.T
    term_gate = dot_nn(x_turned, grad_gate)
    term_up = dot_nn(x_turned, grad_up)
    term_down = dot_nn(gated.T, dz)

    @pl.when(t == 0)
    def _():
        ag[...] = term_gate
        au[...] = term_up
        ad[...] = term_down

    @pl.when(t > 0)
    def _():
        ag[...] += term_gate
        au[...] += term_up
        ad[...] += term_down

    @pl.when(t == last_t)
    def _():
        for r in range(PIECES):
            for b in range(UNIT):
                at = (b * PIECES + r) * ROWS_IN
                low = (b * PIECES + r) * ROWS_OUT
                dw_ref[r, b, :ROWS_IN] = ag[at : at + ROWS_IN].astype(BF16)
                dw_ref[r, b, ROWS_IN : 2 * ROWS_IN] = au[at : at + ROWS_IN].astype(BF16)
                for c in range(2):
                    start = 2 * ROWS_IN + c * ROWS_OUT
                    dw_ref[r, b, start : start + ROWS_OUT] = ad[
                        low : low + ROWS_OUT, c * half : (c + 1) * half
                    ].astype(BF16)


def run_expert(gid, x, dz, router, packed, carried, last):
    tokens, width = x.shape
    hidden = packed.shape[3]
    tile = tokens // 4
    tiles = tokens // tile
    first = carried is None
    kind = BF16 if last else F32

    def whole(t):
        return (0, 0)

    def by_token(t):
        return (t, 0)

    def packed_map(t):
        return (0, 0, 0, 0)

    in_specs = [
        pl.BlockSpec(memory_space=pltpu.SMEM),
        pl.BlockSpec((tile, width), by_token),
        pl.BlockSpec((tile, width + LANES), by_token),
        pl.BlockSpec((width, LANES), whole),
        pl.BlockSpec(packed.shape, packed_map),
    ]
    args = [gid, x, dz, router, packed]
    if not first:
        in_specs += [
            pl.BlockSpec((tile, width), by_token),
            pl.BlockSpec((tile, width), by_token),
            pl.BlockSpec((tile, LANES), by_token),
        ]
        args += list(carried)
    return pl.pallas_call(
        functools.partial(expert_kernel, first),
        grid=(tiles,),
        in_specs=in_specs,
        out_specs=[
            pl.BlockSpec((tile, width), by_token),
            pl.BlockSpec((tile, width), by_token),
            pl.BlockSpec((tile, LANES), by_token),
            pl.BlockSpec(packed.shape, packed_map),
        ],
        out_shape=[
            jax.ShapeDtypeStruct((tokens, width), kind),
            jax.ShapeDtypeStruct((tokens, width), kind),
            jax.ShapeDtypeStruct((tokens, LANES), F32),
            jax.ShapeDtypeStruct(packed.shape, BF16),
        ],
        scratch_shapes=[
            pltpu.VMEM((width, hidden), BF16),
            pltpu.VMEM((width, hidden), BF16),
            pltpu.VMEM((hidden, width), BF16),
            pltpu.VMEM((width, hidden), F32),
            pltpu.VMEM((width, hidden), F32),
            pltpu.VMEM((hidden, width), F32),
        ],
        compiler_params=params(),
        cost_estimate=cost(36.0 * tokens * width * hidden, 2e7),
    )(*args)


def back_kernel(
    p0, parts, g0, gparts, mixed_ref, normed_ref, dz_ref, gain_ref, wr_ref, w_ref,
    gmixed_ref, gbranch_ref, glog_ref, gctx_ref,
):
    count, width = mixed_ref.shape
    dz_all = dz_ref[...]
    dz = dz_all[:, :width].astype(F32)
    gates = soft_gates(normed_ref[...], wr_ref[...], dz_all[:, width:].astype(F32))
    grad_gates = g0[0] + gparts[0] + gparts[1] + gparts[2]
    centre = jnp.sum(gates * grad_gates, axis=-1, keepdims=True)
    glog = (gates * (grad_gates - centre)).astype(BF16)
    glog_ref[...] = glog
    dy = p0[0].astype(F32)
    for n in range(3):
        dy = dy + parts[n].astype(F32)
    dy = dy + dot_nt(glog, wr_ref[...])
    v = mixed_ref[...]
    inverse = lax.rsqrt(jnp.mean(v * v, axis=-1, keepdims=True) + EPS)
    scaled = dy * gain_ref[...]
    mean = jnp.mean(scaled * v, axis=-1, keepdims=True)
    gmixed = dz + scaled * inverse - v * (inverse * inverse * inverse * mean)
    gmixed_ref[...] = gmixed
    gbranch = gmixed.astype(BF16)
    gbranch_ref[...] = gbranch
    gctx = dot_nt(gbranch, w_ref[...]).astype(BF16)
    for b in range(UNIT):
        gctx_ref[b] = gctx[:, b * LANES : (b + 1) * LANES].reshape(gctx_ref.shape[1:])


def input_kernel(graw_ref, w_ref, tok_ref, gain_ref, gmixed_ref, gin_ref, acc):
    b = pl.program_id(0)
    count, width = tok_ref.shape
    term = dot_nt(graw_ref[0].reshape(count, 2 * LANES), w_ref[0])

    @pl.when(b == 0)
    def _():
        acc[...] = term

    @pl.when(b > 0)
    def _():
        acc[...] += term

    @pl.when(b == pl.num_programs(0) - 1)
    def _():
        v = tok_ref[...].astype(F32)
        inverse = lax.rsqrt(jnp.mean(v * v, axis=-1, keepdims=True) + EPS)
        scaled = acc[...] * gain_ref[...]
        mean = jnp.mean(scaled * v, axis=-1, keepdims=True)
        grad = gmixed_ref[...] + scaled * inverse - v * (inverse * inverse * inverse * mean)
        gin_ref[...] = grad.astype(BF16)


def shards(
    copies, tokens, segments, routes, cotangent, norm_attn, w_query, w_key, w_value, w_out, norm_ffn,
    w_router, w_gate, w_up, w_down, rows,
):
    micro, local_len, width = tokens.shape
    length = segments.shape[1]
    count = micro * local_len
    unit_len = UNIT * local_len
    part = w_query.shape[0]
    hidden = w_gate.shape[2]
    seq_size = copies * UNIT
    seq = lax.axis_index("seq")
    row = lax.axis_index("row")
    unit = seq // UNIT
    me = seq % UNIT
    unit_groups = None
    copy_groups = None
    if copies > 1:
        unit_groups = [[a * UNIT + b for b in range(UNIT)] for a in range(copies)]
        copy_groups = [[a * UNIT + b for a in range(copies)] for b in range(UNIT)]

    def exchange(x):
        return lax.all_to_all(x, "seq", 0, 0, tiled=True, axis_index_groups=unit_groups)

    def flip(x, k):
        return lax.ppermute(x, "seq", [(s, s ^ k) for s in range(seq_size)])

    flat_tokens = tokens.reshape(count, width)

    def wait_for(x, *others):
        return lax.optimization_barrier((x,) + others)[0]

    small = jnp.concatenate(
        [
            norm_attn[:, None],
            norm_ffn[:, None],
            w_router,
            jnp.zeros((part, LANES - 2 - E), BF16),
        ],
        axis=1,
    )
    head_part = jnp.concatenate(
        [
            w_query.reshape(part, UNIT, 2 * HD),
            w_key.reshape(part, UNIT, HD),
            w_value.reshape(part, UNIT, HD),
            jnp.broadcast_to(small[:, None], (part, UNIT, LANES)),
        ],
        axis=2,
    ).transpose(1, 0, 2)

    down_halves = w_down.reshape(E, -1, 2, hidden).transpose(0, 2, 1, 3).reshape(E, part, hidden)
    packed_part = jnp.concatenate([w_gate, w_up, down_halves], axis=1)
    packed_part = packed_part.reshape(UNIT, E // UNIT, 3 * part, hidden).transpose(1, 0, 2, 3)
    *packed_mine, heads_all, w_out_rows = begin(
        rows, packed_part[0], packed_part[1], head_part, w_out
    )

    if copies > 1:
        heads_all = lax.all_gather(heads_all, "seq", axis=0, axis_index_groups=copy_groups)
        w_out_rows = lax.all_gather(w_out_rows, "seq", axis=0, axis_index_groups=copy_groups)
    else:
        heads_all = heads_all[None]
        w_out_rows = w_out_rows[None]
    heads_all = heads_all.transpose(0, 2, 1, 3, 4).reshape(width, 4 * HD + LANES)
    w_head = heads_all[:, : 4 * HD]
    small = heads_all[:, 4 * HD :]
    gain_attn = small[:, 0].astype(F32)[None]
    gain_ffn = small[:, 1].astype(F32)[None]
    router = jnp.concatenate([small[:, 2 : 2 + E], jnp.zeros((width, LANES - E), BF16)], axis=1)

    def gather_packed(x):
        x = lax.all_gather(x, "row", axis=0)
        if copies > 1:
            x = lax.all_gather(x, "seq", axis=0, axis_index_groups=copy_groups)
            x = x.transpose(0, 2, 1, 3, 4).reshape(-1, 3 * part, hidden)
            halves = x[:, 2 * part :].reshape(-1, 2, part // 2, hidden).transpose(0, 2, 1, 3)
            return pack(
                x[:, :part].reshape(width, hidden),
                x[:, part : 2 * part].reshape(width, hidden),
                halves.reshape(hidden, width),
            )
        return x

    def pack(gate, up, down):
        gate = gate.reshape(UNIT, PIECES, ROWS_IN, hidden)
        up = up.reshape(UNIT, PIECES, ROWS_IN, hidden)
        down = down.reshape(UNIT, PIECES, ROWS_OUT, 2, hidden).transpose(0, 1, 3, 2, 4)
        down = down.reshape(UNIT, PIECES, ROWS_IN, hidden)
        return jnp.concatenate([gate, up, down], axis=2).transpose(1, 0, 2, 3)

    def repack(x):
        x = x.transpose(1, 0, 2, 3)
        gate = x[:, :, :ROWS_IN].reshape(copies, UNIT, rows, part, hidden)
        up = x[:, :, ROWS_IN : 2 * ROWS_IN].reshape(copies, UNIT, rows, part, hidden)
        down = x[:, :, 2 * ROWS_IN :].reshape(UNIT, PIECES, 2, ROWS_OUT, hidden)
        down = down.transpose(0, 1, 3, 2, 4).reshape(copies, UNIT, rows, part // 2, 2, hidden)
        down = down.transpose(0, 1, 2, 4, 3, 5).reshape(copies, UNIT, rows, part, hidden)
        return jnp.concatenate([gate, up, down], axis=3).transpose(2, 0, 1, 3, 4)

    own_weights = [gather_packed(x) for x in packed_mine]

    tok_all, w_out_all = unit_gather(
        [wait_for(flat_tokens, w_out_rows), w_out_rows.reshape(-1, width)], 1
    )
    tok_all = tok_all.reshape(UNIT, micro, local_len, width)
    w_out_all = w_out_all.reshape(UNIT, copies, rows * part, width)
    w_out_all = w_out_all.transpose(1, 0, 2, 3).reshape(H * HD, width)

    chosen = jnp.any(
        routes.reshape(count, TOPK)[:, :, None] == jnp.arange(LANES, dtype=jnp.int32)[None, None, :],
        axis=1,
    ).astype(BF16)
    dz_own = jnp.concatenate([cotangent.reshape(count, width), chosen], axis=1)
    dz_send = wait_for(dz_own, tok_all)
    dz_pieces = [dz_send] + [flip(dz_send, k) for k in (2, 4, 6)]

    frequency = BASE ** (-2.0 * jnp.arange(HD // 2).astype(F32) / HD)
    places = unit * unit_len + jnp.arange(unit_len, dtype=jnp.int32)
    angles = places.astype(F32)[:, None] * frequency[None, :]
    cos_one = jnp.concatenate([jnp.cos(angles)] * 2, axis=1)
    sin_one = jnp.concatenate([-jnp.sin(angles), jnp.sin(angles)], axis=1)
    cosine = jnp.concatenate([cos_one] * 3 + [jnp.ones_like(cos_one)], axis=1)
    sine = jnp.concatenate([sin_one] * 3 + [jnp.zeros_like(sin_one)], axis=1)

    def by_row4(m):
        return (0, m, 0, 0)

    def by_row3(m):
        return (m, 0, 0)

    def fixed(*_):
        return (0, 0)

    normed_all, q_all, kv_own = pl.pallas_call(
        project_kernel,
        grid=(micro,),
        in_specs=[
            pl.BlockSpec((UNIT, 1, local_len, width), by_row4),
            pl.BlockSpec((1, width), fixed),
            pl.BlockSpec((width, 4 * HD), fixed),
            pl.BlockSpec((unit_len, 4 * HD), fixed),
            pl.BlockSpec((unit_len, 4 * HD), fixed),
        ],
        out_specs=[
            pl.BlockSpec((UNIT, 1, local_len, width), by_row4),
            pl.BlockSpec((1, unit_len, LANES), by_row3),
            pl.BlockSpec((1, unit_len, LANES), by_row3),
        ],
        out_shape=[
            jax.ShapeDtypeStruct((UNIT, micro, local_len, width), BF16),
            jax.ShapeDtypeStruct((micro, unit_len, LANES), BF16),
            jax.ShapeDtypeStruct((micro, unit_len, LANES), BF16),
        ],
        compiler_params=params(),
        cost_estimate=cost(2.0 * UNIT * count * width * 4 * HD, 1.5e7),
    )(tok_all, gain_attn, w_head, cosine, sine)

    kv_all = kv_own
    if copies > 1:
        kv_all = lax.all_gather(kv_own, "seq", axis=1, tiled=True, axis_index_groups=copy_groups)
    seg_keys = segments.astype(F32).reshape(micro, 1, length)
    seg_queries = lax.dynamic_slice_in_dim(seg_keys, unit * unit_len, unit_len, 2)
    skip = copies == 1
    place_row = places[None]
    attention_flops = 4.0 * micro * unit_len * length * 2 * LANES
    attention_specs = [
        pl.BlockSpec((1, unit_len, LANES), by_row3),
        pl.BlockSpec((1, length, LANES), by_row3),
        pl.BlockSpec((1, 1, unit_len), by_row3),
        pl.BlockSpec((1, 1, length), by_row3),
        pl.BlockSpec((1, unit_len), fixed),
    ]
    ctx_heads, lse = pl.pallas_call(
        functools.partial(attention_kernel, skip),
        grid=(micro,),
        in_specs=attention_specs,
        out_specs=[
            pl.BlockSpec((UNIT, 1, local_len, LANES), by_row4),
            pl.BlockSpec((1, 2, unit_len), by_row3),
        ],
        out_shape=[
            jax.ShapeDtypeStruct((UNIT, micro, local_len, LANES), BF16),
            jax.ShapeDtypeStruct((micro, 2, unit_len), F32),
        ],
        compiler_params=params(),
        cost_estimate=cost(attention_flops, 4e6),
    )(q_all, kv_all, seg_queries, seg_keys, place_row)
    ctx_own = exchange(ctx_heads)

    mixed, normed_ffn, context = pl.pallas_call(
        mix_kernel,
        out_shape=[
            jax.ShapeDtypeStruct((count, width), F32),
            jax.ShapeDtypeStruct((count, width), BF16),
            jax.ShapeDtypeStruct((count, H * HD), BF16),
        ],
        compiler_params=params(),
        cost_estimate=cost(2.0 * count * width * width, 8e6),
    )(ctx_own, w_out_all, flat_tokens, gain_ffn)

    x_all, sib_first, dz_all = core_gather(normed_ffn, own_weights[0], dz_pieces, 2)
    x_all = x_all.reshape(4 * count, width)
    dz_all = dz_all.reshape(4 * count, width + LANES)
    w_heads = lax.all_gather(
        wait_for(w_head, x_all), "seq", axis=0, axis_index_groups=unit_groups
    )

    def ids(b, i):
        return jnp.full((1,), 0, jnp.int32) + 2 * b + i

    def call(b, i, packed, carried, last):
        result = run_expert(ids(b, i), x_all, dz_all, router, packed, carried, last)
        return result[:3], result[3]

    carried, term = call(me ^ 1, 0, sib_first, None, False)
    sib_terms = [flip(term, 1)]
    carried, term = call(me, 0, own_weights[0], carried, False)
    own_terms = [term]
    second = wait_for(own_weights[1], term)
    sib_second = flip(second, 1)
    carried, term = call(me, 1, second, carried, False)
    own_terms.append(term)
    carried, term = call(me ^ 1, 1, sib_second, carried, True)
    sib_terms.append(flip(term, 1))
    out_part, dx_part, gg_part = carried

    dx_part = dx_part.reshape(4, count, width)
    gg_part = gg_part.reshape(4, count, LANES)
    dx_back, gg_back = give_back([dx_part, gg_part], 3)
    def zeros2(i):
        return (0, 0)

    def zeros3(i):
        return (0, 0, 0)

    def zeros4(i):
        return (0, 0, 0, 0)

    gmixed, gbranch, glog, gctx = pl.pallas_call(
        back_kernel,
        grid=(1,),
        in_specs=[
            pl.BlockSpec((1, count, width), zeros3),
            pl.BlockSpec((3, count, width), zeros3),
            pl.BlockSpec((1, count, LANES), zeros3),
            pl.BlockSpec((3, count, LANES), zeros3),
            pl.BlockSpec((count, width), zeros2),
            pl.BlockSpec((count, width), zeros2),
            pl.BlockSpec((count, width + LANES), zeros2),
            pl.BlockSpec((1, width), zeros2),
            pl.BlockSpec((width, LANES), zeros2),
            pl.BlockSpec((width, width), zeros2),
        ],
        out_specs=[
            pl.BlockSpec((count, width), zeros2),
            pl.BlockSpec((count, width), zeros2),
            pl.BlockSpec((count, LANES), zeros2),
            pl.BlockSpec((UNIT, micro, local_len, LANES), zeros4),
        ],
        out_shape=[
            jax.ShapeDtypeStruct((count, width), F32),
            jax.ShapeDtypeStruct((count, width), BF16),
            jax.ShapeDtypeStruct((count, LANES), BF16),
            jax.ShapeDtypeStruct((UNIT, micro, local_len, LANES), BF16),
        ],
        compiler_params=params(),
        cost_estimate=cost(2.0 * count * width * width, 1.2e7),
    )(dx_part, dx_back, gg_part, gg_back, mixed, normed_ffn, dz_own, gain_ffn, router, w_out_all)
    do_heads = exchange(gctx)

    def fixed_q(m):
        return (0, 0)

    def fixed_kv(m):
        return (0, 1)

    if copies > 1:
        key_angles = jnp.arange(length, dtype=jnp.int32).astype(F32)[:, None] * frequency[None, :]
        key_cos = jnp.concatenate([jnp.cos(key_angles)] * 2 + [jnp.ones((length, HD), F32)], axis=1)
        key_sin = jnp.concatenate(
            [-jnp.sin(key_angles), jnp.sin(key_angles), jnp.zeros((length, HD), F32)], axis=1
        )
    else:
        key_cos, key_sin = cosine[:, LANES:], sine[:, LANES:]
    graw, head_term = pl.pallas_call(
        functools.partial(attention_back_kernel, skip),
        grid=(micro,),
        in_specs=attention_specs
        + [
            pl.BlockSpec((1, 2, unit_len), by_row3),
            pl.BlockSpec((UNIT, 1, local_len, LANES), by_row4),
            pl.BlockSpec((unit_len, LANES), fixed),
            pl.BlockSpec((unit_len, LANES), fixed),
            pl.BlockSpec((length, LANES), fixed),
            pl.BlockSpec((length, LANES), fixed),
            pl.BlockSpec((UNIT, 1, local_len, width), by_row4),
        ],
        out_specs=[
            pl.BlockSpec((seq_size, 1, local_len, 2 * LANES), by_row4),
            pl.BlockSpec((PIECES, UNIT, ROWS_IN, 2 * LANES), zeros4),
        ],
        out_shape=[
            jax.ShapeDtypeStruct((seq_size, micro, local_len, 2 * LANES), BF16),
            jax.ShapeDtypeStruct((PIECES, UNIT, ROWS_IN, 2 * LANES), BF16),
        ],
        scratch_shapes=[
            pltpu.VMEM((length, LANES), F32),
            pltpu.VMEM((length, LANES), F32),
            pltpu.VMEM((width, 2 * LANES), F32),
        ],
        compiler_params=params(),
        cost_estimate=cost(2.5 * attention_flops, 8e6),
    )(
        q_all, kv_all, seg_queries, seg_keys, place_row, lse, do_heads,
        cosine[:, :LANES], sine[:, :LANES], key_cos, key_sin, normed_all,
    )
    out_term = jnp.einsum("nh,nd->hd", context, gbranch, preferred_element_type=F32)
    router_term = jnp.einsum("nd,ne->de", normed_ffn, glog, preferred_element_type=F32)
    out_term = jnp.concatenate([out_term, router_term], axis=1).astype(BF16)
    if copies > 1:
        graw_kv = lax.psum_scatter(
            graw[..., LANES:], "seq", scatter_dimension=0, tiled=True,
            axis_index_groups=copy_groups,
        )
        graw = jnp.concatenate([graw[:UNIT, ..., :LANES], graw_kv], axis=3)
        head_term = jnp.einsum(
            "nd,nh->dh",
            normed_all.reshape(UNIT * count, width),
            graw.reshape(UNIT * count, 2 * LANES),
            preferred_element_type=F32,
        ).astype(BF16)
        head_term = head_term.reshape(copies, UNIT, rows, part, 2 * LANES)
        head_term = lax.psum_scatter(
            head_term, "seq", scatter_dimension=0, axis_index_groups=copy_groups
        ).transpose(1, 0, 2, 3)
        out_term = out_term.reshape(copies, UNIT, rows, part, width + LANES)
        out_term = lax.psum_scatter(
            out_term, "seq", scatter_dimension=0, axis_index_groups=copy_groups
        )
    else:
        out_term = out_term.reshape(UNIT, rows, part, width + LANES)
    out_mine = exchange(out_term)
    graw_own, head_grad, out_grad = finish(rows, graw, head_term, out_mine, 4)

    def by_head4(b):
        return (b, 0, 0, 0)

    def by_head3(b):
        return (b, 0, 0)

    grad_input = pl.pallas_call(
        input_kernel,
        grid=(UNIT,),
        in_specs=[
            pl.BlockSpec((1, micro, local_len, 2 * LANES), by_head4),
            pl.BlockSpec((1, width, 2 * LANES), by_head3),
            pl.BlockSpec((count, width), fixed),
            pl.BlockSpec((1, width), fixed),
            pl.BlockSpec((count, width), fixed),
        ],
        out_specs=pl.BlockSpec((count, width), fixed),
        out_shape=jax.ShapeDtypeStruct((count, width), BF16),
        scratch_shapes=[pltpu.VMEM((count, width), F32)],
        compiler_params=params(),
        cost_estimate=cost(2.0 * count * width * 2048, 1e7),
    )(graw_own, w_heads, flat_tokens, gain_attn, gmixed)

    out_split = wait_for(out_part, do_heads).reshape(4, count, width)
    out_pieces = [out_split[0]] + [flip(out_split[i], 2 * i) for i in (1, 2, 3)]
    block_out = wait_for(mixed, graw_own)
    for piece in out_pieces:
        block_out = block_out + piece.astype(F32)

    def finish_expert(own, sib):
        total = (own.astype(F32) + sib.astype(F32)).astype(BF16)
        if copies > 1:
            total = repack(total)
            total = lax.psum_scatter(total, "row", scatter_dimension=0)
            total = lax.psum_scatter(
                total, "seq", scatter_dimension=0, axis_index_groups=copy_groups
            )
        else:
            total = lax.psum_scatter(total, "row", scatter_dimension=0)
        return exchange(total)

    finished = [finish_expert(own, sib) for own, sib in zip(own_terms, sib_terms)]
    finished = jnp.stack(finished, axis=1).reshape(E, 3 * part, hidden).astype(F32)
    grad_gate = finished[:, :part]
    grad_up = finished[:, part : 2 * part]
    grad_down = finished[:, 2 * part :].reshape(E, 2, -1, hidden).transpose(0, 2, 1, 3)
    grad_down = grad_down.reshape(E, -1, width)
    head_grad = head_grad.astype(F32)
    grad_query = head_grad[:, :, :LANES].transpose(1, 0, 2).reshape(part, H * HD)
    grad_key = head_grad[:, :, LANES : LANES + HD].transpose(1, 0, 2).reshape(part, KVH * HD)
    grad_value = head_grad[:, :, LANES + HD :].transpose(1, 0, 2).reshape(part, KVH * HD)
    grad_out = out_grad[:, :width]
    grad_router = out_grad[:, width : width + E]

    attn_weights = jnp.concatenate([w_query, w_key, w_value], axis=1).astype(F32)
    attn_grads = jnp.concatenate([grad_query, grad_key, grad_value], axis=1)
    grad_norm_attn = jnp.sum(attn_weights * attn_grads, axis=1) / norm_attn.astype(F32)
    grad_norm_ffn = (
        jnp.sum(w_gate.astype(F32) * grad_gate, axis=(0, 2))
        + jnp.sum(w_up.astype(F32) * grad_up, axis=(0, 2))
        + jnp.sum(w_router.astype(F32) * grad_router, axis=1)
    ) / norm_ffn.astype(F32)
    return (
        block_out.astype(BF16).reshape(tokens.shape),
        grad_input.reshape(tokens.shape),
        grad_norm_attn,
        grad_query,
        grad_key,
        grad_value,
        grad_out,
        grad_norm_ffn,
        grad_router,
        grad_gate,
        grad_up,
        grad_down,
    )


def solution(mesh):
    both = ("seq", "row")
    body = functools.partial(shards, mesh.shape["seq"] // UNIT, rows=mesh.shape["row"])
    return jax.shard_map(
        body,
        mesh=mesh,
        in_specs=(
            P("row", "seq", None),
            P("row", None),
            P("row", "seq", None),
            P("row", "seq", None),
            P(both),
            P(both, None),
            P(both, None),
            P(both, None),
            P(both, None),
            P(both),
            P(both, None),
            P(None, both, None),
            P(None, both, None),
            P(None, both, None),
        ),
        out_specs=(
            P("row", "seq", None),
            P("row", "seq", None),
            P(both),
            P(both, None),
            P(both, None),
            P(both, None),
            P(both, None),
            P(both),
            P(both, None),
            P(None, both, None),
            P(None, both, None),
            P(None, both, None),
        ),
        check_vma=False,
    )
```

```python
import functools

import jax
import jax.numpy as jnp
import numpy as np
from jax import lax
from jax.experimental import pallas as pl
from jax.experimental.pallas import tpu as pltpu
from jax.sharding import PartitionSpec as P

H = 16
KVH = 8
TOPK = 8
HD = 64
E = 16
UNIT = 8
LANES = 128
QBLOCK = 256
PIECES = 4
ROWS_IN = 32
ROWS_OUT = 16

EPS = 1e-05
BASE = 10000.0
NEGATIVE = -1e30
F32 = jnp.float32
BF16 = jnp.bfloat16
VMEM_LIMIT = 60 * 1024 * 1024


def dot_nn(left, right):
    return lax.dot_general(left, right, (((1,), (0,)), ((), ())), preferred_element_type=F32)


def dot_nt(left, right):
    return lax.dot_general(left, right, (((1,), (1,)), ((), ())), preferred_element_type=F32)


def dot_tn(left, right):
    return lax.dot_general(left, right, (((0,), (0,)), ((), ())), preferred_element_type=F32)


def params(**kw):
    return pltpu.CompilerParams(vmem_limit_bytes=VMEM_LIMIT, **kw)


def cost(flops, nbytes):
    return pl.CostEstimate(flops=int(flops), bytes_accessed=int(nbytes), transcendentals=0)


def neighbours(seq):
    core = seq % 2
    chip = (seq // 2) % 4
    base = seq - seq % UNIT

    def at(other, same=True):
        return base + 2 * other + (core if same else 1 - core)

    across = chip + 1 - 2 * (chip % 2)
    along = (chip + 2) % 4
    return at(across), at(along), at(3 - chip), at(chip, False)


def greet(targets):
    barrier = pltpu.get_barrier_semaphore()
    for target in targets:
        pl.semaphore_signal(
            barrier, inc=1, device_id=target, device_id_type=pl.DeviceIdType.MESH
        )
    pl.semaphore_wait(barrier, len(targets))


class Pushes:
    def __init__(self, send, recv):
        self.send, self.recv, self.used = send, recv, 0

    def start(self, source, target, device):
        n = self.used
        self.used += 1
        copy = pltpu.make_async_remote_copy(
            src_ref=source,
            dst_ref=target,
            send_sem=self.send.at[n],
            recv_sem=self.recv.at[n],
            device_id=device,
            device_id_type=pl.DeviceIdType.MESH,
        )
        copy.start()
        return copy


class Bounce:
    def __init__(self, source, middle, target, sems):
        self.inward = pltpu.make_async_copy(source, middle, sems.at[0])
        self.outward = pltpu.make_async_copy(middle, target, sems.at[1])
        self.inward.start()

    def turn(self):
        self.inward.wait()
        self.outward.start()

    def wait(self):
        self.outward.wait()


def begin_kernel(
    rows, packed0, packed1, head_ref, wout_ref, mine0, mine1, head_all, wout_all,
    head_mine, own0, own1, own2, send, recv, local,
):
    seq, row = lax.axis_index("seq"), lax.axis_index("row")
    me = seq % UNIT
    base = seq - me
    unit = [(me + k) % UNIT for k in range(1, UNIT)]
    column = [(row + k) % rows for k in range(1, rows)]
    greet([{"seq": base + b} for b in unit] + [{"row": r} for r in column])
    pushes = Pushes(send, recv)
    first = pltpu.make_async_copy(head_ref.at[me], head_mine.at[me], local.at[3, 0])
    first.start()
    heads = [pushes.start(head_ref.at[b], head_mine.at[me], {"seq": base + b}) for b in unit]
    others = [pushes.start(wout_ref, wout_all.at[row], {"row": r}) for r in column]
    for source, target in ((packed0, mine0), (packed1, mine1)):
        others += [pushes.start(source.at[b], target.at[me], {"seq": base + b}) for b in unit]
    own = [
        Bounce(packed0.at[me], own0, mine0.at[me], local.at[0]),
        Bounce(packed1.at[me], own1, mine1.at[me], local.at[1]),
        Bounce(wout_ref, own2, wout_all.at[row], local.at[2]),
    ]
    for copy in own:
        copy.turn()
    first.wait()
    for copy in heads:
        copy.wait_recv()
    last = pltpu.make_async_copy(head_mine, head_all.at[:, row], local.at[3, 1])
    last.start()
    others += [pushes.start(head_mine, head_all.at[:, row], {"row": r}) for r in column]
    for copy in heads:
        copy.wait_send()
    for copy in own + [last]:
        copy.wait()
    for copy in others:
        copy.wait()


def begin(rows, packed0, packed1, head_part, w_out):
    any_spec = pl.BlockSpec(memory_space=pl.ANY)
    count = 3 * (UNIT - 1) + 2 * (rows - 1)
    like = jax.ShapeDtypeStruct
    return pl.pallas_call(
        functools.partial(begin_kernel, rows),
        in_specs=[any_spec] * 4,
        out_specs=[any_spec] * 4,
        out_shape=[
            like(packed0.shape, BF16),
            like(packed1.shape, BF16),
            like(head_part.shape[:1] + (rows,) + head_part.shape[1:], BF16),
            like((rows,) + w_out.shape, BF16),
        ],
        scratch_shapes=[
            pltpu.VMEM(head_part.shape, BF16),
            pltpu.VMEM(packed0.shape[1:], BF16),
            pltpu.VMEM(packed0.shape[1:], BF16),
            pltpu.VMEM(w_out.shape, BF16),
            pltpu.SemaphoreType.DMA((count,)),
            pltpu.SemaphoreType.DMA((count,)),
            pltpu.SemaphoreType.DMA((4, 2)),
        ],
        compiler_params=pltpu.CompilerParams(collective_id=0, has_side_effects=True),
        cost_estimate=cost(1, 2e7),
    )(packed0, packed1, head_part, w_out)


def unit_gather_kernel(sources, *refs):
    ins, outs = refs[:sources], refs[sources : 2 * sources]
    middles = refs[2 * sources : 3 * sources]
    send, recv, local = refs[3 * sources :]
    seq = lax.axis_index("seq")
    me = seq % UNIT
    base = seq - me
    across, along, _, twin = neighbours(seq)
    a, b, t = across - base, along - base, twin - base
    d = UNIT - 1 - me + 2 * (me % 2) - 1
    greet([{"seq": across}, {"seq": along}, {"seq": twin}])
    pushes = Pushes(send, recv)
    own, done, stage = [], [], []
    for n, (source, target) in enumerate(zip(ins, outs)):
        half = source.shape[0] // 2
        halves = [pl.ds(0, half), pl.ds(half, half)]
        own.append(Bounce(source, middles[n], target.at[me], local.at[n]))

        def part(device, h, source=source, target=target, halves=halves):
            return pushes.start(
                source.at[halves[h]], target.at[me, halves[h]], {"seq": device}
            )

        xa, yb = part(across, 0), part(along, 1)
        xb, ya = part(across, 1), part(along, 0)
        done.append(pushes.start(source, target.at[me], {"seq": twin}))
        stage.append((target, halves, xa, yb, xb, ya))
    for copy in own:
        copy.turn()
    for target, halves, xa, yb, xb, ya in stage:

        def pass_on(slot, h, device, target=target, halves=halves):
            view = target.at[slot, halves[h]]
            return pushes.start(view, view, {"seq": device})

        xa.wait_recv()
        da = pass_on(a, 0, along)
        done.append(pass_on(a, 0, twin))
        yb.wait_recv()
        db = pass_on(b, 1, across)
        done.append(pass_on(b, 1, twin))
        xb.wait_recv()
        done.append(pass_on(a, 1, twin))
        ya.wait_recv()
        done.append(pass_on(b, 0, twin))
        da.wait_recv()
        done.append(pass_on(d, 0, twin))
        db.wait_recv()
        done.append(pass_on(d, 1, twin))
        for copy in (xa, yb, xb, ya, da, db):
            copy.wait_send()
    for copy in own + done:
        copy.wait()


def unit_gather(sources, collective):
    any_spec = pl.BlockSpec(memory_space=pl.ANY)
    n = len(sources)
    return pl.pallas_call(
        functools.partial(unit_gather_kernel, n),
        in_specs=[any_spec] * n,
        out_specs=[any_spec] * n,
        out_shape=[jax.ShapeDtypeStruct((UNIT,) + x.shape, x.dtype) for x in sources],
        scratch_shapes=[pltpu.VMEM(x.shape, x.dtype) for x in sources]
        + [
            pltpu.SemaphoreType.DMA((13 * n,)),
            pltpu.SemaphoreType.DMA((13 * n,)),
            pltpu.SemaphoreType.DMA((n, 2)),
        ],
        compiler_params=params(collective_id=collective, has_side_effects=True),
        cost_estimate=cost(1, 8e7),
    )(*sources)


def bridge_kernel(
    ctx_ref, weights, z0, z1, z2, z3, w_ref, tok_ref, small_ref,
    target, flipped, z_all, mixed_ref, normed_ref, ctx_out,
    ctx_in, z_middle, send, recv, local,
):
    seq = lax.axis_index("seq")
    me = seq % UNIT
    base = seq - me
    unit = [(me + k) % UNIT for k in range(1, UNIT)]
    across, along, _, twin = neighbours(seq)
    greet([{"seq": base + b} for b in unit])
    pushes = Pushes(send, recv)
    arrivals = [pushes.start(ctx_ref.at[b], ctx_in.at[me], {"seq": base + b}) for b in unit]
    mine = pltpu.make_async_copy(ctx_ref.at[me], ctx_in.at[me], local.at[4, 0])
    mine.start()
    turned = pushes.start(weights, flipped, {"seq": twin})
    own = [
        Bounce(piece, z_middle.at[n], z_all.at[n], local.at[n])
        for n, piece in enumerate((z0, z1, z2, z3))
    ]
    count, width = tok_ref.shape
    half = count // 2
    gain = gain_row(small_ref[...], E + 1)
    mine.wait()
    for copy in arrivals:
        copy.wait_recv()
    for b in range(UNIT):
        ctx_out[:, b * LANES : (b + 1) * LANES] = ctx_in[b].reshape(count, LANES)
    halves = [pl.ds(0, half), pl.ds(half, half)]

    def part(device, slot, h):
        return pushes.start(normed_ref.at[halves[h]], target.at[slot, halves[h]], {"seq": device})

    def pass_on(slot, h, device):
        return pushes.start(
            target.at[slot, halves[h]], target.at[3, halves[h]], {"seq": device}
        )

    sent = []
    for h in range(2):
        here = slice(h * half, (h + 1) * half)
        mixed = tok_ref[here].astype(F32) + dot_nn(ctx_out[here], w_ref[...])
        mixed_ref[here] = mixed
        inverse = lax.rsqrt(jnp.mean(mixed * mixed, axis=-1, keepdims=True) + EPS)
        normed_ref[here] = (mixed * inverse * gain).astype(BF16)
        if h == 0:
            xa, ya = part(across, 1, 0), part(along, 2, 0)
        else:
            yb, xb = part(along, 2, 1), part(across, 1, 1)
    last = pltpu.make_async_copy(normed_ref, target.at[0], local.at[4, 1])
    last.start()
    for copy in own:
        copy.turn()
    xa.wait_recv()
    da = pass_on(1, 0, along)
    yb.wait_recv()
    db = pass_on(2, 1, across)
    for copy in (xb, ya, da, db):
        copy.wait_recv()
    for copy in (xa, yb, xb, ya, da, db):
        copy.wait_send()
    for copy in arrivals:
        copy.wait_send()
    turned.wait()
    for copy in own + [last]:
        copy.wait()


def bridge(ctx_heads, weights, z_pieces, w_out, tokens, heads, collective):
    any_spec = pl.BlockSpec(memory_space=pl.ANY)
    like = jax.ShapeDtypeStruct
    count, width = tokens.shape

    def fixed(i):
        return (0, 0)

    return pl.pallas_call(
        bridge_kernel,
        grid=(1,),
        in_specs=[any_spec] * 6
        + [
            pl.BlockSpec(w_out.shape, fixed),
            pl.BlockSpec(tokens.shape, fixed),
            pl.BlockSpec((width, LANES), lambda i: (0, 2)),
        ],
        out_specs=[any_spec] * 3 + [pl.BlockSpec((count, width), fixed)] * 3,
        out_shape=[
            like((4, count, width), BF16),
            like(weights.shape, BF16),
            like((4,) + z_pieces[0].shape, BF16),
            like((count, width), F32),
            like((count, width), BF16),
            like((count, H * HD), BF16),
        ],
        scratch_shapes=[
            pltpu.VMEM(ctx_heads.shape, BF16),
            pltpu.VMEM((4,) + z_pieces[0].shape, BF16),
            pltpu.SemaphoreType.DMA((UNIT + 6,)),
            pltpu.SemaphoreType.DMA((UNIT + 6,)),
            pltpu.SemaphoreType.DMA((5, 2)),
        ],
        compiler_params=params(collective_id=collective, has_side_effects=True),
        cost_estimate=cost(2.0 * count * width * width, 8e7),
    )(ctx_heads, weights, *z_pieces, w_out, tokens, heads)


def finish_kernel(
    rows, graw_ref, head_ref, out_ref, w_ref, tok_ref, small_ref, gmixed_ref,
    head_fin, out_fin, gin_ref,
    head_col, head_sum, out_sum, out_col, raw_in, send, recv, local,
):
    seq, row = lax.axis_index("seq"), lax.axis_index("row")
    me = seq % UNIT
    base = seq - me
    unit = [(me + k) % UNIT for k in range(1, UNIT)]
    senders = [(me + UNIT - k) % UNIT for k in range(1, UNIT)]
    column = [(row + k) % rows for k in range(1, rows)]
    greet([{"seq": base + b} for b in unit] + [{"row": r} for r in column])
    pushes = Pushes(send, recv)
    first = pltpu.make_async_copy(head_ref.at[row], head_col.at[row], local.at[0])
    first.start()
    second = pltpu.make_async_copy(graw_ref.at[me], raw_in.at[me], local.at[1])
    second.start()
    heads = [pushes.start(head_ref.at[r], head_col.at[row], {"row": r}) for r in column]
    raws = [pushes.start(graw_ref.at[b], raw_in.at[me], {"seq": base + b}) for b in unit]
    total = out_ref[0].astype(F32)
    for b in range(1, UNIT):
        total = total + out_ref[b].astype(F32)
    out_sum[...] = total.astype(BF16)
    third = pltpu.make_async_copy(out_sum.at[row], out_col.at[row], local.at[2])
    third.start()
    outs = [pushes.start(out_sum.at[r], out_col.at[row], {"row": r}) for r in column]
    first.wait()
    for copy in heads:
        copy.wait_recv()
    total = head_col[0].astype(F32)
    for r in range(1, rows):
        total = total + head_col[r].astype(F32)
    head_sum[...] = total.astype(BF16)
    fourth = pltpu.make_async_copy(head_sum.at[me], head_fin.at[me], local.at[3])
    fourth.start()
    others = [pushes.start(head_sum.at[b], head_fin.at[me], {"seq": base + b}) for b in unit]
    count, width = tok_ref.shape
    second.wait()
    acc = dot_nt(raw_in[me].reshape(count, 2 * LANES), w_ref[me])
    for b, copy in zip(senders, raws):
        copy.wait_recv()
        acc = acc + dot_nt(raw_in[b].reshape(count, 2 * LANES), w_ref[b])
    v = tok_ref[...].astype(F32)
    inverse = lax.rsqrt(jnp.mean(v * v, axis=-1, keepdims=True) + EPS)
    scaled = acc * gain_row(small_ref[...], E)
    mean = jnp.mean(scaled * v, axis=-1, keepdims=True)
    grad = gmixed_ref[...] + scaled * inverse - v * (inverse * inverse * inverse * mean)
    gin_ref[...] = grad.astype(BF16)
    third.wait()
    for copy in outs:
        copy.wait_recv()
    total = out_col[0].astype(F32)
    for r in range(1, rows):
        total = total + out_col[r].astype(F32)
    out_fin[...] = total
    for copy in heads + outs + raws:
        copy.wait_send()
    fourth.wait()
    for copy in others:
        copy.wait()


def finish(rows, graw, head_term, out_term, w_heads, tokens, heads, gmixed, collective):
    any_spec = pl.BlockSpec(memory_space=pl.ANY)
    like = jax.ShapeDtypeStruct
    pushes = 2 * (UNIT - 1) + 2 * (rows - 1)
    count, width = tokens.shape

    def fixed(i):
        return (0, 0)

    return pl.pallas_call(
        functools.partial(finish_kernel, rows),
        grid=(1,),
        in_specs=[
            any_spec,
            any_spec,
            pl.BlockSpec(out_term.shape, lambda i: (0, 0, 0, 0)),
            pl.BlockSpec(w_heads.shape, lambda i: (0, 0, 0)),
            pl.BlockSpec(tokens.shape, fixed),
            pl.BlockSpec((width, LANES), lambda i: (0, 2)),
            pl.BlockSpec(gmixed.shape, fixed),
        ],
        out_specs=[
            any_spec,
            pl.BlockSpec(out_term.shape[2:], fixed),
            pl.BlockSpec(tokens.shape, fixed),
        ],
        out_shape=[
            like(head_term.shape[1:], BF16),
            like(out_term.shape[2:], F32),
            like(tokens.shape, BF16),
        ],
        scratch_shapes=[
            pltpu.VMEM(head_term.shape, BF16),
            pltpu.VMEM(head_term.shape[1:], BF16),
            pltpu.VMEM(out_term.shape[1:], BF16),
            pltpu.VMEM(out_term.shape[1:], BF16),
            pltpu.VMEM(graw.shape, BF16),
            pltpu.SemaphoreType.DMA((pushes,)),
            pltpu.SemaphoreType.DMA((pushes,)),
            pltpu.SemaphoreType.DMA((4,)),
        ],
        compiler_params=params(collective_id=collective, has_side_effects=True),
        cost_estimate=cost(4.0 * count * width * width, 6e7),
    )(graw, head_term, out_term, w_heads, tokens, heads, gmixed)


def lane_iota(shape):
    return lax.broadcasted_iota(jnp.int32, shape, len(shape) - 1)


def turn(u, cosine, sine):
    low_half = lane_iota(u.shape) % HD < HD // 2
    partner = jnp.where(
        low_half, pltpu.roll(u, LANES - HD // 2, u.ndim - 1), pltpu.roll(u, HD // 2, u.ndim - 1)
    )
    return u * cosine + partner * sine


def value_tables(cosine, sine):
    low = lane_iota(cosine.shape) < HD
    return jnp.where(low, cosine, 1.0), jnp.where(low, sine, 0.0)


def gain_row(small, lane):
    return small.astype(F32).T[lane : lane + 1]


def project_kernel(tok_ref, small_ref, w_ref, cos_ref, sin_ref, normed_ref, q_ref, kv_ref):
    count = q_ref.shape[1]
    width = w_ref.shape[0]
    x = tok_ref[...].reshape(count, width).astype(F32)
    inverse = lax.rsqrt(jnp.mean(x * x, axis=-1, keepdims=True) + EPS)
    normed = (x * inverse * gain_row(small_ref[...], E)).astype(BF16)
    normed_ref[...] = normed.reshape(normed_ref.shape)
    raw = dot_nn(normed, w_ref[...])
    cosine, sine = cos_ref[...], sin_ref[...]
    q = turn(raw[:, :LANES], cosine, sine).astype(BF16)
    q_ref[0] = (q.astype(F32) * HD**-0.5).astype(BF16)
    kv_ref[0] = turn(raw[:, LANES:], *value_tables(cosine, sine)).astype(BF16)


def pair_keys(kv):
    kv = kv.astype(F32)
    rolled = pltpu.roll(kv, HD, 1)
    low = lane_iota(kv.shape) < HD
    return jnp.where(low, kv, rolled), jnp.where(low, rolled, kv)


def bias_block(seg_col, seg_row, q_places, first, length):
    key_places = lax.broadcasted_iota(jnp.int32, (length, q_places.shape[1]), 0)
    allowed = (seg_col[:length] == seg_row) & (key_places <= q_places)
    return jnp.where(allowed, 0.0, NEGATIVE)


def attention_kernel(skip, q_ref, kv_ref, segq_ref, segk_ref, place_ref, ctx_ref, lse_ref):
    length = kv_ref.shape[1]
    queries = q_ref.shape[1]
    kk, vv = pair_keys(kv_ref[0])
    v_t = vv.T.astype(BF16)[:HD]
    kk = kk.astype(BF16)
    seg_col = jnp.broadcast_to(segk_ref[0], (8, length)).T[:, :1]
    for block in range(queries // QBLOCK):
        here = slice(block * QBLOCK, (block + 1) * QBLOCK)
        keys = (block + 1) * QBLOCK if skip else length
        bias = bias_block(seg_col, segq_ref[0][:, here], place_ref[:, here], 0, keys)
        q = q_ref[0, here, :]
        low = lane_iota(q.shape) < HD
        parts = []
        for head in range(2):
            mine = jnp.where(low == (head == 0), q, jnp.zeros_like(q))
            scores = dot_nt(kk[:keys], mine) + bias
            top = jnp.max(scores, axis=0, keepdims=True)
            weight = jnp.exp(scores - top)
            total = jnp.sum(weight, axis=0, keepdims=True)
            prob = (weight * (1.0 / total)).astype(BF16)
            parts.append(dot_nn(v_t[:, :keys], prob))
            lse_ref[0, head : head + 1, here] = top + jnp.log(total)
        ctx = jnp.concatenate(parts, axis=0).T.astype(BF16)
        per = QBLOCK // LANES
        ctx_ref[block * per : (block + 1) * per, 0] = ctx.reshape(per, LANES, LANES)


def attention_back_kernel(
    skip, q_ref, kv_ref, segq_ref, segk_ref, place_ref, lse_ref, do_ref, cosq_ref, sinq_ref,
    cosk_ref, sink_ref, normed_ref, graw_ref, term_ref, dk_acc, dv_acc, term_acc,
):
    length = kv_ref.shape[1]
    queries = q_ref.shape[1]
    kk, vv = pair_keys(kv_ref[0])
    k_t = kk.T.astype(BF16)[:HD]
    kk = kk.astype(BF16)
    vv = vv.astype(BF16)
    seg_col = jnp.broadcast_to(segk_ref[0], (8, length)).T[:, :1]
    dk_acc[...] = jnp.zeros_like(dk_acc)
    dv_acc[...] = jnp.zeros_like(dv_acc)
    per = QBLOCK // LANES
    for block in range(queries // QBLOCK):
        here = slice(block * QBLOCK, (block + 1) * QBLOCK)
        keys = (block + 1) * QBLOCK if skip else length
        bias = bias_block(seg_col, segq_ref[0][:, here], place_ref[:, here], 0, keys)
        q = q_ref[0, here, :]
        do = do_ref[block * per : (block + 1) * per, 0].reshape(QBLOCK, LANES)
        low = lane_iota(q.shape) < HD
        parts = []
        for head in range(2):
            pick = low == (head == 0)
            mine = jnp.where(pick, q, jnp.zeros_like(q))
            mine_do = jnp.where(pick, do, jnp.zeros_like(do))
            scores = dot_nt(kk[:keys], mine) + bias
            weight = jnp.exp(scores - lse_ref[0, head : head + 1, here])
            product = dot_nt(vv[:keys], mine_do)
            delta = jnp.sum(weight * product, axis=0, keepdims=True)
            grad_scores = (weight * (product - delta)).astype(BF16)
            dv_acc[:keys] += dot_nn(weight.astype(BF16), mine_do)
            dk_acc[:keys] += dot_nn(grad_scores, mine)
            parts.append(dot_nn(k_t[:, :keys], grad_scores))
        dq = jnp.concatenate(parts, axis=0).T * HD**-0.5
        dq = turn(dq, cosq_ref[here, :], -sinq_ref[here, :]).astype(BF16)
        graw_ref[block * per : (block + 1) * per, 0, :, :LANES] = dq.reshape(per, LANES, LANES)
    dk = dk_acc[...]
    dv = dv_acc[...]
    dk = dk + pltpu.roll(dk, HD, 1)
    dv = dv + pltpu.roll(dv, HD, 1)
    gkv = jnp.where(lane_iota(dk.shape) < HD, dk, dv)
    key_cos, key_sin = value_tables(cosk_ref[...], sink_ref[...])
    gkv = turn(gkv, key_cos, -key_sin).astype(BF16)
    graw_ref[:, 0, :, LANES:] = gkv.reshape(length // LANES, LANES, LANES)
    if skip:
        normed_t = normed_ref[...].reshape(queries, -1).T
        term = dot_nn(normed_t, graw_ref[...].reshape(queries, 2 * LANES))
        m = pl.program_id(0)

        @pl.when(m == 0)
        def _():
            term_acc[...] = term

        @pl.when(m > 0)
        def _():
            term_acc[...] += term

        @pl.when(m == pl.num_programs(0) - 1)
        def _():
            for b in range(UNIT):
                for r in range(PIECES):
                    at = (b * PIECES + r) * ROWS_IN
                    term_ref[r, b] = term_acc[at : at + ROWS_IN].astype(BF16)


def soft_gates(normed, router, chosen):
    logits = jnp.where(chosen > 0, dot_nn(normed, router), NEGATIVE)
    top = jnp.max(logits, axis=-1, keepdims=True)
    weight = jnp.where(chosen > 0, jnp.exp(logits - top), 0.0)
    return weight / jnp.sum(weight, axis=-1, keepdims=True)


def unpack(w_ref, wg, wu, wd):
    half = wg.shape[1]
    for r in range(PIECES):
        for b in range(UNIT):
            at = (b * PIECES + r) * ROWS_IN
            low = (b * PIECES + r) * ROWS_OUT
            wg[at : at + ROWS_IN] = w_ref[r, b, :ROWS_IN]
            wu[at : at + ROWS_IN] = w_ref[r, b, ROWS_IN : 2 * ROWS_IN]
            for c in range(2):
                start = 2 * ROWS_IN + c * ROWS_OUT
                wd[low : low + ROWS_OUT, c * half : (c + 1) * half] = w_ref[
                    r, b, start : start + ROWS_OUT
                ]


def load_weights(w0_ref, w1_hbm, w1_ref, sem, wg, wu, wd):
    e, t = pl.program_id(0), pl.program_id(1)
    fetch = pltpu.make_async_copy(w1_hbm, w1_ref, sem)

    @pl.when((t == 0) & (e == 0))
    def _():
        fetch.start()
        unpack(w0_ref, wg, wu, wd)

    @pl.when((t == 0) & (e == 1))
    def _():
        fetch.wait()
        unpack(w1_ref, wg, wu, wd)


def collect_terms(x, dz, grad_gate, grad_up, gated, ag, au, ad, stage, dw0, dw1, sems):
    e, t = pl.program_id(0), pl.program_id(1)
    last_t = pl.num_programs(1) - 1
    half = ag.shape[1]

    @pl.when(t == 0)
    def _():
        ag[...] = dot_tn(x, grad_gate)
        au[...] = dot_tn(x, grad_up)
        ad[...] = dot_tn(gated, dz)

    @pl.when((t > 0) & (t < last_t))
    def _():
        ag[...] += dot_tn(x, grad_gate)
        au[...] += dot_tn(x, grad_up)
        ad[...] += dot_tn(gated, dz)

    @pl.when(t == last_t)
    def _():
        for place, acc, grad in ((0, ag, grad_gate), (ROWS_IN, au, grad_up)):
            final = (acc[...] + dot_tn(x, grad)).astype(BF16)
            for r in range(PIECES):
                for b in range(UNIT):
                    at = (b * PIECES + r) * ROWS_IN
                    stage[e, r, b, place : place + ROWS_IN] = final[at : at + ROWS_IN]
        final = (ad[...] + dot_tn(gated, dz)).astype(BF16)
        for r in range(PIECES):
            for b in range(UNIT):
                low = (b * PIECES + r) * ROWS_OUT
                for c in range(2):
                    start = 2 * ROWS_IN + c * ROWS_OUT
                    stage[e, r, b, start : start + ROWS_OUT] = final[
                        low : low + ROWS_OUT, c * half : (c + 1) * half
                    ]

    out0 = pltpu.make_async_copy(stage.at[0], dw0, sems.at[0])
    out1 = pltpu.make_async_copy(stage.at[1], dw1, sems.at[1])

    @pl.when((t == last_t) & (e == 0))
    def _():
        out0.start()

    @pl.when((t == last_t) & (e == 1))
    def _():
        out1.start()
        out0.wait()
        out1.wait()


def sigmoid(v):
    return 0.5 + 0.5 * jnp.tanh(0.5 * v)


def grads_of(gate_act, up_act, back, gate):
    sig = sigmoid(gate_act)
    silu = gate_act * sig
    hidden = silu * up_act
    grad_hidden = back * gate
    grad_gate = (grad_hidden * up_act * (sig + silu * (1.0 - sig))).astype(BF16)
    grad_up = (grad_hidden * silu).astype(BF16)
    return hidden, grad_gate, grad_up


def expert_id(twin, index):
    me = lax.axis_index("seq") % UNIT
    return 2 * (me + twin * (1 - 2 * (me % 2))) + index


def pick_gate(gates, gid):
    mine = lane_iota(gates.shape) == gid
    return mine, jnp.sum(jnp.where(mine, gates, 0.0), axis=1, keepdims=True)


def gate_terms(mine, hidden, back):
    terms = jnp.where(mine, jnp.sum(hidden * back, axis=1, keepdims=True), 0.0)
    return terms.T[:E]


def both_kernel(
    x_ref, dz_ref, wr_ref, w0_ref, w1_hbm, out_ref, dx_ref, gg_ref, gates_ref, dw0, dw1,
    wg, wu, wd, gates_s, ag, au, ad, oacc, dxacc, ggacc, w1_ref, stage, w1_sem, dw_sems,
):
    e, t = pl.program_id(0), pl.program_id(1)
    tile, width = out_ref.shape
    rows = pl.ds(pl.multiple_of(t * tile, tile), tile)
    x = x_ref[...]
    dz = dz_ref[:, :width]
    load_weights(w0_ref, w1_hbm, w1_ref, w1_sem, wg, wu, wd)

    @pl.when(e == 0)
    def _():
        gates_s[rows, :] = soft_gates(x, wr_ref[...], dz_ref[:, width:].astype(F32))

    mine, gate = pick_gate(gates_s[rows, :], expert_id(1 - e, 0))
    gate_act = dot_nn(x, wg[...])
    up_act = dot_nn(x, wu[...])
    back = dot_nt(dz, wd[...])
    hidden, grad_gate, grad_up = grads_of(gate_act, up_act, back, gate)
    ggterm = gate_terms(mine, hidden, back)
    gated = (hidden * gate).astype(BF16)
    out = dot_nn(gated, wd[...])
    dx = dot_nt(grad_gate, wg[...]) + dot_nt(grad_up, wu[...])

    @pl.when(e == 0)
    def _():
        oacc[rows, :] = out
        dxacc[rows, :] = dx
        ggacc[t] = ggterm

    @pl.when(e == 1)
    def _():
        out_ref[...] = (oacc[rows, :] + out).astype(BF16)
        dx_ref[...] = (dxacc[rows, :] + dx).astype(BF16)
        gg_ref[...] = ggacc[t] + ggterm
        gates_ref[...] = gates_s[rows, :]

    collect_terms(x, dz, grad_gate, grad_up, gated, ag, au, ad, stage, dw0, dw1, dw_sems)


def forward_kernel(
    x_ref, gates_ref, w0_ref, w1_hbm, oin_ref, out_ref, gact_ref, uact_ref,
    wg, wu, wd, oacc, w1_ref, w1_sem,
):
    e, t = pl.program_id(0), pl.program_id(1)
    tile = out_ref.shape[0]
    rows = pl.ds(pl.multiple_of(t * tile, tile), tile)
    x = x_ref[...]
    load_weights(w0_ref, w1_hbm, w1_ref, w1_sem, wg, wu, wd)
    _, gate = pick_gate(gates_ref[...], expert_id(e, 1))
    gate_act = dot_nn(x, wg[...])
    up_act = dot_nn(x, wu[...])
    gact_ref[0] = gate_act.astype(BF16)
    uact_ref[0] = up_act.astype(BF16)
    gated = (gate_act * sigmoid(gate_act) * up_act * gate).astype(BF16)
    out = dot_nn(gated, wd[...])

    @pl.when(e == 0)
    def _():
        oacc[rows, :] = oin_ref[...].astype(F32) + out

    @pl.when(e == 1)
    def _():
        out_ref[...] = (oacc[rows, :] + out).astype(BF16)


def backward_kernel(
    x_ref, dz_ref, gates_ref, gact_ref, uact_ref, w0_ref, w1_hbm, dxin_ref, ggin_ref,
    dx_ref, gg_ref, dw0, dw1,
    wg, wu, wd, ag, au, ad, dxacc, ggacc, w1_ref, stage, w1_sem, dw_sems,
):
    e, t = pl.program_id(0), pl.program_id(1)
    tile, width = dx_ref.shape
    rows = pl.ds(pl.multiple_of(t * tile, tile), tile)
    x = x_ref[...]
    dz = dz_ref[...]
    load_weights(w0_ref, w1_hbm, w1_ref, w1_sem, wg, wu, wd)
    mine, gate = pick_gate(gates_ref[...], expert_id(e, 1))
    back = dot_nt(dz, wd[...])
    hidden, grad_gate, grad_up = grads_of(
        gact_ref[0].astype(F32), uact_ref[0].astype(F32), back, gate
    )
    ggterm = gate_terms(mine, hidden, back)
    gated = (hidden * gate).astype(BF16)
    dx = dot_nt(grad_gate, wg[...]) + dot_nt(grad_up, wu[...])

    @pl.when(e == 0)
    def _():
        dxacc[rows, :] = dxin_ref[...].astype(F32) + dx
        ggacc[t] = ggin_ref[...] + ggterm

    @pl.when(e == 1)
    def _():
        dx_ref[...] = (dxacc[rows, :] + dx).astype(BF16)
        gg_ref[...] = ggacc[t] + ggterm

    collect_terms(x, dz, grad_gate, grad_up, gated, ag, au, ad, stage, dw0, dw1, dw_sems)


def run_experts(which, x, dz, weights, router=None, gates=None, carried=None, acts=None):
    tokens, width = x.shape
    packed0, packed1 = weights
    hidden = packed0.shape[3]
    tile = tokens // 3
    tiles = 3
    like = jax.ShapeDtypeStruct
    any_spec = pl.BlockSpec(memory_space=pl.ANY)
    once = pl.Buffered(1)

    def by_token(e, t):
        return (t, 0)

    def at_end(e, t):
        return (jnp.where(e == 1, t, 0), 0)

    def at_start(e, t):
        return (jnp.where(e == 0, t, tiles - 1), 0)

    def lanes_end(e, t):
        return (0, jnp.where(e == 1, t, 0))

    def lanes_start(e, t):
        return (0, jnp.where(e == 0, t, tiles - 1))

    def acts_map(e, t):
        return (e, t, 0)

    x_spec = pl.BlockSpec((tile, width), by_token)
    wide_spec = pl.BlockSpec((tile, width + LANES), by_token)
    gates_spec = pl.BlockSpec((tile, LANES), by_token)
    w_spec = pl.BlockSpec(packed0.shape, lambda e, t: (0, 0, 0, 0), pipeline_mode=once)
    acts_spec = pl.BlockSpec((1, tile, hidden), acts_map)
    token_end = pl.BlockSpec((tile, width), at_end)
    token_start = pl.BlockSpec((tile, width), at_start)
    packed_like = like(packed0.shape, BF16)
    token_like = like((tokens, width), BF16)
    gg_like = like((E, tokens), F32)
    acts_like = like((2, tokens, hidden), BF16)
    unpacked = [
        pltpu.VMEM((width, hidden), BF16),
        pltpu.VMEM((width, hidden), BF16),
        pltpu.VMEM((hidden, width), BF16),
    ]
    terms = [
        pltpu.VMEM((width, hidden), F32),
        pltpu.VMEM((width, hidden), F32),
        pltpu.VMEM((hidden, width), F32),
    ]
    acc = pltpu.VMEM((tokens, width), F32)
    gg_acc = pltpu.VMEM((tiles, E, tile), F32)
    second = pltpu.VMEM(packed1.shape, BF16)
    stage = pltpu.VMEM((2,) + packed0.shape, BF16)
    sem, sems = pltpu.SemaphoreType.DMA, pltpu.SemaphoreType.DMA((2,))
    flops = 4.0 * tokens * width * hidden
    if which == "both":
        return pl.pallas_call(
            both_kernel,
            grid=(2, tiles),
            in_specs=[
                x_spec, wide_spec,
                pl.BlockSpec((width, LANES), lambda e, t: (0, 2), pipeline_mode=once),
                w_spec, any_spec,
            ],
            out_specs=[
                token_end, token_end, pl.BlockSpec((E, tile), lanes_end),
                pl.BlockSpec((tile, LANES), at_end), any_spec, any_spec,
            ],
            out_shape=[
                token_like, token_like, gg_like, like((tokens, LANES), F32),
                packed_like, packed_like,
            ],
            scratch_shapes=unpacked
            + [pltpu.VMEM((tokens, LANES), F32)]
            + terms
            + [acc, acc, gg_acc, second, stage, sem, sems],
            compiler_params=params(),
            cost_estimate=cost(9 * flops, 2e7),
        )(x, dz, router, packed0, packed1)
    if which == "forward":
        return pl.pallas_call(
            forward_kernel,
            grid=(2, tiles),
            in_specs=[x_spec, gates_spec, w_spec, any_spec, token_start],
            out_specs=[token_end, acts_spec, acts_spec],
            out_shape=[token_like, acts_like, acts_like],
            scratch_shapes=unpacked + [acc, second, sem],
            compiler_params=params(),
            cost_estimate=cost(3 * flops, 2e7),
        )(x, gates, packed0, packed1, carried)
    return pl.pallas_call(
        backward_kernel,
        grid=(2, tiles),
        in_specs=[
            x_spec, x_spec, gates_spec, acts_spec, acts_spec, w_spec, any_spec,
            token_start, pl.BlockSpec((E, tile), lanes_start),
        ],
        out_specs=[token_end, pl.BlockSpec((E, tile), lanes_end), any_spec, any_spec],
        out_shape=[token_like, gg_like, packed_like, packed_like],
        scratch_shapes=unpacked + terms + [acc, gg_acc, second, stage, sem, sems],
        compiler_params=params(),
        cost_estimate=cost(6 * flops, 2e7),
    )(x, dz, gates, acts[0], acts[1], packed0, packed1, carried[0], carried[1])


def return_kernel(
    dx_ref, gg_ref, mixed_ref, normed_ref, dz_ref, small_ref, w_ref, ctx_ref,
    do_out, gmixed_ref, term_ref,
    parts, gparts, gctx, send, recv, local,
):
    seq = lax.axis_index("seq")
    me = seq % UNIT
    base = seq - me
    unit = [(me + k) % UNIT for k in range(1, UNIT)]
    peers = neighbours(seq)[:3]
    greet([{"seq": base + b} for b in unit])
    pushes = Pushes(send, recv)
    count, width = mixed_ref.shape
    copies = []
    for n in (2, 0, 1):
        part = gg_ref.at[:, pl.ds((n + 1) * count, count)]
        copies.append(pushes.start(part, gparts.at[n + 1], {"seq": peers[n]}))
        copies.append(pushes.start(dx_ref.at[n + 1], parts.at[n + 1], {"seq": peers[n]}))
    own = [
        pltpu.make_async_copy(dx_ref.at[0], parts.at[0], local.at[0]),
        pltpu.make_async_copy(gg_ref.at[:, pl.ds(0, count)], gparts.at[0], local.at[1]),
    ]
    for copy in own:
        copy.start()
    dz_all = dz_ref[...]
    dz = dz_all[:, :width].astype(F32)
    small = small_ref[...]
    gates = soft_gates(normed_ref[...], small, dz_all[:, width:].astype(F32))
    gain = gain_row(small, E + 1)
    v = mixed_ref[...]
    inverse = lax.rsqrt(jnp.mean(v * v, axis=-1, keepdims=True) + EPS)
    for copy in own:
        copy.wait()
    for copy in copies:
        copy.wait_recv()
    grad_gates = gparts[0] + gparts[1] + gparts[2] + gparts[3]
    grad_gates = jnp.concatenate([grad_gates, jnp.zeros((LANES - E, count), F32)], axis=0).T
    centre = jnp.sum(gates * grad_gates, axis=-1, keepdims=True)
    glog = (gates * (grad_gates - centre)).astype(BF16)
    dy = parts[0].astype(F32)
    for n in range(1, 4):
        dy = dy + parts[n].astype(F32)
    dy = dy + dot_nt(glog, small)
    scaled = dy * gain
    mean = jnp.mean(scaled * v, axis=-1, keepdims=True)
    gmixed = dz + scaled * inverse - v * (inverse * inverse * inverse * mean)
    gmixed_ref[...] = gmixed
    gbranch = gmixed.astype(BF16)
    grad_ctx = dot_nt(gbranch, w_ref[...]).astype(BF16)
    for b in range(UNIT):
        gctx[b] = grad_ctx[:, b * LANES : (b + 1) * LANES].reshape(gctx.shape[1:])
    mine = pltpu.make_async_copy(gctx.at[me], do_out.at[me], local.at[2])
    mine.start()
    sent = [pushes.start(gctx.at[b], do_out.at[me], {"seq": base + b}) for b in unit]
    term_ref[:, :width] = dot_tn(ctx_ref[...], gbranch).astype(BF16)
    term_ref[:, width:] = dot_tn(normed_ref[...], glog).astype(BF16)
    for copy in copies:
        copy.wait_send()
    mine.wait()
    for copy in sent:
        copy.wait()


def return_tokens(dx, gg, mixed, normed, dz, heads, w_out, context, micro, collective):
    any_spec = pl.BlockSpec(memory_space=pl.ANY)
    like = jax.ShapeDtypeStruct
    count, width = mixed.shape
    ctx_shape = (UNIT, micro, count // micro, LANES)

    def fixed(i):
        return (0, 0)

    return pl.pallas_call(
        return_kernel,
        grid=(1,),
        in_specs=[
            any_spec,
            any_spec,
            pl.BlockSpec(mixed.shape, fixed),
            pl.BlockSpec(normed.shape, fixed),
            pl.BlockSpec(dz.shape, fixed),
            pl.BlockSpec((width, LANES), lambda i: (0, 2)),
            pl.BlockSpec(w_out.shape, fixed),
            pl.BlockSpec(context.shape, fixed),
        ],
        out_specs=[
            any_spec,
            pl.BlockSpec((count, width), fixed),
            pl.BlockSpec((width, width + LANES), fixed),
        ],
        out_shape=[
            like(ctx_shape, BF16),
            like((count, width), F32),
            like((width, width + LANES), BF16),
        ],
        scratch_shapes=[
            pltpu.VMEM((4, count, width), BF16),
            pltpu.VMEM((4, E, count), F32),
            pltpu.VMEM(ctx_shape, BF16),
            pltpu.SemaphoreType.DMA((UNIT + 5,)),
            pltpu.SemaphoreType.DMA((UNIT + 5,)),
            pltpu.SemaphoreType.DMA((3,)),
        ],
        compiler_params=params(collective_id=collective, has_side_effects=True),
        cost_estimate=cost(4.0 * count * width * width, 1.2e8),
    )(dx, gg, mixed, normed, dz, heads, w_out, context)


def shards(
    copies, tokens, segments, routes, cotangent, norm_attn, w_query, w_key, w_value, w_out, norm_ffn,
    w_router, w_gate, w_up, w_down, rows,
):
    micro, local_len, width = tokens.shape
    length = segments.shape[1]
    count = micro * local_len
    unit_len = UNIT * local_len
    part = w_query.shape[0]
    hidden = w_gate.shape[2]
    seq_size = copies * UNIT
    seq = lax.axis_index("seq")
    row = lax.axis_index("row")
    unit = seq // UNIT
    me = seq % UNIT
    unit_groups = None
    copy_groups = None
    if copies > 1:
        unit_groups = [[a * UNIT + b for b in range(UNIT)] for a in range(copies)]
        copy_groups = [[a * UNIT + b for a in range(copies)] for b in range(UNIT)]

    def exchange(x):
        return lax.all_to_all(x, "seq", 0, 0, tiled=True, axis_index_groups=unit_groups)

    def flip(x, k):
        return lax.ppermute(x, "seq", [(s, s ^ k) for s in range(seq_size)])

    flat_tokens = tokens.reshape(count, width)

    def wait_for(x, *others):
        return lax.optimization_barrier((x,) + others)[0]

    small = jnp.concatenate(
        [
            w_router,
            norm_attn[:, None],
            norm_ffn[:, None],
            jnp.zeros((part, LANES - 2 - E), BF16),
        ],
        axis=1,
    )
    head_part = jnp.concatenate(
        [
            w_query.reshape(part, UNIT, 2 * HD),
            w_key.reshape(part, UNIT, HD),
            w_value.reshape(part, UNIT, HD),
            jnp.broadcast_to(small[:, None], (part, UNIT, LANES)),
        ],
        axis=2,
    ).transpose(1, 0, 2)

    down_halves = w_down.reshape(E, -1, 2, hidden).transpose(0, 2, 1, 3).reshape(E, part, hidden)
    packed_part = jnp.concatenate([w_gate, w_up, down_halves], axis=1)
    packed_part = packed_part.reshape(UNIT, E // UNIT, 3 * part, hidden).transpose(1, 0, 2, 3)
    *packed_mine, heads_all, w_out_rows = begin(
        rows, packed_part[0], packed_part[1], head_part, w_out
    )

    if copies > 1:
        heads_all = lax.all_gather(heads_all, "seq", axis=0, axis_index_groups=copy_groups)
        w_out_rows = lax.all_gather(w_out_rows, "seq", axis=0, axis_index_groups=copy_groups)
    else:
        w_out_rows = w_out_rows[None]
    heads_all = heads_all.reshape(width, 4 * HD + LANES)

    def gather_packed(x):
        x = lax.all_gather(x, "row", axis=0)
        if copies > 1:
            x = lax.all_gather(x, "seq", axis=0, axis_index_groups=copy_groups)
            x = x.transpose(0, 2, 1, 3, 4).reshape(-1, 3 * part, hidden)
            halves = x[:, 2 * part :].reshape(-1, 2, part // 2, hidden).transpose(0, 2, 1, 3)
            return pack(
                x[:, :part].reshape(width, hidden),
                x[:, part : 2 * part].reshape(width, hidden),
                halves.reshape(hidden, width),
            )
        return x

    def pack(gate, up, down):
        gate = gate.reshape(UNIT, PIECES, ROWS_IN, hidden)
        up = up.reshape(UNIT, PIECES, ROWS_IN, hidden)
        down = down.reshape(UNIT, PIECES, ROWS_OUT, 2, hidden).transpose(0, 1, 3, 2, 4)
        down = down.reshape(UNIT, PIECES, ROWS_IN, hidden)
        return jnp.concatenate([gate, up, down], axis=2).transpose(1, 0, 2, 3)

    def repack(x):
        x = x.transpose(1, 0, 2, 3)
        gate = x[:, :, :ROWS_IN].reshape(copies, UNIT, rows, part, hidden)
        up = x[:, :, ROWS_IN : 2 * ROWS_IN].reshape(copies, UNIT, rows, part, hidden)
        down = x[:, :, 2 * ROWS_IN :].reshape(UNIT, PIECES, 2, ROWS_OUT, hidden)
        down = down.transpose(0, 1, 3, 2, 4).reshape(copies, UNIT, rows, part // 2, 2, hidden)
        down = down.transpose(0, 1, 2, 4, 3, 5).reshape(copies, UNIT, rows, part, hidden)
        return jnp.concatenate([gate, up, down], axis=3).transpose(2, 0, 1, 3, 4)

    own_weights = [gather_packed(x) for x in packed_mine]

    tok_all, w_out_all = unit_gather(
        [wait_for(flat_tokens, w_out_rows), w_out_rows.reshape(-1, width)], 1
    )
    tok_all = tok_all.reshape(UNIT, micro, local_len, width)
    w_out_all = w_out_all.reshape(UNIT, copies, rows * part, width)
    w_out_all = w_out_all.transpose(1, 0, 2, 3).reshape(H * HD, width)

    chosen = jnp.any(
        routes.reshape(count, TOPK)[:, :, None] == jnp.arange(LANES, dtype=jnp.int32)[None, None, :],
        axis=1,
    ).astype(BF16)
    dz_own = jnp.concatenate([cotangent.reshape(count, width), chosen], axis=1)
    dz_send = wait_for(dz_own, tok_all)
    dz_pieces = [dz_send] + [flip(dz_send, k) for k in (2, 4, 6)]

    frequency = BASE ** (-2.0 * np.arange(HD // 2) / HD)
    angles = np.arange(length)[:, None].astype(np.float32) * frequency[None].astype(np.float32)
    key_cos = jnp.asarray(np.tile(np.cos(angles), (1, 4)).astype(np.float32))
    key_sin = np.concatenate([-np.sin(angles), np.sin(angles)] * 2, axis=1)
    key_sin = jnp.asarray(key_sin.astype(np.float32))
    places = unit * unit_len + jnp.arange(unit_len, dtype=jnp.int32)
    cosine, sine = key_cos, key_sin
    if copies > 1:
        cosine = lax.dynamic_slice_in_dim(key_cos, unit * unit_len, unit_len, 0)
        sine = lax.dynamic_slice_in_dim(key_sin, unit * unit_len, unit_len, 0)

    def by_row4(m):
        return (0, m, 0, 0)

    def by_row3(m):
        return (m, 0, 0)

    def fixed(*_):
        return (0, 0)

    def zeros3(*_):
        return (0, 0, 0)

    def zeros4(*_):
        return (0, 0, 0, 0)

    def small_block(*_):
        return (0, 2)

    normed_all, q_all, kv_own = pl.pallas_call(
        project_kernel,
        grid=(micro,),
        in_specs=[
            pl.BlockSpec((UNIT, 1, local_len, width), by_row4),
            pl.BlockSpec((width, LANES), small_block),
            pl.BlockSpec((width, 4 * HD), fixed),
            pl.BlockSpec((unit_len, LANES), fixed),
            pl.BlockSpec((unit_len, LANES), fixed),
        ],
        out_specs=[
            pl.BlockSpec((UNIT, 1, local_len, width), by_row4),
            pl.BlockSpec((1, unit_len, LANES), by_row3),
            pl.BlockSpec((1, unit_len, LANES), by_row3),
        ],
        out_shape=[
            jax.ShapeDtypeStruct((UNIT, micro, local_len, width), BF16),
            jax.ShapeDtypeStruct((micro, unit_len, LANES), BF16),
            jax.ShapeDtypeStruct((micro, unit_len, LANES), BF16),
        ],
        compiler_params=params(),
        cost_estimate=cost(2.0 * UNIT * count * width * 4 * HD, 1.5e7),
    )(tok_all, heads_all, heads_all, cosine, sine)

    kv_all = kv_own
    if copies > 1:
        kv_all = lax.all_gather(kv_own, "seq", axis=1, tiled=True, axis_index_groups=copy_groups)
    seg_keys = segments.astype(F32).reshape(micro, 1, length)
    seg_queries = lax.dynamic_slice_in_dim(seg_keys, unit * unit_len, unit_len, 2)
    skip = copies == 1
    place_row = places[None]
    attention_flops = 4.0 * micro * unit_len * length * 2 * LANES
    attention_specs = [
        pl.BlockSpec((1, unit_len, LANES), by_row3),
        pl.BlockSpec((1, length, LANES), by_row3),
        pl.BlockSpec((1, 1, unit_len), by_row3),
        pl.BlockSpec((1, 1, length), by_row3),
        pl.BlockSpec((1, unit_len), fixed),
    ]
    ctx_heads, lse = pl.pallas_call(
        functools.partial(attention_kernel, skip),
        grid=(micro,),
        in_specs=attention_specs,
        out_specs=[
            pl.BlockSpec((UNIT, 1, local_len, LANES), by_row4),
            pl.BlockSpec((1, 2, unit_len), by_row3),
        ],
        out_shape=[
            jax.ShapeDtypeStruct((UNIT, micro, local_len, LANES), BF16),
            jax.ShapeDtypeStruct((micro, 2, unit_len), F32),
        ],
        compiler_params=params(),
        cost_estimate=cost(attention_flops, 4e6),
    )(q_all, kv_all, seg_queries, seg_keys, place_row)
    x_all, sib_first, dz_all, mixed, normed_ffn, context = bridge(
        ctx_heads, own_weights[0], dz_pieces, w_out_all, flat_tokens, heads_all, 2
    )
    x_all = x_all.reshape(4 * count, width)
    dz_all = dz_all.reshape(4 * count, width + LANES)
    w_heads = lax.all_gather(
        wait_for(heads_all, x_all)[:, : 4 * HD], "seq", axis=0, axis_index_groups=unit_groups
    )

    out_part, dx_part, gg_part, gates_all, sib_term, own_term = run_experts(
        "both", x_all, dz_all, (sib_first, own_weights[0]), router=heads_all
    )
    def merge(own, sib):
        return (own.astype(F32) + sib.astype(F32)).astype(BF16)

    def finish_expert(total):
        if copies > 1:
            total = repack(total)
            total = lax.psum_scatter(total, "row", scatter_dimension=0)
            total = lax.psum_scatter(
                total, "seq", scatter_dimension=0, axis_index_groups=copy_groups
            )
        else:
            total = lax.psum_scatter(total, "row", scatter_dimension=0)
        return total

    total_first = merge(wait_for(own_term, w_heads), flip(sib_term, 1))
    second = wait_for(own_weights[1], x_all)
    pair = (second, flip(second, 1))
    out_part, gate_acts, up_acts = run_experts(
        "forward", x_all, None, pair, gates=gates_all, carried=out_part
    )
    reduced_first = finish_expert(total_first)
    out_split = out_part.reshape(4, count, width)
    out_pieces = [out_split[0]] + [flip(out_split[i], 2 * i) for i in (1, 2, 3)]
    dx_part, gg_part, own_term, sib_term = run_experts(
        "backward", x_all, wait_for(dz_all, total_first), pair, gates=gates_all,
        carried=(dx_part, gg_part), acts=(gate_acts, up_acts),
    )
    reduced_second = finish_expert(merge(own_term, flip(sib_term, 1)))
    do_heads, gmixed, out_term = return_tokens(
        dx_part.reshape(4, count, width), gg_part, mixed, normed_ffn, dz_own, heads_all, w_out_all,
        context, micro, 3,
    )
    graw, head_term = pl.pallas_call(
        functools.partial(attention_back_kernel, skip),
        grid=(micro,),
        in_specs=attention_specs
        + [
            pl.BlockSpec((1, 2, unit_len), by_row3),
            pl.BlockSpec((UNIT, 1, local_len, LANES), by_row4),
            pl.BlockSpec((unit_len, LANES), fixed),
            pl.BlockSpec((unit_len, LANES), fixed),
            pl.BlockSpec((length, LANES), fixed),
            pl.BlockSpec((length, LANES), fixed),
            pl.BlockSpec((UNIT, 1, local_len, width), by_row4),
        ],
        out_specs=[
            pl.BlockSpec((seq_size, 1, local_len, 2 * LANES), by_row4),
            pl.BlockSpec((PIECES, UNIT, ROWS_IN, 2 * LANES), zeros4),
        ],
        out_shape=[
            jax.ShapeDtypeStruct((seq_size, micro, local_len, 2 * LANES), BF16),
            jax.ShapeDtypeStruct((PIECES, UNIT, ROWS_IN, 2 * LANES), BF16),
        ],
        scratch_shapes=[
            pltpu.VMEM((length, LANES), F32),
            pltpu.VMEM((length, LANES), F32),
            pltpu.VMEM((width, 2 * LANES), F32),
        ],
        compiler_params=params(),
        cost_estimate=cost(2.5 * attention_flops, 8e6),
    )(
        q_all, kv_all, seg_queries, seg_keys, place_row, lse, do_heads,
        cosine, sine, key_cos, key_sin, normed_all,
    )
    if copies > 1:
        graw_kv = lax.psum_scatter(
            graw[..., LANES:], "seq", scatter_dimension=0, tiled=True,
            axis_index_groups=copy_groups,
        )
        graw = jnp.concatenate([graw[:UNIT, ..., :LANES], graw_kv], axis=3)
        head_term = jnp.einsum(
            "nd,nh->dh",
            normed_all.reshape(UNIT * count, width),
            graw.reshape(UNIT * count, 2 * LANES),
            preferred_element_type=F32,
        ).astype(BF16)
        head_term = head_term.reshape(copies, UNIT, rows, part, 2 * LANES)
        head_term = lax.psum_scatter(
            head_term, "seq", scatter_dimension=0, axis_index_groups=copy_groups
        ).transpose(1, 0, 2, 3)
        out_term = out_term.reshape(copies, UNIT, rows, part, width + LANES)
        out_term = lax.psum_scatter(
            out_term, "seq", scatter_dimension=0, axis_index_groups=copy_groups
        )
    else:
        out_term = out_term.reshape(UNIT, rows, part, width + LANES)
    out_mine = exchange(out_term)
    head_grad, out_grad, grad_input = finish(
        rows, graw, head_term, out_mine, w_heads, flat_tokens, heads_all, gmixed, 4
    )
    block_out = wait_for(mixed, head_grad)
    for piece in out_pieces:
        block_out = block_out + piece.astype(F32)

    finished = [exchange(reduced_first), exchange(reduced_second)]
    finished = jnp.stack(finished, axis=1).reshape(E, 3 * part, hidden).astype(F32)
    grad_gate = finished[:, :part]
    grad_up = finished[:, part : 2 * part]
    grad_down = finished[:, 2 * part :].reshape(E, 2, -1, hidden).transpose(0, 2, 1, 3)
    grad_down = grad_down.reshape(E, -1, width)
    head_grad = head_grad.astype(F32)
    grad_query = head_grad[:, :, :LANES].transpose(1, 0, 2).reshape(part, H * HD)
    grad_key = head_grad[:, :, LANES : LANES + HD].transpose(1, 0, 2).reshape(part, KVH * HD)
    grad_value = head_grad[:, :, LANES + HD :].transpose(1, 0, 2).reshape(part, KVH * HD)
    grad_out = out_grad[:, :width]
    grad_router = out_grad[:, width : width + E]

    attn_weights = jnp.concatenate([w_query, w_key, w_value], axis=1).astype(F32)
    attn_grads = jnp.concatenate([grad_query, grad_key, grad_value], axis=1)
    grad_norm_attn = jnp.sum(attn_weights * attn_grads, axis=1) / norm_attn.astype(F32)
    grad_norm_ffn = (
        jnp.sum(w_gate.astype(F32) * grad_gate, axis=(0, 2))
        + jnp.sum(w_up.astype(F32) * grad_up, axis=(0, 2))
        + jnp.sum(w_router.astype(F32) * grad_router, axis=1)
    ) / norm_ffn.astype(F32)
    return (
        block_out.astype(BF16).reshape(tokens.shape),
        grad_input.reshape(tokens.shape),
        grad_norm_attn,
        grad_query,
        grad_key,
        grad_value,
        grad_out,
        grad_norm_ffn,
        grad_router,
        grad_gate,
        grad_up,
        grad_down,
    )


def solution(mesh):
    both = ("seq", "row")
    body = functools.partial(shards, mesh.shape["seq"] // UNIT, rows=mesh.shape["row"])
    return jax.shard_map(
        body,
        mesh=mesh,
        in_specs=(
            P("row", "seq", None),
            P("row", None),
            P("row", "seq", None),
            P("row", "seq", None),
            P(both),
            P(both, None),
            P(both, None),
            P(both, None),
            P(both, None),
            P(both),
            P(both, None),
            P(None, both, None),
            P(None, both, None),
            P(None, both, None),
        ),
        out_specs=(
            P("row", "seq", None),
            P("row", "seq", None),
            P(both),
            P(both, None),
            P(both, None),
            P(both, None),
            P(both, None),
            P(both),
            P(both, None),
            P(None, both, None),
            P(None, both, None),
            P(None, both, None),
        ),
        check_vma=False,
    )
```

```python
import functools

import jax
import jax.numpy as jnp
import numpy as np
from jax import lax
from jax.experimental import pallas as pl
from jax.experimental.pallas import tpu as pltpu
from jax.sharding import PartitionSpec as P

H = 16
KVH = 8
TOPK = 8
HD = 64
E = 16
UNIT = 8
LANES = 128
QBLOCK = 256
PIECES = 4
ROWS_IN = 32
ROWS_OUT = 16

EPS = 1e-05
BASE = 10000.0
NEGATIVE = -1e30
F32 = jnp.float32
BF16 = jnp.bfloat16
VMEM_LIMIT = 60 * 1024 * 1024


def dot_nn(left, right):
    return lax.dot_general(left, right, (((1,), (0,)), ((), ())), preferred_element_type=F32)


def dot_nt(left, right):
    return lax.dot_general(left, right, (((1,), (1,)), ((), ())), preferred_element_type=F32)


def dot_tn(left, right):
    return lax.dot_general(left, right, (((0,), (0,)), ((), ())), preferred_element_type=F32)


def params(**kw):
    return pltpu.CompilerParams(vmem_limit_bytes=VMEM_LIMIT, **kw)


def cost(flops, nbytes):
    return pl.CostEstimate(flops=int(flops), bytes_accessed=int(nbytes), transcendentals=0)


def neighbours(seq):
    core = seq % 2
    chip = (seq // 2) % 4
    base = seq - seq % UNIT

    def at(other, same=True):
        return base + 2 * other + (core if same else 1 - core)

    across = chip + 1 - 2 * (chip % 2)
    along = (chip + 2) % 4
    return at(across), at(along), at(3 - chip), at(chip, False)


def greet(targets):
    barrier = pltpu.get_barrier_semaphore()
    for target in targets:
        pl.semaphore_signal(
            barrier, inc=1, device_id=target, device_id_type=pl.DeviceIdType.MESH
        )
    pl.semaphore_wait(barrier, len(targets))


class Pushes:
    def __init__(self, send, recv):
        self.send, self.recv, self.used = send, recv, 0

    def start(self, source, target, device):
        copy = self.make(source, target, device)
        copy.start()
        return copy

    def make(self, source, target, device):
        n = self.used
        self.used += 1
        return pltpu.make_async_remote_copy(
            src_ref=source,
            dst_ref=target,
            send_sem=self.send.at[n],
            recv_sem=self.recv.at[n],
            device_id=device,
            device_id_type=pl.DeviceIdType.MESH,
        )


class Bounce:
    def __init__(self, source, middle, target, sems, start=True):
        self.inward = pltpu.make_async_copy(source, middle, sems.at[0])
        self.outward = pltpu.make_async_copy(middle, target, sems.at[1])
        if start:
            self.inward.start()

    def turn(self):
        self.inward.wait()
        self.outward.start()

    def wait(self):
        self.outward.wait()


def begin_kernel(
    rows, packed0, packed1, head_ref, wout_ref, mine0, mine1, head_all, wout_all,
    head_mine, own0, own1, own2, send, recv, local,
):
    seq, row = lax.axis_index("seq"), lax.axis_index("row")
    me = seq % UNIT
    base = seq - me
    unit = [(me + k) % UNIT for k in range(1, UNIT)]
    column = [(row + k) % rows for k in range(1, rows)]
    greet([{"seq": base + b} for b in unit] + [{"row": r} for r in column])
    pushes = Pushes(send, recv)
    first = pltpu.make_async_copy(head_ref.at[me], head_mine.at[me], local.at[3, 0])
    first.start()
    heads = [pushes.start(head_ref.at[b], head_mine.at[me], {"seq": base + b}) for b in unit]
    others = [pushes.start(wout_ref, wout_all.at[row], {"row": r}) for r in column]
    for source, target in ((packed0, mine0), (packed1, mine1)):
        others += [pushes.start(source.at[b], target.at[me], {"seq": base + b}) for b in unit]
    own = [
        Bounce(packed0.at[me], own0, mine0.at[me], local.at[0]),
        Bounce(packed1.at[me], own1, mine1.at[me], local.at[1]),
        Bounce(wout_ref, own2, wout_all.at[row], local.at[2]),
    ]
    for copy in own:
        copy.turn()
    first.wait()
    for copy in heads:
        copy.wait_recv()
    last = pltpu.make_async_copy(head_mine, head_all.at[:, row], local.at[3, 1])
    last.start()
    others += [pushes.start(head_mine, head_all.at[:, row], {"row": r}) for r in column]
    for copy in heads:
        copy.wait_send()
    for copy in own + [last]:
        copy.wait()
    for copy in others:
        copy.wait()


def begin(rows, packed0, packed1, head_part, w_out):
    any_spec = pl.BlockSpec(memory_space=pl.ANY)
    count = 3 * (UNIT - 1) + 2 * (rows - 1)
    like = jax.ShapeDtypeStruct
    return pl.pallas_call(
        functools.partial(begin_kernel, rows),
        in_specs=[any_spec] * 4,
        out_specs=[any_spec] * 4,
        out_shape=[
            like(packed0.shape, BF16),
            like(packed1.shape, BF16),
            like(head_part.shape[:1] + (rows,) + head_part.shape[1:], BF16),
            like((rows,) + w_out.shape, BF16),
        ],
        scratch_shapes=[
            pltpu.VMEM(head_part.shape, BF16),
            pltpu.VMEM(packed0.shape[1:], BF16),
            pltpu.VMEM(packed0.shape[1:], BF16),
            pltpu.VMEM(w_out.shape, BF16),
            pltpu.SemaphoreType.DMA((count,)),
            pltpu.SemaphoreType.DMA((count,)),
            pltpu.SemaphoreType.DMA((4, 2)),
        ],
        compiler_params=pltpu.CompilerParams(collective_id=0, has_side_effects=True),
        cost_estimate=cost(1, 2e7),
    )(packed0, packed1, head_part, w_out)


def unit_gather_kernel(sources, *refs):
    ins, outs = refs[:sources], refs[sources : 2 * sources]
    middles = refs[2 * sources : 3 * sources]
    send, recv, local = refs[3 * sources :]
    seq = lax.axis_index("seq")
    me = seq % UNIT
    base = seq - me
    across, along, _, twin = neighbours(seq)
    a, b, t = across - base, along - base, twin - base
    d = UNIT - 1 - me + 2 * (me % 2) - 1
    greet([{"seq": across}, {"seq": along}, {"seq": twin}])
    pushes = Pushes(send, recv)
    own, done, stage = [], [], []
    for n, (source, target) in enumerate(zip(ins, outs)):
        half = source.shape[0] // 2
        halves = [pl.ds(0, half), pl.ds(half, half)]
        own.append(Bounce(source, middles[n], target.at[me], local.at[n]))

        def part(device, h, source=source, target=target, halves=halves):
            return pushes.start(
                source.at[halves[h]], target.at[me, halves[h]], {"seq": device}
            )

        xa, yb = part(across, 0), part(along, 1)
        xb, ya = part(across, 1), part(along, 0)
        done.append(pushes.start(source, target.at[me], {"seq": twin}))
        stage.append((target, halves, xa, yb, xb, ya))
    for copy in own:
        copy.turn()
    for target, halves, xa, yb, xb, ya in stage:

        def pass_on(slot, h, device, target=target, halves=halves):
            view = target.at[slot, halves[h]]
            return pushes.start(view, view, {"seq": device})

        xa.wait_recv()
        da = pass_on(a, 0, along)
        done.append(pass_on(a, 0, twin))
        yb.wait_recv()
        db = pass_on(b, 1, across)
        done.append(pass_on(b, 1, twin))
        xb.wait_recv()
        done.append(pass_on(a, 1, twin))
        ya.wait_recv()
        done.append(pass_on(b, 0, twin))
        da.wait_recv()
        done.append(pass_on(d, 0, twin))
        db.wait_recv()
        done.append(pass_on(d, 1, twin))
        for copy in (xa, yb, xb, ya, da, db):
            copy.wait_send()
    for copy in own + done:
        copy.wait()


def unit_gather(sources, collective):
    any_spec = pl.BlockSpec(memory_space=pl.ANY)
    n = len(sources)
    return pl.pallas_call(
        functools.partial(unit_gather_kernel, n),
        in_specs=[any_spec] * n,
        out_specs=[any_spec] * n,
        out_shape=[jax.ShapeDtypeStruct((UNIT,) + x.shape, x.dtype) for x in sources],
        scratch_shapes=[pltpu.VMEM(x.shape, x.dtype) for x in sources]
        + [
            pltpu.SemaphoreType.DMA((13 * n,)),
            pltpu.SemaphoreType.DMA((13 * n,)),
            pltpu.SemaphoreType.DMA((n, 2)),
        ],
        compiler_params=params(collective_id=collective, has_side_effects=True),
        cost_estimate=cost(1, 8e7),
    )(*sources)


def bridge_kernel(
    ctx_ref, weights, z0, z1, z2, z3, w_ref, tok_ref, small_ref,
    target, flipped, z_all, mixed_ref, normed_ref, ctx_out,
    ctx_in, z_middle, send, recv, local,
):
    seq = lax.axis_index("seq")
    me = seq % UNIT
    base = seq - me
    unit = [(me + k) % UNIT for k in range(1, UNIT)]
    across, along, _, twin = neighbours(seq)
    greet([{"seq": base + b} for b in unit])
    pushes = Pushes(send, recv)
    arrivals = [pushes.start(ctx_ref.at[b], ctx_in.at[me], {"seq": base + b}) for b in unit]
    mine = pltpu.make_async_copy(ctx_ref.at[me], ctx_in.at[me], local.at[4, 0])
    mine.start()
    turned = pushes.start(weights, flipped, {"seq": twin})
    own = [
        Bounce(piece, z_middle.at[n], z_all.at[n], local.at[n])
        for n, piece in enumerate((z0, z1, z2, z3))
    ]
    count, width = tok_ref.shape
    half = count // 2
    gain = gain_row(small_ref[...], E + 1)
    mine.wait()
    for copy in arrivals:
        copy.wait_recv()
    for b in range(UNIT):
        ctx_out[:, b * LANES : (b + 1) * LANES] = ctx_in[b].reshape(count, LANES)
    halves = [pl.ds(0, half), pl.ds(half, half)]

    def part(device, slot, h):
        return pushes.start(normed_ref.at[halves[h]], target.at[slot, halves[h]], {"seq": device})

    def pass_on(slot, h, device):
        return pushes.start(
            target.at[slot, halves[h]], target.at[3, halves[h]], {"seq": device}
        )

    sent = []
    for h in range(2):
        here = slice(h * half, (h + 1) * half)
        mixed = tok_ref[here].astype(F32) + dot_nn(ctx_out[here], w_ref[...])
        mixed_ref[here] = mixed
        inverse = lax.rsqrt(jnp.mean(mixed * mixed, axis=-1, keepdims=True) + EPS)
        normed_ref[here] = (mixed * inverse * gain).astype(BF16)
        if h == 0:
            xa, ya = part(across, 1, 0), part(along, 2, 0)
        else:
            yb, xb = part(along, 2, 1), part(across, 1, 1)
    last = pltpu.make_async_copy(normed_ref, target.at[0], local.at[4, 1])
    last.start()
    for copy in own:
        copy.turn()
    xa.wait_recv()
    da = pass_on(1, 0, along)
    yb.wait_recv()
    db = pass_on(2, 1, across)
    for copy in (xb, ya, da, db):
        copy.wait_recv()
    for copy in (xa, yb, xb, ya, da, db):
        copy.wait_send()
    for copy in arrivals:
        copy.wait_send()
    turned.wait()
    for copy in own + [last]:
        copy.wait()


def bridge(ctx_heads, weights, z_pieces, w_out, tokens, heads, collective):
    any_spec = pl.BlockSpec(memory_space=pl.ANY)
    like = jax.ShapeDtypeStruct
    count, width = tokens.shape

    def fixed(i):
        return (0, 0)

    return pl.pallas_call(
        bridge_kernel,
        grid=(1,),
        in_specs=[any_spec] * 6
        + [
            pl.BlockSpec(w_out.shape, fixed),
            pl.BlockSpec(tokens.shape, fixed),
            pl.BlockSpec((width, LANES), lambda i: (0, 2)),
        ],
        out_specs=[any_spec] * 3 + [pl.BlockSpec((count, width), fixed)] * 3,
        out_shape=[
            like((4, count, width), BF16),
            like(weights.shape, BF16),
            like((4,) + z_pieces[0].shape, BF16),
            like((count, width), F32),
            like((count, width), BF16),
            like((count, H * HD), BF16),
        ],
        scratch_shapes=[
            pltpu.VMEM(ctx_heads.shape, BF16),
            pltpu.VMEM((4,) + z_pieces[0].shape, BF16),
            pltpu.SemaphoreType.DMA((UNIT + 6,)),
            pltpu.SemaphoreType.DMA((UNIT + 6,)),
            pltpu.SemaphoreType.DMA((5, 2)),
        ],
        compiler_params=params(collective_id=collective, has_side_effects=True),
        cost_estimate=cost(2.0 * count * width * width, 8e7),
    )(ctx_heads, weights, *z_pieces, w_out, tokens, heads)


def finish_kernel(
    rows, graw_ref, head_ref, red_ref, pre_ref, out_ref, w_ref, tok_ref, small_ref, gmixed_ref,
    head_fin, red_out, out_fin, gin_ref,
    head_col, head_sum, out_sum, out_col, raw_in, red_own, send, recv, local,
):
    seq, row = lax.axis_index("seq"), lax.axis_index("row")
    me = seq % UNIT
    base = seq - me
    unit = [(me + k) % UNIT for k in range(1, UNIT)]
    senders = [(me + UNIT - k) % UNIT for k in range(1, UNIT)]
    column = [(row + k) % rows for k in range(1, rows)]
    greet([{"seq": base + b} for b in unit] + [{"row": r} for r in column])
    pushes = Pushes(send, recv)
    first = pltpu.make_async_copy(head_ref.at[row], head_col.at[row], local.at[0, 0])
    first.start()
    second = pltpu.make_async_copy(graw_ref.at[me], raw_in.at[me], local.at[1, 0])
    second.start()
    heads = [pushes.start(head_ref.at[r], head_col.at[row], {"row": r}) for r in column]
    raws = [pushes.start(graw_ref.at[b], raw_in.at[me], {"seq": base + b}) for b in unit]
    others = [pushes.start(red_ref.at[b], red_out.at[me], {"seq": base + b}) for b in unit]
    bounce = Bounce(red_ref.at[me], red_own, red_out.at[me], local.at[4])
    total = pre_ref[me // 2].astype(F32)
    for n in range(3):
        total = total + out_ref[n].astype(F32)
    out_sum[...] = total.astype(BF16)
    bounce.turn()
    third = pltpu.make_async_copy(out_sum.at[row], out_col.at[row], local.at[2, 0])
    third.start()
    outs = [pushes.start(out_sum.at[r], out_col.at[row], {"row": r}) for r in column]
    first.wait()
    for copy in heads:
        copy.wait_recv()
    total = head_col[0].astype(F32)
    for r in range(1, rows):
        total = total + head_col[r].astype(F32)
    head_sum[...] = total.astype(BF16)
    fourth = pltpu.make_async_copy(head_sum.at[me], head_fin.at[me], local.at[3, 0])
    fourth.start()
    others += [pushes.start(head_sum.at[b], head_fin.at[me], {"seq": base + b}) for b in unit]
    count, width = tok_ref.shape
    second.wait()
    acc = dot_nt(raw_in[me].reshape(count, 2 * LANES), w_ref[me])
    for b, copy in zip(senders, raws):
        copy.wait_recv()
        acc = acc + dot_nt(raw_in[b].reshape(count, 2 * LANES), w_ref[b])
    v = tok_ref[...].astype(F32)
    inverse = lax.rsqrt(jnp.mean(v * v, axis=-1, keepdims=True) + EPS)
    scaled = acc * gain_row(small_ref[...], E)
    mean = jnp.mean(scaled * v, axis=-1, keepdims=True)
    grad = gmixed_ref[...] + scaled * inverse - v * (inverse * inverse * inverse * mean)
    gin_ref[...] = grad.astype(BF16)
    third.wait()
    for copy in outs:
        copy.wait_recv()
    total = out_col[0].astype(F32)
    for r in range(1, rows):
        total = total + out_col[r].astype(F32)
    out_fin[...] = total
    for copy in heads + outs + raws:
        copy.wait_send()
    fourth.wait()
    bounce.wait()
    for copy in others:
        copy.wait()


def finish(
    rows, graw, head_term, reduced, pre, out_in, w_heads, tokens, heads, gmixed, collective
):
    any_spec = pl.BlockSpec(memory_space=pl.ANY)
    like = jax.ShapeDtypeStruct
    pushes = 3 * (UNIT - 1) + 2 * (rows - 1)
    count, width = tokens.shape

    def fixed(i):
        return (0, 0)

    return pl.pallas_call(
        functools.partial(finish_kernel, rows),
        grid=(1,),
        in_specs=[
            any_spec,
            any_spec,
            any_spec,
            pl.BlockSpec(pre.shape, lambda i: (0, 0, 0, 0)),
            pl.BlockSpec(out_in.shape, lambda i: (0, 0, 0, 0)),
            pl.BlockSpec(w_heads.shape, lambda i: (0, 0, 0)),
            pl.BlockSpec(tokens.shape, fixed),
            pl.BlockSpec((width, LANES), lambda i: (0, 2)),
            pl.BlockSpec(gmixed.shape, fixed),
        ],
        out_specs=[
            any_spec,
            any_spec,
            pl.BlockSpec(pre.shape[2:], fixed),
            pl.BlockSpec(tokens.shape, fixed),
        ],
        out_shape=[
            like(head_term.shape[1:], BF16),
            like(reduced.shape, BF16),
            like(pre.shape[2:], F32),
            like(tokens.shape, BF16),
        ],
        scratch_shapes=[
            pltpu.VMEM(head_term.shape, BF16),
            pltpu.VMEM(head_term.shape[1:], BF16),
            pltpu.VMEM(pre.shape[1:], BF16),
            pltpu.VMEM(pre.shape[1:], BF16),
            pltpu.VMEM(graw.shape, BF16),
            pltpu.VMEM(reduced.shape[1:], BF16),
            pltpu.SemaphoreType.DMA((pushes,)),
            pltpu.SemaphoreType.DMA((pushes,)),
            pltpu.SemaphoreType.DMA((5, 2)),
        ],
        compiler_params=params(collective_id=collective, has_side_effects=True),
        cost_estimate=cost(4.0 * count * width * width, 6e7),
    )(graw, head_term, reduced, pre, out_in, w_heads, tokens, heads, gmixed)


def lane_iota(shape):
    return lax.broadcasted_iota(jnp.int32, shape, len(shape) - 1)


def turn(u, cosine, sine):
    low_half = lane_iota(u.shape) % HD < HD // 2
    partner = jnp.where(
        low_half, pltpu.roll(u, LANES - HD // 2, u.ndim - 1), pltpu.roll(u, HD // 2, u.ndim - 1)
    )
    return u * cosine + partner * sine


def value_tables(cosine, sine):
    low = lane_iota(cosine.shape) < HD
    return jnp.where(low, cosine, 1.0), jnp.where(low, sine, 0.0)


def gain_row(small, lane):
    return small.astype(F32).T[lane : lane + 1]


def project_kernel(tok_ref, small_ref, w_ref, cos_ref, sin_ref, normed_ref, q_ref, kv_ref):
    count = q_ref.shape[1]
    width = w_ref.shape[0]
    x = tok_ref[...].reshape(count, width).astype(F32)
    inverse = lax.rsqrt(jnp.mean(x * x, axis=-1, keepdims=True) + EPS)
    normed = (x * inverse * gain_row(small_ref[...], E)).astype(BF16)
    normed_ref[...] = normed.reshape(normed_ref.shape)
    raw = dot_nn(normed, w_ref[...])
    cosine, sine = cos_ref[...], sin_ref[...]
    q = turn(raw[:, :LANES], cosine, sine).astype(BF16)
    q_ref[0] = (q.astype(F32) * HD**-0.5).astype(BF16)
    kv_ref[0] = turn(raw[:, LANES:], *value_tables(cosine, sine)).astype(BF16)


def pair_keys(kv):
    kv = kv.astype(F32)
    rolled = pltpu.roll(kv, HD, 1)
    low = lane_iota(kv.shape) < HD
    return jnp.where(low, kv, rolled), jnp.where(low, rolled, kv)


def bias_block(seg_col, seg_row, q_places, first, length):
    key_places = lax.broadcasted_iota(jnp.int32, (length, q_places.shape[1]), 0)
    allowed = (seg_col[:length] == seg_row) & (key_places <= q_places)
    return jnp.where(allowed, 0.0, NEGATIVE)


def attention_kernel(skip, q_ref, kv_ref, segq_ref, segk_ref, place_ref, ctx_ref, lse_ref):
    length = kv_ref.shape[1]
    queries = q_ref.shape[1]
    kk, vv = pair_keys(kv_ref[0])
    v_t = vv.T.astype(BF16)[:HD]
    kk = kk.astype(BF16)
    seg_col = jnp.broadcast_to(segk_ref[0], (8, length)).T[:, :1]
    for block in range(queries // QBLOCK):
        here = slice(block * QBLOCK, (block + 1) * QBLOCK)
        keys = (block + 1) * QBLOCK if skip else length
        bias = bias_block(seg_col, segq_ref[0][:, here], place_ref[:, here], 0, keys)
        q = q_ref[0, here, :]
        low = lane_iota(q.shape) < HD
        parts = []
        for head in range(2):
            mine = jnp.where(low == (head == 0), q, jnp.zeros_like(q))
            scores = dot_nt(kk[:keys], mine) + bias
            top = jnp.max(scores, axis=0, keepdims=True)
            weight = jnp.exp(scores - top)
            total = jnp.sum(weight, axis=0, keepdims=True)
            prob = (weight * (1.0 / total)).astype(BF16)
            parts.append(dot_nn(v_t[:, :keys], prob))
            lse_ref[0, head : head + 1, here] = top + jnp.log(total)
        ctx = jnp.concatenate(parts, axis=0).T.astype(BF16)
        per = QBLOCK // LANES
        ctx_ref[block * per : (block + 1) * per, 0] = ctx.reshape(per, LANES, LANES)


def attention_back_kernel(
    skip, q_ref, kv_ref, segq_ref, segk_ref, place_ref, lse_ref, do_ref, cosq_ref, sinq_ref,
    cosk_ref, sink_ref, normed_ref, pre_ref, red_ref, graw_ref, term_ref, pre_in, red_out,
    dk_acc, dv_acc, term_acc, red_own, send, recv, local,
):
    seq = lax.axis_index("seq")
    me = seq % UNIT
    base = seq - me
    unit = [(me + k) % UNIT for k in range(1, UNIT)]
    pushes = Pushes(send, recv)
    sides = []
    for n, peer in enumerate(neighbours(seq)[:3]):
        sides.append(pushes.make(pre_ref.at[(peer - base) // 2], pre_in.at[n], {"seq": peer}))
    for b in unit:
        sides.append(pushes.make(red_ref.at[b], red_out.at[me], {"seq": base + b}))
    bounce = Bounce(red_ref.at[me], red_own, red_out.at[me], local, False)
    m = pl.program_id(0)

    @pl.when(m == 0)
    def _():
        greet([{"seq": base + b} for b in unit])
        bounce.inward.start()
        for copy in sides:
            copy.start()
        bounce.turn()

    length = kv_ref.shape[1]
    queries = q_ref.shape[1]
    kk, vv = pair_keys(kv_ref[0])
    k_t = kk.T.astype(BF16)[:HD]
    kk = kk.astype(BF16)
    vv = vv.astype(BF16)
    seg_col = jnp.broadcast_to(segk_ref[0], (8, length)).T[:, :1]
    dk_acc[...] = jnp.zeros_like(dk_acc)
    dv_acc[...] = jnp.zeros_like(dv_acc)
    per = QBLOCK // LANES
    for block in range(queries // QBLOCK):
        here = slice(block * QBLOCK, (block + 1) * QBLOCK)
        keys = (block + 1) * QBLOCK if skip else length
        bias = bias_block(seg_col, segq_ref[0][:, here], place_ref[:, here], 0, keys)
        q = q_ref[0, here, :]
        do = do_ref[block * per : (block + 1) * per, 0].reshape(QBLOCK, LANES)
        low = lane_iota(q.shape) < HD
        parts = []
        for head in range(2):
            pick = low == (head == 0)
            mine = jnp.where(pick, q, jnp.zeros_like(q))
            mine_do = jnp.where(pick, do, jnp.zeros_like(do))
            scores = dot_nt(kk[:keys], mine) + bias
            weight = jnp.exp(scores - lse_ref[0, head : head + 1, here])
            product = dot_nt(vv[:keys], mine_do)
            delta = jnp.sum(weight * product, axis=0, keepdims=True)
            grad_scores = (weight * (product - delta)).astype(BF16)
            dv_acc[:keys] += dot_nn(weight.astype(BF16), mine_do)
            dk_acc[:keys] += dot_nn(grad_scores, mine)
            parts.append(dot_nn(k_t[:, :keys], grad_scores))
        dq = jnp.concatenate(parts, axis=0).T * HD**-0.5
        dq = turn(dq, cosq_ref[here, :], -sinq_ref[here, :]).astype(BF16)
        graw_ref[block * per : (block + 1) * per, 0, :, :LANES] = dq.reshape(per, LANES, LANES)
    dk = dk_acc[...]
    dv = dv_acc[...]
    dk = dk + pltpu.roll(dk, HD, 1)
    dv = dv + pltpu.roll(dv, HD, 1)
    gkv = jnp.where(lane_iota(dk.shape) < HD, dk, dv)
    key_cos, key_sin = value_tables(cosk_ref[...], sink_ref[...])
    gkv = turn(gkv, key_cos, -key_sin).astype(BF16)
    graw_ref[:, 0, :, LANES:] = gkv.reshape(length // LANES, LANES, LANES)
    if skip:
        normed_t = normed_ref[...].reshape(queries, -1).T
        term = dot_nn(normed_t, graw_ref[...].reshape(queries, 2 * LANES))
        @pl.when(m == 0)
        def _():
            term_acc[...] = term

        @pl.when(m > 0)
        def _():
            term_acc[...] += term

        @pl.when(m == pl.num_programs(0) - 1)
        def _():
            for b in range(UNIT):
                for r in range(PIECES):
                    at = (b * PIECES + r) * ROWS_IN
                    term_ref[r, b] = term_acc[at : at + ROWS_IN].astype(BF16)

    @pl.when(m == pl.num_programs(0) - 1)
    def _():
        for copy in sides:
            copy.wait()
        bounce.wait()


def soft_gates(normed, router, chosen):
    logits = jnp.where(chosen > 0, dot_nn(normed, router), NEGATIVE)
    top = jnp.max(logits, axis=-1, keepdims=True)
    weight = jnp.where(chosen > 0, jnp.exp(logits - top), 0.0)
    return weight / jnp.sum(weight, axis=-1, keepdims=True)


def unpack(w_ref, wg, wu, wd):
    half = wg.shape[1]
    for r in range(PIECES):
        for b in range(UNIT):
            at = (b * PIECES + r) * ROWS_IN
            low = (b * PIECES + r) * ROWS_OUT
            wg[at : at + ROWS_IN] = w_ref[r, b, :ROWS_IN]
            wu[at : at + ROWS_IN] = w_ref[r, b, ROWS_IN : 2 * ROWS_IN]
            for c in range(2):
                start = 2 * ROWS_IN + c * ROWS_OUT
                wd[low : low + ROWS_OUT, c * half : (c + 1) * half] = w_ref[
                    r, b, start : start + ROWS_OUT
                ]


def load_weights(w0_ref, w1_hbm, w1_ref, sem, wg, wu, wd, twin=False, out=False):
    e, t = pl.program_id(0), pl.program_id(1)
    fetch = pltpu.make_async_copy(w1_hbm, w1_ref, sem)

    @pl.when((t == 0) & (e == 0))
    def _():
        fetch.start()
        if twin:
            peers = neighbours(lax.axis_index("seq"))
            greet([{"seq": peer} for peer in (peers if out else peers[3:])])
        unpack(w0_ref, wg, wu, wd)

    @pl.when((t == 0) & (e == 1))
    def _():
        fetch.wait()
        unpack(w1_ref, wg, wu, wd)


def twin_push(source, target, send, recv):
    twin = neighbours(lax.axis_index("seq"))[3]
    return pltpu.make_async_remote_copy(
        src_ref=source,
        dst_ref=target,
        send_sem=send,
        recv_sem=recv,
        device_id={"seq": twin},
        device_id_type=pl.DeviceIdType.MESH,
    )


def collect_terms(x, dz, grad_gate, grad_up, gated, ag, au, ad, stage, total, dw, sems):
    e, t = pl.program_id(0), pl.program_id(1)
    last_t = pl.num_programs(1) - 1
    half = ag.shape[1]

    @pl.when(t == 0)
    def _():
        ag[...] = dot_tn(x, grad_gate)
        au[...] = dot_tn(x, grad_up)
        ad[...] = dot_tn(gated, dz)

    @pl.when((t > 0) & (t < last_t))
    def _():
        ag[...] += dot_tn(x, grad_gate)
        au[...] += dot_tn(x, grad_up)
        ad[...] += dot_tn(gated, dz)

    send, recv, local = sems
    push = twin_push(stage, total, send.at[0], recv.at[0])
    out = pltpu.make_async_copy(stage, dw, local.at[1])

    def store(write):
        for place, acc, grad in ((0, ag, grad_gate), (ROWS_IN, au, grad_up)):
            final = acc[...] + dot_tn(x, grad)
            for r in range(PIECES):
                for b in range(UNIT):
                    at = (b * PIECES + r) * ROWS_IN
                    write(r, b, place, final[at : at + ROWS_IN])
        final = ad[...] + dot_tn(gated, dz)
        for r in range(PIECES):
            for b in range(UNIT):
                low = (b * PIECES + r) * ROWS_OUT
                for c in range(2):
                    start = 2 * ROWS_IN + c * ROWS_OUT
                    write(r, b, start, final[low : low + ROWS_OUT, c * half : (c + 1) * half])

    @pl.when((t == last_t) & (e == 0))
    def _():
        def write(r, b, place, value):
            stage[r, b, place : place + value.shape[0]] = value.astype(BF16)

        store(write)
        push.start()

    @pl.when((t == last_t) & (e == 1))
    def _():
        push.wait()

        def write(r, b, place, value):
            here = slice(place, place + value.shape[0])
            stage[r, b, here] = (value + total[r, b, here].astype(F32)).astype(BF16)

        store(write)
        out.start()
        out.wait()


def sigmoid(v):
    return 0.5 + 0.5 * jnp.tanh(0.5 * v)


def grads_of(gate_act, up_act, back, gate):
    sig = sigmoid(gate_act)
    silu = gate_act * sig
    hidden = silu * up_act
    grad_hidden = back * gate
    grad_gate = (grad_hidden * up_act * (sig + silu * (1.0 - sig))).astype(BF16)
    grad_up = (grad_hidden * silu).astype(BF16)
    return hidden, grad_gate, grad_up


def expert_id(twin, index):
    me = lax.axis_index("seq") % UNIT
    return 2 * (me + twin * (1 - 2 * (me % 2))) + index


def pick_gate(gates, gid):
    mine = lane_iota(gates.shape) == gid
    return mine, jnp.sum(jnp.where(mine, gates, 0.0), axis=1, keepdims=True)


def gate_terms(mine, hidden, back):
    terms = jnp.where(mine, jnp.sum(hidden * back, axis=1, keepdims=True), 0.0)
    return terms.T[:E]


def both_kernel(
    x_ref, dz_ref, wr_ref, w0_ref, w1_hbm, w2_hbm, out_ref, dx_ref, gg_ref, gates_ref, dw,
    w2_twin, wg, wu, wd, gates_s, ag, au, ad, oacc, dxacc, ggacc, w1_ref, stage, total,
    send, recv, local,
):
    e, t = pl.program_id(0), pl.program_id(1)
    tile, width = out_ref.shape
    rows = pl.ds(pl.multiple_of(t * tile, tile), tile)
    x = x_ref[...]
    dz = dz_ref[:, :width]
    load_weights(w0_ref, w1_hbm, w1_ref, local.at[0], wg, wu, wd, True)
    turned = twin_push(w2_hbm, w2_twin, send.at[1], recv.at[1])

    @pl.when((e == 0) & (t == 0))
    def _():
        turned.start()

    @pl.when(e == 0)
    def _():
        gates_s[rows, :] = soft_gates(x, wr_ref[...], dz_ref[:, width:].astype(F32))

    mine, gate = pick_gate(gates_s[rows, :], expert_id(1 - e, 0))
    gate_act = dot_nn(x, wg[...])
    up_act = dot_nn(x, wu[...])
    back = dot_nt(dz, wd[...])
    hidden, grad_gate, grad_up = grads_of(gate_act, up_act, back, gate)
    ggterm = gate_terms(mine, hidden, back)
    gated = (hidden * gate).astype(BF16)
    out = dot_nn(gated, wd[...])
    dx = dot_nt(grad_gate, wg[...]) + dot_nt(grad_up, wu[...])

    @pl.when(e == 0)
    def _():
        oacc[rows, :] = out
        dxacc[rows, :] = dx
        ggacc[t] = ggterm

    @pl.when(e == 1)
    def _():
        out_ref[...] = (oacc[rows, :] + out).astype(BF16)
        dx_ref[...] = (dxacc[rows, :] + dx).astype(BF16)
        gg_ref[...] = ggacc[t] + ggterm
        gates_ref[...] = gates_s[rows, :]

    sems = (send, recv, local)
    collect_terms(x, dz, grad_gate, grad_up, gated, ag, au, ad, stage, total, dw, sems)

    @pl.when((e == 1) & (t == pl.num_programs(1) - 1))
    def _():
        turned.wait()


def forward_kernel(
    x_ref, gates_ref, w0_ref, w1_hbm, oin_ref, out_ref, gact_ref, uact_ref,
    wg, wu, wd, oacc, w1_ref, w1_sem,
):
    e, t = pl.program_id(0), pl.program_id(1)
    tile = out_ref.shape[0]
    rows = pl.ds(pl.multiple_of(t * tile, tile), tile)
    x = x_ref[...]
    load_weights(w0_ref, w1_hbm, w1_ref, w1_sem, wg, wu, wd)
    _, gate = pick_gate(gates_ref[...], expert_id(1 - e, 1))
    gate_act = dot_nn(x, wg[...])
    up_act = dot_nn(x, wu[...])
    gact_ref[0] = gate_act.astype(BF16)
    uact_ref[0] = up_act.astype(BF16)
    gated = (gate_act * sigmoid(gate_act) * up_act * gate).astype(BF16)
    out = dot_nn(gated, wd[...])

    @pl.when(e == 0)
    def _():
        oacc[rows, :] = oin_ref[...].astype(F32) + out

    @pl.when(e == 1)
    def _():
        out_ref[...] = (oacc[rows, :] + out).astype(BF16)


def backward_kernel(
    x_ref, dz_ref, gates_ref, gact_ref, uact_ref, w0_ref, w1_hbm, dxin_ref, ggin_ref,
    out_hbm, dx_ref, gg_ref, dw, out_in,
    wg, wu, wd, ag, au, ad, dxacc, ggacc, w1_ref, stage, total, send, recv, local,
):
    e, t = pl.program_id(0), pl.program_id(1)
    tile, width = dx_ref.shape
    rows = pl.ds(pl.multiple_of(t * tile, tile), tile)
    x = x_ref[...]
    dz = dz_ref[...]
    load_weights(w0_ref, w1_hbm, w1_ref, local.at[0], wg, wu, wd, True, True)
    out_copies = []
    pushes = Pushes(send, recv)
    pushes.used = 1
    for n, peer in enumerate(neighbours(lax.axis_index("seq"))[:3]):
        out_copies.append(pushes.make(out_hbm.at[n + 1], out_in.at[n], {"seq": peer}))

    @pl.when((e == 0) & (t == 0))
    def _():
        for copy in out_copies:
            copy.start()
    mine, gate = pick_gate(gates_ref[...], expert_id(1 - e, 1))
    back = dot_nt(dz, wd[...])
    hidden, grad_gate, grad_up = grads_of(
        gact_ref[0].astype(F32), uact_ref[0].astype(F32), back, gate
    )
    ggterm = gate_terms(mine, hidden, back)
    gated = (hidden * gate).astype(BF16)
    dx = dot_nt(grad_gate, wg[...]) + dot_nt(grad_up, wu[...])

    @pl.when(e == 0)
    def _():
        dxacc[rows, :] = dxin_ref[...].astype(F32) + dx
        ggacc[t] = ggin_ref[...] + ggterm

    @pl.when(e == 1)
    def _():
        dx_ref[...] = (dxacc[rows, :] + dx).astype(BF16)
        gg_ref[...] = ggacc[t] + ggterm

    sems = (send, recv, local)
    collect_terms(x, dz, grad_gate, grad_up, gated, ag, au, ad, stage, total, dw, sems)

    @pl.when((e == 1) & (t == pl.num_programs(1) - 1))
    def _():
        for copy in out_copies:
            copy.wait()


def run_experts(which, x, dz, weights, router=None, gates=None, carried=None, acts=None, pushed=None):
    tokens, width = x.shape
    packed0, packed1 = weights
    hidden = packed0.shape[3]
    tile = tokens // 3
    tiles = 3
    like = jax.ShapeDtypeStruct
    any_spec = pl.BlockSpec(memory_space=pl.ANY)
    once = pl.Buffered(1)

    def by_token(e, t):
        return (t, 0)

    def at_end(e, t):
        return (jnp.where(e == 1, t, 0), 0)

    def at_start(e, t):
        return (jnp.where(e == 0, t, tiles - 1), 0)

    def lanes_end(e, t):
        return (0, jnp.where(e == 1, t, 0))

    def lanes_start(e, t):
        return (0, jnp.where(e == 0, t, tiles - 1))

    def acts_map(e, t):
        return (e, t, 0)

    x_spec = pl.BlockSpec((tile, width), by_token)
    wide_spec = pl.BlockSpec((tile, width + LANES), by_token)
    gates_spec = pl.BlockSpec((tile, LANES), by_token)
    w_spec = pl.BlockSpec(packed0.shape, lambda e, t: (0, 0, 0, 0), pipeline_mode=once)
    acts_spec = pl.BlockSpec((1, tile, hidden), acts_map)
    token_end = pl.BlockSpec((tile, width), at_end)
    token_start = pl.BlockSpec((tile, width), at_start)
    packed_like = like(packed0.shape, BF16)
    token_like = like((tokens, width), BF16)
    gg_like = like((E, tokens), F32)
    acts_like = like((2, tokens, hidden), BF16)
    unpacked = [
        pltpu.VMEM((width, hidden), BF16),
        pltpu.VMEM((width, hidden), BF16),
        pltpu.VMEM((hidden, width), BF16),
    ]
    terms = [
        pltpu.VMEM((width, hidden), F32),
        pltpu.VMEM((width, hidden), F32),
        pltpu.VMEM((hidden, width), F32),
    ]
    acc = pltpu.VMEM((tokens, width), F32)
    gg_acc = pltpu.VMEM((tiles, E, tile), F32)
    second = pltpu.VMEM(packed1.shape, BF16)
    stage = pltpu.VMEM(packed0.shape, BF16)
    sem, sems = pltpu.SemaphoreType.DMA, pltpu.SemaphoreType.DMA((2,))
    flops = 4.0 * tokens * width * hidden
    if which == "both":
        return pl.pallas_call(
            both_kernel,
            grid=(2, tiles),
            in_specs=[
                x_spec, wide_spec,
                pl.BlockSpec((width, LANES), lambda e, t: (0, 2), pipeline_mode=once),
                w_spec, any_spec, any_spec,
            ],
            out_specs=[
                token_end, token_end, pl.BlockSpec((E, tile), lanes_end),
                pl.BlockSpec((tile, LANES), at_end), any_spec, any_spec,
            ],
            out_shape=[
                token_like, token_like, gg_like, like((tokens, LANES), F32),
                packed_like, packed_like,
            ],
            scratch_shapes=unpacked
            + [pltpu.VMEM((tokens, LANES), F32)]
            + terms
            + [acc, acc, gg_acc, second, stage, stage, sems, sems, sems],
            compiler_params=params(collective_id=5, has_side_effects=True),
            cost_estimate=cost(9 * flops, 2e7),
        )(x, dz, router, packed0, packed1, pushed)
    if which == "forward":
        return pl.pallas_call(
            forward_kernel,
            grid=(2, tiles),
            in_specs=[x_spec, gates_spec, w_spec, any_spec, token_start],
            out_specs=[token_end, acts_spec, acts_spec],
            out_shape=[token_like, acts_like, acts_like],
            scratch_shapes=unpacked + [acc, second, sem],
            compiler_params=params(),
            cost_estimate=cost(3 * flops, 2e7),
        )(x, gates, packed0, packed1, carried)
    return pl.pallas_call(
        backward_kernel,
        grid=(2, tiles),
        in_specs=[
            x_spec, x_spec, gates_spec, acts_spec, acts_spec, w_spec, any_spec,
            token_start, pl.BlockSpec((E, tile), lanes_start), any_spec,
        ],
        out_specs=[token_end, pl.BlockSpec((E, tile), lanes_end), any_spec, any_spec],
        out_shape=[
            token_like, gg_like, packed_like, like((3,) + pushed.shape[1:], BF16),
        ],
        scratch_shapes=unpacked + terms + [acc, gg_acc, second, stage, stage]
        + [pltpu.SemaphoreType.DMA((4,)), pltpu.SemaphoreType.DMA((4,)), sems],
        compiler_params=params(collective_id=6, has_side_effects=True),
        cost_estimate=cost(6 * flops, 2e7),
    )(x, dz, gates, acts[0], acts[1], packed0, packed1, carried[0], carried[1], pushed)


def return_kernel(
    micro, copies, dx_ref, gg_ref, mixed_ref, normed_ref, dz_ref, small_ref, w_ref, ctx_ref,
    do_out, gmixed_ref, pre_ref,
    parts, gparts, gctx, gbranch, glogs, term, twin_term, send, recv, local,
):
    seq = lax.axis_index("seq")
    me = seq % UNIT
    core = me % 2
    base = seq - me
    unit = [(me + k) % UNIT for k in range(1, UNIT)]
    *peers, twin = neighbours(seq)
    greet([{"seq": base + b} for b in unit])
    pushes = Pushes(send, recv)
    count, width = mixed_ref.shape
    step = count // micro
    chunks = [pl.ds(m * step, step) for m in range(micro)]
    first = []
    for n in (2, 0, 1):
        part = gg_ref.at[:, pl.ds((n + 1) * count, count)]
        first.append(pushes.start(part, gparts.at[n + 1], {"seq": peers[n]}))
    arrivals = [
        [
            pushes.start(dx_ref.at[n + 1, here], parts.at[n + 1, here], {"seq": peers[n]})
            for n in (2, 0, 1)
        ]
        for here in chunks
    ]
    own = [
        pltpu.make_async_copy(dx_ref.at[0], parts.at[0], local.at[0]),
        pltpu.make_async_copy(gg_ref.at[:, pl.ds(0, count)], gparts.at[0], local.at[1]),
    ]
    for copy in own:
        copy.start()
    small = small_ref[...]
    gain = gain_row(small, E + 1)
    gates = soft_gates(normed_ref[...], small, dz_ref[:, width:].astype(F32))
    for copy in own:
        copy.wait()
    for copy in first:
        copy.wait_recv()
    grad_gates = gparts[0] + gparts[1] + gparts[2] + gparts[3]
    grad_gates = jnp.concatenate([grad_gates, jnp.zeros((LANES - E, count), F32)], axis=0).T
    centre = jnp.sum(gates * grad_gates, axis=-1, keepdims=True)
    glogs[...] = (gates * (grad_gates - centre)).astype(BF16)
    sent = []
    for m, here in enumerate(chunks):
        for copy in arrivals[m]:
            copy.wait_recv()
        dy = parts[0, here].astype(F32)
        for n in range(1, 4):
            dy = dy + parts[n, here].astype(F32)
        dy = dy + dot_nt(glogs[here], small)
        v = mixed_ref[here]
        inverse = lax.rsqrt(jnp.mean(v * v, axis=-1, keepdims=True) + EPS)
        scaled = dy * gain
        mean = jnp.mean(scaled * v, axis=-1, keepdims=True)
        gmixed = dz_ref[here, :width].astype(F32) + scaled * inverse
        gmixed = gmixed - v * (inverse * inverse * inverse * mean)
        gmixed_ref[here] = gmixed
        branch = gmixed.astype(BF16)
        gbranch[here] = branch
        grad_ctx = dot_nt(branch, w_ref[...]).astype(BF16)
        for b in range(UNIT):
            gctx[b, m] = grad_ctx[:, b * LANES : (b + 1) * LANES]
        mine = pltpu.make_async_copy(gctx.at[me, m], do_out.at[me, m], local.at[2 + m])
        mine.start()
        own.append(mine)
        sent += [pushes.start(gctx.at[b, m], do_out.at[me, m], {"seq": base + b}) for b in unit]
    rest = width // (copies * UNIT)
    out_term = dot_tn(ctx_ref[...], gbranch[...]).astype(BF16)
    router_term = dot_tn(normed_ref[...], glogs[...]).astype(BF16)
    for a in range(copies):
        for b in range(UNIT):
            at = (a * UNIT + b) * rest
            term[a, b, :, :width] = out_term[at : at + rest]
            term[a, b, :, width:] = router_term[at : at + rest]
    turned = [
        pushes.start(term.at[:, 2 * j + 1 - core], twin_term.at[j], {"seq": twin})
        for j in range(4)
    ]
    for j, copy in enumerate(turned):
        copy.wait_recv()
        summed = term[:, 2 * j + core].astype(F32) + twin_term[j].astype(F32)
        pre_ref[j] = summed.astype(BF16)
    for group in [first] + arrivals:
        for copy in group:
            copy.wait_send()
    for copy in turned:
        copy.wait_send()
    for copy in own[2:] + sent:
        copy.wait()


def return_tokens(
    dx, gg, mixed, normed, dz, heads, w_out, context, micro, copies, collective
):
    any_spec = pl.BlockSpec(memory_space=pl.ANY)
    like = jax.ShapeDtypeStruct
    count, width = mixed.shape
    ctx_shape = (UNIT, micro, count // micro, LANES)
    pre_shape = (4, copies, width // (copies * UNIT), width + LANES)
    pushes = 3 + 3 * micro + (UNIT - 1) * micro + 4

    def fixed(i):
        return (0, 0)

    return pl.pallas_call(
        functools.partial(return_kernel, micro, copies),
        grid=(1,),
        in_specs=[
            any_spec,
            any_spec,
            pl.BlockSpec(mixed.shape, fixed),
            pl.BlockSpec(normed.shape, fixed),
            pl.BlockSpec(dz.shape, fixed),
            pl.BlockSpec((width, LANES), lambda i: (0, 2)),
            pl.BlockSpec(w_out.shape, fixed),
            pl.BlockSpec(context.shape, fixed),
        ],
        out_specs=[
            any_spec,
            pl.BlockSpec((count, width), fixed),
            pl.BlockSpec(pre_shape, lambda i: (0, 0, 0, 0)),
        ],
        out_shape=[
            like(ctx_shape, BF16),
            like((count, width), F32),
            like(pre_shape, BF16),
        ],
        scratch_shapes=[
            pltpu.VMEM((4, count, width), BF16),
            pltpu.VMEM((4, E, count), F32),
            pltpu.VMEM(ctx_shape, BF16),
            pltpu.VMEM((count, width), BF16),
            pltpu.VMEM((count, LANES), BF16),
            pltpu.VMEM((copies, UNIT) + pre_shape[2:], BF16),
            pltpu.VMEM(pre_shape, BF16),
            pltpu.SemaphoreType.DMA((pushes,)),
            pltpu.SemaphoreType.DMA((pushes,)),
            pltpu.SemaphoreType.DMA((2 + micro,)),
        ],
        compiler_params=params(collective_id=collective, has_side_effects=True),
        cost_estimate=cost(4.0 * count * width * width, 1.2e8),
    )(dx, gg, mixed, normed, dz, heads, w_out, context)


def shards(
    copies, tokens, segments, routes, cotangent, norm_attn, w_query, w_key, w_value, w_out, norm_ffn,
    w_router, w_gate, w_up, w_down, rows,
):
    micro, local_len, width = tokens.shape
    length = segments.shape[1]
    count = micro * local_len
    unit_len = UNIT * local_len
    part = w_query.shape[0]
    hidden = w_gate.shape[2]
    seq_size = copies * UNIT
    seq = lax.axis_index("seq")
    row = lax.axis_index("row")
    unit = seq // UNIT
    me = seq % UNIT
    unit_groups = None
    copy_groups = None
    if copies > 1:
        unit_groups = [[a * UNIT + b for b in range(UNIT)] for a in range(copies)]
        copy_groups = [[a * UNIT + b for a in range(copies)] for b in range(UNIT)]

    def exchange(x):
        return lax.all_to_all(x, "seq", 0, 0, tiled=True, axis_index_groups=unit_groups)

    def flip(x, k):
        return lax.ppermute(x, "seq", [(s, s ^ k) for s in range(seq_size)])

    flat_tokens = tokens.reshape(count, width)

    def wait_for(x, *others):
        return lax.optimization_barrier((x,) + others)[0]

    small = jnp.concatenate(
        [
            w_router,
            norm_attn[:, None],
            norm_ffn[:, None],
            jnp.zeros((part, LANES - 2 - E), BF16),
        ],
        axis=1,
    )
    head_part = jnp.concatenate(
        [
            w_query.reshape(part, UNIT, 2 * HD),
            w_key.reshape(part, UNIT, HD),
            w_value.reshape(part, UNIT, HD),
            jnp.broadcast_to(small[:, None], (part, UNIT, LANES)),
        ],
        axis=2,
    ).transpose(1, 0, 2)

    down_halves = w_down.reshape(E, -1, 2, hidden).transpose(0, 2, 1, 3).reshape(E, part, hidden)
    packed_part = jnp.concatenate([w_gate, w_up, down_halves], axis=1)
    packed_part = packed_part.reshape(UNIT, E // UNIT, 3 * part, hidden).transpose(1, 0, 2, 3)
    *packed_mine, heads_all, w_out_rows = begin(
        rows, packed_part[0], packed_part[1], head_part, w_out
    )

    if copies > 1:
        heads_all = lax.all_gather(heads_all, "seq", axis=0, axis_index_groups=copy_groups)
        w_out_rows = lax.all_gather(w_out_rows, "seq", axis=0, axis_index_groups=copy_groups)
    else:
        w_out_rows = w_out_rows[None]
    heads_all = heads_all.reshape(width, 4 * HD + LANES)

    def gather_packed(x):
        x = lax.all_gather(x, "row", axis=0)
        if copies > 1:
            x = lax.all_gather(x, "seq", axis=0, axis_index_groups=copy_groups)
            x = x.transpose(0, 2, 1, 3, 4).reshape(-1, 3 * part, hidden)
            halves = x[:, 2 * part :].reshape(-1, 2, part // 2, hidden).transpose(0, 2, 1, 3)
            return pack(
                x[:, :part].reshape(width, hidden),
                x[:, part : 2 * part].reshape(width, hidden),
                halves.reshape(hidden, width),
            )
        return x

    def pack(gate, up, down):
        gate = gate.reshape(UNIT, PIECES, ROWS_IN, hidden)
        up = up.reshape(UNIT, PIECES, ROWS_IN, hidden)
        down = down.reshape(UNIT, PIECES, ROWS_OUT, 2, hidden).transpose(0, 1, 3, 2, 4)
        down = down.reshape(UNIT, PIECES, ROWS_IN, hidden)
        return jnp.concatenate([gate, up, down], axis=2).transpose(1, 0, 2, 3)

    def repack(x):
        x = x.transpose(1, 0, 2, 3)
        gate = x[:, :, :ROWS_IN].reshape(copies, UNIT, rows, part, hidden)
        up = x[:, :, ROWS_IN : 2 * ROWS_IN].reshape(copies, UNIT, rows, part, hidden)
        down = x[:, :, 2 * ROWS_IN :].reshape(UNIT, PIECES, 2, ROWS_OUT, hidden)
        down = down.transpose(0, 1, 3, 2, 4).reshape(copies, UNIT, rows, part // 2, 2, hidden)
        down = down.transpose(0, 1, 2, 4, 3, 5).reshape(copies, UNIT, rows, part, hidden)
        return jnp.concatenate([gate, up, down], axis=3).transpose(2, 0, 1, 3, 4)

    own_weights = [gather_packed(x) for x in packed_mine]

    tok_all, w_out_all = unit_gather(
        [wait_for(flat_tokens, w_out_rows), w_out_rows.reshape(-1, width)], 1
    )
    tok_all = tok_all.reshape(UNIT, micro, local_len, width)
    w_out_all = w_out_all.reshape(UNIT, copies, rows * part, width)
    w_out_all = w_out_all.transpose(1, 0, 2, 3).reshape(H * HD, width)

    chosen = jnp.any(
        routes.reshape(count, TOPK)[:, :, None] == jnp.arange(LANES, dtype=jnp.int32)[None, None, :],
        axis=1,
    ).astype(BF16)
    dz_own = jnp.concatenate([cotangent.reshape(count, width), chosen], axis=1)
    dz_send = wait_for(dz_own, tok_all)
    dz_pieces = [dz_send] + [flip(dz_send, k) for k in (2, 4, 6)]

    frequency = BASE ** (-2.0 * np.arange(HD // 2) / HD)
    angles = np.arange(length)[:, None].astype(np.float32) * frequency[None].astype(np.float32)
    key_cos = jnp.asarray(np.tile(np.cos(angles), (1, 4)).astype(np.float32))
    key_sin = np.concatenate([-np.sin(angles), np.sin(angles)] * 2, axis=1)
    key_sin = jnp.asarray(key_sin.astype(np.float32))
    places = unit * unit_len + jnp.arange(unit_len, dtype=jnp.int32)
    cosine, sine = key_cos, key_sin
    if copies > 1:
        cosine = lax.dynamic_slice_in_dim(key_cos, unit * unit_len, unit_len, 0)
        sine = lax.dynamic_slice_in_dim(key_sin, unit * unit_len, unit_len, 0)

    def by_row4(m):
        return (0, m, 0, 0)

    def by_row3(m):
        return (m, 0, 0)

    def fixed(*_):
        return (0, 0)

    def zeros3(*_):
        return (0, 0, 0)

    def zeros4(*_):
        return (0, 0, 0, 0)

    def small_block(*_):
        return (0, 2)

    normed_all, q_all, kv_own = pl.pallas_call(
        project_kernel,
        grid=(micro,),
        in_specs=[
            pl.BlockSpec((UNIT, 1, local_len, width), by_row4),
            pl.BlockSpec((width, LANES), small_block),
            pl.BlockSpec((width, 4 * HD), fixed),
            pl.BlockSpec((unit_len, LANES), fixed),
            pl.BlockSpec((unit_len, LANES), fixed),
        ],
        out_specs=[
            pl.BlockSpec((UNIT, 1, local_len, width), by_row4),
            pl.BlockSpec((1, unit_len, LANES), by_row3),
            pl.BlockSpec((1, unit_len, LANES), by_row3),
        ],
        out_shape=[
            jax.ShapeDtypeStruct((UNIT, micro, local_len, width), BF16),
            jax.ShapeDtypeStruct((micro, unit_len, LANES), BF16),
            jax.ShapeDtypeStruct((micro, unit_len, LANES), BF16),
        ],
        compiler_params=params(),
        cost_estimate=cost(2.0 * UNIT * count * width * 4 * HD, 1.5e7),
    )(tok_all, heads_all, heads_all, cosine, sine)

    kv_all = kv_own
    if copies > 1:
        kv_all = lax.all_gather(kv_own, "seq", axis=1, tiled=True, axis_index_groups=copy_groups)
    seg_keys = segments.astype(F32).reshape(micro, 1, length)
    seg_queries = lax.dynamic_slice_in_dim(seg_keys, unit * unit_len, unit_len, 2)
    skip = copies == 1
    place_row = places[None]
    attention_flops = 4.0 * micro * unit_len * length * 2 * LANES
    attention_specs = [
        pl.BlockSpec((1, unit_len, LANES), by_row3),
        pl.BlockSpec((1, length, LANES), by_row3),
        pl.BlockSpec((1, 1, unit_len), by_row3),
        pl.BlockSpec((1, 1, length), by_row3),
        pl.BlockSpec((1, unit_len), fixed),
    ]
    ctx_heads, lse = pl.pallas_call(
        functools.partial(attention_kernel, skip),
        grid=(micro,),
        in_specs=attention_specs,
        out_specs=[
            pl.BlockSpec((UNIT, 1, local_len, LANES), by_row4),
            pl.BlockSpec((1, 2, unit_len), by_row3),
        ],
        out_shape=[
            jax.ShapeDtypeStruct((UNIT, micro, local_len, LANES), BF16),
            jax.ShapeDtypeStruct((micro, 2, unit_len), F32),
        ],
        compiler_params=params(),
        cost_estimate=cost(attention_flops, 4e6),
    )(q_all, kv_all, seg_queries, seg_keys, place_row)
    x_all, sib_first, dz_all, mixed, normed_ffn, context = bridge(
        ctx_heads, own_weights[0], dz_pieces, w_out_all, flat_tokens, heads_all, 2
    )
    x_all = x_all.reshape(4 * count, width)
    dz_all = dz_all.reshape(4 * count, width + LANES)
    w_heads = lax.all_gather(
        wait_for(heads_all, x_all)[:, : 4 * HD], "seq", axis=0, axis_index_groups=unit_groups
    )

    out_part, dx_part, gg_part, gates_all, total_first, sib_second = run_experts(
        "both", x_all, dz_all, (sib_first, own_weights[0]), router=heads_all,
        pushed=own_weights[1],
    )

    def finish_expert(total):
        if copies > 1:
            total = repack(total)
            total = lax.psum_scatter(total, "row", scatter_dimension=0)
            total = lax.psum_scatter(
                total, "seq", scatter_dimension=0, axis_index_groups=copy_groups
            )
        else:
            total = lax.psum_scatter(total, "row", scatter_dimension=0)
        return total

    reduced_first = finish_expert(wait_for(total_first, w_heads))
    pair = (sib_second, own_weights[1])
    out_part, gate_acts, up_acts = run_experts(
        "forward", x_all, None, pair, gates=gates_all, carried=out_part
    )
    out_split = out_part.reshape(4, count, width)
    dx_part, gg_part, total_second, out_back = run_experts(
        "backward", x_all, dz_all, pair, gates=gates_all,
        carried=(dx_part, gg_part), acts=(gate_acts, up_acts), pushed=out_split,
    )
    reduced_second = finish_expert(total_second)
    do_heads, gmixed, out_pre = return_tokens(
        dx_part.reshape(4, count, width), gg_part, mixed, normed_ffn, dz_own, heads_all, w_out_all,
        context, micro, copies, 3,
    )
    if copies > 1:
        out_pre = lax.psum_scatter(
            out_pre, "seq", scatter_dimension=1, axis_index_groups=copy_groups
        )
    out_pre = out_pre.reshape(4, rows, part, width + LANES)
    graw, head_term, out_in, exchanged = pl.pallas_call(
        functools.partial(attention_back_kernel, skip),
        grid=(micro,),
        in_specs=attention_specs
        + [
            pl.BlockSpec((1, 2, unit_len), by_row3),
            pl.BlockSpec((UNIT, 1, local_len, LANES), by_row4),
            pl.BlockSpec((unit_len, LANES), fixed),
            pl.BlockSpec((unit_len, LANES), fixed),
            pl.BlockSpec((length, LANES), fixed),
            pl.BlockSpec((length, LANES), fixed),
            pl.BlockSpec((UNIT, 1, local_len, width), by_row4),
            pl.BlockSpec(memory_space=pl.ANY),
            pl.BlockSpec(memory_space=pl.ANY),
        ],
        out_specs=[
            pl.BlockSpec((seq_size, 1, local_len, 2 * LANES), by_row4),
            pl.BlockSpec((PIECES, UNIT, ROWS_IN, 2 * LANES), zeros4),
            pl.BlockSpec(memory_space=pl.ANY),
            pl.BlockSpec(memory_space=pl.ANY),
        ],
        out_shape=[
            jax.ShapeDtypeStruct((seq_size, micro, local_len, 2 * LANES), BF16),
            jax.ShapeDtypeStruct((PIECES, UNIT, ROWS_IN, 2 * LANES), BF16),
            jax.ShapeDtypeStruct((3,) + out_pre.shape[1:], BF16),
            jax.ShapeDtypeStruct(reduced_first.shape, BF16),
        ],
        scratch_shapes=[
            pltpu.VMEM((length, LANES), F32),
            pltpu.VMEM((length, LANES), F32),
            pltpu.VMEM((width, 2 * LANES), F32),
            pltpu.VMEM(reduced_first.shape[1:], BF16),
            pltpu.SemaphoreType.DMA((UNIT + 2,)),
            pltpu.SemaphoreType.DMA((UNIT + 2,)),
            pltpu.SemaphoreType.DMA((2,)),
        ],
        compiler_params=params(collective_id=7, has_side_effects=True),
        cost_estimate=cost(2.5 * attention_flops, 8e6),
    )(
        q_all, kv_all, seg_queries, seg_keys, place_row, lse, do_heads,
        cosine, sine, key_cos, key_sin, normed_all, out_pre, reduced_first,
    )
    if copies > 1:
        graw_kv = lax.psum_scatter(
            graw[..., LANES:], "seq", scatter_dimension=0, tiled=True,
            axis_index_groups=copy_groups,
        )
        graw = jnp.concatenate([graw[:UNIT, ..., :LANES], graw_kv], axis=3)
        head_term = jnp.einsum(
            "nd,nh->dh",
            normed_all.reshape(UNIT * count, width),
            graw.reshape(UNIT * count, 2 * LANES),
            preferred_element_type=F32,
        ).astype(BF16)
        head_term = head_term.reshape(copies, UNIT, rows, part, 2 * LANES)
        head_term = lax.psum_scatter(
            head_term, "seq", scatter_dimension=0, axis_index_groups=copy_groups
        ).transpose(1, 0, 2, 3)
    head_grad, exchanged_second, out_grad, grad_input = finish(
        rows, graw, head_term, reduced_second, out_pre, out_in, w_heads, flat_tokens, heads_all,
        gmixed, 4,
    )
    block_out = wait_for(mixed, head_grad) + out_split[0].astype(F32)
    for n in range(3):
        block_out = block_out + out_back[n].astype(F32)

    finished = [exchanged, exchanged_second]
    finished = jnp.stack(finished, axis=1).reshape(E, 3 * part, hidden).astype(F32)
    grad_gate = finished[:, :part]
    grad_up = finished[:, part : 2 * part]
    grad_down = finished[:, 2 * part :].reshape(E, 2, -1, hidden).transpose(0, 2, 1, 3)
    grad_down = grad_down.reshape(E, -1, width)
    head_grad = head_grad.astype(F32)
    grad_query = head_grad[:, :, :LANES].transpose(1, 0, 2).reshape(part, H * HD)
    grad_key = head_grad[:, :, LANES : LANES + HD].transpose(1, 0, 2).reshape(part, KVH * HD)
    grad_value = head_grad[:, :, LANES + HD :].transpose(1, 0, 2).reshape(part, KVH * HD)
    grad_out = out_grad[:, :width]
    grad_router = out_grad[:, width : width + E]

    attn_weights = jnp.concatenate([w_query, w_key, w_value], axis=1).astype(F32)
    attn_grads = jnp.concatenate([grad_query, grad_key, grad_value], axis=1)
    grad_norm_attn = jnp.sum(attn_weights * attn_grads, axis=1) / norm_attn.astype(F32)
    grad_norm_ffn = (
        jnp.sum(w_gate.astype(F32) * grad_gate, axis=(0, 2))
        + jnp.sum(w_up.astype(F32) * grad_up, axis=(0, 2))
        + jnp.sum(w_router.astype(F32) * grad_router, axis=1)
    ) / norm_ffn.astype(F32)
    return (
        block_out.astype(BF16).reshape(tokens.shape),
        grad_input.reshape(tokens.shape),
        grad_norm_attn,
        grad_query,
        grad_key,
        grad_value,
        grad_out,
        grad_norm_ffn,
        grad_router,
        grad_gate,
        grad_up,
        grad_down,
    )


def solution(mesh):
    both = ("seq", "row")
    body = functools.partial(shards, mesh.shape["seq"] // UNIT, rows=mesh.shape["row"])
    return jax.shard_map(
        body,
        mesh=mesh,
        in_specs=(
            P("row", "seq", None),
            P("row", None),
            P("row", "seq", None),
            P("row", "seq", None),
            P(both),
            P(both, None),
            P(both, None),
            P(both, None),
            P(both, None),
            P(both),
            P(both, None),
            P(None, both, None),
            P(None, both, None),
            P(None, both, None),
        ),
        out_specs=(
            P("row", "seq", None),
            P("row", "seq", None),
            P(both),
            P(both, None),
            P(both, None),
            P(both, None),
            P(both, None),
            P(both),
            P(both, None),
            P(None, both, None),
            P(None, both, None),
            P(None, both, None),
        ),
        check_vma=False,
    )
```

```python
import functools

import jax
import jax.numpy as jnp
import numpy as np
from jax import lax
from jax.experimental import pallas as pl
from jax.experimental.pallas import tpu as pltpu
from jax.sharding import PartitionSpec as P

H = 16
KVH = 8
TOPK = 8
HD = 64
E = 16
UNIT = 8
LANES = 128
QBLOCK = 256
PIECES = 4
ROWS_IN = 32
ROWS_OUT = 16

EPS = 1e-05
BASE = 10000.0
NEGATIVE = -1e30
F32 = jnp.float32
BF16 = jnp.bfloat16
VMEM_LIMIT = 60 * 1024 * 1024


def dot_nn(left, right):
    return lax.dot_general(left, right, (((1,), (0,)), ((), ())), preferred_element_type=F32)


def dot_nt(left, right):
    return lax.dot_general(left, right, (((1,), (1,)), ((), ())), preferred_element_type=F32)


def dot_tn(left, right):
    return lax.dot_general(left, right, (((0,), (0,)), ((), ())), preferred_element_type=F32)


def params(**kw):
    return pltpu.CompilerParams(vmem_limit_bytes=VMEM_LIMIT, **kw)


def cost(flops, nbytes):
    return pl.CostEstimate(flops=int(flops), bytes_accessed=int(nbytes), transcendentals=0)


def neighbours(seq):
    core = seq % 2
    chip = (seq // 2) % 4
    base = seq - seq % UNIT

    def at(other, same=True):
        return base + 2 * other + (core if same else 1 - core)

    across = chip + 1 - 2 * (chip % 2)
    along = (chip + 2) % 4
    return at(across), at(along), at(3 - chip), at(chip, False)


def greet(targets):
    barrier = pltpu.get_barrier_semaphore()
    for target in targets:
        pl.semaphore_signal(
            barrier, inc=1, device_id=target, device_id_type=pl.DeviceIdType.MESH
        )
    pl.semaphore_wait(barrier, len(targets))


class Pushes:
    def __init__(self, send, recv):
        self.send, self.recv, self.used = send, recv, 0

    def start(self, source, target, device):
        copy = self.make(source, target, device)
        copy.start()
        return copy

    def make(self, source, target, device):
        n = self.used
        self.used += 1
        return pltpu.make_async_remote_copy(
            src_ref=source,
            dst_ref=target,
            send_sem=self.send.at[n],
            recv_sem=self.recv.at[n],
            device_id=device,
            device_id_type=pl.DeviceIdType.MESH,
        )


class Bounce:
    def __init__(self, source, middle, target, sems, start=True):
        self.inward = pltpu.make_async_copy(source, middle, sems.at[0])
        self.outward = pltpu.make_async_copy(middle, target, sems.at[1])
        if start:
            self.inward.start()

    def turn(self):
        self.inward.wait()
        self.outward.start()

    def wait(self):
        self.outward.wait()


def pack_kernel_inputs(
    gate_ref, up_ref, down_ref, query_ref, key_ref, value_ref, router_ref, attn_ref, ffn_ref,
    packed, head_ref, gains,
):
    part, hidden = gate_ref.shape[1:]
    half = part // 2
    for n in range(2):
        for b in range(UNIT):
            e = 2 * b + n
            packed[n, b, :part] = gate_ref[e]
            packed[n, b, part : 2 * part] = up_ref[e]
            for c in range(2):
                start = 2 * part + c * half
                packed[n, b, start : start + half] = down_ref[e, :, c * hidden : (c + 1) * hidden]
    gains[...] = jnp.zeros_like(gains)
    gains[E : E + 1, :part] = attn_ref[...].astype(F32)
    gains[E + 1 : E + 2, :part] = ffn_ref[...].astype(F32)
    router = router_ref[...].astype(F32)
    small = jnp.concatenate([router, jnp.zeros((part, LANES - E), F32)], axis=1)
    small = (small + gains[...].T[:part]).astype(BF16)
    low = lane_iota((part, LANES)) < HD
    for pair in range(UNIT // 2):
        lanes = slice(pair * LANES, (pair + 1) * LANES)
        key = key_ref[:, lanes].astype(F32)
        value = value_ref[:, lanes].astype(F32)
        even = jnp.where(low, key, pltpu.roll(value, HD, 1)).astype(BF16)
        odd = jnp.where(low, pltpu.roll(key, HD, 1), value).astype(BF16)
        for b, mixed in ((2 * pair, even), (2 * pair + 1, odd)):
            head_ref[b, :, :LANES] = query_ref[:, b * LANES : (b + 1) * LANES]
            head_ref[b, :, LANES : 2 * LANES] = mixed
            head_ref[b, :, 2 * LANES :] = small


def begin_kernel(rows, raw, *refs):
    inputs, refs = refs[:raw], refs[raw:]
    wout_ref, mine0, mine1, mine2, head_all, wout_all, *refs = refs
    if raw > 2:
        head_mine, packed, head_ref, gains, send, recv, local = refs
    else:
        (packed, head_ref), (head_mine, send, recv, local) = inputs, refs
    seq, row = lax.axis_index("seq"), lax.axis_index("row")
    me = seq % UNIT
    base = seq - me
    unit = [(me + k) % UNIT for k in range(1, UNIT)]
    column = [(row + k) % rows for k in range(1, rows)]
    greet([{"seq": base + b} for b in unit] + [{"row": r} for r in column])
    if raw > 2:
        pack_kernel_inputs(*inputs, packed, head_ref, gains)
    pushes = Pushes(send, recv)
    inner = mine1.shape[1]
    upper, lower = pl.ds(0, inner), pl.ds(inner, mine2.shape[1])
    first = pltpu.make_async_copy(head_ref.at[me], head_mine.at[me], local.at[0])
    own = [
        pltpu.make_async_copy(packed.at[0, me], mine0.at[me], local.at[1]),
        pltpu.make_async_copy(packed.at[1, me, upper], mine1.at[me], local.at[2]),
        pltpu.make_async_copy(packed.at[1, me, lower], mine2.at[me], local.at[3]),
        pltpu.make_async_copy(wout_ref, wout_all.at[row], local.at[4]),
    ]
    first.start()
    heads = [pushes.start(head_ref.at[b], head_mine.at[me], {"seq": base + b}) for b in unit]
    others = [pushes.start(wout_ref, wout_all.at[row], {"row": r}) for r in column]
    for source, target in (
        (lambda b: packed.at[0, b], mine0),
        (lambda b: packed.at[1, b, upper], mine1),
        (lambda b: packed.at[1, b, lower], mine2),
    ):
        others += [pushes.start(source(b), target.at[me], {"seq": base + b}) for b in unit]
    for copy in own:
        copy.start()
    first.wait()
    for copy in heads:
        copy.wait_recv()
    last = pltpu.make_async_copy(head_mine, head_all.at[:, row], local.at[5])
    last.start()
    others += [pushes.start(head_mine, head_all.at[:, row], {"row": r}) for r in column]
    for copy in heads:
        copy.wait_send()
    for copy in own + [last]:
        copy.wait()
    for copy in others:
        copy.wait()


def begin(rows, part, hidden, inputs, w_out):
    any_spec = pl.BlockSpec(memory_space=pl.ANY)
    vmem_spec = pl.BlockSpec(memory_space=pltpu.VMEM)
    count = 4 * (UNIT - 1) + 2 * (rows - 1)
    like = jax.ShapeDtypeStruct
    deep, inner = 3 * part, 2 * part
    head_shape = (UNIT, part, 4 * HD + LANES)
    built = [
        pltpu.VMEM((2, UNIT, deep, hidden), BF16),
        pltpu.VMEM(head_shape, BF16),
        pltpu.VMEM((LANES, LANES), F32),
    ]
    return pl.pallas_call(
        functools.partial(begin_kernel, rows, len(inputs)),
        in_specs=[vmem_spec] * (len(inputs) + 1),
        out_specs=[any_spec] * 5,
        out_shape=[
            like((UNIT, deep, hidden), BF16),
            like((UNIT, inner, hidden), BF16),
            like((UNIT, deep - inner, hidden), BF16),
            like((UNIT, rows) + head_shape[1:], BF16),
            like((rows,) + w_out.shape, BF16),
        ],
        scratch_shapes=[pltpu.VMEM(head_shape, BF16)]
        + (built if len(inputs) > 2 else [])
        + [
            pltpu.SemaphoreType.DMA((count,)),
            pltpu.SemaphoreType.DMA((count,)),
            pltpu.SemaphoreType.DMA((6,)),
        ],
        compiler_params=params(collective_id=0, has_side_effects=True),
        cost_estimate=cost(1, 2e7),
    )(*inputs, w_out)


def unit_gather_kernel(sources, *refs):
    ins, outs = refs[:sources], refs[sources : 2 * sources]
    middles = refs[2 * sources : 3 * sources]
    send, recv, local = refs[3 * sources :]
    seq = lax.axis_index("seq")
    me = seq % UNIT
    base = seq - me
    across, along, _, twin = neighbours(seq)
    a, b, t = across - base, along - base, twin - base
    d = UNIT - 1 - me + 2 * (me % 2) - 1
    greet([{"seq": across}, {"seq": along}, {"seq": twin}])
    pushes = Pushes(send, recv)
    own, done, stage = [], [], []
    for n, (source, target) in enumerate(zip(ins, outs)):
        half = source.shape[0] // 2
        halves = [pl.ds(0, half), pl.ds(half, half)]
        own.append(Bounce(source, middles[n], target.at[me], local.at[n]))

        def part(device, h, source=source, target=target, halves=halves):
            return pushes.start(
                source.at[halves[h]], target.at[me, halves[h]], {"seq": device}
            )

        xa, yb = part(across, 0), part(along, 1)
        xb, ya = part(across, 1), part(along, 0)
        done.append(pushes.start(source, target.at[me], {"seq": twin}))
        stage.append((target, halves, xa, yb, xb, ya))
    for copy in own:
        copy.turn()
    for target, halves, xa, yb, xb, ya in stage:

        def pass_on(slot, h, device, target=target, halves=halves):
            view = target.at[slot, halves[h]]
            return pushes.start(view, view, {"seq": device})

        xa.wait_recv()
        da = pass_on(a, 0, along)
        done.append(pass_on(a, 0, twin))
        yb.wait_recv()
        db = pass_on(b, 1, across)
        done.append(pass_on(b, 1, twin))
        xb.wait_recv()
        done.append(pass_on(a, 1, twin))
        ya.wait_recv()
        done.append(pass_on(b, 0, twin))
        da.wait_recv()
        done.append(pass_on(d, 0, twin))
        db.wait_recv()
        done.append(pass_on(d, 1, twin))
        for copy in (xa, yb, xb, ya, da, db):
            copy.wait_send()
    for copy in own + done:
        copy.wait()


def unit_gather(sources, collective):
    any_spec = pl.BlockSpec(memory_space=pl.ANY)
    n = len(sources)
    return pl.pallas_call(
        functools.partial(unit_gather_kernel, n),
        in_specs=[any_spec] * n,
        out_specs=[any_spec] * n,
        out_shape=[jax.ShapeDtypeStruct((UNIT,) + x.shape, x.dtype) for x in sources],
        scratch_shapes=[pltpu.VMEM(x.shape, x.dtype) for x in sources]
        + [
            pltpu.SemaphoreType.DMA((13 * n,)),
            pltpu.SemaphoreType.DMA((13 * n,)),
            pltpu.SemaphoreType.DMA((n, 2)),
        ],
        compiler_params=params(collective_id=collective, has_side_effects=True),
        cost_estimate=cost(1, 8e7),
    )(*sources)


def bridge_kernel(
    micro, ctx_ref, weights, w_ref, tok_ref, small_ref,
    target, flipped, mixed_ref, normed_ref, ctx_out,
    ctx_in, send, recv, local,
):
    seq = lax.axis_index("seq")
    me = seq % UNIT
    base = seq - me
    unit = [(me + k) % UNIT for k in range(1, UNIT)]
    across, along, _, twin = neighbours(seq)
    greet([{"seq": base + b} for b in unit])
    pushes = Pushes(send, recv)
    arrivals = [
        [pushes.start(ctx_ref.at[b, m], ctx_in.at[me, m], {"seq": base + b}) for b in unit]
        for m in range(micro)
    ]
    mine = pltpu.make_async_copy(ctx_ref.at[me], ctx_in.at[me], local.at[0])
    mine.start()
    turned = pushes.start(weights, flipped, {"seq": twin})
    count, width = tok_ref.shape
    step = count // micro
    half = step // 2
    gain = gain_row(small_ref[...], E + 1)
    mine.wait()
    sent = []

    def forward(m):
        top, low = pl.ds(m * step, half), pl.ds(m * step + half, half)
        xa, yb, xb, ya = sent[m]
        xa.wait_recv()
        da = pushes.start(target.at[1, top], target.at[3, top], {"seq": along})
        yb.wait_recv()
        db = pushes.start(target.at[2, low], target.at[3, low], {"seq": across})
        sent[m] = (xa, yb, xb, ya, da, db)

    for m in range(micro):
        here = slice(m * step, (m + 1) * step)
        for copy in arrivals[m]:
            copy.wait_recv()
        for b in range(UNIT):
            ctx_out[here, b * LANES : (b + 1) * LANES] = ctx_in[b, m]
        mixed = tok_ref[here].astype(F32) + dot_nn(ctx_out[here], w_ref[...])
        mixed_ref[here] = mixed
        inverse = lax.rsqrt(jnp.mean(mixed * mixed, axis=-1, keepdims=True) + EPS)
        normed_ref[here] = (mixed * inverse * gain).astype(BF16)
        top, low = pl.ds(m * step, half), pl.ds(m * step + half, half)
        sent.append(
            (
                pushes.start(normed_ref.at[top], target.at[1, top], {"seq": across}),
                pushes.start(normed_ref.at[low], target.at[2, low], {"seq": along}),
                pushes.start(normed_ref.at[low], target.at[1, low], {"seq": across}),
                pushes.start(normed_ref.at[top], target.at[2, top], {"seq": along}),
            )
        )
        if m > 0:
            forward(m - 1)
    last = pltpu.make_async_copy(normed_ref, target.at[0], local.at[1])
    last.start()
    forward(micro - 1)
    for group in sent:
        for copy in group[2:]:
            copy.wait_recv()
        for copy in group:
            copy.wait_send()
    for group in arrivals:
        for copy in group:
            copy.wait_send()
    turned.wait()
    last.wait()


def bridge(ctx_heads, weights, w_out, tokens, heads, collective):
    any_spec = pl.BlockSpec(memory_space=pl.ANY)
    like = jax.ShapeDtypeStruct
    count, width = tokens.shape
    micro = ctx_heads.shape[1]
    pushes = (UNIT - 1) * micro + 6 * micro + 1

    def fixed(i):
        return (0, 0)

    return pl.pallas_call(
        functools.partial(bridge_kernel, micro),
        grid=(1,),
        in_specs=[any_spec] * 2
        + [
            pl.BlockSpec(w_out.shape, fixed),
            pl.BlockSpec(tokens.shape, fixed),
            pl.BlockSpec((width, LANES), lambda i: (0, 2)),
        ],
        out_specs=[any_spec] * 2 + [pl.BlockSpec((count, width), fixed)] * 3,
        out_shape=[
            like((4, count, width), BF16),
            like(weights.shape, BF16),
            like((count, width), F32),
            like((count, width), BF16),
            like((count, H * HD), BF16),
        ],
        scratch_shapes=[
            pltpu.VMEM(ctx_heads.shape, BF16),
            pltpu.SemaphoreType.DMA((pushes,)),
            pltpu.SemaphoreType.DMA((pushes,)),
            pltpu.SemaphoreType.DMA((2,)),
        ],
        compiler_params=params(collective_id=collective, has_side_effects=True),
        cost_estimate=cost(2.0 * count * width * width, 8e7),
    )(ctx_heads, weights, w_out, tokens, heads)


def finish_kernel(
    rows, graw_ref, head_ref, red_ref, pre_ref, out_ref, w_ref, own_ref, tok_ref, small_ref, gmixed_ref,
    head_fin, red_out, out_fin, gin_ref,
    head_col, head_sum, out_sum, out_col, raw_in, red_own, send, recv, local,
):
    seq, row = lax.axis_index("seq"), lax.axis_index("row")
    me = seq % UNIT
    base = seq - me
    unit = [(me + k) % UNIT for k in range(1, UNIT)]
    senders = [(me + UNIT - k) % UNIT for k in range(1, UNIT)]
    column = [(row + k) % rows for k in range(1, rows)]
    greet([{"seq": base + b} for b in unit] + [{"row": r} for r in column])
    pushes = Pushes(send, recv)
    first = pltpu.make_async_copy(head_ref.at[row], head_col.at[row], local.at[0, 0])
    first.start()
    second = pltpu.make_async_copy(graw_ref.at[me], raw_in.at[me], local.at[1, 0])
    second.start()
    heads = [pushes.start(head_ref.at[r], head_col.at[row], {"row": r}) for r in column]
    raws = [pushes.start(graw_ref.at[b], raw_in.at[me], {"seq": base + b}) for b in unit]
    others = [pushes.start(red_ref.at[b], red_out.at[me], {"seq": base + b}) for b in unit]
    bounce = Bounce(red_ref.at[me], red_own, red_out.at[me], local.at[4])
    total = pre_ref[me // 2].astype(F32)
    for n in range(3):
        total = total + out_ref[n].astype(F32)
    out_sum[...] = total.astype(BF16)
    bounce.turn()
    third = pltpu.make_async_copy(out_sum.at[row], out_col.at[row], local.at[2, 0])
    third.start()
    outs = [pushes.start(out_sum.at[r], out_col.at[row], {"row": r}) for r in column]
    first.wait()
    for copy in heads:
        copy.wait_recv()
    total = head_col[0].astype(F32)
    for r in range(1, rows):
        total = total + head_col[r].astype(F32)
    head_sum[...] = total.astype(BF16)
    fourth = pltpu.make_async_copy(head_sum.at[me], head_fin.at[me], local.at[3, 0])
    fourth.start()
    others += [pushes.start(head_sum.at[b], head_fin.at[me], {"seq": base + b}) for b in unit]
    count, width = tok_ref.shape
    second.wait()
    acc = dot_nt(raw_in[me].reshape(count, 2 * LANES), own_ref[...])
    for b, copy in zip(senders, raws):
        copy.wait_recv()
        acc = acc + dot_nt(raw_in[b].reshape(count, 2 * LANES), w_ref[b])
    v = tok_ref[...].astype(F32)
    inverse = lax.rsqrt(jnp.mean(v * v, axis=-1, keepdims=True) + EPS)
    scaled = acc * gain_row(small_ref[...], E)
    mean = jnp.mean(scaled * v, axis=-1, keepdims=True)
    grad = gmixed_ref[...] + scaled * inverse - v * (inverse * inverse * inverse * mean)
    gin_ref[...] = grad.astype(BF16)
    third.wait()
    for copy in outs:
        copy.wait_recv()
    total = out_col[0].astype(F32)
    for r in range(1, rows):
        total = total + out_col[r].astype(F32)
    out_fin[...] = total
    for copy in heads + outs + raws:
        copy.wait_send()
    fourth.wait()
    bounce.wait()
    for copy in others:
        copy.wait()


def finish(
    rows, graw, head_term, reduced, pre, out_in, w_heads, tokens, heads, gmixed, collective
):
    any_spec = pl.BlockSpec(memory_space=pl.ANY)
    like = jax.ShapeDtypeStruct
    pushes = 3 * (UNIT - 1) + 2 * (rows - 1)
    count, width = tokens.shape

    def fixed(i):
        return (0, 0)

    return pl.pallas_call(
        functools.partial(finish_kernel, rows),
        grid=(1,),
        in_specs=[
            any_spec,
            any_spec,
            any_spec,
            pl.BlockSpec(pre.shape, lambda i: (0, 0, 0, 0)),
            pl.BlockSpec(out_in.shape, lambda i: (0, 0, 0, 0)),
            pl.BlockSpec(w_heads.shape, lambda i: (0, 0, 0)),
            pl.BlockSpec((width, 4 * HD), fixed),
            pl.BlockSpec(tokens.shape, fixed),
            pl.BlockSpec((width, LANES), lambda i: (0, 2)),
            pl.BlockSpec(gmixed.shape, fixed),
        ],
        out_specs=[
            any_spec,
            any_spec,
            pl.BlockSpec(pre.shape[2:], fixed),
            pl.BlockSpec(tokens.shape, fixed),
        ],
        out_shape=[
            like(head_term.shape[1:], BF16),
            like(reduced.shape, BF16),
            like(pre.shape[2:], F32),
            like(tokens.shape, BF16),
        ],
        scratch_shapes=[
            pltpu.VMEM(head_term.shape, BF16),
            pltpu.VMEM(head_term.shape[1:], BF16),
            pltpu.VMEM(pre.shape[1:], BF16),
            pltpu.VMEM(pre.shape[1:], BF16),
            pltpu.VMEM(graw.shape, BF16),
            pltpu.VMEM(reduced.shape[1:], BF16),
            pltpu.SemaphoreType.DMA((pushes,)),
            pltpu.SemaphoreType.DMA((pushes,)),
            pltpu.SemaphoreType.DMA((5, 2)),
        ],
        compiler_params=params(collective_id=collective, has_side_effects=True),
        cost_estimate=cost(4.0 * count * width * width, 6e7),
    )(graw, head_term, reduced, pre, out_in, w_heads, heads, tokens, heads, gmixed)


def lane_iota(shape):
    return lax.broadcasted_iota(jnp.int32, shape, len(shape) - 1)


def turn(u, cosine, sine):
    low_half = lane_iota(u.shape) % HD < HD // 2
    partner = jnp.where(
        low_half, pltpu.roll(u, LANES - HD // 2, u.ndim - 1), pltpu.roll(u, HD // 2, u.ndim - 1)
    )
    return u * cosine + partner * sine


def value_tables(cosine, sine):
    low = lane_iota(cosine.shape) < HD
    return jnp.where(low, cosine, 1.0), jnp.where(low, sine, 0.0)


def gain_row(small, lane):
    return small.astype(F32).T[lane : lane + 1]


def project_kernel(tok_ref, small_ref, w_ref, cos_ref, sin_ref, normed_ref, q_ref, kv_ref):
    count = q_ref.shape[1]
    width = w_ref.shape[0]
    x = tok_ref[...].reshape(count, width).astype(F32)
    inverse = lax.rsqrt(jnp.mean(x * x, axis=-1, keepdims=True) + EPS)
    normed = (x * inverse * gain_row(small_ref[...], E)).astype(BF16)
    normed_ref[...] = normed.reshape(normed_ref.shape)
    raw = dot_nn(normed, w_ref[...])
    cosine, sine = cos_ref[...], sin_ref[...]
    q = turn(raw[:, :LANES], cosine, sine).astype(BF16)
    q_ref[0] = (q.astype(F32) * HD**-0.5).astype(BF16)
    kv_ref[0] = turn(raw[:, LANES:], *value_tables(cosine, sine)).astype(BF16)


def pair_keys(kv):
    kv = kv.astype(F32)
    rolled = pltpu.roll(kv, HD, 1)
    low = lane_iota(kv.shape) < HD
    return jnp.where(low, kv, rolled), jnp.where(low, rolled, kv)


def bias_block(seg_col, seg_row, q_places, first, length):
    key_places = lax.broadcasted_iota(jnp.int32, (length, q_places.shape[1]), 0)
    allowed = (seg_col[:length] == seg_row) & (key_places <= q_places)
    return jnp.where(allowed, 0.0, NEGATIVE)


def attention_kernel(skip, q_ref, kv_ref, segq_ref, segk_ref, place_ref, ctx_ref, lse_ref):
    length = kv_ref.shape[1]
    queries = q_ref.shape[1]
    kk, vv = pair_keys(kv_ref[0])
    v_t = vv.T.astype(BF16)[:HD]
    kk = kk.astype(BF16)
    seg_col = jnp.broadcast_to(segk_ref[0], (8, length)).T[:, :1]
    for block in range(queries // QBLOCK):
        here = slice(block * QBLOCK, (block + 1) * QBLOCK)
        keys = (block + 1) * QBLOCK if skip else length
        bias = bias_block(seg_col, segq_ref[0][:, here], place_ref[:, here], 0, keys)
        q = q_ref[0, here, :]
        low = lane_iota(q.shape) < HD
        parts = []
        for head in range(2):
            mine = jnp.where(low == (head == 0), q, jnp.zeros_like(q))
            scores = dot_nt(kk[:keys], mine) + bias
            top = jnp.max(scores, axis=0, keepdims=True)
            weight = jnp.exp(scores - top)
            total = jnp.sum(weight, axis=0, keepdims=True)
            prob = (weight * (1.0 / total)).astype(BF16)
            parts.append(dot_nn(v_t[:, :keys], prob))
            lse_ref[0, head : head + 1, here] = top + jnp.log(total)
        ctx = jnp.concatenate(parts, axis=0).T.astype(BF16)
        per = QBLOCK // LANES
        ctx_ref[block * per : (block + 1) * per, 0] = ctx.reshape(per, LANES, LANES)


def attend_kernel(
    tok_ref, small_ref, w_ref, cos_ref, sin_ref, segq_ref, segk_ref, place_ref, z_ref, c_ref,
    normed_ref, q_ref, kv_ref, ctx_ref, lse_ref, z_all, c_all,
    z_middle, c_middle, send, recv, local,
):
    m = pl.program_id(0)
    across, along, far, _ = neighbours(lax.axis_index("seq"))
    pushes = Pushes(send, recv)
    count = z_ref.shape[0]
    half = count // 2
    top, low = pl.ds(0, half), pl.ds(half, half)
    first = [
        pushes.make(z_ref.at[top], z_all.at[1, top], {"seq": across}),
        pushes.make(z_ref.at[low], z_all.at[2, low], {"seq": along}),
        pushes.make(z_ref.at[low], z_all.at[1, low], {"seq": across}),
        pushes.make(z_ref.at[top], z_all.at[2, top], {"seq": along}),
    ]
    for n, peer in enumerate((across, along, far)):
        place = pl.ds((n + 1) * count, count)
        first.append(pushes.make(c_ref, c_all.at[:, place], {"seq": peer}))
    second = [
        pushes.make(z_all.at[1, top], z_all.at[3, top], {"seq": along}),
        pushes.make(z_all.at[2, low], z_all.at[3, low], {"seq": across}),
    ]
    bounces = [
        Bounce(z_ref, z_middle, z_all.at[0], local.at[0], False),
        Bounce(c_ref, c_middle, c_all.at[:, pl.ds(0, count)], local.at[1], False),
    ]

    @pl.when(m == 0)
    def _():
        greet([{"seq": across}, {"seq": along}, {"seq": far}])
        for copy in first:
            copy.start()
        for copy in bounces:
            copy.inward.start()
        for copy in bounces:
            copy.turn()

    project_kernel(tok_ref, small_ref, w_ref, cos_ref, sin_ref, normed_ref, q_ref, kv_ref)

    @pl.when(m == 1)
    def _():
        for copy, onward in zip(first, second):
            copy.wait_recv()
            onward.start()

    attention_kernel(True, q_ref, kv_ref, segq_ref, segk_ref, place_ref, ctx_ref, lse_ref)

    @pl.when(m == pl.num_programs(0) - 1)
    def _():
        for copy in first[2:] + second:
            copy.wait_recv()
        for copy in first + second:
            copy.wait_send()
        for copy in bounces:
            copy.wait()


def attention_back_kernel(
    skip, q_ref, kv_ref, segq_ref, segk_ref, place_ref, lse_ref, do_ref, cosq_ref, sinq_ref,
    cosk_ref, sink_ref, normed_ref, pre_ref, red_ref, graw_ref, term_ref, pre_in, red_out,
    dk_acc, dv_acc, term_acc, red_own, send, recv, local,
):
    seq = lax.axis_index("seq")
    me = seq % UNIT
    base = seq - me
    unit = [(me + k) % UNIT for k in range(1, UNIT)]
    pushes = Pushes(send, recv)
    sides = []
    for n, peer in enumerate(neighbours(seq)[:3]):
        sides.append(pushes.make(pre_ref.at[(peer - base) // 2], pre_in.at[n], {"seq": peer}))
    for b in unit:
        sides.append(pushes.make(red_ref.at[b], red_out.at[me], {"seq": base + b}))
    bounce = Bounce(red_ref.at[me], red_own, red_out.at[me], local, False)
    m = pl.program_id(0)

    @pl.when(m == 0)
    def _():
        greet([{"seq": base + b} for b in unit])
        bounce.inward.start()
        for copy in sides:
            copy.start()
        bounce.turn()

    length = kv_ref.shape[1]
    queries = q_ref.shape[1]
    kk, vv = pair_keys(kv_ref[0])
    k_t = kk.T.astype(BF16)[:HD]
    kk = kk.astype(BF16)
    vv = vv.astype(BF16)
    seg_col = jnp.broadcast_to(segk_ref[0], (8, length)).T[:, :1]
    dk_acc[...] = jnp.zeros_like(dk_acc)
    dv_acc[...] = jnp.zeros_like(dv_acc)
    per = QBLOCK // LANES
    for block in range(queries // QBLOCK):
        here = slice(block * QBLOCK, (block + 1) * QBLOCK)
        keys = (block + 1) * QBLOCK if skip else length
        bias = bias_block(seg_col, segq_ref[0][:, here], place_ref[:, here], 0, keys)
        q = q_ref[0, here, :]
        do = do_ref[block * per : (block + 1) * per, 0].reshape(QBLOCK, LANES)
        low = lane_iota(q.shape) < HD
        parts = []
        for head in range(2):
            pick = low == (head == 0)
            mine = jnp.where(pick, q, jnp.zeros_like(q))
            mine_do = jnp.where(pick, do, jnp.zeros_like(do))
            scores = dot_nt(kk[:keys], mine) + bias
            weight = jnp.exp(scores - lse_ref[0, head : head + 1, here])
            product = dot_nt(vv[:keys], mine_do)
            delta = jnp.sum(weight * product, axis=0, keepdims=True)
            grad_scores = (weight * (product - delta)).astype(BF16)
            dv_acc[:keys] += dot_nn(weight.astype(BF16), mine_do)
            dk_acc[:keys] += dot_nn(grad_scores, mine)
            parts.append(dot_nn(k_t[:, :keys], grad_scores))
        dq = jnp.concatenate(parts, axis=0).T * HD**-0.5
        dq = turn(dq, cosq_ref[here, :], -sinq_ref[here, :]).astype(BF16)
        graw_ref[block * per : (block + 1) * per, 0, :, :LANES] = dq.reshape(per, LANES, LANES)
    dk = dk_acc[...]
    dv = dv_acc[...]
    dk = dk + pltpu.roll(dk, HD, 1)
    dv = dv + pltpu.roll(dv, HD, 1)
    gkv = jnp.where(lane_iota(dk.shape) < HD, dk, dv)
    key_cos, key_sin = value_tables(cosk_ref[...], sink_ref[...])
    gkv = turn(gkv, key_cos, -key_sin).astype(BF16)
    graw_ref[:, 0, :, LANES:] = gkv.reshape(length // LANES, LANES, LANES)
    if skip:
        normed_t = normed_ref[...].reshape(queries, -1).T
        term = dot_nn(normed_t, graw_ref[...].reshape(queries, 2 * LANES))
        @pl.when(m == 0)
        def _():
            term_acc[...] = term

        @pl.when(m > 0)
        def _():
            term_acc[...] += term

        @pl.when(m == pl.num_programs(0) - 1)
        def _():
            for b in range(UNIT):
                for r in range(PIECES):
                    at = (b * PIECES + r) * ROWS_IN
                    term_ref[r, b] = term_acc[at : at + ROWS_IN].astype(BF16)

    @pl.when(m == pl.num_programs(0) - 1)
    def _():
        for copy in sides:
            copy.wait()
        bounce.wait()


def spread(rows):
    rest = jnp.zeros((LANES - E, rows.shape[1]), F32)
    return jnp.concatenate([rows.astype(F32), rest], axis=0).T


def soft_gates(normed, router, chosen):
    logits = jnp.where(chosen > 0, dot_nn(normed, router), NEGATIVE)
    top = jnp.max(logits, axis=-1, keepdims=True)
    weight = jnp.where(chosen > 0, jnp.exp(logits - top), 0.0)
    return weight / jnp.sum(weight, axis=-1, keepdims=True)


def unpack(inner_ref, down_ref, first, wg, wu, wd):
    half = wg.shape[1]
    for r in range(PIECES):
        for b in range(UNIT):
            at = (b * PIECES + r) * ROWS_IN
            low = (b * PIECES + r) * ROWS_OUT
            wg[at : at + ROWS_IN] = inner_ref[r, b, :ROWS_IN]
            wu[at : at + ROWS_IN] = inner_ref[r, b, ROWS_IN : 2 * ROWS_IN]
            for c in range(2):
                start = first + c * ROWS_OUT
                wd[low : low + ROWS_OUT, c * half : (c + 1) * half] = down_ref[
                    r, b, start : start + ROWS_OUT
                ]


def load_weights(now, later, first, fetches, wg, wu, wd, greeted):
    e, t = pl.program_id(0), pl.program_id(1)

    @pl.when((t == 0) & (e == 0))
    def _():
        for copy in fetches:
            copy.start()
        greet([{"seq": peer} for peer in greeted])
        unpack(*now, first, wg, wu, wd)

    @pl.when((t == 0) & (e == 1))
    def _():
        for copy in fetches:
            copy.wait()
        unpack(*later, first, wg, wu, wd)


def twin_push(source, target, send, recv):
    twin = neighbours(lax.axis_index("seq"))[3]
    return pltpu.make_async_remote_copy(
        src_ref=source,
        dst_ref=target,
        send_sem=send,
        recv_sem=recv,
        device_id={"seq": twin},
        device_id_type=pl.DeviceIdType.MESH,
    )


def collect_terms(x, dz, grad_gate, grad_up, gated, ag, au, ad, stage, total, dw, sems):
    e, t = pl.program_id(0), pl.program_id(1)
    last_t = pl.num_programs(1) - 1
    half = ag.shape[1]

    @pl.when(t == 0)
    def _():
        ag[...] = dot_tn(x, grad_gate)
        au[...] = dot_tn(x, grad_up)
        ad[...] = dot_tn(gated, dz)

    @pl.when((t > 0) & (t < last_t))
    def _():
        ag[...] += dot_tn(x, grad_gate)
        au[...] += dot_tn(x, grad_up)
        ad[...] += dot_tn(gated, dz)

    send, recv, local = sems
    push = twin_push(stage, total, send.at[0], recv.at[0])
    out = pltpu.make_async_copy(stage, dw, local.at[1])

    def store(write):
        for place, acc, grad in ((0, ag, grad_gate), (ROWS_IN, au, grad_up)):
            final = acc[...] + dot_tn(x, grad)
            for r in range(PIECES):
                for b in range(UNIT):
                    at = (b * PIECES + r) * ROWS_IN
                    write(r, b, place, final[at : at + ROWS_IN])
        final = ad[...] + dot_tn(gated, dz)
        for r in range(PIECES):
            for b in range(UNIT):
                low = (b * PIECES + r) * ROWS_OUT
                for c in range(2):
                    start = 2 * ROWS_IN + c * ROWS_OUT
                    write(r, b, start, final[low : low + ROWS_OUT, c * half : (c + 1) * half])

    @pl.when((t == last_t) & (e == 0))
    def _():
        def write(r, b, place, value):
            stage[r, b, place : place + value.shape[0]] = value.astype(BF16)

        store(write)
        push.start()

    @pl.when((t == last_t) & (e == 1))
    def _():
        push.wait()

        def write(r, b, place, value):
            here = slice(place, place + value.shape[0])
            stage[r, b, here] = (value + total[r, b, here].astype(F32)).astype(BF16)

        store(write)
        out.start()
        out.wait()


def sigmoid(v):
    return 0.5 + 0.5 * jnp.tanh(0.5 * v)


def grads_of(gate_act, up_act, back, gate):
    sig = sigmoid(gate_act)
    silu = gate_act * sig
    hidden = silu * up_act
    grad_hidden = back * gate
    grad_gate = (grad_hidden * up_act * (sig + silu * (1.0 - sig))).astype(BF16)
    grad_up = (grad_hidden * silu).astype(BF16)
    return hidden, grad_gate, grad_up


def expert_id(twin, index):
    me = lax.axis_index("seq") % UNIT
    return 2 * (me + twin * (1 - 2 * (me % 2))) + index


def pick_gate(gates, gid):
    mine = lane_iota(gates.shape) == gid
    return mine, jnp.sum(jnp.where(mine, gates, 0.0), axis=1, keepdims=True)


def gate_terms(mine, hidden, back):
    terms = jnp.where(mine, jnp.sum(hidden * back, axis=1, keepdims=True), 0.0)
    return terms.T[:E]


def both_kernel(
    x_ref, dz_ref, chosen_ref, wr_ref, w0_ref, w1_hbm, heads_ref,
    out_ref, dx_ref, gg_ref, gates_ref, dw, w_heads,
    wg, wu, wd, gates_s, ag, au, ad, oacc, dxacc, ggacc, w1_ref, stage, total,
    send, recv, local,
):
    e, t = pl.program_id(0), pl.program_id(1)
    tile, width = out_ref.shape
    rows = pl.ds(pl.multiple_of(t * tile, tile), tile)
    x = x_ref[...]
    dz = dz_ref[...]
    last_t = pl.num_programs(1) - 1
    across, along, _, twin = neighbours(lax.axis_index("seq"))
    fetch = pltpu.make_async_copy(w1_hbm, w1_ref, local.at[0])
    packed = (w0_ref, w0_ref)
    load_weights(
        packed, (w1_ref, w1_ref), 2 * ROWS_IN, [fetch], wg, wu, wd, (across, along, twin)
    )

    me = lax.axis_index("seq") % UNIT
    base = lax.axis_index("seq") - me
    a, b, d = across - base, along - base, 6 - me + 2 * (me % 2)
    half = heads_ref.shape[0] // 2
    top, low = pl.ds(0, half), pl.ds(half, half)
    lanes = pl.ds(0, w_heads.shape[2])
    pushes = Pushes(send, recv)
    pushes.used = 1

    def own_part(part, device):
        return pushes.make(heads_ref.at[part, lanes], w_heads.at[me, part], {"seq": device})

    def passed(slot, part, device):
        view = w_heads.at[slot, part]
        return pushes.make(view, view, {"seq": device})

    hop1 = [own_part(top, across), own_part(low, along), own_part(low, across), own_part(top, along)]
    hop1 += [own_part(top, twin), own_part(low, twin)]
    hop2 = [passed(a, top, along), passed(b, low, across), passed(a, top, twin), passed(b, low, twin)]
    hop3 = [passed(a, low, twin), passed(b, top, twin)]
    hop4 = [passed(d, top, twin), passed(d, low, twin)]
    events = (
        (0, 0, (), hop1),
        (0, 1, hop1[:2], hop2),
        (0, last_t, hop1[2:4], hop3),
        (1, 0, hop2[:2], hop4),
    )
    for at_e, at_t, arrived, onward in events:

        @pl.when((e == at_e) & (t == at_t))
        def _(arrived=arrived, onward=onward):
            for copy in arrived:
                copy.wait_recv()
            for copy in onward:
                copy.start()

    @pl.when(e == 0)
    def _():
        gates_s[rows, :] = soft_gates(x, wr_ref[...], spread(chosen_ref[...]))

    mine, gate = pick_gate(gates_s[rows, :], expert_id(1 - e, 0))
    gate_act = dot_nn(x, wg[...])
    up_act = dot_nn(x, wu[...])
    back = dot_nt(dz, wd[...])
    hidden, grad_gate, grad_up = grads_of(gate_act, up_act, back, gate)
    ggterm = gate_terms(mine, hidden, back)
    gated = (hidden * gate).astype(BF16)
    out = dot_nn(gated, wd[...])
    dx = dot_nt(grad_gate, wg[...]) + dot_nt(grad_up, wu[...])

    @pl.when(e == 0)
    def _():
        oacc[rows, :] = out
        dxacc[rows, :] = dx
        ggacc[t] = ggterm

    @pl.when(e == 1)
    def _():
        out_ref[...] = (oacc[rows, :] + out).astype(BF16)
        dx_ref[...] = (dxacc[rows, :] + dx).astype(BF16)
        gg_ref[...] = ggacc[t] + ggterm
        gates_ref[...] = gates_s[rows, :]

    sems = (send, recv, local)
    collect_terms(x, dz, grad_gate, grad_up, gated, ag, au, ad, stage, total, dw, sems)

    @pl.when((e == 1) & (t == last_t))
    def _():
        for copy in hop1[4:] + hop2[2:] + hop3 + hop4:
            copy.wait_recv()
        for copy in hop1 + hop2 + hop3 + hop4:
            copy.wait_send()


def forward_kernel(
    x_ref, gates_ref, inner_ref, down_ref, inner_hbm, down_hbm, oin_ref,
    out_ref, gact_ref, uact_ref, inner_twin, down_twin,
    wg, wu, wd, oacc, inner_next, down_next, send, recv, local,
):
    e, t = pl.program_id(0), pl.program_id(1)
    tile = out_ref.shape[0]
    rows = pl.ds(pl.multiple_of(t * tile, tile), tile)
    x = x_ref[...]
    last_t = pl.num_programs(1) - 1
    turned = [
        twin_push(inner_hbm, inner_twin, send.at[0], recv.at[0]),
        twin_push(down_hbm, down_twin, send.at[1], recv.at[1]),
    ]
    fetches = [
        pltpu.make_async_copy(inner_twin, inner_next, local.at[0]),
        pltpu.make_async_copy(down_twin, down_next, local.at[1]),
    ]

    @pl.when((e == 0) & (t == 0))
    def _():
        greet([{"seq": neighbours(lax.axis_index("seq"))[3]}])
        for copy in turned:
            copy.start()
        unpack(inner_ref, down_ref, 0, wg, wu, wd)

    @pl.when((e == 1) & (t == 0))
    def _():
        for copy in fetches:
            copy.wait()
        unpack(inner_next, down_next, 0, wg, wu, wd)

    _, gate = pick_gate(gates_ref[...], expert_id(e, 1))
    gate_act = dot_nn(x, wg[...])
    up_act = dot_nn(x, wu[...])
    gact_ref[0] = gate_act.astype(BF16)
    uact_ref[0] = up_act.astype(BF16)
    gated = (gate_act * sigmoid(gate_act) * up_act * gate).astype(BF16)
    out = dot_nn(gated, wd[...])

    @pl.when(e == 0)
    def _():
        oacc[rows, :] = oin_ref[...].astype(F32) + out

    @pl.when(e == 1)
    def _():
        out_ref[...] = (oacc[rows, :] + out).astype(BF16)

    @pl.when((e == 0) & (t == last_t))
    def _():
        for copy in turned:
            copy.wait()
        for copy in fetches:
            copy.start()


def backward_kernel(
    x_ref, dz_ref, gates_ref, gact_ref, uact_ref, inner_ref, down_ref,
    inner_hbm, down_hbm, dxin_ref, ggin_ref,
    out_hbm, dx_ref, gg_ref, dw, out_in,
    wg, wu, wd, ag, au, ad, dxacc, ggacc, inner_next, down_next, stage, total,
    diag_x, diag_y, own_x, own_y, send, recv, local,
):
    e, t = pl.program_id(0), pl.program_id(1)
    tile, width = dx_ref.shape
    rows = pl.ds(pl.multiple_of(t * tile, tile), tile)
    x = x_ref[...]
    dz = dz_ref[...]
    fetches = [
        pltpu.make_async_copy(inner_hbm, inner_next, local.at[0]),
        pltpu.make_async_copy(down_hbm, down_next, local.at[4]),
    ]
    load_weights(
        (inner_ref, down_ref), (inner_next, down_next), 0, fetches, wg, wu, wd,
        neighbours(lax.axis_index("seq")),
    )
    across, along, _, _ = neighbours(lax.axis_index("seq"))
    pushes = Pushes(send, recv)
    pushes.used = 1
    half = own_x.shape[0]
    top, low = pl.ds(0, half), pl.ds(half, half)
    first = [
        pushes.make(out_hbm.at[3, top], diag_x, {"seq": across}),
        pushes.make(out_hbm.at[3, low], diag_y, {"seq": along}),
        pushes.make(out_hbm.at[1, top], out_in.at[0, top], {"seq": across}),
        pushes.make(out_hbm.at[2, low], out_in.at[1, low], {"seq": along}),
    ]
    second = [
        pushes.make(own_x, out_in.at[0, low], {"seq": across}),
        pushes.make(own_y, out_in.at[1, top], {"seq": along}),
    ]
    loads = [
        pltpu.make_async_copy(out_hbm.at[1, low], own_x, local.at[2]),
        pltpu.make_async_copy(out_hbm.at[2, top], own_y, local.at[3]),
    ]

    @pl.when((e == 0) & (t == 0))
    def _():
        for copy in first + loads:
            copy.start()

    mine, gate = pick_gate(gates_ref[...], expert_id(1 - e, 1))
    back = dot_nt(dz, wd[...])
    hidden, grad_gate, grad_up = grads_of(
        gact_ref[0].astype(F32), uact_ref[0].astype(F32), back, gate
    )
    ggterm = gate_terms(mine, hidden, back)
    gated = (hidden * gate).astype(BF16)
    dx = dot_nt(grad_gate, wg[...]) + dot_nt(grad_up, wu[...])

    @pl.when(e == 0)
    def _():
        dxacc[rows, :] = dxin_ref[...].astype(F32) + dx
        ggacc[t] = ggin_ref[...] + ggterm

    @pl.when(e == 1)
    def _():
        dx_ref[...] = (dxacc[rows, :] + dx).astype(BF16)
        gg_ref[...] = ggacc[t] + ggterm

    sems = (send, recv, local)
    collect_terms(x, dz, grad_gate, grad_up, gated, ag, au, ad, stage, total, dw, sems)

    @pl.when((e == 0) & (t == pl.num_programs(1) - 1))
    def _():
        for copy in loads:
            copy.wait()
        first[0].wait_recv()
        first[1].wait_recv()
        own_x[...] = (own_x[...].astype(F32) + diag_y[...].astype(F32)).astype(BF16)
        own_y[...] = (own_y[...].astype(F32) + diag_x[...].astype(F32)).astype(BF16)
        for copy in second:
            copy.start()

    @pl.when((e == 1) & (t == pl.num_programs(1) - 1))
    def _():
        first[0].wait_send()
        first[1].wait_send()
        for copy in first[2:] + second:
            copy.wait()


def run_experts(which, x, dz, chosen, weights, router=None, gates=None, carried=None, acts=None, pushed=None):
    tokens, width = x.shape
    hidden = weights[0].shape[3]
    packed_shape = (PIECES, UNIT, 3 * ROWS_IN, hidden)
    inner_shape = (PIECES, UNIT, 2 * ROWS_IN, hidden)
    down_shape = (PIECES, UNIT, ROWS_IN, hidden)
    tile = tokens // 3
    tiles = 3
    like = jax.ShapeDtypeStruct
    any_spec = pl.BlockSpec(memory_space=pl.ANY)
    once = pl.Buffered(1)

    def by_token(e, t):
        return (t, 0)

    def at_end(e, t):
        return (jnp.where(e == 1, t, 0), 0)

    def at_start(e, t):
        return (jnp.where(e == 0, t, tiles - 1), 0)

    def lanes_end(e, t):
        return (0, jnp.where(e == 1, t, 0))

    def lanes_start(e, t):
        return (0, jnp.where(e == 0, t, tiles - 1))

    def acts_map(e, t):
        return (e, t, 0)

    x_spec = pl.BlockSpec((tile, width), by_token)
    gates_spec = pl.BlockSpec((tile, LANES), by_token)

    def weight_spec(shape):
        return pl.BlockSpec(shape, lambda e, t: (0, 0, 0, 0), pipeline_mode=once)

    acts_spec = pl.BlockSpec((1, tile, hidden), acts_map)
    acts_back = pl.BlockSpec((1, tile, hidden), lambda e, t: (1 - e, t, 0))
    token_end = pl.BlockSpec((tile, width), at_end)
    token_start = pl.BlockSpec((tile, width), at_start)
    packed_like = like(packed_shape, BF16)
    pair_like = [like(inner_shape, BF16), like(down_shape, BF16)]
    pair_vmem = [pltpu.VMEM(inner_shape, BF16), pltpu.VMEM(down_shape, BF16)]
    pair_specs = [weight_spec(inner_shape), weight_spec(down_shape), any_spec, any_spec]
    token_like = like((tokens, width), BF16)
    gg_like = like((E, tokens), F32)
    acts_like = like((2, tokens, hidden), BF16)
    unpacked = [
        pltpu.VMEM((width, hidden), BF16),
        pltpu.VMEM((width, hidden), BF16),
        pltpu.VMEM((hidden, width), BF16),
    ]
    terms = [
        pltpu.VMEM((width, hidden), F32),
        pltpu.VMEM((width, hidden), F32),
        pltpu.VMEM((hidden, width), F32),
    ]
    acc = pltpu.VMEM((tokens, width), F32)
    gg_acc = pltpu.VMEM((tiles, E, tile), F32)
    second = pltpu.VMEM(packed_shape, BF16)
    stage = pltpu.VMEM(packed_shape, BF16)
    sem, sems = pltpu.SemaphoreType.DMA, pltpu.SemaphoreType.DMA((2,))
    flops = 4.0 * tokens * width * hidden
    if which == "both":
        return pl.pallas_call(
            both_kernel,
            grid=(2, tiles),
            in_specs=[
                x_spec, x_spec, pl.BlockSpec((E, tile), lambda e, t: (0, t)),
                pl.BlockSpec((width, LANES), lambda e, t: (0, 2), pipeline_mode=once),
                weight_spec(packed_shape), any_spec, any_spec,
            ],
            out_specs=[
                token_end, token_end, pl.BlockSpec((E, tile), lanes_end),
                pl.BlockSpec((tile, LANES), at_end), any_spec, any_spec,
            ],
            out_shape=[
                token_like, token_like, gg_like, like((tokens, LANES), F32),
                packed_like, like((UNIT, width, 4 * HD), BF16),
            ],
            scratch_shapes=unpacked
            + [pltpu.VMEM((tokens, LANES), F32)]
            + terms
            + [acc, acc, gg_acc, second, stage, stage]
            + [pltpu.SemaphoreType.DMA((15,)), pltpu.SemaphoreType.DMA((15,)), sems],
            compiler_params=params(collective_id=5, has_side_effects=True),
            cost_estimate=cost(1, 1e5),
        )(x, dz, chosen, router, *weights, router)
    if which == "forward":
        return pl.pallas_call(
            forward_kernel,
            grid=(2, tiles),
            in_specs=[x_spec, gates_spec] + pair_specs + [token_start],
            out_specs=[token_end, acts_spec, acts_spec, any_spec, any_spec],
            out_shape=[token_like, acts_like, acts_like] + pair_like,
            scratch_shapes=unpacked + [acc] + pair_vmem + [sems, sems, sems],
            compiler_params=params(collective_id=9, has_side_effects=True),
            cost_estimate=cost(3 * flops, 2e7),
        )(x, gates, *weights, *weights, carried)
    return pl.pallas_call(
        backward_kernel,
        grid=(2, tiles),
        in_specs=[
            x_spec, x_spec, gates_spec, acts_back, acts_back, *pair_specs,
            token_start, pl.BlockSpec((E, tile), lanes_start), any_spec,
        ],
        out_specs=[token_end, pl.BlockSpec((E, tile), lanes_end), any_spec, any_spec],
        out_shape=[
            token_like, gg_like, packed_like, like((2,) + pushed.shape[1:], BF16),
        ],
        scratch_shapes=unpacked + terms + [acc, gg_acc]
        + pair_vmem
        + [stage, stage]
        + [pltpu.VMEM((pushed.shape[1] // 2, width), BF16)] * 4
        + [pltpu.SemaphoreType.DMA((7,)), pltpu.SemaphoreType.DMA((7,))]
        + [pltpu.SemaphoreType.DMA((5,))],
        compiler_params=params(collective_id=6, has_side_effects=True),
        cost_estimate=cost(6 * flops, 2e7),
    )(x, dz, gates, acts[0], acts[1], *weights, carried[0], carried[1], pushed)


def return_kernel(
    micro, copies, dx_ref, gg_ref, mixed_ref, normed_ref, dz_ref, chosen_ref, small_ref, w_ref,
    ctx_ref, own_out, back_out, do_out, gmixed_ref, pre_ref, block_ref,
    mine_dx, from_x, from_y, diag_x, diag_y, sum_x, sum_y, gparts, gctx, gbranch, glogs, term, twin_term, send, recv, local,
):
    seq = lax.axis_index("seq")
    me = seq % UNIT
    core = me % 2
    base = seq - me
    unit = [(me + k) % UNIT for k in range(1, UNIT)]
    *peers, twin = neighbours(seq)
    greet([{"seq": base + b} for b in unit])
    pushes = Pushes(send, recv)
    count, width = mixed_ref.shape
    step = count // micro
    half = step // 2
    chunks = [pl.ds(m * step, step) for m in range(micro)]
    tops = [pl.ds(m * step, half) for m in range(micro)]
    lows = [pl.ds(m * step + half, half) for m in range(micro)]
    across, along = peers[:2]
    own = [
        pltpu.make_async_copy(dx_ref, mine_dx, local.at[0]),
        pltpu.make_async_copy(gg_ref.at[:, pl.ds(0, count)], gparts.at[0], local.at[1]),
    ]
    for copy in own:
        copy.start()
    diagonal, direct, sums = [], [], []

    def send_diagonal(m):
        diagonal.append(
            (
                pushes.start(dx_ref.at[3, tops[m]], diag_x.at[m], {"seq": across}),
                pushes.start(dx_ref.at[3, lows[m]], diag_y.at[m], {"seq": along}),
            )
        )

    def send_direct(m):
        direct.append(
            (
                pushes.start(dx_ref.at[1, tops[m]], from_x.at[tops[m]], {"seq": across}),
                pushes.start(dx_ref.at[2, lows[m]], from_y.at[lows[m]], {"seq": along}),
            )
        )

    def send_sums(m):
        for copy in diagonal[m]:
            copy.wait_recv()
        own_y = mine_dx[2, tops[m]].astype(F32) + diag_x[m].astype(F32)
        own_x = mine_dx[1, lows[m]].astype(F32) + diag_y[m].astype(F32)
        sum_y[m] = own_y.astype(BF16)
        sum_x[m] = own_x.astype(BF16)
        sums.append(
            (
                pushes.start(sum_y.at[m], from_y.at[tops[m]], {"seq": along}),
                pushes.start(sum_x.at[m], from_x.at[lows[m]], {"seq": across}),
            )
        )

    send_diagonal(0)
    first = []
    for n in (2, 0, 1):
        part = gg_ref.at[:, pl.ds((n + 1) * count, count)]
        first.append(pushes.start(part, gparts.at[n + 1], {"seq": peers[n]}))
    send_direct(0)
    if micro > 1:
        send_diagonal(1)
    small = small_ref[...]
    gain = gain_row(small, E + 1)
    gates = soft_gates(normed_ref[...], small, spread(chosen_ref[...]))
    block = mixed_ref[...] + own_out[0].astype(F32) + back_out[0].astype(F32)
    block_ref[...] = (block + back_out[1].astype(F32)).astype(BF16)
    for copy in own:
        copy.wait()
    for copy in first:
        copy.wait_recv()
    grad_gates = gparts[0] + gparts[1] + gparts[2] + gparts[3]
    grad_gates = spread(grad_gates)
    centre = jnp.sum(gates * grad_gates, axis=-1, keepdims=True)
    glogs[...] = (gates * (grad_gates - centre)).astype(BF16)
    sent = []

    def compute(m):
        here = chunks[m]
        for copy in direct[m] + sums[m]:
            copy.wait_recv()
        dy = mine_dx[0, here].astype(F32) + from_x[here].astype(F32) + from_y[here].astype(F32)
        dy = dy + dot_nt(glogs[here], small)
        v = mixed_ref[here]
        inverse = lax.rsqrt(jnp.mean(v * v, axis=-1, keepdims=True) + EPS)
        scaled = dy * gain
        mean = jnp.mean(scaled * v, axis=-1, keepdims=True)
        gmixed = dz_ref[here].astype(F32) + scaled * inverse
        gmixed = gmixed - v * (inverse * inverse * inverse * mean)
        gmixed_ref[here] = gmixed
        branch = gmixed.astype(BF16)
        gbranch[here] = branch
        grad_ctx = dot_nt(branch, w_ref[...]).astype(BF16)
        for b in range(UNIT):
            gctx[b, m] = grad_ctx[:, b * LANES : (b + 1) * LANES]
        mine = pltpu.make_async_copy(gctx.at[me, m], do_out.at[me, m], local.at[2 + m])
        mine.start()
        own.append(mine)
        for b in unit:
            sent.append(pushes.start(gctx.at[b, m], do_out.at[me, m], {"seq": base + b}))

    for m in range(micro):
        send_sums(m)
        if m + 1 < micro:
            send_direct(m + 1)
        if m + 2 < micro:
            send_diagonal(m + 2)
        if m > 0:
            compute(m - 1)
    compute(micro - 1)
    rest = width // (copies * UNIT)
    out_term = dot_tn(ctx_ref[...], gbranch[...]).astype(BF16)
    router_term = dot_tn(normed_ref[...], glogs[...]).astype(BF16)
    for a in range(copies):
        for b in range(UNIT):
            at = (a * UNIT + b) * rest
            term[a, b, :, :width] = out_term[at : at + rest]
            term[a, b, :, width:] = router_term[at : at + rest]
    turned = [
        pushes.start(term.at[:, 2 * j + 1 - core], twin_term.at[j], {"seq": twin})
        for j in range(4)
    ]
    for j, copy in enumerate(turned):
        copy.wait_recv()
        summed = term[:, 2 * j + core].astype(F32) + twin_term[j].astype(F32)
        pre_ref[j] = summed.astype(BF16)
    for group in [first] + diagonal + direct + sums:
        for copy in group:
            copy.wait_send()
    for copy in turned:
        copy.wait_send()
    for copy in own[2:] + sent:
        copy.wait()


def return_tokens(
    dx, gg, mixed, normed, dz, chosen, heads, w_out, context, own_out, back_out, micro, copies, collective
):
    any_spec = pl.BlockSpec(memory_space=pl.ANY)
    like = jax.ShapeDtypeStruct
    count, width = mixed.shape
    ctx_shape = (UNIT, micro, count // micro, LANES)
    pre_shape = (4, copies, width // (copies * UNIT), width + LANES)
    pushes = 3 + 6 * micro + (UNIT - 1) * micro + 4
    piece = (micro, count // micro // 2, width)

    def fixed(i):
        return (0, 0)

    return pl.pallas_call(
        functools.partial(return_kernel, micro, copies),
        grid=(1,),
        in_specs=[
            any_spec,
            any_spec,
            pl.BlockSpec(mixed.shape, fixed),
            pl.BlockSpec(normed.shape, fixed),
            pl.BlockSpec(dz.shape, fixed),
            pl.BlockSpec(chosen.shape, fixed),
            pl.BlockSpec((width, LANES), lambda i: (0, 2)),
            pl.BlockSpec(w_out.shape, fixed),
            pl.BlockSpec(context.shape, fixed),
            pl.BlockSpec((1, count, width), lambda i: (0, 0, 0)),
            pl.BlockSpec((2, count, width), lambda i: (0, 0, 0)),
        ],
        out_specs=[
            any_spec,
            pl.BlockSpec((count, width), fixed),
            pl.BlockSpec(pre_shape, lambda i: (0, 0, 0, 0)),
            pl.BlockSpec((count, width), fixed),
        ],
        out_shape=[
            like(ctx_shape, BF16),
            like((count, width), F32),
            like(pre_shape, BF16),
            like((count, width), BF16),
        ],
        scratch_shapes=[
            pltpu.VMEM((4, count, width), BF16),
            pltpu.VMEM((count, width), BF16),
            pltpu.VMEM((count, width), BF16),
            pltpu.VMEM(piece, BF16),
            pltpu.VMEM(piece, BF16),
            pltpu.VMEM(piece, BF16),
            pltpu.VMEM(piece, BF16),
            pltpu.VMEM((4, E, count), F32),
            pltpu.VMEM(ctx_shape, BF16),
            pltpu.VMEM((count, width), BF16),
            pltpu.VMEM((count, LANES), BF16),
            pltpu.VMEM((copies, UNIT) + pre_shape[2:], BF16),
            pltpu.VMEM(pre_shape, BF16),
            pltpu.SemaphoreType.DMA((pushes,)),
            pltpu.SemaphoreType.DMA((pushes,)),
            pltpu.SemaphoreType.DMA((2 + micro,)),
        ],
        compiler_params=params(collective_id=collective, has_side_effects=True),
        cost_estimate=cost(4.0 * count * width * width, 1.2e8),
    )(dx, gg, mixed, normed, dz, chosen, heads, w_out, context, own_out, back_out)


def unpack_grads_kernel(
    ex0, ex1, head_ref, out_ref, gate_w, up_w, query_w, key_w, value_w, router_w, attn_ref, ffn_ref,
    gattn, gquery, gkey, gvalue, gout, gffn, grouter, ggate, gup, gdown,
):
    part, hidden = gate_w.shape[1:]
    half = part // 2
    width = gout.shape[1]
    ffn = jnp.zeros((part, hidden), F32)
    for n, source in enumerate((ex0, ex1)):
        for b in range(UNIT):
            e = 2 * b + n
            gate = source[b, :part].astype(F32)
            up = source[b, part : 2 * part].astype(F32)
            ggate[e] = gate
            gup[e] = up
            ffn = ffn + gate * gate_w[e].astype(F32) + up * up_w[e].astype(F32)
            for c in range(2):
                start = 2 * part + c * half
                gdown[e, :, c * hidden : (c + 1) * hidden] = source[b, start : start + half].astype(
                    F32
                )
    router = out_ref[:, width : width + E]
    grouter[...] = router
    gout[...] = out_ref[:, :width]
    low = lane_iota((part, LANES)) < HD
    attn = jnp.zeros((part, LANES), F32)
    for pair in range(UNIT // 2):
        lanes = slice(pair * LANES, (pair + 1) * LANES)
        even = head_ref[2 * pair, :, LANES:].astype(F32)
        odd = head_ref[2 * pair + 1, :, LANES:].astype(F32)
        key = jnp.where(low, even, pltpu.roll(odd, HD, 1))
        value = jnp.where(low, pltpu.roll(even, HD, 1), odd)
        gkey[:, lanes] = key
        gvalue[:, lanes] = value
        attn = attn + key * key_w[:, lanes].astype(F32) + value * value_w[:, lanes].astype(F32)
    for b in range(UNIT):
        lanes = slice(b * LANES, (b + 1) * LANES)
        query = head_ref[b, :, :LANES].astype(F32)
        gquery[:, lanes] = query
        attn = attn + query * query_w[:, lanes].astype(F32)

    def as_row(column):
        return jnp.broadcast_to(column, (part, LANES)).T[:1]

    attn = jnp.sum(attn, axis=1, keepdims=True)
    ffn = jnp.sum(ffn, axis=1, keepdims=True)
    ffn = ffn + jnp.sum(router * router_w[...].astype(F32), axis=1, keepdims=True)
    gattn[...] = as_row(attn) / attn_ref[...].astype(F32)
    gffn[...] = as_row(ffn) / ffn_ref[...].astype(F32)


def shards(
    copies, tokens, segments, routes, cotangent, norm_attn, w_query, w_key, w_value, w_out, norm_ffn,
    w_router, w_gate, w_up, w_down, rows,
):
    micro, local_len, width = tokens.shape
    length = segments.shape[1]
    count = micro * local_len
    unit_len = UNIT * local_len
    part = w_query.shape[0]
    hidden = w_gate.shape[2]
    seq_size = copies * UNIT
    seq = lax.axis_index("seq")
    row = lax.axis_index("row")
    unit = seq // UNIT
    me = seq % UNIT
    unit_groups = None
    copy_groups = None
    if copies > 1:
        unit_groups = [[a * UNIT + b for b in range(UNIT)] for a in range(copies)]
        copy_groups = [[a * UNIT + b for a in range(copies)] for b in range(UNIT)]

    def exchange(x):
        return lax.all_to_all(x, "seq", 0, 0, tiled=True, axis_index_groups=unit_groups)

    def flip(x, k):
        return lax.ppermute(x, "seq", [(s, s ^ k) for s in range(seq_size)])

    flat_tokens = tokens.reshape(count, width)

    def wait_for(x, *others):
        return lax.optimization_barrier((x,) + others)[0]

    if copies == 1:
        inputs = [
            w_gate, w_up, w_down, w_query, w_key, w_value, w_router, norm_attn[None],
            norm_ffn[None],
        ]
    else:
        small = jnp.concatenate(
            [w_router.T, norm_attn[None], norm_ffn[None], jnp.zeros((LANES - 2 - E, part), BF16)], axis=0
        ).T
        head_part = jnp.concatenate(
            [
                w_query.reshape(part, UNIT, 2 * HD),
                w_key.reshape(part, UNIT, HD),
                w_value.reshape(part, UNIT, HD),
                jnp.broadcast_to(small[:, None], (part, UNIT, LANES)),
            ],
            axis=2,
        ).transpose(1, 0, 2)

        down_halves = w_down.reshape(E, -1, 2, hidden).transpose(0, 2, 1, 3).reshape(E, part, hidden)
        packed_part = jnp.concatenate([w_gate, w_up, down_halves], axis=1)
        packed_part = packed_part.reshape(UNIT, E // UNIT, 3 * part, hidden).transpose(1, 0, 2, 3)
        inputs = [packed_part, head_part]
    *packed_mine, heads_all, w_out_rows = begin(rows, part, hidden, inputs, w_out)

    if copies > 1:
        heads_all = lax.all_gather(heads_all, "seq", axis=0, axis_index_groups=copy_groups)
        w_out_rows = lax.all_gather(w_out_rows, "seq", axis=0, axis_index_groups=copy_groups)
    else:
        w_out_rows = w_out_rows[None]
    heads_all = heads_all.reshape(width, 4 * HD + LANES)

    def gather_packed(x):
        x = lax.all_gather(x, "row", axis=0)
        if copies > 1:
            x = lax.all_gather(x, "seq", axis=0, axis_index_groups=copy_groups)
            x = x.transpose(0, 2, 1, 3, 4).reshape(-1, 3 * part, hidden)
            halves = x[:, 2 * part :].reshape(-1, 2, part // 2, hidden).transpose(0, 2, 1, 3)
            return pack(
                x[:, :part].reshape(width, hidden),
                x[:, part : 2 * part].reshape(width, hidden),
                halves.reshape(hidden, width),
            )
        return x

    def pack(gate, up, down):
        gate = gate.reshape(UNIT, PIECES, ROWS_IN, hidden)
        up = up.reshape(UNIT, PIECES, ROWS_IN, hidden)
        down = down.reshape(UNIT, PIECES, ROWS_OUT, 2, hidden).transpose(0, 1, 3, 2, 4)
        down = down.reshape(UNIT, PIECES, ROWS_IN, hidden)
        return jnp.concatenate([gate, up, down], axis=2).transpose(1, 0, 2, 3)

    def repack(x):
        x = x.transpose(1, 0, 2, 3)
        gate = x[:, :, :ROWS_IN].reshape(copies, UNIT, rows, part, hidden)
        up = x[:, :, ROWS_IN : 2 * ROWS_IN].reshape(copies, UNIT, rows, part, hidden)
        down = x[:, :, 2 * ROWS_IN :].reshape(UNIT, PIECES, 2, ROWS_OUT, hidden)
        down = down.transpose(0, 1, 3, 2, 4).reshape(copies, UNIT, rows, part // 2, 2, hidden)
        down = down.transpose(0, 1, 2, 4, 3, 5).reshape(copies, UNIT, rows, part, hidden)
        return jnp.concatenate([gate, up, down], axis=3).transpose(2, 0, 1, 3, 4)

    own_first = gather_packed(packed_mine[0])
    if copies > 1:
        whole_second = gather_packed(jnp.concatenate(packed_mine[1:], axis=1))
        own_second = (whole_second[:, :, : 2 * ROWS_IN], whole_second[:, :, 2 * ROWS_IN :])
    else:
        own_second = tuple(gather_packed(x) for x in packed_mine[1:])

    tok_all, w_out_all = unit_gather(
        [wait_for(flat_tokens, w_out_rows), w_out_rows.reshape(-1, width)], 1
    )
    tok_all = tok_all.reshape(UNIT, micro, local_len, width)
    w_out_all = w_out_all.reshape(UNIT, copies, rows * part, width)
    w_out_all = w_out_all.transpose(1, 0, 2, 3).reshape(H * HD, width)

    chosen = jnp.any(
        routes.reshape(count, TOPK).T[:, None, :] == jnp.arange(E, dtype=jnp.int32)[None, :, None],
        axis=0,
    ).astype(BF16)
    dz_own = cotangent.reshape(count, width)

    frequency = BASE ** (-2.0 * np.arange(HD // 2) / HD)
    angles = np.arange(length)[:, None].astype(np.float32) * frequency[None].astype(np.float32)
    key_cos = jnp.asarray(np.tile(np.cos(angles), (1, 4)).astype(np.float32))
    key_sin = np.concatenate([-np.sin(angles), np.sin(angles)] * 2, axis=1)
    key_sin = jnp.asarray(key_sin.astype(np.float32))
    places = unit * unit_len + jnp.arange(unit_len, dtype=jnp.int32)
    cosine, sine = key_cos, key_sin
    if copies > 1:
        cosine = lax.dynamic_slice_in_dim(key_cos, unit * unit_len, unit_len, 0)
        sine = lax.dynamic_slice_in_dim(key_sin, unit * unit_len, unit_len, 0)

    def by_row4(m):
        return (0, m, 0, 0)

    def by_row3(m):
        return (m, 0, 0)

    def fixed(*_):
        return (0, 0)

    def zeros3(*_):
        return (0, 0, 0)

    def zeros4(*_):
        return (0, 0, 0, 0)

    def small_block(*_):
        return (0, 2)

    seg_keys = segments.astype(F32).reshape(micro, 1, length)
    seg_queries = lax.dynamic_slice_in_dim(seg_keys, unit * unit_len, unit_len, 2)
    skip = copies == 1
    place_row = places[None]
    attention_flops = 4.0 * micro * unit_len * length * 2 * LANES
    attention_specs = [
        pl.BlockSpec((1, unit_len, LANES), by_row3),
        pl.BlockSpec((1, length, LANES), by_row3),
        pl.BlockSpec((1, 1, unit_len), by_row3),
        pl.BlockSpec((1, 1, length), by_row3),
        pl.BlockSpec((1, unit_len), fixed),
    ]
    if copies == 1:
        normed_all, q_all, kv_all, ctx_heads, lse, dz_all, chosen_all = pl.pallas_call(
            attend_kernel,
            grid=(micro,),
            in_specs=[
                pl.BlockSpec((UNIT, 1, local_len, width), by_row4),
                pl.BlockSpec((width, LANES), small_block),
                pl.BlockSpec((width, 4 * HD), fixed),
                pl.BlockSpec((unit_len, LANES), fixed),
                pl.BlockSpec((unit_len, LANES), fixed),
            ]
            + attention_specs[2:]
            + [pl.BlockSpec(memory_space=pl.ANY)] * 2,
            out_specs=[
                pl.BlockSpec((UNIT, 1, local_len, width), by_row4),
                pl.BlockSpec((1, unit_len, LANES), by_row3),
                pl.BlockSpec((1, unit_len, LANES), by_row3),
                pl.BlockSpec((UNIT, 1, local_len, LANES), by_row4),
                pl.BlockSpec((1, 2, unit_len), by_row3),
                pl.BlockSpec(memory_space=pl.ANY),
                pl.BlockSpec(memory_space=pl.ANY),
            ],
            out_shape=[
                jax.ShapeDtypeStruct((UNIT, micro, local_len, width), BF16),
                jax.ShapeDtypeStruct((micro, unit_len, LANES), BF16),
                jax.ShapeDtypeStruct((micro, unit_len, LANES), BF16),
                jax.ShapeDtypeStruct((UNIT, micro, local_len, LANES), BF16),
                jax.ShapeDtypeStruct((micro, 2, unit_len), F32),
                jax.ShapeDtypeStruct((4, count, width), BF16),
                jax.ShapeDtypeStruct((E, 4 * count), BF16),
            ],
            scratch_shapes=[
                pltpu.VMEM((count, width), BF16),
                pltpu.VMEM((E, count), BF16),
                pltpu.SemaphoreType.DMA((9,)),
                pltpu.SemaphoreType.DMA((9,)),
                pltpu.SemaphoreType.DMA((2, 2)),
            ],
            compiler_params=params(collective_id=8, has_side_effects=True),
            cost_estimate=cost(attention_flops, 4e6),
        )(
            tok_all, heads_all, heads_all, cosine, sine, seg_queries, seg_keys, place_row, dz_own,
            chosen,
        )
    else:
        normed_all, q_all, kv_own = pl.pallas_call(
            project_kernel,
            grid=(micro,),
            in_specs=[
                pl.BlockSpec((UNIT, 1, local_len, width), by_row4),
                pl.BlockSpec((width, LANES), small_block),
                pl.BlockSpec((width, 4 * HD), fixed),
                pl.BlockSpec((unit_len, LANES), fixed),
                pl.BlockSpec((unit_len, LANES), fixed),
            ],
            out_specs=[
                pl.BlockSpec((UNIT, 1, local_len, width), by_row4),
                pl.BlockSpec((1, unit_len, LANES), by_row3),
                pl.BlockSpec((1, unit_len, LANES), by_row3),
            ],
            out_shape=[
                jax.ShapeDtypeStruct((UNIT, micro, local_len, width), BF16),
                jax.ShapeDtypeStruct((micro, unit_len, LANES), BF16),
                jax.ShapeDtypeStruct((micro, unit_len, LANES), BF16),
            ],
            compiler_params=params(),
            cost_estimate=cost(2.0 * UNIT * count * width * 4 * HD, 1.5e7),
        )(tok_all, heads_all, heads_all, cosine, sine)
        kv_all = lax.all_gather(kv_own, "seq", axis=1, tiled=True, axis_index_groups=copy_groups)
        ctx_heads, lse = pl.pallas_call(
            functools.partial(attention_kernel, skip),
            grid=(micro,),
            in_specs=attention_specs,
            out_specs=[
                pl.BlockSpec((UNIT, 1, local_len, LANES), by_row4),
                pl.BlockSpec((1, 2, unit_len), by_row3),
            ],
            out_shape=[
                jax.ShapeDtypeStruct((UNIT, micro, local_len, LANES), BF16),
                jax.ShapeDtypeStruct((micro, 2, unit_len), F32),
            ],
            compiler_params=params(),
            cost_estimate=cost(attention_flops, 4e6),
        )(q_all, kv_all, seg_queries, seg_keys, place_row)
        dz_all = jnp.stack([dz_own] + [flip(dz_own, k) for k in (2, 4, 6)])
        chosen_all = jnp.concatenate([chosen] + [flip(chosen, k) for k in (2, 4, 6)], axis=1)

    x_all, sib_first, mixed, normed_ffn, context = bridge(
        ctx_heads, own_first, w_out_all, flat_tokens, heads_all, 2
    )
    x_all = x_all.reshape(4 * count, width)
    dz_all = dz_all.reshape(4 * count, width)
    out_part, dx_part, gg_part, gates_all, total_first, w_heads = run_experts(
        "both", x_all, dz_all, chosen_all, (sib_first, own_first),
        router=heads_all,
    )

    def finish_expert(total):
        if copies > 1:
            total = repack(total)
            total = lax.psum_scatter(total, "row", scatter_dimension=0)
            total = lax.psum_scatter(
                total, "seq", scatter_dimension=0, axis_index_groups=copy_groups
            )
        else:
            total = lax.psum_scatter(total, "row", scatter_dimension=0)
        return total

    reduced_first = finish_expert(total_first)
    out_part, gate_acts, up_acts, *sib_second = run_experts(
        "forward", x_all, None, None, own_second, gates=gates_all, carried=out_part
    )
    out_split = out_part.reshape(4, count, width)
    dx_part, gg_part, total_second, out_back = run_experts(
        "backward", x_all, dz_all, None, (*sib_second, *own_second), gates=gates_all,
        carried=(dx_part, gg_part), acts=(gate_acts, up_acts), pushed=out_split,
    )
    reduced_second = finish_expert(total_second)
    do_heads, gmixed, out_pre, block_out = return_tokens(
        dx_part.reshape(4, count, width), gg_part, mixed, normed_ffn, dz_own, chosen, heads_all,
        w_out_all, context, out_split, out_back, micro, copies, 3,
    )
    if copies > 1:
        out_pre = lax.psum_scatter(
            out_pre, "seq", scatter_dimension=1, axis_index_groups=copy_groups
        )
    out_pre = out_pre.reshape(4, rows, part, width + LANES)
    graw, head_term, out_in, exchanged = pl.pallas_call(
        functools.partial(attention_back_kernel, skip),
        grid=(micro,),
        in_specs=attention_specs
        + [
            pl.BlockSpec((1, 2, unit_len), by_row3),
            pl.BlockSpec((UNIT, 1, local_len, LANES), by_row4),
            pl.BlockSpec((unit_len, LANES), fixed),
            pl.BlockSpec((unit_len, LANES), fixed),
            pl.BlockSpec((length, LANES), fixed),
            pl.BlockSpec((length, LANES), fixed),
            pl.BlockSpec((UNIT, 1, local_len, width), by_row4),
            pl.BlockSpec(memory_space=pl.ANY),
            pl.BlockSpec(memory_space=pl.ANY),
        ],
        out_specs=[
            pl.BlockSpec((seq_size, 1, local_len, 2 * LANES), by_row4),
            pl.BlockSpec((PIECES, UNIT, ROWS_IN, 2 * LANES), zeros4),
            pl.BlockSpec(memory_space=pl.ANY),
            pl.BlockSpec(memory_space=pl.ANY),
        ],
        out_shape=[
            jax.ShapeDtypeStruct((seq_size, micro, local_len, 2 * LANES), BF16),
            jax.ShapeDtypeStruct((PIECES, UNIT, ROWS_IN, 2 * LANES), BF16),
            jax.ShapeDtypeStruct((3,) + out_pre.shape[1:], BF16),
            jax.ShapeDtypeStruct(reduced_first.shape, BF16),
        ],
        scratch_shapes=[
            pltpu.VMEM((length, LANES), F32),
            pltpu.VMEM((length, LANES), F32),
            pltpu.VMEM((width, 2 * LANES), F32),
            pltpu.VMEM(reduced_first.shape[1:], BF16),
            pltpu.SemaphoreType.DMA((UNIT + 2,)),
            pltpu.SemaphoreType.DMA((UNIT + 2,)),
            pltpu.SemaphoreType.DMA((2,)),
        ],
        compiler_params=params(collective_id=7, has_side_effects=True),
        cost_estimate=cost(2.5 * attention_flops, 8e6),
    )(
        q_all, kv_all, seg_queries, seg_keys, place_row, lse, do_heads,
        cosine, sine, key_cos, key_sin, normed_all, out_pre, reduced_first,
    )
    if copies > 1:
        graw_kv = lax.psum_scatter(
            graw[..., LANES:], "seq", scatter_dimension=0, tiled=True,
            axis_index_groups=copy_groups,
        )
        graw = jnp.concatenate([graw[:UNIT, ..., :LANES], graw_kv], axis=3)
        head_term = jnp.einsum(
            "nd,nh->dh",
            normed_all.reshape(UNIT * count, width),
            graw.reshape(UNIT * count, 2 * LANES),
            preferred_element_type=F32,
        ).astype(BF16)
        head_term = head_term.reshape(copies, UNIT, rows, part, 2 * LANES)
        head_term = lax.psum_scatter(
            head_term, "seq", scatter_dimension=0, axis_index_groups=copy_groups
        ).transpose(1, 0, 2, 3)
    head_grad, exchanged_second, out_grad, grad_input = finish(
        rows, graw, head_term, reduced_second, out_pre, out_in, w_heads, flat_tokens, heads_all,
        gmixed, 4,
    )
    if copies == 1:
        like = jax.ShapeDtypeStruct
        (
            grad_norm_attn, grad_query, grad_key, grad_value, grad_out, grad_norm_ffn, grad_router,
            grad_gate, grad_up, grad_down,
        ) = pl.pallas_call(
            unpack_grads_kernel,
            out_shape=[
                like((1, part), F32), like(w_query.shape, F32), like(w_key.shape, F32),
                like(w_value.shape, F32), like(w_out.shape, F32), like((1, part), F32),
                like(w_router.shape, F32), like(w_gate.shape, F32), like(w_up.shape, F32),
                like(w_down.shape, F32),
            ],
            compiler_params=params(),
            cost_estimate=cost(1, 1e7),
        )(
            exchanged, exchanged_second, head_grad, out_grad, w_gate, w_up, w_query, w_key, w_value,
            w_router, norm_attn[None], norm_ffn[None],
        )
        grad_norm_attn = grad_norm_attn.reshape(part)
        grad_norm_ffn = grad_norm_ffn.reshape(part)
    else:
        finished = [exchanged, exchanged_second]
        finished = jnp.stack(finished, axis=1).reshape(E, 3 * part, hidden).astype(F32)
        grad_gate = finished[:, :part]
        grad_up = finished[:, part : 2 * part]
        grad_down = finished[:, 2 * part :].reshape(E, 2, -1, hidden).transpose(0, 2, 1, 3)
        grad_down = grad_down.reshape(E, -1, width)
        head_grad = head_grad.astype(F32)
        grad_query = head_grad[:, :, :LANES].transpose(1, 0, 2).reshape(part, H * HD)
        grad_key = head_grad[:, :, LANES : LANES + HD].transpose(1, 0, 2).reshape(part, KVH * HD)
        grad_value = head_grad[:, :, LANES + HD :].transpose(1, 0, 2).reshape(part, KVH * HD)
        grad_out = out_grad[:, :width]
        grad_router = out_grad[:, width : width + E]

        attn_weights = jnp.concatenate([w_query, w_key, w_value], axis=1).astype(F32)
        attn_grads = jnp.concatenate([grad_query, grad_key, grad_value], axis=1)
        grad_norm_attn = jnp.sum(attn_weights * attn_grads, axis=1) / norm_attn.astype(F32)
        grad_norm_ffn = (
            jnp.sum(w_gate.astype(F32) * grad_gate, axis=(0, 2))
            + jnp.sum(w_up.astype(F32) * grad_up, axis=(0, 2))
            + jnp.sum(w_router.astype(F32) * grad_router, axis=1)
        ) / norm_ffn.astype(F32)
    return (
        block_out.reshape(tokens.shape),
        grad_input.reshape(tokens.shape),
        grad_norm_attn,
        grad_query,
        grad_key,
        grad_value,
        grad_out,
        grad_norm_ffn,
        grad_router,
        grad_gate,
        grad_up,
        grad_down,
    )


def solution(mesh):
    both = ("seq", "row")
    body = functools.partial(shards, mesh.shape["seq"] // UNIT, rows=mesh.shape["row"])
    return jax.shard_map(
        body,
        mesh=mesh,
        in_specs=(
            P("row", "seq", None),
            P("row", None),
            P("row", "seq", None),
            P("row", "seq", None),
            P(both),
            P(both, None),
            P(both, None),
            P(both, None),
            P(both, None),
            P(both),
            P(both, None),
            P(None, both, None),
            P(None, both, None),
            P(None, both, None),
        ),
        out_specs=(
            P("row", "seq", None),
            P("row", "seq", None),
            P(both),
            P(both, None),
            P(both, None),
            P(both, None),
            P(both, None),
            P(both),
            P(both, None),
            P(None, both, None),
            P(None, both, None),
            P(None, both, None),
        ),
        check_vma=False,
    )
```

```python
import functools

import jax
import jax.numpy as jnp
import numpy as np
from jax import lax
from jax.experimental import pallas as pl
from jax.experimental.pallas import tpu as pltpu
from jax.sharding import PartitionSpec as P

H = 16
KVH = 8
TOPK = 8
HD = 64
E = 16
UNIT = 8
LANES = 128
QBLOCK = 256
PIECES = 4
ROWS_IN = 32
ROWS_OUT = 16

EPS = 1e-05
BASE = 10000.0
NEGATIVE = -1e30
F32 = jnp.float32
BF16 = jnp.bfloat16
VMEM_LIMIT = 60 * 1024 * 1024


def dot_nn(left, right):
    return lax.dot_general(left, right, (((1,), (0,)), ((), ())), preferred_element_type=F32)


def dot_nt(left, right):
    return lax.dot_general(left, right, (((1,), (1,)), ((), ())), preferred_element_type=F32)


def dot_tn(left, right):
    return lax.dot_general(left, right, (((0,), (0,)), ((), ())), preferred_element_type=F32)


def params(**kw):
    return pltpu.CompilerParams(vmem_limit_bytes=VMEM_LIMIT, **kw)


def cost(flops, nbytes):
    return pl.CostEstimate(flops=int(flops), bytes_accessed=int(nbytes), transcendentals=0)


def neighbours(seq):
    core = seq % 2
    chip = (seq // 2) % 4
    base = seq - seq % UNIT

    def at(other, same=True):
        return base + 2 * other + (core if same else 1 - core)

    across = chip + 1 - 2 * (chip % 2)
    along = (chip + 2) % 4
    return at(across), at(along), at(3 - chip), at(chip, False)


def greet(targets):
    barrier = pltpu.get_barrier_semaphore()
    for target in targets:
        pl.semaphore_signal(
            barrier, inc=1, device_id=target, device_id_type=pl.DeviceIdType.MESH
        )
    pl.semaphore_wait(barrier, len(targets))


class Pushes:
    def __init__(self, send, recv):
        self.send, self.recv, self.used = send, recv, 0

    def start(self, source, target, device):
        copy = self.make(source, target, device)
        copy.start()
        return copy

    def make(self, source, target, device):
        n = self.used
        self.used += 1
        return pltpu.make_async_remote_copy(
            src_ref=source,
            dst_ref=target,
            send_sem=self.send.at[n],
            recv_sem=self.recv.at[n],
            device_id=device,
            device_id_type=pl.DeviceIdType.MESH,
        )


class Late:
    def __init__(self, places):
        self.places = places

    def specs(self, count):
        return [pl.BlockSpec(memory_space=pl.ANY)] * count

    def scratch(self):
        buffers = [pltpu.VMEM(shape, kind) for _, shape, kind, _ in self.places]
        return buffers + [pltpu.SemaphoreType.DMA((len(self.places),))]

    def wrap(self, kernel, count):
        def wrapped(*refs):
            extra = len(self.places) + 1
            ins, rest = list(refs[:count]), refs[count:-extra]
            *buffers, sems = refs[-extra:]
            copies = []
            for n, (place, _, _, view) in enumerate(self.places):
                source = ins[place] if view is None else view(ins[place])
                copies.append(pltpu.make_async_copy(source, buffers[n], sems.at[n]))
                copies[n].start()
                ins[place] = buffers[n]

            def ready():
                for copy in copies:
                    copy.wait()

            kernel(ready, *ins, *rest)

        return wrapped


def small_view(ref):
    return ref.at[:, pl.ds(2 * LANES, LANES)]


class Bounce:
    def __init__(self, source, middle, target, sems, start=True):
        self.inward = pltpu.make_async_copy(source, middle, sems.at[0])
        self.outward = pltpu.make_async_copy(middle, target, sems.at[1])
        if start:
            self.inward.start()

    def turn(self):
        self.inward.wait()
        self.outward.start()

    def wait(self):
        self.outward.wait()


def pack_kernel_inputs(
    gate_ref, up_ref, down_ref, query_ref, key_ref, value_ref, router_ref, attn_ref, ffn_ref,
    packed, head_ref, gains,
):
    part, hidden = gate_ref.shape[1:]
    half = part // 2
    for n in range(2):
        for b in range(UNIT):
            e = 2 * b + n
            packed[n, b, :part] = gate_ref[e]
            packed[n, b, part : 2 * part] = up_ref[e]
            for c in range(2):
                start = 2 * part + c * half
                packed[n, b, start : start + half] = down_ref[e, :, c * hidden : (c + 1) * hidden]
    gains[...] = jnp.zeros_like(gains)
    gains[E : E + 1, :part] = attn_ref[...].astype(F32)
    gains[E + 1 : E + 2, :part] = ffn_ref[...].astype(F32)
    router = router_ref[...].astype(F32)
    small = jnp.concatenate([router, jnp.zeros((part, LANES - E), F32)], axis=1)
    small = (small + gains[...].T[:part]).astype(BF16)
    low = lane_iota((part, LANES)) < HD
    for pair in range(UNIT // 2):
        lanes = slice(pair * LANES, (pair + 1) * LANES)
        key = key_ref[:, lanes].astype(F32)
        value = value_ref[:, lanes].astype(F32)
        even = jnp.where(low, key, pltpu.roll(value, HD, 1)).astype(BF16)
        odd = jnp.where(low, pltpu.roll(key, HD, 1), value).astype(BF16)
        for b, mixed in ((2 * pair, even), (2 * pair + 1, odd)):
            head_ref[b, :, :LANES] = query_ref[:, b * LANES : (b + 1) * LANES]
            head_ref[b, :, LANES : 2 * LANES] = mixed
            head_ref[b, :, 2 * LANES :] = small


def begin_kernel(rows, raw, *refs):
    inputs, refs = refs[:raw], refs[raw:]
    wout_ref, mine0, mine1, mine2, head_all, wout_all, wout_mid, *refs = refs
    if raw > 2:
        head_mine, packed, head_ref, gains, send, recv, local = refs
    else:
        (packed, head_ref), (head_mine, send, recv, local) = inputs, refs
    seq, row = lax.axis_index("seq"), lax.axis_index("row")
    me = seq % UNIT
    base = seq - me
    unit = [(me + k) % UNIT for k in range(1, UNIT)]
    column = [(row + k) % rows for k in range(1, rows)]
    greet([{"seq": base + b} for b in unit] + [{"row": r} for r in column])
    if raw > 2:
        pack_kernel_inputs(*inputs, packed, head_ref, gains)
    pushes = Pushes(send, recv)
    inner = mine1.shape[1]
    upper, lower = pl.ds(0, inner), pl.ds(inner, mine2.shape[1])
    first = pltpu.make_async_copy(head_ref.at[me], head_mine.at[me], local.at[0])
    own = [
        pltpu.make_async_copy(packed.at[0, me], mine0.at[me], local.at[1]),
        pltpu.make_async_copy(packed.at[1, me, upper], mine1.at[me], local.at[2]),
        pltpu.make_async_copy(packed.at[1, me, lower], mine2.at[me], local.at[3]),
    ]
    first.start()
    heads = [pushes.start(head_ref.at[b], head_mine.at[me], {"seq": base + b}) for b in unit]
    outs = [pushes.start(wout_ref, wout_mid.at[row], {"row": r}) for r in column]
    kept = pltpu.make_async_copy(wout_ref, wout_mid.at[row], local.at[4])
    kept.start()
    others = []
    for source, target in (
        (lambda b: packed.at[0, b], mine0),
        (lambda b: packed.at[1, b, upper], mine1),
        (lambda b: packed.at[1, b, lower], mine2),
    ):
        others += [pushes.start(source(b), target.at[me], {"seq": base + b}) for b in unit]
    for copy in own:
        copy.start()
    first.wait()
    for copy in heads:
        copy.wait_recv()
    last = pltpu.make_async_copy(head_mine, head_all.at[:, row], local.at[5])
    last.start()
    others += [pushes.start(head_mine, head_all.at[:, row], {"row": r}) for r in column]
    kept.wait()
    for copy in outs:
        copy.wait_recv()
    own.append(pltpu.make_async_copy(wout_mid, wout_all.at[me], local.at[6]))
    own[-1].start()
    across, along, _, twin = neighbours(seq)
    a, b, d = across - base, along - base, 6 - me + 2 * (me % 2)
    half = rows // 2
    top, low = pl.ds(0, half), pl.ds(half, rows - half)

    def own_part(part, device):
        return pushes.start(wout_mid.at[part], wout_all.at[me, part], {"seq": device})

    def passed(slot, part, device):
        view = wout_all.at[slot, part]
        others.append(pushes.start(view, view, {"seq": device}))
        return others[-1]

    xa, yb, xb, ya = (
        own_part(top, across), own_part(low, along), own_part(low, across), own_part(top, along)
    )
    others += [own_part(top, twin), own_part(low, twin)]
    xa.wait_recv()
    da = passed(a, top, along)
    passed(a, top, twin)
    yb.wait_recv()
    db = passed(b, low, across)
    passed(b, low, twin)
    xb.wait_recv()
    passed(a, low, twin)
    ya.wait_recv()
    passed(b, top, twin)
    da.wait_recv()
    passed(d, top, twin)
    db.wait_recv()
    passed(d, low, twin)
    others = [copy for copy in others if copy is not da and copy is not db]
    for copy in heads + outs + [xa, yb, xb, ya, da, db]:
        copy.wait_send()
    for copy in own + [last]:
        copy.wait()
    for copy in others:
        copy.wait()


def begin(rows, part, hidden, inputs, w_out):
    any_spec = pl.BlockSpec(memory_space=pl.ANY)
    vmem_spec = pl.BlockSpec(memory_space=pltpu.VMEM)
    count = 4 * (UNIT - 1) + 2 * (rows - 1) + 14
    like = jax.ShapeDtypeStruct
    deep, inner = 3 * part, 2 * part
    head_shape = (UNIT, part, 4 * HD + LANES)
    built = [
        pltpu.VMEM((2, UNIT, deep, hidden), BF16),
        pltpu.VMEM(head_shape, BF16),
        pltpu.VMEM((LANES, LANES), F32),
    ]
    return pl.pallas_call(
        functools.partial(begin_kernel, rows, len(inputs)),
        in_specs=[vmem_spec] * (len(inputs) + 1),
        out_specs=[any_spec] * 5,
        out_shape=[
            like((UNIT, deep, hidden), BF16),
            like((UNIT, inner, hidden), BF16),
            like((UNIT, deep - inner, hidden), BF16),
            like((UNIT, rows) + head_shape[1:], BF16),
            like((UNIT, rows) + w_out.shape, BF16),
        ],
        scratch_shapes=[pltpu.VMEM((rows,) + w_out.shape, BF16), pltpu.VMEM(head_shape, BF16)]
        + (built if len(inputs) > 2 else [])
        + [
            pltpu.SemaphoreType.DMA((count,)),
            pltpu.SemaphoreType.DMA((count,)),
            pltpu.SemaphoreType.DMA((7,)),
        ],
        compiler_params=params(collective_id=0, has_side_effects=True),
        cost_estimate=cost(1, 2e7),
    )(*inputs, w_out)


def unit_gather_kernel(sources, *refs):
    ins, outs = refs[:sources], refs[sources : 2 * sources]
    middles = refs[2 * sources : 3 * sources]
    send, recv, local = refs[3 * sources :]
    seq = lax.axis_index("seq")
    me = seq % UNIT
    base = seq - me
    across, along, _, twin = neighbours(seq)
    a, b, t = across - base, along - base, twin - base
    d = UNIT - 1 - me + 2 * (me % 2) - 1
    greet([{"seq": across}, {"seq": along}, {"seq": twin}])
    pushes = Pushes(send, recv)
    own, done, stage = [], [], []
    for n, (source, target) in enumerate(zip(ins, outs)):
        half = source.shape[0] // 2
        halves = [pl.ds(0, half), pl.ds(half, half)]
        own.append(Bounce(source, middles[n], target.at[me], local.at[n]))

        def part(device, h, source=source, target=target, halves=halves):
            return pushes.start(
                source.at[halves[h]], target.at[me, halves[h]], {"seq": device}
            )

        xa, yb = part(across, 0), part(along, 1)
        xb, ya = part(across, 1), part(along, 0)
        done.append(pushes.start(source, target.at[me], {"seq": twin}))
        stage.append((target, halves, xa, yb, xb, ya))
    for copy in own:
        copy.turn()
    for target, halves, xa, yb, xb, ya in stage:

        def pass_on(slot, h, device, target=target, halves=halves):
            view = target.at[slot, halves[h]]
            return pushes.start(view, view, {"seq": device})

        xa.wait_recv()
        da = pass_on(a, 0, along)
        done.append(pass_on(a, 0, twin))
        yb.wait_recv()
        db = pass_on(b, 1, across)
        done.append(pass_on(b, 1, twin))
        xb.wait_recv()
        done.append(pass_on(a, 1, twin))
        ya.wait_recv()
        done.append(pass_on(b, 0, twin))
        da.wait_recv()
        done.append(pass_on(d, 0, twin))
        db.wait_recv()
        done.append(pass_on(d, 1, twin))
        for copy in (xa, yb, xb, ya, da, db):
            copy.wait_send()
    for copy in own + done:
        copy.wait()


def unit_gather(sources, collective):
    any_spec = pl.BlockSpec(memory_space=pl.ANY)
    n = len(sources)
    return pl.pallas_call(
        functools.partial(unit_gather_kernel, n),
        in_specs=[any_spec] * n,
        out_specs=[any_spec] * n,
        out_shape=[jax.ShapeDtypeStruct((UNIT,) + x.shape, x.dtype) for x in sources],
        scratch_shapes=[pltpu.VMEM(x.shape, x.dtype) for x in sources]
        + [
            pltpu.SemaphoreType.DMA((13 * n,)),
            pltpu.SemaphoreType.DMA((13 * n,)),
            pltpu.SemaphoreType.DMA((n, 2)),
        ],
        compiler_params=params(collective_id=collective, has_side_effects=True),
        cost_estimate=cost(1, 8e7),
    )(*sources)


def bridge_kernel(
    micro, ready, ctx_ref, weights, w_ref, tok_ref, small_ref,
    target, flipped, mixed_ref, normed_ref, ctx_out,
    ctx_in, send, recv, local,
):
    seq = lax.axis_index("seq")
    me = seq % UNIT
    base = seq - me
    unit = [(me + k) % UNIT for k in range(1, UNIT)]
    across, along, _, twin = neighbours(seq)
    greet([{"seq": base + b} for b in unit])
    pushes = Pushes(send, recv)
    arrivals = [
        [pushes.start(ctx_ref.at[b, m], ctx_in.at[me, m], {"seq": base + b}) for b in unit]
        for m in range(micro)
    ]
    mine = pltpu.make_async_copy(ctx_ref.at[me], ctx_in.at[me], local.at[0])
    mine.start()
    turned = pushes.start(weights, flipped, {"seq": twin})
    count, width = tok_ref.shape
    step = count // micro
    half = step // 2
    ready()
    gain = gain_row(small_ref[...], E + 1)
    mine.wait()
    sent = []

    def forward(m):
        top, low = pl.ds(m * step, half), pl.ds(m * step + half, half)
        xa, yb, xb, ya = sent[m]
        xa.wait_recv()
        da = pushes.start(target.at[1, top], target.at[3, top], {"seq": along})
        yb.wait_recv()
        db = pushes.start(target.at[2, low], target.at[3, low], {"seq": across})
        sent[m] = (xa, yb, xb, ya, da, db)

    for m in range(micro):
        here = slice(m * step, (m + 1) * step)
        for copy in arrivals[m]:
            copy.wait_recv()
        for b in range(UNIT):
            ctx_out[here, b * LANES : (b + 1) * LANES] = ctx_in[b, m]
        mixed = tok_ref[here].astype(F32) + dot_nn(ctx_out[here], w_ref[...])
        mixed_ref[here] = mixed
        inverse = lax.rsqrt(jnp.mean(mixed * mixed, axis=-1, keepdims=True) + EPS)
        normed_ref[here] = (mixed * inverse * gain).astype(BF16)
        top, low = pl.ds(m * step, half), pl.ds(m * step + half, half)
        sent.append(
            (
                pushes.start(normed_ref.at[top], target.at[1, top], {"seq": across}),
                pushes.start(normed_ref.at[low], target.at[2, low], {"seq": along}),
                pushes.start(normed_ref.at[low], target.at[1, low], {"seq": across}),
                pushes.start(normed_ref.at[top], target.at[2, top], {"seq": along}),
            )
        )
        if m > 0:
            forward(m - 1)
    last = pltpu.make_async_copy(normed_ref, target.at[0], local.at[1])
    last.start()
    forward(micro - 1)
    for group in sent:
        for copy in group[2:]:
            copy.wait_recv()
        for copy in group:
            copy.wait_send()
    for group in arrivals:
        for copy in group:
            copy.wait_send()
    turned.wait()
    last.wait()


def bridge(ctx_heads, weights, w_out, tokens, heads, collective):
    any_spec = pl.BlockSpec(memory_space=pl.ANY)
    like = jax.ShapeDtypeStruct
    count, width = tokens.shape
    micro = ctx_heads.shape[1]
    pushes = (UNIT - 1) * micro + 6 * micro + 1

    def fixed(i):
        return (0, 0)

    late = Late(
        [
            (2, w_out.shape, BF16, None),
            (3, tokens.shape, BF16, None),
            (4, (width, LANES), BF16, small_view),
        ]
    )

    return pl.pallas_call(
        late.wrap(functools.partial(bridge_kernel, micro), 5),
        grid=(1,),
        in_specs=late.specs(5),
        out_specs=[any_spec] * 2 + [pl.BlockSpec((count, width), fixed)] * 3,
        out_shape=[
            like((4, count, width), BF16),
            like(weights.shape, BF16),
            like((count, width), F32),
            like((count, width), BF16),
            like((count, H * HD), BF16),
        ],
        scratch_shapes=[
            pltpu.VMEM(ctx_heads.shape, BF16),
            pltpu.SemaphoreType.DMA((pushes,)),
            pltpu.SemaphoreType.DMA((pushes,)),
            pltpu.SemaphoreType.DMA((2,)),
        ]
        + late.scratch(),
        compiler_params=params(collective_id=collective, has_side_effects=True),
        cost_estimate=cost(2.0 * count * width * width, 8e7),
    )(ctx_heads, weights, w_out, tokens, heads)


def finish_kernel(
    rows, ready, graw_ref, head_ref, red_ref, pre_ref, out_ref, w_ref, own_ref, tok_ref, small_ref, gmixed_ref,
    head_fin, red_out, out_fin, gin_ref,
    head_col, head_sum, out_sum, out_col, raw_in, red_own, send, recv, local,
):
    seq, row = lax.axis_index("seq"), lax.axis_index("row")
    me = seq % UNIT
    base = seq - me
    unit = [(me + k) % UNIT for k in range(1, UNIT)]
    senders = [(me + UNIT - k) % UNIT for k in range(1, UNIT)]
    column = [(row + k) % rows for k in range(1, rows)]
    greet([{"seq": base + b} for b in unit] + [{"row": r} for r in column])
    pushes = Pushes(send, recv)
    first = pltpu.make_async_copy(head_ref.at[row], head_col.at[row], local.at[0, 0])
    first.start()
    second = pltpu.make_async_copy(graw_ref.at[me], raw_in.at[me], local.at[1, 0])
    second.start()
    heads = [pushes.start(head_ref.at[r], head_col.at[row], {"row": r}) for r in column]
    raws = [pushes.start(graw_ref.at[b], raw_in.at[me], {"seq": base + b}) for b in unit]
    others = [pushes.start(red_ref.at[b], red_out.at[me], {"seq": base + b}) for b in unit]
    bounce = Bounce(red_ref.at[me], red_own, red_out.at[me], local.at[4])
    ready()
    total = pre_ref[me // 2].astype(F32)
    for n in range(3):
        total = total + out_ref[n].astype(F32)
    out_sum[...] = total.astype(BF16)
    bounce.turn()
    third = pltpu.make_async_copy(out_sum.at[row], out_col.at[row], local.at[2, 0])
    third.start()
    outs = [pushes.start(out_sum.at[r], out_col.at[row], {"row": r}) for r in column]
    first.wait()
    for copy in heads:
        copy.wait_recv()
    total = head_col[0].astype(F32)
    for r in range(1, rows):
        total = total + head_col[r].astype(F32)
    head_sum[...] = total.astype(BF16)
    fourth = pltpu.make_async_copy(head_sum.at[me], head_fin.at[me], local.at[3, 0])
    fourth.start()
    others += [pushes.start(head_sum.at[b], head_fin.at[me], {"seq": base + b}) for b in unit]
    count, width = tok_ref.shape
    second.wait()
    acc = dot_nt(raw_in[me].reshape(count, 2 * LANES), own_ref[...])
    for b, copy in zip(senders, raws):
        copy.wait_recv()
        acc = acc + dot_nt(raw_in[b].reshape(count, 2 * LANES), w_ref[b])
    v = tok_ref[...].astype(F32)
    inverse = lax.rsqrt(jnp.mean(v * v, axis=-1, keepdims=True) + EPS)
    scaled = acc * gain_row(small_ref[...], E)
    mean = jnp.mean(scaled * v, axis=-1, keepdims=True)
    grad = gmixed_ref[...] + scaled * inverse - v * (inverse * inverse * inverse * mean)
    gin_ref[...] = grad.astype(BF16)
    third.wait()
    for copy in outs:
        copy.wait_recv()
    total = out_col[0].astype(F32)
    for r in range(1, rows):
        total = total + out_col[r].astype(F32)
    out_fin[...] = total
    for copy in heads + outs + raws:
        copy.wait_send()
    fourth.wait()
    bounce.wait()
    for copy in others:
        copy.wait()


def finish(
    rows, graw, head_term, reduced, pre, out_in, w_heads, tokens, heads, gmixed, collective
):
    any_spec = pl.BlockSpec(memory_space=pl.ANY)
    like = jax.ShapeDtypeStruct
    pushes = 3 * (UNIT - 1) + 2 * (rows - 1)
    count, width = tokens.shape

    def fixed(i):
        return (0, 0)

    late = Late(
        [
            (3, pre.shape, BF16, None),
            (4, out_in.shape, BF16, None),
            (5, w_heads.shape, BF16, None),
            (6, (width, 4 * HD), BF16, lambda ref: ref.at[:, pl.ds(0, 4 * HD)]),
            (7, tokens.shape, BF16, None),
            (8, (width, LANES), BF16, small_view),
            (9, gmixed.shape, F32, None),
        ]
    )

    return pl.pallas_call(
        late.wrap(functools.partial(finish_kernel, rows), 10),
        grid=(1,),
        in_specs=late.specs(10),
        out_specs=[
            any_spec,
            any_spec,
            pl.BlockSpec(pre.shape[2:], fixed),
            pl.BlockSpec(tokens.shape, fixed),
        ],
        out_shape=[
            like(head_term.shape[1:], BF16),
            like(reduced.shape, BF16),
            like(pre.shape[2:], F32),
            like(tokens.shape, BF16),
        ],
        scratch_shapes=[
            pltpu.VMEM(head_term.shape, BF16),
            pltpu.VMEM(head_term.shape[1:], BF16),
            pltpu.VMEM(pre.shape[1:], BF16),
            pltpu.VMEM(pre.shape[1:], BF16),
            pltpu.VMEM(graw.shape, BF16),
            pltpu.VMEM(reduced.shape[1:], BF16),
            pltpu.SemaphoreType.DMA((pushes,)),
            pltpu.SemaphoreType.DMA((pushes,)),
            pltpu.SemaphoreType.DMA((5, 2)),
        ]
        + late.scratch(),
        compiler_params=params(collective_id=collective, has_side_effects=True),
        cost_estimate=cost(4.0 * count * width * width, 6e7),
    )(graw, head_term, reduced, pre, out_in, w_heads, heads, tokens, heads, gmixed)


def lane_iota(shape):
    return lax.broadcasted_iota(jnp.int32, shape, len(shape) - 1)


def turn(u, cosine, sine):
    low_half = lane_iota(u.shape) % HD < HD // 2
    partner = jnp.where(
        low_half, pltpu.roll(u, LANES - HD // 2, u.ndim - 1), pltpu.roll(u, HD // 2, u.ndim - 1)
    )
    return u * cosine + partner * sine


def value_tables(cosine, sine):
    low = lane_iota(cosine.shape) < HD
    return jnp.where(low, cosine, 1.0), jnp.where(low, sine, 0.0)


def gain_row(small, lane):
    return small.astype(F32).T[lane : lane + 1]


def project_kernel(tok_ref, small_ref, w_ref, cos_ref, sin_ref, normed_ref, q_ref, kv_ref):
    count = q_ref.shape[1]
    width = w_ref.shape[0]
    x = tok_ref[...].reshape(count, width).astype(F32)
    inverse = lax.rsqrt(jnp.mean(x * x, axis=-1, keepdims=True) + EPS)
    normed = (x * inverse * gain_row(small_ref[...], E)).astype(BF16)
    normed_ref[...] = normed.reshape(normed_ref.shape)
    raw = dot_nn(normed, w_ref[...])
    cosine, sine = cos_ref[...], sin_ref[...]
    q = turn(raw[:, :LANES], cosine, sine).astype(BF16)
    q_ref[0] = (q.astype(F32) * HD**-0.5).astype(BF16)
    kv_ref[0] = turn(raw[:, LANES:], *value_tables(cosine, sine)).astype(BF16)


def pair_keys(kv):
    kv = kv.astype(F32)
    rolled = pltpu.roll(kv, HD, 1)
    low = lane_iota(kv.shape) < HD
    return jnp.where(low, kv, rolled), jnp.where(low, rolled, kv)


def bias_block(seg_col, seg_row, q_places, first, length):
    key_places = lax.broadcasted_iota(jnp.int32, (length, q_places.shape[1]), 0)
    allowed = (seg_col[:length] == seg_row) & (key_places <= q_places)
    return jnp.where(allowed, 0.0, NEGATIVE)


def attention_kernel(skip, q_ref, kv_ref, segq_ref, segk_ref, place_ref, ctx_ref, lse_ref):
    length = kv_ref.shape[1]
    queries = q_ref.shape[1]
    kk, vv = pair_keys(kv_ref[0])
    v_t = vv.T.astype(BF16)[:HD]
    kk = kk.astype(BF16)
    seg_col = jnp.broadcast_to(segk_ref[0], (8, length)).T[:, :1]
    for block in range(queries // QBLOCK):
        here = slice(block * QBLOCK, (block + 1) * QBLOCK)
        keys = (block + 1) * QBLOCK if skip else length
        bias = bias_block(seg_col, segq_ref[0][:, here], place_ref[:, here], 0, keys)
        q = q_ref[0, here, :]
        low = lane_iota(q.shape) < HD
        parts = []
        for head in range(2):
            mine = jnp.where(low == (head == 0), q, jnp.zeros_like(q))
            scores = dot_nt(kk[:keys], mine) + bias
            top = jnp.max(scores, axis=0, keepdims=True)
            weight = jnp.exp(scores - top)
            total = jnp.sum(weight, axis=0, keepdims=True)
            prob = (weight * (1.0 / total)).astype(BF16)
            parts.append(dot_nn(v_t[:, :keys], prob))
            lse_ref[0, head : head + 1, here] = top + jnp.log(total)
        ctx = jnp.concatenate(parts, axis=0).T.astype(BF16)
        per = QBLOCK // LANES
        ctx_ref[block * per : (block + 1) * per, 0] = ctx.reshape(per, LANES, LANES)


def attend_kernel(
    tok_ref, small_ref, w_ref, cos_ref, sin_ref, segq_ref, segk_ref, place_ref, z_ref, c_ref,
    normed_ref, q_ref, kv_ref, ctx_ref, lse_ref, z_all, c_all,
    z_middle, c_middle, send, recv, local,
):
    m = pl.program_id(0)
    across, along, far, _ = neighbours(lax.axis_index("seq"))
    pushes = Pushes(send, recv)
    count = z_ref.shape[0]
    half = count // 2
    top, low = pl.ds(0, half), pl.ds(half, half)
    first = [
        pushes.make(z_ref.at[top], z_all.at[1, top], {"seq": across}),
        pushes.make(z_ref.at[low], z_all.at[2, low], {"seq": along}),
        pushes.make(z_ref.at[low], z_all.at[1, low], {"seq": across}),
        pushes.make(z_ref.at[top], z_all.at[2, top], {"seq": along}),
    ]
    for n, peer in enumerate((across, along, far)):
        place = pl.ds((n + 1) * count, count)
        first.append(pushes.make(c_ref, c_all.at[:, place], {"seq": peer}))
    second = [
        pushes.make(z_all.at[1, top], z_all.at[3, top], {"seq": along}),
        pushes.make(z_all.at[2, low], z_all.at[3, low], {"seq": across}),
    ]
    bounces = [
        Bounce(z_ref, z_middle, z_all.at[0], local.at[0], False),
        Bounce(c_ref, c_middle, c_all.at[:, pl.ds(0, count)], local.at[1], False),
    ]

    @pl.when(m == 0)
    def _():
        greet([{"seq": across}, {"seq": along}, {"seq": far}])
        for copy in first:
            copy.start()
        for copy in bounces:
            copy.inward.start()
        for copy in bounces:
            copy.turn()

    project_kernel(tok_ref, small_ref, w_ref, cos_ref, sin_ref, normed_ref, q_ref, kv_ref)

    @pl.when(m == 1)
    def _():
        for copy, onward in zip(first, second):
            copy.wait_recv()
            onward.start()

    attention_kernel(True, q_ref, kv_ref, segq_ref, segk_ref, place_ref, ctx_ref, lse_ref)

    @pl.when(m == pl.num_programs(0) - 1)
    def _():
        for copy in first[2:] + second:
            copy.wait_recv()
        for copy in first + second:
            copy.wait_send()
        for copy in bounces:
            copy.wait()


def attention_back_kernel(
    skip, q_ref, kv_ref, segq_ref, segk_ref, place_ref, lse_ref, do_ref, cosq_ref, sinq_ref,
    cosk_ref, sink_ref, normed_ref, pre_ref, red_ref, graw_ref, term_ref, pre_in, red_out,
    dk_acc, dv_acc, term_acc, red_own, send, recv, local,
):
    seq = lax.axis_index("seq")
    me = seq % UNIT
    base = seq - me
    unit = [(me + k) % UNIT for k in range(1, UNIT)]
    pushes = Pushes(send, recv)
    sides = []
    for n, peer in enumerate(neighbours(seq)[:3]):
        sides.append(pushes.make(pre_ref.at[(peer - base) // 2], pre_in.at[n], {"seq": peer}))
    for b in unit:
        sides.append(pushes.make(red_ref.at[b], red_out.at[me], {"seq": base + b}))
    bounce = Bounce(red_ref.at[me], red_own, red_out.at[me], local, False)
    m = pl.program_id(0)

    @pl.when(m == 0)
    def _():
        greet([{"seq": base + b} for b in unit])
        bounce.inward.start()
        for copy in sides:
            copy.start()
        bounce.turn()

    length = kv_ref.shape[1]
    queries = q_ref.shape[1]
    kk, vv = pair_keys(kv_ref[0])
    k_t = kk.T.astype(BF16)[:HD]
    kk = kk.astype(BF16)
    vv = vv.astype(BF16)
    seg_col = jnp.broadcast_to(segk_ref[0], (8, length)).T[:, :1]
    dk_acc[...] = jnp.zeros_like(dk_acc)
    dv_acc[...] = jnp.zeros_like(dv_acc)
    per = QBLOCK // LANES
    for block in range(queries // QBLOCK):
        here = slice(block * QBLOCK, (block + 1) * QBLOCK)
        keys = (block + 1) * QBLOCK if skip else length
        bias = bias_block(seg_col, segq_ref[0][:, here], place_ref[:, here], 0, keys)
        q = q_ref[0, here, :]
        do = do_ref[block * per : (block + 1) * per, 0].reshape(QBLOCK, LANES)
        low = lane_iota(q.shape) < HD
        parts = []
        for head in range(2):
            pick = low == (head == 0)
            mine = jnp.where(pick, q, jnp.zeros_like(q))
            mine_do = jnp.where(pick, do, jnp.zeros_like(do))
            scores = dot_nt(kk[:keys], mine) + bias
            weight = jnp.exp(scores - lse_ref[0, head : head + 1, here])
            product = dot_nt(vv[:keys], mine_do)
            delta = jnp.sum(weight * product, axis=0, keepdims=True)
            grad_scores = (weight * (product - delta)).astype(BF16)
            dv_acc[:keys] += dot_nn(weight.astype(BF16), mine_do)
            dk_acc[:keys] += dot_nn(grad_scores, mine)
            parts.append(dot_nn(k_t[:, :keys], grad_scores))
        dq = jnp.concatenate(parts, axis=0).T * HD**-0.5
        dq = turn(dq, cosq_ref[here, :], -sinq_ref[here, :]).astype(BF16)
        graw_ref[block * per : (block + 1) * per, 0, :, :LANES] = dq.reshape(per, LANES, LANES)
    dk = dk_acc[...]
    dv = dv_acc[...]
    dk = dk + pltpu.roll(dk, HD, 1)
    dv = dv + pltpu.roll(dv, HD, 1)
    gkv = jnp.where(lane_iota(dk.shape) < HD, dk, dv)
    key_cos, key_sin = value_tables(cosk_ref[...], sink_ref[...])
    gkv = turn(gkv, key_cos, -key_sin).astype(BF16)
    graw_ref[:, 0, :, LANES:] = gkv.reshape(length // LANES, LANES, LANES)
    if skip:
        normed_t = normed_ref[...].reshape(queries, -1).T
        term = dot_nn(normed_t, graw_ref[...].reshape(queries, 2 * LANES))
        @pl.when(m == 0)
        def _():
            term_acc[...] = term

        @pl.when(m > 0)
        def _():
            term_acc[...] += term

        @pl.when(m == pl.num_programs(0) - 1)
        def _():
            for b in range(UNIT):
                for r in range(PIECES):
                    at = (b * PIECES + r) * ROWS_IN
                    term_ref[r, b] = term_acc[at : at + ROWS_IN].astype(BF16)

    @pl.when(m == pl.num_programs(0) - 1)
    def _():
        for copy in sides:
            copy.wait()
        bounce.wait()


def spread(rows):
    rest = jnp.zeros((LANES - E, rows.shape[1]), F32)
    return jnp.concatenate([rows.astype(F32), rest], axis=0).T


def soft_gates(normed, router, chosen):
    logits = jnp.where(chosen > 0, dot_nn(normed, router), NEGATIVE)
    top = jnp.max(logits, axis=-1, keepdims=True)
    weight = jnp.where(chosen > 0, jnp.exp(logits - top), 0.0)
    return weight / jnp.sum(weight, axis=-1, keepdims=True)


def unpack(inner_ref, down_ref, first, wg, wu, wd):
    half = wg.shape[1]
    for r in range(PIECES):
        for b in range(UNIT):
            at = (b * PIECES + r) * ROWS_IN
            low = (b * PIECES + r) * ROWS_OUT
            wg[at : at + ROWS_IN] = inner_ref[r, b, :ROWS_IN]
            wu[at : at + ROWS_IN] = inner_ref[r, b, ROWS_IN : 2 * ROWS_IN]
            for c in range(2):
                start = first + c * ROWS_OUT
                wd[low : low + ROWS_OUT, c * half : (c + 1) * half] = down_ref[
                    r, b, start : start + ROWS_OUT
                ]


def load_weights(now, later, first, fetches, wg, wu, wd, greeted):
    e, t = pl.program_id(0), pl.program_id(1)

    @pl.when((t == 0) & (e == 0))
    def _():
        for copy in fetches:
            copy.start()
        greet([{"seq": peer} for peer in greeted])
        unpack(*now, first, wg, wu, wd)

    @pl.when((t == 0) & (e == 1))
    def _():
        for copy in fetches:
            copy.wait()
        unpack(*later, first, wg, wu, wd)


def twin_push(source, target, send, recv):
    twin = neighbours(lax.axis_index("seq"))[3]
    return pltpu.make_async_remote_copy(
        src_ref=source,
        dst_ref=target,
        send_sem=send,
        recv_sem=recv,
        device_id={"seq": twin},
        device_id_type=pl.DeviceIdType.MESH,
    )


def collect_terms(x, dz, grad_gate, grad_up, gated, ag, au, ad, stage, total, dw, sems):
    e, t = pl.program_id(0), pl.program_id(1)
    last_t = pl.num_programs(1) - 1
    half = ag.shape[1]

    @pl.when(t == 0)
    def _():
        ag[...] = dot_tn(x, grad_gate)
        au[...] = dot_tn(x, grad_up)
        ad[...] = dot_tn(gated, dz)

    @pl.when((t > 0) & (t < last_t))
    def _():
        ag[...] += dot_tn(x, grad_gate)
        au[...] += dot_tn(x, grad_up)
        ad[...] += dot_tn(gated, dz)

    send, recv, local = sems
    push = twin_push(stage, total, send.at[0], recv.at[0])
    out = pltpu.make_async_copy(stage, dw, local.at[1])

    def store(write):
        for place, acc, grad in ((0, ag, grad_gate), (ROWS_IN, au, grad_up)):
            final = acc[...] + dot_tn(x, grad)
            for r in range(PIECES):
                for b in range(UNIT):
                    at = (b * PIECES + r) * ROWS_IN
                    write(r, b, place, final[at : at + ROWS_IN])
        final = ad[...] + dot_tn(gated, dz)
        for r in range(PIECES):
            for b in range(UNIT):
                low = (b * PIECES + r) * ROWS_OUT
                for c in range(2):
                    start = 2 * ROWS_IN + c * ROWS_OUT
                    write(r, b, start, final[low : low + ROWS_OUT, c * half : (c + 1) * half])

    @pl.when((t == last_t) & (e == 0))
    def _():
        def write(r, b, place, value):
            stage[r, b, place : place + value.shape[0]] = value.astype(BF16)

        store(write)
        push.start()

    @pl.when((t == last_t) & (e == 1))
    def _():
        push.wait()

        def write(r, b, place, value):
            here = slice(place, place + value.shape[0])
            stage[r, b, here] = (value + total[r, b, here].astype(F32)).astype(BF16)

        store(write)
        out.start()
        out.wait()


def sigmoid(v):
    return 0.5 + 0.5 * jnp.tanh(0.5 * v)


def grads_of(gate_act, up_act, back, gate):
    sig = sigmoid(gate_act)
    silu = gate_act * sig
    hidden = silu * up_act
    grad_hidden = back * gate
    grad_gate = (grad_hidden * up_act * (sig + silu * (1.0 - sig))).astype(BF16)
    grad_up = (grad_hidden * silu).astype(BF16)
    return hidden, grad_gate, grad_up


def expert_id(twin, index):
    me = lax.axis_index("seq") % UNIT
    return 2 * (me + twin * (1 - 2 * (me % 2))) + index


def pick_gate(gates, gid):
    mine = lane_iota(gates.shape) == gid
    return mine, jnp.sum(jnp.where(mine, gates, 0.0), axis=1, keepdims=True)


def gate_terms(mine, hidden, back):
    terms = jnp.where(mine, jnp.sum(hidden * back, axis=1, keepdims=True), 0.0)
    return terms.T[:E]


def both_kernel(
    x_ref, dz_ref, chosen_ref, wr_ref, w0_ref, w1_hbm, heads_ref,
    out_ref, dx_ref, gg_ref, gates_ref, dw, w_heads,
    wg, wu, wd, gates_s, ag, au, ad, oacc, dxacc, ggacc, w1_ref, stage, total,
    send, recv, local,
):
    e, t = pl.program_id(0), pl.program_id(1)
    tile, width = out_ref.shape
    rows = pl.ds(pl.multiple_of(t * tile, tile), tile)
    x = x_ref[...]
    dz = dz_ref[...]
    last_t = pl.num_programs(1) - 1
    across, along, _, twin = neighbours(lax.axis_index("seq"))
    fetch = pltpu.make_async_copy(w1_hbm, w1_ref, local.at[0])
    packed = (w0_ref, w0_ref)
    load_weights(
        packed, (w1_ref, w1_ref), 2 * ROWS_IN, [fetch], wg, wu, wd, (across, along, twin)
    )

    me = lax.axis_index("seq") % UNIT
    base = lax.axis_index("seq") - me
    a, b, d = across - base, along - base, 6 - me + 2 * (me % 2)
    half = heads_ref.shape[0] // 2
    top, low = pl.ds(0, half), pl.ds(half, half)
    lanes = pl.ds(0, w_heads.shape[2])
    pushes = Pushes(send, recv)
    pushes.used = 1

    def own_part(part, device):
        return pushes.make(heads_ref.at[part, lanes], w_heads.at[me, part], {"seq": device})

    def passed(slot, part, device):
        view = w_heads.at[slot, part]
        return pushes.make(view, view, {"seq": device})

    hop1 = [own_part(top, across), own_part(low, along), own_part(low, across), own_part(top, along)]
    hop1 += [own_part(top, twin), own_part(low, twin)]
    hop2 = [passed(a, top, along), passed(b, low, across), passed(a, top, twin), passed(b, low, twin)]
    hop3 = [passed(a, low, twin), passed(b, top, twin)]
    hop4 = [passed(d, top, twin), passed(d, low, twin)]
    events = (
        (0, 0, (), hop1),
        (0, last_t, hop1[:2], hop2),
        (1, 0, hop1[2:4], hop3),
        (1, 1, hop2[:2], hop4),
    )
    for at_e, at_t, arrived, onward in events:

        @pl.when((e == at_e) & (t == at_t))
        def _(arrived=arrived, onward=onward):
            for copy in arrived:
                copy.wait_recv()
            for copy in onward:
                copy.start()

    @pl.when(e == 0)
    def _():
        gates_s[rows, :] = soft_gates(x, wr_ref[...], spread(chosen_ref[...]))

    mine, gate = pick_gate(gates_s[rows, :], expert_id(1 - e, 0))
    gate_act = dot_nn(x, wg[...])
    up_act = dot_nn(x, wu[...])
    back = dot_nt(dz, wd[...])
    hidden, grad_gate, grad_up = grads_of(gate_act, up_act, back, gate)
    ggterm = gate_terms(mine, hidden, back)
    gated = (hidden * gate).astype(BF16)
    out = dot_nn(gated, wd[...])
    dx = dot_nt(grad_gate, wg[...]) + dot_nt(grad_up, wu[...])

    @pl.when(e == 0)
    def _():
        oacc[rows, :] = out
        dxacc[rows, :] = dx
        ggacc[t] = ggterm

    @pl.when(e == 1)
    def _():
        out_ref[...] = (oacc[rows, :] + out).astype(BF16)
        dx_ref[...] = (dxacc[rows, :] + dx).astype(BF16)
        gg_ref[...] = ggacc[t] + ggterm
        gates_ref[...] = gates_s[rows, :]

    sems = (send, recv, local)
    collect_terms(x, dz, grad_gate, grad_up, gated, ag, au, ad, stage, total, dw, sems)

    @pl.when((e == 1) & (t == last_t))
    def _():
        for copy in hop1[4:] + hop2[2:] + hop3 + hop4:
            copy.wait_recv()
        for copy in hop1 + hop2 + hop3 + hop4:
            copy.wait_send()


def forward_kernel(
    x_ref, gates_ref, inner_ref, down_ref, inner_hbm, down_hbm, oin_ref,
    out_ref, gact_ref, uact_ref, inner_twin, down_twin,
    wg, wu, wd, oacc, inner_next, down_next, send, recv, local,
):
    e, t = pl.program_id(0), pl.program_id(1)
    tile = out_ref.shape[0]
    rows = pl.ds(pl.multiple_of(t * tile, tile), tile)
    x = x_ref[...]
    last_t = pl.num_programs(1) - 1
    turned = [
        twin_push(inner_hbm, inner_next, send.at[0], recv.at[0]),
        twin_push(down_hbm, down_next, send.at[1], recv.at[1]),
    ]
    keeps = [
        pltpu.make_async_copy(inner_next, inner_twin, local.at[0]),
        pltpu.make_async_copy(down_next, down_twin, local.at[1]),
    ]

    @pl.when((e == 0) & (t == 0))
    def _():
        greet([{"seq": neighbours(lax.axis_index("seq"))[3]}])
        for copy in turned:
            copy.start()
        unpack(inner_ref, down_ref, 0, wg, wu, wd)

    @pl.when((e == 1) & (t == 0))
    def _():
        for copy in turned:
            copy.wait()
        for copy in keeps:
            copy.start()
        unpack(inner_next, down_next, 0, wg, wu, wd)

    _, gate = pick_gate(gates_ref[...], expert_id(e, 1))
    gate_act = dot_nn(x, wg[...])
    up_act = dot_nn(x, wu[...])
    gact_ref[0] = gate_act.astype(BF16)
    uact_ref[0] = up_act.astype(BF16)
    gated = (gate_act * sigmoid(gate_act) * up_act * gate).astype(BF16)
    out = dot_nn(gated, wd[...])

    @pl.when(e == 0)
    def _():
        oacc[rows, :] = oin_ref[...].astype(F32) + out

    @pl.when(e == 1)
    def _():
        out_ref[...] = (oacc[rows, :] + out).astype(BF16)

    @pl.when((e == 1) & (t == last_t))
    def _():
        for copy in keeps:
            copy.wait()


def backward_kernel(
    x_ref, dz_ref, gates_ref, gact_ref, uact_ref, inner_ref, down_ref,
    inner_hbm, down_hbm, dxin_ref, ggin_ref,
    out_hbm, dx_ref, gg_ref, dw, out_in,
    wg, wu, wd, ag, au, ad, dxacc, ggacc, inner_next, down_next, stage, total,
    diag_x, diag_y, own_x, own_y, send, recv, local,
):
    e, t = pl.program_id(0), pl.program_id(1)
    tile, width = dx_ref.shape
    rows = pl.ds(pl.multiple_of(t * tile, tile), tile)
    x = x_ref[...]
    dz = dz_ref[...]
    fetches = [
        pltpu.make_async_copy(inner_hbm, inner_next, local.at[0]),
        pltpu.make_async_copy(down_hbm, down_next, local.at[4]),
    ]
    load_weights(
        (inner_ref, down_ref), (inner_next, down_next), 0, fetches, wg, wu, wd,
        neighbours(lax.axis_index("seq")),
    )
    across, along, _, _ = neighbours(lax.axis_index("seq"))
    pushes = Pushes(send, recv)
    pushes.used = 1
    half = own_x.shape[0]
    top, low = pl.ds(0, half), pl.ds(half, half)
    first = [
        pushes.make(out_hbm.at[3, top], diag_x, {"seq": across}),
        pushes.make(out_hbm.at[3, low], diag_y, {"seq": along}),
        pushes.make(out_hbm.at[1, top], out_in.at[0, top], {"seq": across}),
        pushes.make(out_hbm.at[2, low], out_in.at[1, low], {"seq": along}),
    ]
    second = [
        pushes.make(own_x, out_in.at[0, low], {"seq": across}),
        pushes.make(own_y, out_in.at[1, top], {"seq": along}),
    ]
    loads = [
        pltpu.make_async_copy(out_hbm.at[1, low], own_x, local.at[2]),
        pltpu.make_async_copy(out_hbm.at[2, top], own_y, local.at[3]),
    ]

    @pl.when((e == 0) & (t == 0))
    def _():
        for copy in first + loads:
            copy.start()

    mine, gate = pick_gate(gates_ref[...], expert_id(1 - e, 1))
    back = dot_nt(dz, wd[...])
    hidden, grad_gate, grad_up = grads_of(
        gact_ref[0].astype(F32), uact_ref[0].astype(F32), back, gate
    )
    ggterm = gate_terms(mine, hidden, back)
    gated = (hidden * gate).astype(BF16)
    dx = dot_nt(grad_gate, wg[...]) + dot_nt(grad_up, wu[...])

    @pl.when(e == 0)
    def _():
        dxacc[rows, :] = dxin_ref[...].astype(F32) + dx
        ggacc[t] = ggin_ref[...] + ggterm

    @pl.when(e == 1)
    def _():
        dx_ref[...] = (dxacc[rows, :] + dx).astype(BF16)
        gg_ref[...] = ggacc[t] + ggterm

    sems = (send, recv, local)
    collect_terms(x, dz, grad_gate, grad_up, gated, ag, au, ad, stage, total, dw, sems)

    @pl.when((e == 0) & (t == pl.num_programs(1) - 1))
    def _():
        for copy in loads:
            copy.wait()
        first[0].wait_recv()
        first[1].wait_recv()
        own_x[...] = (own_x[...].astype(F32) + diag_y[...].astype(F32)).astype(BF16)
        own_y[...] = (own_y[...].astype(F32) + diag_x[...].astype(F32)).astype(BF16)
        for copy in second:
            copy.start()

    @pl.when((e == 1) & (t == pl.num_programs(1) - 1))
    def _():
        first[0].wait_send()
        first[1].wait_send()
        for copy in first[2:] + second:
            copy.wait()


def run_experts(which, x, dz, chosen, weights, router=None, gates=None, carried=None, acts=None, pushed=None):
    tokens, width = x.shape
    hidden = weights[0].shape[3]
    packed_shape = (PIECES, UNIT, 3 * ROWS_IN, hidden)
    inner_shape = (PIECES, UNIT, 2 * ROWS_IN, hidden)
    down_shape = (PIECES, UNIT, ROWS_IN, hidden)
    tile = tokens // 3
    tiles = 3
    like = jax.ShapeDtypeStruct
    any_spec = pl.BlockSpec(memory_space=pl.ANY)
    once = pl.Buffered(1)

    def by_token(e, t):
        return (t, 0)

    def at_end(e, t):
        return (jnp.where(e == 1, t, 0), 0)

    def at_start(e, t):
        return (jnp.where(e == 0, t, tiles - 1), 0)

    def lanes_end(e, t):
        return (0, jnp.where(e == 1, t, 0))

    def lanes_start(e, t):
        return (0, jnp.where(e == 0, t, tiles - 1))

    def acts_map(e, t):
        return (e, t, 0)

    x_spec = pl.BlockSpec((tile, width), by_token)
    gates_spec = pl.BlockSpec((tile, LANES), by_token)

    def weight_spec(shape):
        return pl.BlockSpec(shape, lambda e, t: (0, 0, 0, 0), pipeline_mode=once)

    acts_spec = pl.BlockSpec((1, tile, hidden), acts_map)
    acts_back = pl.BlockSpec((1, tile, hidden), lambda e, t: (1 - e, t, 0))
    token_end = pl.BlockSpec((tile, width), at_end)
    token_start = pl.BlockSpec((tile, width), at_start)
    packed_like = like(packed_shape, BF16)
    pair_like = [like(inner_shape, BF16), like(down_shape, BF16)]
    pair_vmem = [pltpu.VMEM(inner_shape, BF16), pltpu.VMEM(down_shape, BF16)]
    pair_specs = [weight_spec(inner_shape), weight_spec(down_shape), any_spec, any_spec]
    token_like = like((tokens, width), BF16)
    gg_like = like((E, tokens), F32)
    acts_like = like((2, tokens, hidden), BF16)
    unpacked = [
        pltpu.VMEM((width, hidden), BF16),
        pltpu.VMEM((width, hidden), BF16),
        pltpu.VMEM((hidden, width), BF16),
    ]
    terms = [
        pltpu.VMEM((width, hidden), F32),
        pltpu.VMEM((width, hidden), F32),
        pltpu.VMEM((hidden, width), F32),
    ]
    acc = pltpu.VMEM((tokens, width), F32)
    gg_acc = pltpu.VMEM((tiles, E, tile), F32)
    second = pltpu.VMEM(packed_shape, BF16)
    stage = pltpu.VMEM(packed_shape, BF16)
    sem, sems = pltpu.SemaphoreType.DMA, pltpu.SemaphoreType.DMA((2,))
    flops = 4.0 * tokens * width * hidden
    if which == "both":
        return pl.pallas_call(
            both_kernel,
            grid=(2, tiles),
            in_specs=[
                x_spec, x_spec, pl.BlockSpec((E, tile), lambda e, t: (0, t)),
                pl.BlockSpec((width, LANES), lambda e, t: (0, 2), pipeline_mode=once),
                weight_spec(packed_shape), any_spec, any_spec,
            ],
            out_specs=[
                token_end, token_end, pl.BlockSpec((E, tile), lanes_end),
                pl.BlockSpec((tile, LANES), at_end), any_spec, any_spec,
            ],
            out_shape=[
                token_like, token_like, gg_like, like((tokens, LANES), F32),
                packed_like, like((UNIT, width, 4 * HD), BF16),
            ],
            scratch_shapes=unpacked
            + [pltpu.VMEM((tokens, LANES), F32)]
            + terms
            + [acc, acc, gg_acc, second, stage, stage]
            + [pltpu.SemaphoreType.DMA((15,)), pltpu.SemaphoreType.DMA((15,)), sems],
            compiler_params=params(collective_id=5, has_side_effects=True),
            cost_estimate=cost(1, 1e5),
        )(x, dz, chosen, router, *weights, router)
    if which == "forward":
        return pl.pallas_call(
            forward_kernel,
            grid=(2, tiles),
            in_specs=[x_spec, gates_spec] + pair_specs + [token_start],
            out_specs=[token_end, acts_spec, acts_spec, any_spec, any_spec],
            out_shape=[token_like, acts_like, acts_like] + pair_like,
            scratch_shapes=unpacked + [acc] + pair_vmem + [sems, sems, sems],
            compiler_params=params(collective_id=9, has_side_effects=True),
            cost_estimate=cost(3 * flops, 2e7),
        )(x, gates, *weights, *weights, carried)
    return pl.pallas_call(
        backward_kernel,
        grid=(2, tiles),
        in_specs=[
            x_spec, x_spec, gates_spec, acts_back, acts_back, *pair_specs,
            token_start, pl.BlockSpec((E, tile), lanes_start), any_spec,
        ],
        out_specs=[token_end, pl.BlockSpec((E, tile), lanes_end), any_spec, any_spec],
        out_shape=[
            token_like, gg_like, packed_like, like((2,) + pushed.shape[1:], BF16),
        ],
        scratch_shapes=unpacked + terms + [acc, gg_acc]
        + pair_vmem
        + [stage, stage]
        + [pltpu.VMEM((pushed.shape[1] // 2, width), BF16)] * 4
        + [pltpu.SemaphoreType.DMA((7,)), pltpu.SemaphoreType.DMA((7,))]
        + [pltpu.SemaphoreType.DMA((5,))],
        compiler_params=params(collective_id=6, has_side_effects=True),
        cost_estimate=cost(6 * flops, 2e7),
    )(x, dz, gates, acts[0], acts[1], *weights, carried[0], carried[1], pushed)


def return_kernel(
    micro, copies, ready, dx_ref, gg_ref, mixed_ref, normed_ref, dz_ref, chosen_ref, small_ref, w_ref,
    ctx_ref, own_out, back_out, do_out, gmixed_ref, pre_ref, block_ref,
    mine_dx, from_x, from_y, diag_x, diag_y, sum_x, sum_y, gparts, gctx, gbranch, glogs, term, twin_term, send, recv, local,
):
    seq = lax.axis_index("seq")
    me = seq % UNIT
    core = me % 2
    base = seq - me
    unit = [(me + k) % UNIT for k in range(1, UNIT)]
    *peers, twin = neighbours(seq)
    greet([{"seq": base + b} for b in unit])
    pushes = Pushes(send, recv)
    count, width = mixed_ref.shape
    step = count // micro
    half = step // 2
    chunks = [pl.ds(m * step, step) for m in range(micro)]
    tops = [pl.ds(m * step, half) for m in range(micro)]
    lows = [pl.ds(m * step + half, half) for m in range(micro)]
    across, along = peers[:2]
    own = [
        pltpu.make_async_copy(dx_ref, mine_dx, local.at[0]),
        pltpu.make_async_copy(gg_ref.at[:, pl.ds(0, count)], gparts.at[0], local.at[1]),
    ]
    for copy in own:
        copy.start()
    diagonal, direct, sums = [], [], []

    def send_diagonal(m):
        diagonal.append(
            (
                pushes.start(dx_ref.at[3, tops[m]], diag_x.at[m], {"seq": across}),
                pushes.start(dx_ref.at[3, lows[m]], diag_y.at[m], {"seq": along}),
            )
        )

    def send_direct(m):
        direct.append(
            (
                pushes.start(dx_ref.at[1, tops[m]], from_x.at[tops[m]], {"seq": across}),
                pushes.start(dx_ref.at[2, lows[m]], from_y.at[lows[m]], {"seq": along}),
            )
        )

    def send_sums(m):
        for copy in diagonal[m]:
            copy.wait_recv()
        own_y = mine_dx[2, tops[m]].astype(F32) + diag_x[m].astype(F32)
        own_x = mine_dx[1, lows[m]].astype(F32) + diag_y[m].astype(F32)
        sum_y[m] = own_y.astype(BF16)
        sum_x[m] = own_x.astype(BF16)
        sums.append(
            (
                pushes.start(sum_y.at[m], from_y.at[tops[m]], {"seq": along}),
                pushes.start(sum_x.at[m], from_x.at[lows[m]], {"seq": across}),
            )
        )

    send_diagonal(0)
    first = []
    for n in (2, 0, 1):
        part = gg_ref.at[:, pl.ds((n + 1) * count, count)]
        first.append(pushes.start(part, gparts.at[n + 1], {"seq": peers[n]}))
    send_direct(0)
    if micro > 1:
        send_diagonal(1)
    ready()
    small = small_ref[...]
    gain = gain_row(small, E + 1)
    gates = soft_gates(normed_ref[...], small, spread(chosen_ref[...]))
    block = mixed_ref[...] + own_out[0].astype(F32) + back_out[0].astype(F32)
    block_ref[...] = (block + back_out[1].astype(F32)).astype(BF16)
    for copy in own:
        copy.wait()
    for copy in first:
        copy.wait_recv()
    grad_gates = gparts[0] + gparts[1] + gparts[2] + gparts[3]
    grad_gates = spread(grad_gates)
    centre = jnp.sum(gates * grad_gates, axis=-1, keepdims=True)
    glogs[...] = (gates * (grad_gates - centre)).astype(BF16)
    sent = []

    def compute(m):
        here = chunks[m]
        for copy in direct[m] + sums[m]:
            copy.wait_recv()
        dy = mine_dx[0, here].astype(F32) + from_x[here].astype(F32) + from_y[here].astype(F32)
        dy = dy + dot_nt(glogs[here], small)
        v = mixed_ref[here]
        inverse = lax.rsqrt(jnp.mean(v * v, axis=-1, keepdims=True) + EPS)
        scaled = dy * gain
        mean = jnp.mean(scaled * v, axis=-1, keepdims=True)
        gmixed = dz_ref[here].astype(F32) + scaled * inverse
        gmixed = gmixed - v * (inverse * inverse * inverse * mean)
        gmixed_ref[here] = gmixed
        branch = gmixed.astype(BF16)
        gbranch[here] = branch
        grad_ctx = dot_nt(branch, w_ref[...]).astype(BF16)
        for b in range(UNIT):
            gctx[b, m] = grad_ctx[:, b * LANES : (b + 1) * LANES]
        mine = pltpu.make_async_copy(gctx.at[me, m], do_out.at[me, m], local.at[2 + m])
        mine.start()
        own.append(mine)
        for b in unit:
            sent.append(pushes.start(gctx.at[b, m], do_out.at[me, m], {"seq": base + b}))

    for m in range(micro):
        send_sums(m)
        if m + 1 < micro:
            send_direct(m + 1)
        if m + 2 < micro:
            send_diagonal(m + 2)
        if m > 0:
            compute(m - 1)
    compute(micro - 1)
    rest = width // (copies * UNIT)
    out_term = dot_tn(ctx_ref[...], gbranch[...]).astype(BF16)
    router_term = dot_tn(normed_ref[...], glogs[...]).astype(BF16)
    for a in range(copies):
        for b in range(UNIT):
            at = (a * UNIT + b) * rest
            term[a, b, :, :width] = out_term[at : at + rest]
            term[a, b, :, width:] = router_term[at : at + rest]
    turned = [
        pushes.start(term.at[:, 2 * j + 1 - core], twin_term.at[j], {"seq": twin})
        for j in range(4)
    ]
    for j, copy in enumerate(turned):
        copy.wait_recv()
        summed = term[:, 2 * j + core].astype(F32) + twin_term[j].astype(F32)
        pre_ref[j] = summed.astype(BF16)
    for group in [first] + diagonal + direct + sums:
        for copy in group:
            copy.wait_send()
    for copy in turned:
        copy.wait_send()
    for copy in own[2:] + sent:
        copy.wait()


def return_tokens(
    dx, gg, mixed, normed, dz, chosen, heads, w_out, context, own_out, back_out, micro, copies, collective
):
    any_spec = pl.BlockSpec(memory_space=pl.ANY)
    like = jax.ShapeDtypeStruct
    count, width = mixed.shape
    ctx_shape = (UNIT, micro, count // micro, LANES)
    pre_shape = (4, copies, width // (copies * UNIT), width + LANES)
    pushes = 3 + 6 * micro + (UNIT - 1) * micro + 4
    piece = (micro, count // micro // 2, width)

    def fixed(i):
        return (0, 0)

    late = Late(
        [
            (2, mixed.shape, F32, None),
            (3, normed.shape, BF16, None),
            (4, dz.shape, BF16, None),
            (5, chosen.shape, BF16, None),
            (6, (width, LANES), BF16, small_view),
            (7, w_out.shape, BF16, None),
            (8, context.shape, BF16, None),
            (9, (1, count, width), BF16, lambda ref: ref.at[pl.ds(0, 1)]),
            (10, back_out.shape, BF16, None),
        ]
    )

    return pl.pallas_call(
        late.wrap(functools.partial(return_kernel, micro, copies), 11),
        grid=(1,),
        in_specs=late.specs(11),
        out_specs=[
            any_spec,
            pl.BlockSpec((count, width), fixed),
            pl.BlockSpec(pre_shape, lambda i: (0, 0, 0, 0)),
            pl.BlockSpec((count, width), fixed),
        ],
        out_shape=[
            like(ctx_shape, BF16),
            like((count, width), F32),
            like(pre_shape, BF16),
            like((count, width), BF16),
        ],
        scratch_shapes=[
            pltpu.VMEM((4, count, width), BF16),
            pltpu.VMEM((count, width), BF16),
            pltpu.VMEM((count, width), BF16),
            pltpu.VMEM(piece, BF16),
            pltpu.VMEM(piece, BF16),
            pltpu.VMEM(piece, BF16),
            pltpu.VMEM(piece, BF16),
            pltpu.VMEM((4, E, count), F32),
            pltpu.VMEM(ctx_shape, BF16),
            pltpu.VMEM((count, width), BF16),
            pltpu.VMEM((count, LANES), BF16),
            pltpu.VMEM((copies, UNIT) + pre_shape[2:], BF16),
            pltpu.VMEM(pre_shape, BF16),
            pltpu.SemaphoreType.DMA((pushes,)),
            pltpu.SemaphoreType.DMA((pushes,)),
            pltpu.SemaphoreType.DMA((2 + micro,)),
        ]
        + late.scratch(),
        compiler_params=params(collective_id=collective, has_side_effects=True),
        cost_estimate=cost(4.0 * count * width * width, 1.2e8),
    )(dx, gg, mixed, normed, dz, chosen, heads, w_out, context, own_out, back_out)


def unpack_grads_kernel(
    ex0, ex1, head_ref, out_ref, gate_w, up_w, query_w, key_w, value_w, router_w, attn_ref, ffn_ref,
    gattn, gquery, gkey, gvalue, gout, gffn, grouter, ggate, gup, gdown,
):
    part, hidden = gate_w.shape[1:]
    half = part // 2
    width = gout.shape[1]
    ffn = jnp.zeros((part, hidden), F32)
    for n, source in enumerate((ex0, ex1)):
        for b in range(UNIT):
            e = 2 * b + n
            gate = source[b, :part].astype(F32)
            up = source[b, part : 2 * part].astype(F32)
            ggate[e] = gate
            gup[e] = up
            ffn = ffn + gate * gate_w[e].astype(F32) + up * up_w[e].astype(F32)
            for c in range(2):
                start = 2 * part + c * half
                gdown[e, :, c * hidden : (c + 1) * hidden] = source[b, start : start + half].astype(
                    F32
                )
    router = out_ref[:, width : width + E]
    grouter[...] = router
    gout[...] = out_ref[:, :width]
    low = lane_iota((part, LANES)) < HD
    attn = jnp.zeros((part, LANES), F32)
    for pair in range(UNIT // 2):
        lanes = slice(pair * LANES, (pair + 1) * LANES)
        even = head_ref[2 * pair, :, LANES:].astype(F32)
        odd = head_ref[2 * pair + 1, :, LANES:].astype(F32)
        key = jnp.where(low, even, pltpu.roll(odd, HD, 1))
        value = jnp.where(low, pltpu.roll(even, HD, 1), odd)
        gkey[:, lanes] = key
        gvalue[:, lanes] = value
        attn = attn + key * key_w[:, lanes].astype(F32) + value * value_w[:, lanes].astype(F32)
    for b in range(UNIT):
        lanes = slice(b * LANES, (b + 1) * LANES)
        query = head_ref[b, :, :LANES].astype(F32)
        gquery[:, lanes] = query
        attn = attn + query * query_w[:, lanes].astype(F32)

    def as_row(column):
        return jnp.broadcast_to(column, (part, LANES)).T[:1]

    attn = jnp.sum(attn, axis=1, keepdims=True)
    ffn = jnp.sum(ffn, axis=1, keepdims=True)
    ffn = ffn + jnp.sum(router * router_w[...].astype(F32), axis=1, keepdims=True)
    gattn[...] = as_row(attn) / attn_ref[...].astype(F32)
    gffn[...] = as_row(ffn) / ffn_ref[...].astype(F32)


def shards(
    copies, tokens, segments, routes, cotangent, norm_attn, w_query, w_key, w_value, w_out, norm_ffn,
    w_router, w_gate, w_up, w_down, rows,
):
    micro, local_len, width = tokens.shape
    length = segments.shape[1]
    count = micro * local_len
    unit_len = UNIT * local_len
    part = w_query.shape[0]
    hidden = w_gate.shape[2]
    seq_size = copies * UNIT
    seq = lax.axis_index("seq")
    row = lax.axis_index("row")
    unit = seq // UNIT
    me = seq % UNIT
    unit_groups = None
    copy_groups = None
    if copies > 1:
        unit_groups = [[a * UNIT + b for b in range(UNIT)] for a in range(copies)]
        copy_groups = [[a * UNIT + b for a in range(copies)] for b in range(UNIT)]

    def exchange(x):
        return lax.all_to_all(x, "seq", 0, 0, tiled=True, axis_index_groups=unit_groups)

    def flip(x, k):
        return lax.ppermute(x, "seq", [(s, s ^ k) for s in range(seq_size)])

    flat_tokens = tokens.reshape(count, width)

    def wait_for(x, *others):
        return lax.optimization_barrier((x,) + others)[0]

    if copies == 1:
        inputs = [
            w_gate, w_up, w_down, w_query, w_key, w_value, w_router, norm_attn[None],
            norm_ffn[None],
        ]
    else:
        small = jnp.concatenate(
            [w_router.T, norm_attn[None], norm_ffn[None], jnp.zeros((LANES - 2 - E, part), BF16)], axis=0
        ).T
        head_part = jnp.concatenate(
            [
                w_query.reshape(part, UNIT, 2 * HD),
                w_key.reshape(part, UNIT, HD),
                w_value.reshape(part, UNIT, HD),
                jnp.broadcast_to(small[:, None], (part, UNIT, LANES)),
            ],
            axis=2,
        ).transpose(1, 0, 2)

        down_halves = w_down.reshape(E, -1, 2, hidden).transpose(0, 2, 1, 3).reshape(E, part, hidden)
        packed_part = jnp.concatenate([w_gate, w_up, down_halves], axis=1)
        packed_part = packed_part.reshape(UNIT, E // UNIT, 3 * part, hidden).transpose(1, 0, 2, 3)
        inputs = [packed_part, head_part]
    *packed_mine, heads_all, w_out_rows = begin(rows, part, hidden, inputs, w_out)

    if copies > 1:
        heads_all = lax.all_gather(heads_all, "seq", axis=0, axis_index_groups=copy_groups)
        w_out_rows = lax.all_gather(w_out_rows, "seq", axis=0, axis_index_groups=copy_groups)
    w_out_all = w_out_rows.reshape(H * HD, width)
    heads_all = heads_all.reshape(width, 4 * HD + LANES)

    def gather_packed(x):
        x = lax.all_gather(x, "row", axis=0)
        if copies > 1:
            x = lax.all_gather(x, "seq", axis=0, axis_index_groups=copy_groups)
            x = x.transpose(0, 2, 1, 3, 4).reshape(-1, 3 * part, hidden)
            halves = x[:, 2 * part :].reshape(-1, 2, part // 2, hidden).transpose(0, 2, 1, 3)
            return pack(
                x[:, :part].reshape(width, hidden),
                x[:, part : 2 * part].reshape(width, hidden),
                halves.reshape(hidden, width),
            )
        return x

    def pack(gate, up, down):
        gate = gate.reshape(UNIT, PIECES, ROWS_IN, hidden)
        up = up.reshape(UNIT, PIECES, ROWS_IN, hidden)
        down = down.reshape(UNIT, PIECES, ROWS_OUT, 2, hidden).transpose(0, 1, 3, 2, 4)
        down = down.reshape(UNIT, PIECES, ROWS_IN, hidden)
        return jnp.concatenate([gate, up, down], axis=2).transpose(1, 0, 2, 3)

    def repack(x):
        x = x.transpose(1, 0, 2, 3)
        gate = x[:, :, :ROWS_IN].reshape(copies, UNIT, rows, part, hidden)
        up = x[:, :, ROWS_IN : 2 * ROWS_IN].reshape(copies, UNIT, rows, part, hidden)
        down = x[:, :, 2 * ROWS_IN :].reshape(UNIT, PIECES, 2, ROWS_OUT, hidden)
        down = down.transpose(0, 1, 3, 2, 4).reshape(copies, UNIT, rows, part // 2, 2, hidden)
        down = down.transpose(0, 1, 2, 4, 3, 5).reshape(copies, UNIT, rows, part, hidden)
        return jnp.concatenate([gate, up, down], axis=3).transpose(2, 0, 1, 3, 4)

    own_first = gather_packed(packed_mine[0])
    if copies > 1:
        whole_second = gather_packed(jnp.concatenate(packed_mine[1:], axis=1))
        own_second = (whole_second[:, :, : 2 * ROWS_IN], whole_second[:, :, 2 * ROWS_IN :])
    else:
        own_second = tuple(gather_packed(x) for x in packed_mine[1:])

    (tok_all,) = unit_gather([wait_for(flat_tokens, w_out_all)], 1)
    tok_all = tok_all.reshape(UNIT, micro, local_len, width)

    chosen = jnp.any(
        routes.reshape(count, TOPK).T[:, None, :] == jnp.arange(E, dtype=jnp.int32)[None, :, None],
        axis=0,
    ).astype(BF16)
    dz_own = cotangent.reshape(count, width)

    frequency = BASE ** (-2.0 * np.arange(HD // 2) / HD)
    angles = np.arange(length)[:, None].astype(np.float32) * frequency[None].astype(np.float32)
    key_cos = jnp.asarray(np.tile(np.cos(angles), (1, 4)).astype(np.float32))
    key_sin = np.concatenate([-np.sin(angles), np.sin(angles)] * 2, axis=1)
    key_sin = jnp.asarray(key_sin.astype(np.float32))
    places = jnp.asarray(np.arange(unit_len, dtype=np.int32))
    cosine, sine = key_cos, key_sin
    if copies > 1:
        places = unit * unit_len + places
        cosine = lax.dynamic_slice_in_dim(key_cos, unit * unit_len, unit_len, 0)
        sine = lax.dynamic_slice_in_dim(key_sin, unit * unit_len, unit_len, 0)

    def by_row4(m):
        return (0, m, 0, 0)

    def by_row3(m):
        return (m, 0, 0)

    def fixed(*_):
        return (0, 0)

    def zeros3(*_):
        return (0, 0, 0)

    def zeros4(*_):
        return (0, 0, 0, 0)

    def small_block(*_):
        return (0, 2)

    seg_keys = segments.astype(F32).reshape(micro, 1, length)
    seg_queries = seg_keys
    if copies > 1:
        seg_queries = lax.dynamic_slice_in_dim(seg_keys, unit * unit_len, unit_len, 2)
    skip = copies == 1
    place_row = places[None]
    attention_flops = 4.0 * micro * unit_len * length * 2 * LANES
    attention_specs = [
        pl.BlockSpec((1, unit_len, LANES), by_row3),
        pl.BlockSpec((1, length, LANES), by_row3),
        pl.BlockSpec((1, 1, unit_len), by_row3),
        pl.BlockSpec((1, 1, length), by_row3),
        pl.BlockSpec((1, unit_len), fixed),
    ]
    if copies == 1:
        normed_all, q_all, kv_all, ctx_heads, lse, dz_all, chosen_all = pl.pallas_call(
            attend_kernel,
            grid=(micro,),
            in_specs=[
                pl.BlockSpec((UNIT, 1, local_len, width), by_row4),
                pl.BlockSpec((width, LANES), small_block),
                pl.BlockSpec((width, 4 * HD), fixed),
                pl.BlockSpec((unit_len, LANES), fixed),
                pl.BlockSpec((unit_len, LANES), fixed),
            ]
            + attention_specs[2:]
            + [pl.BlockSpec(memory_space=pl.ANY)] * 2,
            out_specs=[
                pl.BlockSpec((UNIT, 1, local_len, width), by_row4),
                pl.BlockSpec((1, unit_len, LANES), by_row3),
                pl.BlockSpec((1, unit_len, LANES), by_row3),
                pl.BlockSpec((UNIT, 1, local_len, LANES), by_row4),
                pl.BlockSpec((1, 2, unit_len), by_row3),
                pl.BlockSpec(memory_space=pl.ANY),
                pl.BlockSpec(memory_space=pl.ANY),
            ],
            out_shape=[
                jax.ShapeDtypeStruct((UNIT, micro, local_len, width), BF16),
                jax.ShapeDtypeStruct((micro, unit_len, LANES), BF16),
                jax.ShapeDtypeStruct((micro, unit_len, LANES), BF16),
                jax.ShapeDtypeStruct((UNIT, micro, local_len, LANES), BF16),
                jax.ShapeDtypeStruct((micro, 2, unit_len), F32),
                jax.ShapeDtypeStruct((4, count, width), BF16),
                jax.ShapeDtypeStruct((E, 4 * count), BF16),
            ],
            scratch_shapes=[
                pltpu.VMEM((count, width), BF16),
                pltpu.VMEM((E, count), BF16),
                pltpu.SemaphoreType.DMA((9,)),
                pltpu.SemaphoreType.DMA((9,)),
                pltpu.SemaphoreType.DMA((2, 2)),
            ],
            compiler_params=params(collective_id=8, has_side_effects=True),
            cost_estimate=cost(attention_flops, 4e6),
        )(
            tok_all, heads_all, heads_all, cosine, sine, seg_queries, seg_keys, place_row, dz_own,
            chosen,
        )
    else:
        normed_all, q_all, kv_own = pl.pallas_call(
            project_kernel,
            grid=(micro,),
            in_specs=[
                pl.BlockSpec((UNIT, 1, local_len, width), by_row4),
                pl.BlockSpec((width, LANES), small_block),
                pl.BlockSpec((width, 4 * HD), fixed),
                pl.BlockSpec((unit_len, LANES), fixed),
                pl.BlockSpec((unit_len, LANES), fixed),
            ],
            out_specs=[
                pl.BlockSpec((UNIT, 1, local_len, width), by_row4),
                pl.BlockSpec((1, unit_len, LANES), by_row3),
                pl.BlockSpec((1, unit_len, LANES), by_row3),
            ],
            out_shape=[
                jax.ShapeDtypeStruct((UNIT, micro, local_len, width), BF16),
                jax.ShapeDtypeStruct((micro, unit_len, LANES), BF16),
                jax.ShapeDtypeStruct((micro, unit_len, LANES), BF16),
            ],
            compiler_params=params(),
            cost_estimate=cost(2.0 * UNIT * count * width * 4 * HD, 1.5e7),
        )(tok_all, heads_all, heads_all, cosine, sine)
        kv_all = lax.all_gather(kv_own, "seq", axis=1, tiled=True, axis_index_groups=copy_groups)
        ctx_heads, lse = pl.pallas_call(
            functools.partial(attention_kernel, skip),
            grid=(micro,),
            in_specs=attention_specs,
            out_specs=[
                pl.BlockSpec((UNIT, 1, local_len, LANES), by_row4),
                pl.BlockSpec((1, 2, unit_len), by_row3),
            ],
            out_shape=[
                jax.ShapeDtypeStruct((UNIT, micro, local_len, LANES), BF16),
                jax.ShapeDtypeStruct((micro, 2, unit_len), F32),
            ],
            compiler_params=params(),
            cost_estimate=cost(attention_flops, 4e6),
        )(q_all, kv_all, seg_queries, seg_keys, place_row)
        dz_all = jnp.stack([dz_own] + [flip(dz_own, k) for k in (2, 4, 6)])
        chosen_all = jnp.concatenate([chosen] + [flip(chosen, k) for k in (2, 4, 6)], axis=1)

    x_all, sib_first, mixed, normed_ffn, context = bridge(
        ctx_heads, own_first, w_out_all, flat_tokens, heads_all, 2
    )
    x_all = x_all.reshape(4 * count, width)
    dz_all = dz_all.reshape(4 * count, width)
    out_part, dx_part, gg_part, gates_all, total_first, w_heads = run_experts(
        "both", x_all, dz_all, chosen_all, (sib_first, own_first),
        router=heads_all,
    )

    def finish_expert(total):
        if copies > 1:
            total = repack(total)
            total = lax.psum_scatter(total, "row", scatter_dimension=0)
            total = lax.psum_scatter(
                total, "seq", scatter_dimension=0, axis_index_groups=copy_groups
            )
        else:
            total = lax.psum_scatter(total, "row", scatter_dimension=0)
        return total

    reduced_first = finish_expert(total_first)
    out_part, gate_acts, up_acts, *sib_second = run_experts(
        "forward", x_all, None, None, own_second, gates=gates_all, carried=out_part
    )
    out_split = out_part.reshape(4, count, width)
    dx_part, gg_part, total_second, out_back = run_experts(
        "backward", x_all, dz_all, None, (*sib_second, *own_second), gates=gates_all,
        carried=(dx_part, gg_part), acts=(gate_acts, up_acts), pushed=out_split,
    )
    reduced_second = finish_expert(total_second)
    do_heads, gmixed, out_pre, block_out = return_tokens(
        dx_part.reshape(4, count, width), gg_part, mixed, normed_ffn, dz_own, chosen, heads_all,
        w_out_all, context, out_split, out_back, micro, copies, 3,
    )
    if copies > 1:
        out_pre = lax.psum_scatter(
            out_pre, "seq", scatter_dimension=1, axis_index_groups=copy_groups
        )
    out_pre = out_pre.reshape(4, rows, part, width + LANES)
    graw, head_term, out_in, exchanged = pl.pallas_call(
        functools.partial(attention_back_kernel, skip),
        grid=(micro,),
        in_specs=attention_specs
        + [
            pl.BlockSpec((1, 2, unit_len), by_row3),
            pl.BlockSpec((UNIT, 1, local_len, LANES), by_row4),
            pl.BlockSpec((unit_len, LANES), fixed),
            pl.BlockSpec((unit_len, LANES), fixed),
            pl.BlockSpec((length, LANES), fixed),
            pl.BlockSpec((length, LANES), fixed),
            pl.BlockSpec((UNIT, 1, local_len, width), by_row4),
            pl.BlockSpec(memory_space=pl.ANY),
            pl.BlockSpec(memory_space=pl.ANY),
        ],
        out_specs=[
            pl.BlockSpec((seq_size, 1, local_len, 2 * LANES), by_row4),
            pl.BlockSpec((PIECES, UNIT, ROWS_IN, 2 * LANES), zeros4),
            pl.BlockSpec(memory_space=pl.ANY),
            pl.BlockSpec(memory_space=pl.ANY),
        ],
        out_shape=[
            jax.ShapeDtypeStruct((seq_size, micro, local_len, 2 * LANES), BF16),
            jax.ShapeDtypeStruct((PIECES, UNIT, ROWS_IN, 2 * LANES), BF16),
            jax.ShapeDtypeStruct((3,) + out_pre.shape[1:], BF16),
            jax.ShapeDtypeStruct(reduced_first.shape, BF16),
        ],
        scratch_shapes=[
            pltpu.VMEM((length, LANES), F32),
            pltpu.VMEM((length, LANES), F32),
            pltpu.VMEM((width, 2 * LANES), F32),
            pltpu.VMEM(reduced_first.shape[1:], BF16),
            pltpu.SemaphoreType.DMA((UNIT + 2,)),
            pltpu.SemaphoreType.DMA((UNIT + 2,)),
            pltpu.SemaphoreType.DMA((2,)),
        ],
        compiler_params=params(collective_id=7, has_side_effects=True),
        cost_estimate=cost(2.5 * attention_flops, 8e6),
    )(
        q_all, kv_all, seg_queries, seg_keys, place_row, lse, do_heads,
        cosine, sine, key_cos, key_sin, normed_all, out_pre, reduced_first,
    )
    if copies > 1:
        graw_kv = lax.psum_scatter(
            graw[..., LANES:], "seq", scatter_dimension=0, tiled=True,
            axis_index_groups=copy_groups,
        )
        graw = jnp.concatenate([graw[:UNIT, ..., :LANES], graw_kv], axis=3)
        head_term = jnp.einsum(
            "nd,nh->dh",
            normed_all.reshape(UNIT * count, width),
            graw.reshape(UNIT * count, 2 * LANES),
            preferred_element_type=F32,
        ).astype(BF16)
        head_term = head_term.reshape(copies, UNIT, rows, part, 2 * LANES)
        head_term = lax.psum_scatter(
            head_term, "seq", scatter_dimension=0, axis_index_groups=copy_groups
        ).transpose(1, 0, 2, 3)
    head_grad, exchanged_second, out_grad, grad_input = finish(
        rows, graw, head_term, reduced_second, out_pre, out_in, w_heads, flat_tokens, heads_all,
        gmixed, 4,
    )
    if copies == 1:
        like = jax.ShapeDtypeStruct
        (
            grad_norm_attn, grad_query, grad_key, grad_value, grad_out, grad_norm_ffn, grad_router,
            grad_gate, grad_up, grad_down,
        ) = pl.pallas_call(
            unpack_grads_kernel,
            out_shape=[
                like((1, part), F32), like(w_query.shape, F32), like(w_key.shape, F32),
                like(w_value.shape, F32), like(w_out.shape, F32), like((1, part), F32),
                like(w_router.shape, F32), like(w_gate.shape, F32), like(w_up.shape, F32),
                like(w_down.shape, F32),
            ],
            compiler_params=params(),
            cost_estimate=cost(1, 1e7),
        )(
            exchanged, exchanged_second, head_grad, out_grad, w_gate, w_up, w_query, w_key, w_value,
            w_router, norm_attn[None], norm_ffn[None],
        )
        grad_norm_attn = grad_norm_attn.reshape(part)
        grad_norm_ffn = grad_norm_ffn.reshape(part)
    else:
        finished = [exchanged, exchanged_second]
        finished = jnp.stack(finished, axis=1).reshape(E, 3 * part, hidden).astype(F32)
        grad_gate = finished[:, :part]
        grad_up = finished[:, part : 2 * part]
        grad_down = finished[:, 2 * part :].reshape(E, 2, -1, hidden).transpose(0, 2, 1, 3)
        grad_down = grad_down.reshape(E, -1, width)
        head_grad = head_grad.astype(F32)
        grad_query = head_grad[:, :, :LANES].transpose(1, 0, 2).reshape(part, H * HD)
        grad_key = head_grad[:, :, LANES : LANES + HD].transpose(1, 0, 2).reshape(part, KVH * HD)
        grad_value = head_grad[:, :, LANES + HD :].transpose(1, 0, 2).reshape(part, KVH * HD)
        grad_out = out_grad[:, :width]
        grad_router = out_grad[:, width : width + E]

        attn_weights = jnp.concatenate([w_query, w_key, w_value], axis=1).astype(F32)
        attn_grads = jnp.concatenate([grad_query, grad_key, grad_value], axis=1)
        grad_norm_attn = jnp.sum(attn_weights * attn_grads, axis=1) / norm_attn.astype(F32)
        grad_norm_ffn = (
            jnp.sum(w_gate.astype(F32) * grad_gate, axis=(0, 2))
            + jnp.sum(w_up.astype(F32) * grad_up, axis=(0, 2))
            + jnp.sum(w_router.astype(F32) * grad_router, axis=1)
        ) / norm_ffn.astype(F32)
    return (
        block_out.reshape(tokens.shape),
        grad_input.reshape(tokens.shape),
        grad_norm_attn,
        grad_query,
        grad_key,
        grad_value,
        grad_out,
        grad_norm_ffn,
        grad_router,
        grad_gate,
        grad_up,
        grad_down,
    )


def solution(mesh):
    both = ("seq", "row")
    body = functools.partial(shards, mesh.shape["seq"] // UNIT, rows=mesh.shape["row"])
    return jax.shard_map(
        body,
        mesh=mesh,
        in_specs=(
            P("row", "seq", None),
            P("row", None),
            P("row", "seq", None),
            P("row", "seq", None),
            P(both),
            P(both, None),
            P(both, None),
            P(both, None),
            P(both, None),
            P(both),
            P(both, None),
            P(None, both, None),
            P(None, both, None),
            P(None, both, None),
        ),
        out_specs=(
            P("row", "seq", None),
            P("row", "seq", None),
            P(both),
            P(both, None),
            P(both, None),
            P(both, None),
            P(both, None),
            P(both),
            P(both, None),
            P(None, both, None),
            P(None, both, None),
            P(None, both, None),
        ),
        check_vma=False,
    )
```

```python
import functools

import jax
import jax.numpy as jnp
import numpy as np
from jax import lax
from jax.experimental import pallas as pl
from jax.experimental.pallas import tpu as pltpu
from jax.sharding import PartitionSpec as P

H = 16
KVH = 8
TOPK = 8
HD = 64
E = 16
UNIT = 8
LANES = 128
QBLOCK = 256
PIECES = 4
ROWS_IN = 32
ROWS_OUT = 16

EPS = 1e-05
BASE = 10000.0
NEGATIVE = -1e30
F32 = jnp.float32
BF16 = jnp.bfloat16
VMEM_LIMIT = 60 * 1024 * 1024


def dot_nn(left, right):
    return lax.dot_general(left, right, (((1,), (0,)), ((), ())), preferred_element_type=F32)


def dot_nt(left, right):
    return lax.dot_general(left, right, (((1,), (1,)), ((), ())), preferred_element_type=F32)


def dot_tn(left, right):
    return lax.dot_general(left, right, (((0,), (0,)), ((), ())), preferred_element_type=F32)


def params(**kw):
    return pltpu.CompilerParams(vmem_limit_bytes=VMEM_LIMIT, **kw)


def cost(flops, nbytes):
    return pl.CostEstimate(flops=int(flops), bytes_accessed=int(nbytes), transcendentals=0)


def neighbours(seq):
    core = seq % 2
    chip = (seq // 2) % 4
    base = seq - seq % UNIT

    def at(other, same=True):
        return base + 2 * other + (core if same else 1 - core)

    across = chip + 1 - 2 * (chip % 2)
    along = (chip + 2) % 4
    return at(across), at(along), at(3 - chip), at(chip, False)


def greet(targets):
    barrier = pltpu.get_barrier_semaphore()
    for target in targets:
        pl.semaphore_signal(
            barrier, inc=1, device_id=target, device_id_type=pl.DeviceIdType.MESH
        )
    pl.semaphore_wait(barrier, len(targets))


class Pushes:
    def __init__(self, send, recv):
        self.send, self.recv, self.used = send, recv, 0

    def start(self, source, target, device):
        copy = self.make(source, target, device)
        copy.start()
        return copy

    def make(self, source, target, device):
        n = self.used
        self.used += 1
        return pltpu.make_async_remote_copy(
            src_ref=source,
            dst_ref=target,
            send_sem=self.send.at[n],
            recv_sem=self.recv.at[n],
            device_id=device,
            device_id_type=pl.DeviceIdType.MESH,
        )


class Late:
    def __init__(self, places):
        self.places = places

    def specs(self, count):
        return [pl.BlockSpec(memory_space=pl.ANY)] * count

    def scratch(self):
        buffers = [pltpu.VMEM(shape, kind) for _, shape, kind, _ in self.places]
        return buffers + [pltpu.SemaphoreType.DMA((len(self.places),))]

    def wrap(self, kernel, count):
        def wrapped(*refs):
            extra = len(self.places) + 1
            ins, rest = list(refs[:count]), refs[count:-extra]
            *buffers, sems = refs[-extra:]
            copies = []
            for n, (place, _, _, view) in enumerate(self.places):
                source = ins[place] if view is None else view(ins[place])
                copies.append(pltpu.make_async_copy(source, buffers[n], sems.at[n]))
                copies[n].start()
                ins[place] = buffers[n]

            def ready():
                for copy in copies:
                    copy.wait()

            kernel(ready, *ins, *rest)

        return wrapped


def small_view(ref):
    return ref.at[:, pl.ds(2 * LANES, LANES)]


class Bounce:
    def __init__(self, source, middle, target, sems, start=True):
        self.inward = pltpu.make_async_copy(source, middle, sems.at[0])
        self.outward = pltpu.make_async_copy(middle, target, sems.at[1])
        if start:
            self.inward.start()

    def turn(self):
        self.inward.wait()
        self.outward.start()

    def wait(self):
        self.outward.wait()


def pack_kernel_inputs(
    gate_ref, up_ref, down_ref, query_ref, key_ref, value_ref, router_ref, attn_ref, ffn_ref,
    packed, head_ref, gains,
):
    part, hidden = gate_ref.shape[1:]
    half = part // 2
    for n in range(2):
        for b in range(UNIT):
            e = 2 * b + n
            packed[n, b, :part] = gate_ref[e]
            packed[n, b, part : 2 * part] = up_ref[e]
            for c in range(2):
                start = 2 * part + c * half
                packed[n, b, start : start + half] = down_ref[e, :, c * hidden : (c + 1) * hidden]
    gains[...] = jnp.zeros_like(gains)
    gains[:E, :part] = router_ref[...].astype(F32)
    gains[E : E + 1, :part] = attn_ref[...].astype(F32)
    gains[E + 1 : E + 2, :part] = ffn_ref[...].astype(F32)
    small = gains[...].T[:part].astype(BF16)
    low = lane_iota((part, LANES)) < HD
    for pair in range(UNIT // 2):
        lanes = slice(pair * LANES, (pair + 1) * LANES)
        key = key_ref[:, lanes].astype(F32)
        value = value_ref[:, lanes].astype(F32)
        even = jnp.where(low, key, pltpu.roll(value, HD, 1)).astype(BF16)
        odd = jnp.where(low, pltpu.roll(key, HD, 1), value).astype(BF16)
        for b, mixed in ((2 * pair, even), (2 * pair + 1, odd)):
            head_ref[b, :, :LANES] = query_ref[:, b * LANES : (b + 1) * LANES]
            head_ref[b, :, LANES : 2 * LANES] = mixed
            head_ref[b, :, 2 * LANES :] = small


def begin_kernel(rows, raw, *refs):
    inputs, refs = refs[:raw], refs[raw:]
    wout_ref, mine0, mine1, mine2, head_all, wout_all, wout_mid, *refs = refs
    if raw > 2:
        head_mine, packed, head_ref, gains, send, recv, local = refs
    else:
        (packed, head_ref), (head_mine, send, recv, local) = inputs, refs
    seq, row = lax.axis_index("seq"), lax.axis_index("row")
    me = seq % UNIT
    base = seq - me
    unit = [(me + k) % UNIT for k in range(1, UNIT)]
    column = [(row + k) % rows for k in range(1, rows)]
    greet([{"seq": base + b} for b in unit] + [{"row": r} for r in column])
    pushes = Pushes(send, recv)
    outs = [pushes.start(wout_ref, wout_mid.at[row], {"row": r}) for r in column]
    kept = pltpu.make_async_copy(wout_ref, wout_mid.at[row], local.at[4])
    kept.start()
    if raw > 2:
        pack_kernel_inputs(*inputs, packed, head_ref, gains)
    inner = mine1.shape[1]
    upper, lower = pl.ds(0, inner), pl.ds(inner, mine2.shape[1])
    first = pltpu.make_async_copy(head_ref.at[me], head_mine.at[me], local.at[0])
    own = [
        pltpu.make_async_copy(packed.at[0, me], mine0.at[me], local.at[1]),
        pltpu.make_async_copy(packed.at[1, me, upper], mine1.at[me], local.at[2]),
        pltpu.make_async_copy(packed.at[1, me, lower], mine2.at[me], local.at[3]),
    ]
    first.start()
    heads = [pushes.start(head_ref.at[b], head_mine.at[me], {"seq": base + b}) for b in unit]
    others = []
    for source, target in (
        (lambda b: packed.at[0, b], mine0),
        (lambda b: packed.at[1, b, upper], mine1),
        (lambda b: packed.at[1, b, lower], mine2),
    ):
        others += [pushes.start(source(b), target.at[me], {"seq": base + b}) for b in unit]
    for copy in own:
        copy.start()
    first.wait()
    for copy in heads:
        copy.wait_recv()
    last = pltpu.make_async_copy(head_mine, head_all.at[:, row], local.at[5])
    last.start()
    others += [pushes.start(head_mine, head_all.at[:, row], {"row": r}) for r in column]
    kept.wait()
    for copy in outs:
        copy.wait_recv()
    own.append(pltpu.make_async_copy(wout_mid, wout_all.at[me], local.at[6]))
    own[-1].start()
    across, along, _, twin = neighbours(seq)
    a, b, d = across - base, along - base, 6 - me + 2 * (me % 2)
    half = rows // 2
    top, low = pl.ds(0, half), pl.ds(half, rows - half)

    def own_part(part, device):
        return pushes.start(wout_mid.at[part], wout_all.at[me, part], {"seq": device})

    def passed(slot, part, device):
        view = wout_all.at[slot, part]
        others.append(pushes.start(view, view, {"seq": device}))
        return others[-1]

    xa, yb, xb, ya = (
        own_part(top, across), own_part(low, along), own_part(low, across), own_part(top, along)
    )
    others += [own_part(top, twin), own_part(low, twin)]
    xa.wait_recv()
    da = passed(a, top, along)
    passed(a, top, twin)
    yb.wait_recv()
    db = passed(b, low, across)
    passed(b, low, twin)
    xb.wait_recv()
    passed(a, low, twin)
    ya.wait_recv()
    passed(b, top, twin)
    da.wait_recv()
    passed(d, top, twin)
    db.wait_recv()
    passed(d, low, twin)
    others = [copy for copy in others if copy is not da and copy is not db]
    for copy in heads + outs + [xa, yb, xb, ya, da, db]:
        copy.wait_send()
    for copy in own + [last]:
        copy.wait()
    for copy in others:
        copy.wait()


def begin(rows, part, hidden, inputs, w_out):
    any_spec = pl.BlockSpec(memory_space=pl.ANY)
    vmem_spec = pl.BlockSpec(memory_space=pltpu.VMEM)
    count = 4 * (UNIT - 1) + 2 * (rows - 1) + 14
    like = jax.ShapeDtypeStruct
    deep, inner = 3 * part, 2 * part
    head_shape = (UNIT, part, 4 * HD + LANES)
    built = [
        pltpu.VMEM((2, UNIT, deep, hidden), BF16),
        pltpu.VMEM(head_shape, BF16),
        pltpu.VMEM((LANES, LANES), F32),
    ]
    return pl.pallas_call(
        functools.partial(begin_kernel, rows, len(inputs)),
        in_specs=[vmem_spec] * (len(inputs) + 1),
        out_specs=[any_spec] * 5,
        out_shape=[
            like((UNIT, deep, hidden), BF16),
            like((UNIT, inner, hidden), BF16),
            like((UNIT, deep - inner, hidden), BF16),
            like((UNIT, rows) + head_shape[1:], BF16),
            like((UNIT, rows) + w_out.shape, BF16),
        ],
        scratch_shapes=[pltpu.VMEM((rows,) + w_out.shape, BF16), pltpu.VMEM(head_shape, BF16)]
        + (built if len(inputs) > 2 else [])
        + [
            pltpu.SemaphoreType.DMA((count,)),
            pltpu.SemaphoreType.DMA((count,)),
            pltpu.SemaphoreType.DMA((7,)),
        ],
        compiler_params=params(collective_id=0, has_side_effects=True),
        cost_estimate=cost(1, 2e7),
    )(*inputs, w_out)


def unit_gather_kernel(sources, *refs):
    ins, outs = refs[:sources], refs[sources : 2 * sources]
    middles = refs[2 * sources : 3 * sources]
    send, recv, local = refs[3 * sources :]
    seq = lax.axis_index("seq")
    me = seq % UNIT
    base = seq - me
    across, along, _, twin = neighbours(seq)
    a, b, t = across - base, along - base, twin - base
    d = UNIT - 1 - me + 2 * (me % 2) - 1
    greet([{"seq": across}, {"seq": along}, {"seq": twin}])
    pushes = Pushes(send, recv)
    own, done, stage = [], [], []
    for n, (source, target) in enumerate(zip(ins, outs)):
        half = source.shape[0] // 2
        halves = [pl.ds(0, half), pl.ds(half, half)]
        own.append(Bounce(source, middles[n], target.at[me], local.at[n]))

        def part(device, h, source=source, target=target, halves=halves):
            return pushes.start(
                source.at[halves[h]], target.at[me, halves[h]], {"seq": device}
            )

        xa, yb = part(across, 0), part(along, 1)
        xb, ya = part(across, 1), part(along, 0)
        done.append(pushes.start(source, target.at[me], {"seq": twin}))
        stage.append((target, halves, xa, yb, xb, ya))
    for copy in own:
        copy.turn()
    for target, halves, xa, yb, xb, ya in stage:

        def pass_on(slot, h, device, target=target, halves=halves):
            view = target.at[slot, halves[h]]
            return pushes.start(view, view, {"seq": device})

        xa.wait_recv()
        da = pass_on(a, 0, along)
        done.append(pass_on(a, 0, twin))
        yb.wait_recv()
        db = pass_on(b, 1, across)
        done.append(pass_on(b, 1, twin))
        xb.wait_recv()
        done.append(pass_on(a, 1, twin))
        ya.wait_recv()
        done.append(pass_on(b, 0, twin))
        da.wait_recv()
        done.append(pass_on(d, 0, twin))
        db.wait_recv()
        done.append(pass_on(d, 1, twin))
        for copy in (xa, yb, xb, ya, da, db):
            copy.wait_send()
    for copy in own + done:
        copy.wait()


def unit_gather(sources, collective):
    any_spec = pl.BlockSpec(memory_space=pl.ANY)
    n = len(sources)
    return pl.pallas_call(
        functools.partial(unit_gather_kernel, n),
        in_specs=[any_spec] * n,
        out_specs=[any_spec] * n,
        out_shape=[jax.ShapeDtypeStruct((UNIT,) + x.shape, x.dtype) for x in sources],
        scratch_shapes=[pltpu.VMEM(x.shape, x.dtype) for x in sources]
        + [
            pltpu.SemaphoreType.DMA((13 * n,)),
            pltpu.SemaphoreType.DMA((13 * n,)),
            pltpu.SemaphoreType.DMA((n, 2)),
        ],
        compiler_params=params(collective_id=collective, has_side_effects=True),
        cost_estimate=cost(1, 8e7),
    )(*sources)


def bridge_kernel(
    micro, ready, ctx_ref, weights, w_ref, tok_ref, small_ref,
    target, flipped, mixed_ref, normed_ref, ctx_out,
    ctx_in, send, recv, local,
):
    seq = lax.axis_index("seq")
    me = seq % UNIT
    base = seq - me
    unit = [(me + k) % UNIT for k in range(1, UNIT)]
    across, along, _, twin = neighbours(seq)
    greet([{"seq": base + b} for b in unit])
    pushes = Pushes(send, recv)
    arrivals = [
        [pushes.start(ctx_ref.at[b, m], ctx_in.at[me, m], {"seq": base + b}) for b in unit]
        for m in range(micro)
    ]
    mine = pltpu.make_async_copy(ctx_ref.at[me], ctx_in.at[me], local.at[0])
    mine.start()
    turned = pushes.start(weights, flipped, {"seq": twin})
    count, width = tok_ref.shape
    step = count // micro
    half = step // 2
    ready()
    gain = gain_row(small_ref[...], E + 1)
    mine.wait()
    sent = []

    def forward(m):
        top, low = pl.ds(m * step, half), pl.ds(m * step + half, half)
        xa, yb, xb, ya = sent[m]
        xa.wait_recv()
        da = pushes.start(target.at[1, top], target.at[3, top], {"seq": along})
        yb.wait_recv()
        db = pushes.start(target.at[2, low], target.at[3, low], {"seq": across})
        sent[m] = (xa, yb, xb, ya, da, db)

    for m in range(micro):
        here = slice(m * step, (m + 1) * step)
        for copy in arrivals[m]:
            copy.wait_recv()
        for b in range(UNIT):
            ctx_out[here, b * LANES : (b + 1) * LANES] = ctx_in[b, m]
        mixed = tok_ref[here].astype(F32) + dot_nn(ctx_out[here], w_ref[...])
        mixed_ref[here] = mixed
        inverse = lax.rsqrt(jnp.mean(mixed * mixed, axis=-1, keepdims=True) + EPS)
        normed_ref[here] = (mixed * inverse * gain).astype(BF16)
        top, low = pl.ds(m * step, half), pl.ds(m * step + half, half)
        sent.append(
            (
                pushes.start(normed_ref.at[top], target.at[1, top], {"seq": across}),
                pushes.start(normed_ref.at[low], target.at[2, low], {"seq": along}),
                pushes.start(normed_ref.at[low], target.at[1, low], {"seq": across}),
                pushes.start(normed_ref.at[top], target.at[2, top], {"seq": along}),
            )
        )
        if m > 0:
            forward(m - 1)
    last = pltpu.make_async_copy(normed_ref, target.at[0], local.at[1])
    last.start()
    forward(micro - 1)
    for group in sent:
        for copy in group[2:]:
            copy.wait_recv()
        for copy in group:
            copy.wait_send()
    for group in arrivals:
        for copy in group:
            copy.wait_send()
    turned.wait()
    last.wait()


def bridge(ctx_heads, weights, w_out, tokens, heads, collective):
    any_spec = pl.BlockSpec(memory_space=pl.ANY)
    like = jax.ShapeDtypeStruct
    count, width = tokens.shape
    micro = ctx_heads.shape[1]
    pushes = (UNIT - 1) * micro + 6 * micro + 1

    def fixed(i):
        return (0, 0)

    late = Late(
        [
            (2, w_out.shape, BF16, None),
            (3, tokens.shape, BF16, None),
            (4, (width, LANES), BF16, small_view),
        ]
    )

    return pl.pallas_call(
        late.wrap(functools.partial(bridge_kernel, micro), 5),
        grid=(1,),
        in_specs=late.specs(5),
        out_specs=[any_spec] * 2 + [pl.BlockSpec((count, width), fixed)] * 3,
        out_shape=[
            like((4, count, width), BF16),
            like(weights.shape, BF16),
            like((count, width), F32),
            like((count, width), BF16),
            like((count, H * HD), BF16),
        ],
        scratch_shapes=[
            pltpu.VMEM(ctx_heads.shape, BF16),
            pltpu.SemaphoreType.DMA((pushes,)),
            pltpu.SemaphoreType.DMA((pushes,)),
            pltpu.SemaphoreType.DMA((2,)),
        ]
        + late.scratch(),
        compiler_params=params(collective_id=collective, has_side_effects=True),
        cost_estimate=cost(2.0 * count * width * width, 8e7),
    )(ctx_heads, weights, w_out, tokens, heads)


def finish_kernel(
    rows, ready, graw_ref, head_ref, red_ref, pre_ref, out_ref, w_ref, own_ref, tok_ref, small_ref, gmixed_ref,
    head_fin, red_out, out_fin, gin_ref,
    head_col, head_sum, out_sum, out_col, raw_in, red_own, send, recv, local,
):
    seq, row = lax.axis_index("seq"), lax.axis_index("row")
    me = seq % UNIT
    base = seq - me
    unit = [(me + k) % UNIT for k in range(1, UNIT)]
    senders = [(me + UNIT - k) % UNIT for k in range(1, UNIT)]
    column = [(row + k) % rows for k in range(1, rows)]
    greet([{"seq": base + b} for b in unit] + [{"row": r} for r in column])
    pushes = Pushes(send, recv)
    first = pltpu.make_async_copy(head_ref.at[row], head_col.at[row], local.at[0, 0])
    first.start()
    second = pltpu.make_async_copy(graw_ref.at[me], raw_in.at[me], local.at[1, 0])
    second.start()
    heads = [pushes.start(head_ref.at[r], head_col.at[row], {"row": r}) for r in column]
    raws = [pushes.start(graw_ref.at[b], raw_in.at[me], {"seq": base + b}) for b in unit]
    others = [pushes.start(red_ref.at[b], red_out.at[me], {"seq": base + b}) for b in unit]
    bounce = Bounce(red_ref.at[me], red_own, red_out.at[me], local.at[4])
    ready()
    total = pre_ref[me // 2].astype(F32)
    for n in range(3):
        total = total + out_ref[n].astype(F32)
    out_sum[...] = total.astype(BF16)
    bounce.turn()
    third = pltpu.make_async_copy(out_sum.at[row], out_col.at[row], local.at[2, 0])
    third.start()
    outs = [pushes.start(out_sum.at[r], out_col.at[row], {"row": r}) for r in column]
    first.wait()
    for copy in heads:
        copy.wait_recv()
    total = head_col[0].astype(F32)
    for r in range(1, rows):
        total = total + head_col[r].astype(F32)
    head_sum[...] = total.astype(BF16)
    fourth = pltpu.make_async_copy(head_sum.at[me], head_fin.at[me], local.at[3, 0])
    fourth.start()
    others += [pushes.start(head_sum.at[b], head_fin.at[me], {"seq": base + b}) for b in unit]
    count, width = tok_ref.shape
    second.wait()
    acc = dot_nt(raw_in[me].reshape(count, 2 * LANES), own_ref[...])
    for b, copy in zip(senders, raws):
        copy.wait_recv()
        acc = acc + dot_nt(raw_in[b].reshape(count, 2 * LANES), w_ref[b])
    v = tok_ref[...].astype(F32)
    inverse = lax.rsqrt(jnp.mean(v * v, axis=-1, keepdims=True) + EPS)
    scaled = acc * gain_row(small_ref[...], E)
    mean = jnp.mean(scaled * v, axis=-1, keepdims=True)
    grad = gmixed_ref[...] + scaled * inverse - v * (inverse * inverse * inverse * mean)
    gin_ref[...] = grad.astype(BF16)
    third.wait()
    for copy in outs:
        copy.wait_recv()
    total = out_col[0].astype(F32)
    for r in range(1, rows):
        total = total + out_col[r].astype(F32)
    out_fin[...] = total
    for copy in heads + outs + raws:
        copy.wait_send()
    fourth.wait()
    bounce.wait()
    for copy in others:
        copy.wait()


def finish(
    rows, graw, head_term, reduced, pre, out_in, w_heads, tokens, heads, gmixed, collective
):
    any_spec = pl.BlockSpec(memory_space=pl.ANY)
    like = jax.ShapeDtypeStruct
    pushes = 3 * (UNIT - 1) + 2 * (rows - 1)
    count, width = tokens.shape

    def fixed(i):
        return (0, 0)

    late = Late(
        [
            (3, pre.shape, BF16, None),
            (4, out_in.shape, BF16, None),
            (5, w_heads.shape, BF16, None),
            (6, (width, 4 * HD), BF16, lambda ref: ref.at[:, pl.ds(0, 4 * HD)]),
            (7, tokens.shape, BF16, None),
            (8, (width, LANES), BF16, small_view),
            (9, gmixed.shape, F32, None),
        ]
    )

    return pl.pallas_call(
        late.wrap(functools.partial(finish_kernel, rows), 10),
        grid=(1,),
        in_specs=late.specs(10),
        out_specs=[
            any_spec,
            any_spec,
            pl.BlockSpec(pre.shape[2:], fixed),
            pl.BlockSpec(tokens.shape, fixed),
        ],
        out_shape=[
            like(head_term.shape[1:], BF16),
            like(reduced.shape, BF16),
            like(pre.shape[2:], F32),
            like(tokens.shape, BF16),
        ],
        scratch_shapes=[
            pltpu.VMEM(head_term.shape, BF16),
            pltpu.VMEM(head_term.shape[1:], BF16),
            pltpu.VMEM(pre.shape[1:], BF16),
            pltpu.VMEM(pre.shape[1:], BF16),
            pltpu.VMEM(graw.shape, BF16),
            pltpu.VMEM(reduced.shape[1:], BF16),
            pltpu.SemaphoreType.DMA((pushes,)),
            pltpu.SemaphoreType.DMA((pushes,)),
            pltpu.SemaphoreType.DMA((5, 2)),
        ]
        + late.scratch(),
        compiler_params=params(collective_id=collective, has_side_effects=True),
        cost_estimate=cost(4.0 * count * width * width, 6e7),
    )(graw, head_term, reduced, pre, out_in, w_heads, heads, tokens, heads, gmixed)


def lane_iota(shape):
    return lax.broadcasted_iota(jnp.int32, shape, len(shape) - 1)


def turn(u, cosine, sine):
    low_half = lane_iota(u.shape) % HD < HD // 2
    partner = jnp.where(
        low_half, pltpu.roll(u, LANES - HD // 2, u.ndim - 1), pltpu.roll(u, HD // 2, u.ndim - 1)
    )
    return u * cosine + partner * sine


def value_tables(cosine, sine):
    low = lane_iota(cosine.shape) < HD
    return jnp.where(low, cosine, 1.0), jnp.where(low, sine, 0.0)


def gain_row(small, lane):
    return small.astype(F32).T[lane : lane + 1]


def project_kernel(tok_ref, small_ref, w_ref, cos_ref, sin_ref, normed_ref, q_ref, kv_ref):
    count = q_ref.shape[1]
    width = w_ref.shape[0]
    x = tok_ref[...].reshape(count, width).astype(F32)
    inverse = lax.rsqrt(jnp.mean(x * x, axis=-1, keepdims=True) + EPS)
    normed = (x * inverse * gain_row(small_ref[...], E)).astype(BF16)
    normed_ref[...] = normed.reshape(normed_ref.shape)
    raw = dot_nn(normed, w_ref[...])
    cosine, sine = cos_ref[...], sin_ref[...]
    q = turn(raw[:, :LANES], cosine, sine).astype(BF16)
    q_ref[0] = (q.astype(F32) * HD**-0.5).astype(BF16)
    kv_ref[0] = turn(raw[:, LANES:], *value_tables(cosine, sine)).astype(BF16)


def pair_keys(kv):
    kv = kv.astype(F32)
    rolled = pltpu.roll(kv, HD, 1)
    low = lane_iota(kv.shape) < HD
    return jnp.where(low, kv, rolled), jnp.where(low, rolled, kv)


def bias_block(seg_col, seg_row, q_places, first, length):
    key_places = lax.broadcasted_iota(jnp.int32, (length, q_places.shape[1]), 0)
    allowed = (seg_col[:length] == seg_row) & (key_places <= q_places)
    return jnp.where(allowed, 0.0, NEGATIVE)


def attention_kernel(skip, q_ref, kv_ref, segq_ref, segk_ref, place_ref, ctx_ref, lse_ref):
    length = kv_ref.shape[1]
    queries = q_ref.shape[1]
    kk, vv = pair_keys(kv_ref[0])
    v_t = vv.T.astype(BF16)[:HD]
    kk = kk.astype(BF16)
    seg_col = jnp.broadcast_to(segk_ref[0], (8, length)).T[:, :1]
    for block in range(queries // QBLOCK):
        here = slice(block * QBLOCK, (block + 1) * QBLOCK)
        keys = (block + 1) * QBLOCK if skip else length
        bias = bias_block(seg_col, segq_ref[0][:, here], place_ref[:, here], 0, keys)
        q = q_ref[0, here, :]
        low = lane_iota(q.shape) < HD
        parts = []
        for head in range(2):
            mine = jnp.where(low == (head == 0), q, jnp.zeros_like(q))
            scores = dot_nt(kk[:keys], mine) + bias
            top = jnp.max(scores, axis=0, keepdims=True)
            weight = jnp.exp(scores - top)
            total = jnp.sum(weight, axis=0, keepdims=True)
            prob = (weight * (1.0 / total)).astype(BF16)
            parts.append(dot_nn(v_t[:, :keys], prob))
            lse_ref[0, head : head + 1, here] = top + jnp.log(total)
        ctx = jnp.concatenate(parts, axis=0).T.astype(BF16)
        per = QBLOCK // LANES
        ctx_ref[block * per : (block + 1) * per, 0] = ctx.reshape(per, LANES, LANES)


def attend_kernel(
    tok_ref, small_ref, w_ref, cos_ref, sin_ref, segq_ref, segk_ref, place_ref, z_ref, c_ref,
    normed_ref, q_ref, kv_ref, ctx_ref, lse_ref, z_all, c_all,
    z_middle, c_middle, send, recv, local,
):
    m = pl.program_id(0)
    across, along, far, _ = neighbours(lax.axis_index("seq"))
    pushes = Pushes(send, recv)
    count = z_ref.shape[0]
    half = count // 2
    top, low = pl.ds(0, half), pl.ds(half, half)
    first = [
        pushes.make(z_ref.at[top], z_all.at[1, top], {"seq": across}),
        pushes.make(z_ref.at[low], z_all.at[2, low], {"seq": along}),
        pushes.make(z_ref.at[low], z_all.at[1, low], {"seq": across}),
        pushes.make(z_ref.at[top], z_all.at[2, top], {"seq": along}),
    ]
    for n, peer in enumerate((across, along, far)):
        place = pl.ds((n + 1) * count, count)
        first.append(pushes.make(c_ref, c_all.at[:, place], {"seq": peer}))
    second = [
        pushes.make(z_all.at[1, top], z_all.at[3, top], {"seq": along}),
        pushes.make(z_all.at[2, low], z_all.at[3, low], {"seq": across}),
    ]
    bounces = [
        Bounce(z_ref, z_middle, z_all.at[0], local.at[0], False),
        Bounce(c_ref, c_middle, c_all.at[:, pl.ds(0, count)], local.at[1], False),
    ]

    @pl.when(m == 0)
    def _():
        greet([{"seq": across}, {"seq": along}, {"seq": far}])
        for copy in first[:2] + first[4:]:
            copy.start()
        for copy in bounces:
            copy.inward.start()
        for copy in bounces:
            copy.turn()

    project_kernel(tok_ref, small_ref, w_ref, cos_ref, sin_ref, normed_ref, q_ref, kv_ref)

    @pl.when(m == 1)
    def _():
        for copy, onward in zip(first, second):
            copy.wait_recv()
            onward.start()

    attention_kernel(True, q_ref, kv_ref, segq_ref, segk_ref, place_ref, ctx_ref, lse_ref)

    @pl.when(m == 0)
    def _():
        for copy in first[2:4]:
            copy.start()

    @pl.when(m == pl.num_programs(0) - 1)
    def _():
        for copy in first[2:] + second:
            copy.wait_recv()
        for copy in first + second:
            copy.wait_send()
        for copy in bounces:
            copy.wait()


def attention_back_kernel(
    skip, q_ref, kv_ref, segq_ref, segk_ref, place_ref, lse_ref, do_ref, cosq_ref, sinq_ref,
    cosk_ref, sink_ref, normed_ref, pre_ref, red_ref, graw_ref, term_ref, pre_in, red_out,
    dk_acc, dv_acc, term_acc, red_own, send, recv, local,
):
    seq = lax.axis_index("seq")
    me = seq % UNIT
    base = seq - me
    unit = [(me + k) % UNIT for k in range(1, UNIT)]
    pushes = Pushes(send, recv)
    sides = []
    for n, peer in enumerate(neighbours(seq)[:3]):
        sides.append(pushes.make(pre_ref.at[(peer - base) // 2], pre_in.at[n], {"seq": peer}))
    for b in unit:
        sides.append(pushes.make(red_ref.at[b], red_out.at[me], {"seq": base + b}))
    bounce = Bounce(red_ref.at[me], red_own, red_out.at[me], local, False)
    m = pl.program_id(0)

    @pl.when(m == 0)
    def _():
        greet([{"seq": base + b} for b in unit])
        bounce.inward.start()
        for copy in sides:
            copy.start()
        bounce.turn()

    length = kv_ref.shape[1]
    queries = q_ref.shape[1]
    kk, vv = pair_keys(kv_ref[0])
    k_t = kk.T.astype(BF16)[:HD]
    kk = kk.astype(BF16)
    vv = vv.astype(BF16)
    seg_col = jnp.broadcast_to(segk_ref[0], (8, length)).T[:, :1]
    dk_acc[...] = jnp.zeros_like(dk_acc)
    dv_acc[...] = jnp.zeros_like(dv_acc)
    per = QBLOCK // LANES
    for block in range(queries // QBLOCK):
        here = slice(block * QBLOCK, (block + 1) * QBLOCK)
        keys = (block + 1) * QBLOCK if skip else length
        bias = bias_block(seg_col, segq_ref[0][:, here], place_ref[:, here], 0, keys)
        q = q_ref[0, here, :]
        do = do_ref[block * per : (block + 1) * per, 0].reshape(QBLOCK, LANES)
        low = lane_iota(q.shape) < HD
        parts = []
        for head in range(2):
            pick = low == (head == 0)
            mine = jnp.where(pick, q, jnp.zeros_like(q))
            mine_do = jnp.where(pick, do, jnp.zeros_like(do))
            scores = dot_nt(kk[:keys], mine) + bias
            weight = jnp.exp(scores - lse_ref[0, head : head + 1, here])
            product = dot_nt(vv[:keys], mine_do)
            delta = jnp.sum(weight * product, axis=0, keepdims=True)
            grad_scores = (weight * (product - delta)).astype(BF16)
            dv_acc[:keys] += dot_nn(weight.astype(BF16), mine_do)
            dk_acc[:keys] += dot_nn(grad_scores, mine)
            parts.append(dot_nn(k_t[:, :keys], grad_scores))
        dq = jnp.concatenate(parts, axis=0).T * HD**-0.5
        dq = turn(dq, cosq_ref[here, :], -sinq_ref[here, :]).astype(BF16)
        graw_ref[block * per : (block + 1) * per, 0, :, :LANES] = dq.reshape(per, LANES, LANES)
    dk = dk_acc[...]
    dv = dv_acc[...]
    dk = dk + pltpu.roll(dk, HD, 1)
    dv = dv + pltpu.roll(dv, HD, 1)
    gkv = jnp.where(lane_iota(dk.shape) < HD, dk, dv)
    key_cos, key_sin = value_tables(cosk_ref[...], sink_ref[...])
    gkv = turn(gkv, key_cos, -key_sin).astype(BF16)
    graw_ref[:, 0, :, LANES:] = gkv.reshape(length // LANES, LANES, LANES)
    if skip:
        normed_t = normed_ref[...].reshape(queries, -1).T
        term = dot_nn(normed_t, graw_ref[...].reshape(queries, 2 * LANES))
        @pl.when(m == 0)
        def _():
            term_acc[...] = term

        @pl.when(m > 0)
        def _():
            term_acc[...] += term

        @pl.when(m == pl.num_programs(0) - 1)
        def _():
            for b in range(UNIT):
                for r in range(PIECES):
                    at = (b * PIECES + r) * ROWS_IN
                    term_ref[r, b] = term_acc[at : at + ROWS_IN].astype(BF16)

    @pl.when(m == pl.num_programs(0) - 1)
    def _():
        for copy in sides:
            copy.wait()
        bounce.wait()


def spread(rows):
    rest = jnp.zeros((LANES - E, rows.shape[1]), F32)
    return jnp.concatenate([rows.astype(F32), rest], axis=0).T


def soft_gates(normed, router, chosen):
    logits = jnp.where(chosen > 0, dot_nn(normed, router), NEGATIVE)
    top = jnp.max(logits, axis=-1, keepdims=True)
    weight = jnp.where(chosen > 0, jnp.exp(logits - top), 0.0)
    return weight / jnp.sum(weight, axis=-1, keepdims=True)


def unpack(inner_ref, down_ref, first, wg, wu, wd):
    half = wg.shape[1]
    for r in range(PIECES):
        for b in range(UNIT):
            at = (b * PIECES + r) * ROWS_IN
            low = (b * PIECES + r) * ROWS_OUT
            wg[at : at + ROWS_IN] = inner_ref[r, b, :ROWS_IN]
            wu[at : at + ROWS_IN] = inner_ref[r, b, ROWS_IN : 2 * ROWS_IN]
            for c in range(2):
                start = first + c * ROWS_OUT
                wd[low : low + ROWS_OUT, c * half : (c + 1) * half] = down_ref[
                    r, b, start : start + ROWS_OUT
                ]


def load_weights(now, later, first, fetches, wg, wu, wd, greeted):
    e, t = pl.program_id(0), pl.program_id(1)

    @pl.when((t == 0) & (e == 0))
    def _():
        for copy in fetches:
            copy.start()
        greet([{"seq": peer} for peer in greeted])
        unpack(*now, first, wg, wu, wd)

    @pl.when((t == 0) & (e == 1))
    def _():
        for copy in fetches:
            copy.wait()
        unpack(*later, first, wg, wu, wd)


def twin_push(source, target, send, recv):
    twin = neighbours(lax.axis_index("seq"))[3]
    return pltpu.make_async_remote_copy(
        src_ref=source,
        dst_ref=target,
        send_sem=send,
        recv_sem=recv,
        device_id={"seq": twin},
        device_id_type=pl.DeviceIdType.MESH,
    )


def collect_terms(x, dz, grad_gate, grad_up, gated, ag, au, ad, stage, total, dw, sems):
    e, t = pl.program_id(0), pl.program_id(1)
    last_t = pl.num_programs(1) - 1
    half = ag.shape[1]

    @pl.when(t == 0)
    def _():
        ag[...] = dot_tn(x, grad_gate)
        au[...] = dot_tn(x, grad_up)
        ad[...] = dot_tn(gated, dz)

    @pl.when((t > 0) & (t < last_t))
    def _():
        ag[...] += dot_tn(x, grad_gate)
        au[...] += dot_tn(x, grad_up)
        ad[...] += dot_tn(gated, dz)

    send, recv, local = sems
    push = twin_push(stage, total, send.at[0], recv.at[0])
    out = pltpu.make_async_copy(stage, dw, local.at[1])

    def store(write):
        for place, acc, grad in ((0, ag, grad_gate), (ROWS_IN, au, grad_up)):
            final = acc[...] + dot_tn(x, grad)
            for r in range(PIECES):
                for b in range(UNIT):
                    at = (b * PIECES + r) * ROWS_IN
                    write(r, b, place, final[at : at + ROWS_IN])
        final = ad[...] + dot_tn(gated, dz)
        for r in range(PIECES):
            for b in range(UNIT):
                low = (b * PIECES + r) * ROWS_OUT
                for c in range(2):
                    start = 2 * ROWS_IN + c * ROWS_OUT
                    write(r, b, start, final[low : low + ROWS_OUT, c * half : (c + 1) * half])

    @pl.when((t == last_t) & (e == 0))
    def _():
        def write(r, b, place, value):
            stage[r, b, place : place + value.shape[0]] = value.astype(BF16)

        store(write)
        push.start()

    @pl.when((t == last_t) & (e == 1))
    def _():
        push.wait()

        def write(r, b, place, value):
            here = slice(place, place + value.shape[0])
            stage[r, b, here] = (value + total[r, b, here].astype(F32)).astype(BF16)

        store(write)
        out.start()
        out.wait()


def sigmoid(v):
    return 0.5 + 0.5 * jnp.tanh(0.5 * v)


def grads_of(gate_act, up_act, back, gate):
    sig = sigmoid(gate_act)
    silu = gate_act * sig
    hidden = silu * up_act
    grad_hidden = back * gate
    grad_gate = (grad_hidden * up_act * (sig + silu * (1.0 - sig))).astype(BF16)
    grad_up = (grad_hidden * silu).astype(BF16)
    return hidden, grad_gate, grad_up


def expert_id(twin, index):
    me = lax.axis_index("seq") % UNIT
    return 2 * (me + twin * (1 - 2 * (me % 2))) + index


def pick_gate(gates, gid):
    mine = lane_iota(gates.shape) == gid
    return mine, jnp.sum(jnp.where(mine, gates, 0.0), axis=1, keepdims=True)


def gate_terms(mine, hidden, back):
    terms = jnp.where(mine, jnp.sum(hidden * back, axis=1, keepdims=True), 0.0)
    return terms.T[:E]


def both_kernel(
    x_ref, dz_ref, chosen_ref, wr_ref, w0_ref, w1_hbm, heads_ref,
    out_ref, dx_ref, gg_ref, gates_ref, dw, w_heads,
    wg, wu, wd, gates_s, ag, au, ad, oacc, dxacc, ggacc, w1_ref, stage, total,
    send, recv, local,
):
    e, t = pl.program_id(0), pl.program_id(1)
    tile, width = out_ref.shape
    rows = pl.ds(pl.multiple_of(t * tile, tile), tile)
    x = x_ref[...]
    dz = dz_ref[...]
    last_t = pl.num_programs(1) - 1
    across, along, _, twin = neighbours(lax.axis_index("seq"))
    fetch = pltpu.make_async_copy(w1_hbm, w1_ref, local.at[0])
    packed = (w0_ref, w0_ref)
    load_weights(
        packed, (w1_ref, w1_ref), 2 * ROWS_IN, [fetch], wg, wu, wd, (across, along, twin)
    )

    me = lax.axis_index("seq") % UNIT
    base = lax.axis_index("seq") - me
    a, b, d = across - base, along - base, 6 - me + 2 * (me % 2)
    half = heads_ref.shape[0] // 2
    top, low = pl.ds(0, half), pl.ds(half, half)
    lanes = pl.ds(0, w_heads.shape[2])
    pushes = Pushes(send, recv)
    pushes.used = 1

    def own_part(part, device):
        return pushes.make(heads_ref.at[part, lanes], w_heads.at[me, part], {"seq": device})

    def passed(slot, part, device):
        view = w_heads.at[slot, part]
        return pushes.make(view, view, {"seq": device})

    hop1 = [own_part(top, across), own_part(low, along), own_part(low, across), own_part(top, along)]
    hop1 += [own_part(top, twin), own_part(low, twin)]
    hop2 = [passed(a, top, along), passed(b, low, across), passed(a, top, twin), passed(b, low, twin)]
    hop3 = [passed(a, low, twin), passed(b, top, twin)]
    hop4 = [passed(d, top, twin), passed(d, low, twin)]
    events = (
        (0, 0, (), hop1),
        (0, last_t, hop1[:2], hop2),
        (1, 0, hop1[2:4], hop3),
        (1, 1, hop2[:2], hop4),
    )
    for at_e, at_t, arrived, onward in events:

        @pl.when((e == at_e) & (t == at_t))
        def _(arrived=arrived, onward=onward):
            for copy in arrived:
                copy.wait_recv()
            for copy in onward:
                copy.start()

    @pl.when(e == 0)
    def _():
        gates_s[rows, :] = soft_gates(x, wr_ref[...], spread(chosen_ref[...]))

    mine, gate = pick_gate(gates_s[rows, :], expert_id(1 - e, 0))
    gate_act = dot_nn(x, wg[...])
    up_act = dot_nn(x, wu[...])
    back = dot_nt(dz, wd[...])
    hidden, grad_gate, grad_up = grads_of(gate_act, up_act, back, gate)
    ggterm = gate_terms(mine, hidden, back)
    gated = (hidden * gate).astype(BF16)
    out = dot_nn(gated, wd[...])
    dx = dot_nt(grad_gate, wg[...]) + dot_nt(grad_up, wu[...])

    @pl.when(e == 0)
    def _():
        oacc[rows, :] = out
        dxacc[rows, :] = dx
        ggacc[t] = ggterm

    @pl.when(e == 1)
    def _():
        out_ref[...] = (oacc[rows, :] + out).astype(BF16)
        dx_ref[...] = (dxacc[rows, :] + dx).astype(BF16)
        gg_ref[...] = ggacc[t] + ggterm
        gates_ref[...] = gates_s[rows, :]

    sems = (send, recv, local)
    collect_terms(x, dz, grad_gate, grad_up, gated, ag, au, ad, stage, total, dw, sems)

    @pl.when((e == 1) & (t == last_t))
    def _():
        for copy in hop1[4:] + hop2[2:] + hop3 + hop4:
            copy.wait_recv()
        for copy in hop1 + hop2 + hop3 + hop4:
            copy.wait_send()


def forward_kernel(
    x_ref, gates_ref, inner_ref, down_ref, inner_hbm, down_hbm, oin_ref,
    out_ref, gact_ref, uact_ref, inner_twin, down_twin,
    wg, wu, wd, oacc, inner_next, down_next, send, recv, local,
):
    e, t = pl.program_id(0), pl.program_id(1)
    tile = out_ref.shape[0]
    rows = pl.ds(pl.multiple_of(t * tile, tile), tile)
    x = x_ref[...]
    last_t = pl.num_programs(1) - 1
    turned = [
        twin_push(inner_hbm, inner_next, send.at[0], recv.at[0]),
        twin_push(down_hbm, down_next, send.at[1], recv.at[1]),
    ]
    keeps = [
        pltpu.make_async_copy(inner_next, inner_twin, local.at[0]),
        pltpu.make_async_copy(down_next, down_twin, local.at[1]),
    ]

    @pl.when((e == 0) & (t == 0))
    def _():
        greet([{"seq": neighbours(lax.axis_index("seq"))[3]}])
        for copy in turned:
            copy.start()
        unpack(inner_ref, down_ref, 0, wg, wu, wd)

    @pl.when((e == 1) & (t == 0))
    def _():
        for copy in turned:
            copy.wait()
        for copy in keeps:
            copy.start()
        unpack(inner_next, down_next, 0, wg, wu, wd)

    _, gate = pick_gate(gates_ref[...], expert_id(e, 1))
    gate_act = dot_nn(x, wg[...])
    up_act = dot_nn(x, wu[...])
    gact_ref[0] = gate_act.astype(BF16)
    uact_ref[0] = up_act.astype(BF16)
    gated = (gate_act * sigmoid(gate_act) * up_act * gate).astype(BF16)
    out = dot_nn(gated, wd[...])

    @pl.when(e == 0)
    def _():
        oacc[rows, :] = oin_ref[...].astype(F32) + out

    @pl.when(e == 1)
    def _():
        out_ref[...] = (oacc[rows, :] + out).astype(BF16)

    @pl.when((e == 1) & (t == last_t))
    def _():
        for copy in keeps:
            copy.wait()


def backward_kernel(
    x_ref, dz_ref, gates_ref, gact_ref, uact_ref, inner_ref, down_ref,
    inner_hbm, down_hbm, dxin_ref, ggin_ref,
    out_hbm, dx_ref, gg_ref, dw, out_in,
    wg, wu, wd, ag, au, ad, dxacc, ggacc, inner_next, down_next, stage, total,
    diag_x, diag_y, own_x, own_y, send, recv, local,
):
    e, t = pl.program_id(0), pl.program_id(1)
    tile, width = dx_ref.shape
    rows = pl.ds(pl.multiple_of(t * tile, tile), tile)
    x = x_ref[...]
    dz = dz_ref[...]
    fetches = [
        pltpu.make_async_copy(inner_hbm, inner_next, local.at[0]),
        pltpu.make_async_copy(down_hbm, down_next, local.at[4]),
    ]
    load_weights(
        (inner_ref, down_ref), (inner_next, down_next), 0, fetches, wg, wu, wd,
        neighbours(lax.axis_index("seq")),
    )
    across, along, _, _ = neighbours(lax.axis_index("seq"))
    pushes = Pushes(send, recv)
    pushes.used = 1
    half = own_x.shape[0]
    top, low = pl.ds(0, half), pl.ds(half, half)
    first = [
        pushes.make(out_hbm.at[3, top], diag_x, {"seq": across}),
        pushes.make(out_hbm.at[3, low], diag_y, {"seq": along}),
        pushes.make(out_hbm.at[1, top], out_in.at[0, top], {"seq": across}),
        pushes.make(out_hbm.at[2, low], out_in.at[1, low], {"seq": along}),
    ]
    second = [
        pushes.make(own_x, out_in.at[0, low], {"seq": across}),
        pushes.make(own_y, out_in.at[1, top], {"seq": along}),
    ]
    loads = [
        pltpu.make_async_copy(out_hbm.at[1, low], own_x, local.at[2]),
        pltpu.make_async_copy(out_hbm.at[2, top], own_y, local.at[3]),
    ]

    @pl.when((e == 0) & (t == 0))
    def _():
        for copy in first[:2] + loads:
            copy.start()

    @pl.when((e == 0) & (t == 1))
    def _():
        for copy in first[2:]:
            copy.start()

    mine, gate = pick_gate(gates_ref[...], expert_id(1 - e, 1))
    back = dot_nt(dz, wd[...])
    hidden, grad_gate, grad_up = grads_of(
        gact_ref[0].astype(F32), uact_ref[0].astype(F32), back, gate
    )
    ggterm = gate_terms(mine, hidden, back)
    gated = (hidden * gate).astype(BF16)
    dx = dot_nt(grad_gate, wg[...]) + dot_nt(grad_up, wu[...])

    @pl.when(e == 0)
    def _():
        dxacc[rows, :] = dxin_ref[...].astype(F32) + dx
        ggacc[t] = ggin_ref[...] + ggterm

    @pl.when(e == 1)
    def _():
        dx_ref[...] = (dxacc[rows, :] + dx).astype(BF16)
        gg_ref[...] = ggacc[t] + ggterm

    sems = (send, recv, local)
    collect_terms(x, dz, grad_gate, grad_up, gated, ag, au, ad, stage, total, dw, sems)

    @pl.when((e == 0) & (t == pl.num_programs(1) - 1))
    def _():
        for copy in loads:
            copy.wait()
        first[0].wait_recv()
        first[1].wait_recv()
        own_x[...] = (own_x[...].astype(F32) + diag_y[...].astype(F32)).astype(BF16)
        own_y[...] = (own_y[...].astype(F32) + diag_x[...].astype(F32)).astype(BF16)
        for copy in second:
            copy.start()

    @pl.when((e == 1) & (t == pl.num_programs(1) - 1))
    def _():
        first[0].wait_send()
        first[1].wait_send()
        for copy in first[2:] + second:
            copy.wait()


def run_experts(which, x, dz, chosen, weights, router=None, gates=None, carried=None, acts=None, pushed=None):
    tokens, width = x.shape
    hidden = weights[0].shape[3]
    packed_shape = (PIECES, UNIT, 3 * ROWS_IN, hidden)
    inner_shape = (PIECES, UNIT, 2 * ROWS_IN, hidden)
    down_shape = (PIECES, UNIT, ROWS_IN, hidden)
    tile = tokens // 3
    tiles = 3
    like = jax.ShapeDtypeStruct
    any_spec = pl.BlockSpec(memory_space=pl.ANY)
    once = pl.Buffered(1)

    def by_token(e, t):
        return (t, 0)

    def at_end(e, t):
        return (jnp.where(e == 1, t, 0), 0)

    def at_start(e, t):
        return (jnp.where(e == 0, t, tiles - 1), 0)

    def lanes_end(e, t):
        return (0, jnp.where(e == 1, t, 0))

    def lanes_start(e, t):
        return (0, jnp.where(e == 0, t, tiles - 1))

    def acts_map(e, t):
        return (e, t, 0)

    x_spec = pl.BlockSpec((tile, width), by_token)
    gates_spec = pl.BlockSpec((tile, LANES), by_token)

    def weight_spec(shape):
        return pl.BlockSpec(shape, lambda e, t: (0, 0, 0, 0), pipeline_mode=once)

    acts_spec = pl.BlockSpec((1, tile, hidden), acts_map)
    acts_back = pl.BlockSpec((1, tile, hidden), lambda e, t: (1 - e, t, 0))
    token_end = pl.BlockSpec((tile, width), at_end)
    token_start = pl.BlockSpec((tile, width), at_start)
    packed_like = like(packed_shape, BF16)
    pair_like = [like(inner_shape, BF16), like(down_shape, BF16)]
    pair_vmem = [pltpu.VMEM(inner_shape, BF16), pltpu.VMEM(down_shape, BF16)]
    pair_specs = [weight_spec(inner_shape), weight_spec(down_shape), any_spec, any_spec]
    token_like = like((tokens, width), BF16)
    gg_like = like((E, tokens), F32)
    acts_like = like((2, tokens, hidden), BF16)
    unpacked = [
        pltpu.VMEM((width, hidden), BF16),
        pltpu.VMEM((width, hidden), BF16),
        pltpu.VMEM((hidden, width), BF16),
    ]
    terms = [
        pltpu.VMEM((width, hidden), F32),
        pltpu.VMEM((width, hidden), F32),
        pltpu.VMEM((hidden, width), F32),
    ]
    acc = pltpu.VMEM((tokens, width), F32)
    gg_acc = pltpu.VMEM((tiles, E, tile), F32)
    second = pltpu.VMEM(packed_shape, BF16)
    stage = pltpu.VMEM(packed_shape, BF16)
    sem, sems = pltpu.SemaphoreType.DMA, pltpu.SemaphoreType.DMA((2,))
    flops = 4.0 * tokens * width * hidden
    if which == "both":
        return pl.pallas_call(
            both_kernel,
            grid=(2, tiles),
            in_specs=[
                x_spec, x_spec, pl.BlockSpec((E, tile), lambda e, t: (0, t)),
                pl.BlockSpec((width, LANES), lambda e, t: (0, 2), pipeline_mode=once),
                weight_spec(packed_shape), any_spec, any_spec,
            ],
            out_specs=[
                token_end, token_end, pl.BlockSpec((E, tile), lanes_end),
                pl.BlockSpec((tile, LANES), at_end), any_spec, any_spec,
            ],
            out_shape=[
                token_like, token_like, gg_like, like((tokens, LANES), F32),
                packed_like, like((UNIT, width, 4 * HD), BF16),
            ],
            scratch_shapes=unpacked
            + [pltpu.VMEM((tokens, LANES), F32)]
            + terms
            + [acc, acc, gg_acc, second, stage, stage]
            + [pltpu.SemaphoreType.DMA((15,)), pltpu.SemaphoreType.DMA((15,)), sems],
            compiler_params=params(collective_id=5, has_side_effects=True),
            cost_estimate=cost(1, 1e5),
        )(x, dz, chosen, router, *weights, router)
    if which == "forward":
        return pl.pallas_call(
            forward_kernel,
            grid=(2, tiles),
            in_specs=[x_spec, gates_spec] + pair_specs + [token_start],
            out_specs=[token_end, acts_spec, acts_spec, any_spec, any_spec],
            out_shape=[token_like, acts_like, acts_like] + pair_like,
            scratch_shapes=unpacked + [acc] + pair_vmem + [sems, sems, sems],
            compiler_params=params(collective_id=9, has_side_effects=True),
            cost_estimate=cost(3 * flops, 2e7),
        )(x, gates, *weights, *weights, carried)
    return pl.pallas_call(
        backward_kernel,
        grid=(2, tiles),
        in_specs=[
            x_spec, x_spec, gates_spec, acts_back, acts_back, *pair_specs,
            token_start, pl.BlockSpec((E, tile), lanes_start), any_spec,
        ],
        out_specs=[token_end, pl.BlockSpec((E, tile), lanes_end), any_spec, any_spec],
        out_shape=[
            token_like, gg_like, packed_like, like((2,) + pushed.shape[1:], BF16),
        ],
        scratch_shapes=unpacked + terms + [acc, gg_acc]
        + pair_vmem
        + [stage, stage]
        + [pltpu.VMEM((pushed.shape[1] // 2, width), BF16)] * 4
        + [pltpu.SemaphoreType.DMA((7,)), pltpu.SemaphoreType.DMA((7,))]
        + [pltpu.SemaphoreType.DMA((5,))],
        compiler_params=params(collective_id=6, has_side_effects=True),
        cost_estimate=cost(6 * flops, 2e7),
    )(x, dz, gates, acts[0], acts[1], *weights, carried[0], carried[1], pushed)


def return_kernel(
    micro, copies, ready, dx_ref, gg_ref, mixed_ref, normed_ref, dz_ref, chosen_ref, small_ref, w_ref,
    ctx_ref, own_out, back_out, do_out, gmixed_ref, pre_ref, block_ref,
    mine_dx, from_x, from_y, diag_x, diag_y, sum_x, sum_y, gparts, gctx, gbranch, glogs, term, twin_term, send, recv, local,
):
    seq = lax.axis_index("seq")
    me = seq % UNIT
    core = me % 2
    base = seq - me
    unit = [(me + k) % UNIT for k in range(1, UNIT)]
    *peers, twin = neighbours(seq)
    greet([{"seq": base + b} for b in unit])
    pushes = Pushes(send, recv)
    count, width = mixed_ref.shape
    step = count // micro
    half = step // 2
    chunks = [pl.ds(m * step, step) for m in range(micro)]
    tops = [pl.ds(m * step, half) for m in range(micro)]
    lows = [pl.ds(m * step + half, half) for m in range(micro)]
    across, along = peers[:2]
    own = [
        pltpu.make_async_copy(dx_ref, mine_dx, local.at[0]),
        pltpu.make_async_copy(gg_ref.at[:, pl.ds(0, count)], gparts.at[0], local.at[1]),
    ]
    for copy in own:
        copy.start()
    diagonal, direct, sums = [], [], []

    def send_diagonal(m):
        diagonal.append(
            (
                pushes.start(dx_ref.at[3, tops[m]], diag_x.at[m], {"seq": across}),
                pushes.start(dx_ref.at[3, lows[m]], diag_y.at[m], {"seq": along}),
            )
        )

    def send_direct(m):
        direct.append(
            (
                pushes.start(dx_ref.at[1, tops[m]], from_x.at[tops[m]], {"seq": across}),
                pushes.start(dx_ref.at[2, lows[m]], from_y.at[lows[m]], {"seq": along}),
            )
        )

    def send_sums(m):
        for copy in diagonal[m]:
            copy.wait_recv()
        own_y = mine_dx[2, tops[m]].astype(F32) + diag_x[m].astype(F32)
        own_x = mine_dx[1, lows[m]].astype(F32) + diag_y[m].astype(F32)
        sum_y[m] = own_y.astype(BF16)
        sum_x[m] = own_x.astype(BF16)
        sums.append(
            (
                pushes.start(sum_y.at[m], from_y.at[tops[m]], {"seq": along}),
                pushes.start(sum_x.at[m], from_x.at[lows[m]], {"seq": across}),
            )
        )

    send_diagonal(0)
    first = []
    for n in (2, 0, 1):
        part = gg_ref.at[:, pl.ds((n + 1) * count, count)]
        first.append(pushes.start(part, gparts.at[n + 1], {"seq": peers[n]}))
    send_direct(0)
    if micro > 1:
        send_diagonal(1)
    ready()
    small = small_ref[...]
    gain = gain_row(small, E + 1)
    gates = soft_gates(normed_ref[...], small, spread(chosen_ref[...]))
    block = mixed_ref[...] + own_out[0].astype(F32) + back_out[0].astype(F32)
    block_ref[...] = (block + back_out[1].astype(F32)).astype(BF16)
    for copy in own:
        copy.wait()
    for copy in first:
        copy.wait_recv()
    grad_gates = gparts[0] + gparts[1] + gparts[2] + gparts[3]
    grad_gates = spread(grad_gates)
    centre = jnp.sum(gates * grad_gates, axis=-1, keepdims=True)
    glogs[...] = (gates * (grad_gates - centre)).astype(BF16)
    sent = []

    def compute(m):
        here = chunks[m]
        for copy in direct[m] + sums[m]:
            copy.wait_recv()
        dy = mine_dx[0, here].astype(F32) + from_x[here].astype(F32) + from_y[here].astype(F32)
        dy = dy + dot_nt(glogs[here], small)
        v = mixed_ref[here]
        inverse = lax.rsqrt(jnp.mean(v * v, axis=-1, keepdims=True) + EPS)
        scaled = dy * gain
        mean = jnp.mean(scaled * v, axis=-1, keepdims=True)
        gmixed = dz_ref[here].astype(F32) + scaled * inverse
        gmixed = gmixed - v * (inverse * inverse * inverse * mean)
        gmixed_ref[here] = gmixed
        branch = gmixed.astype(BF16)
        gbranch[here] = branch
        grad_ctx = dot_nt(branch, w_ref[...]).astype(BF16)
        for b in range(UNIT):
            gctx[b, m] = grad_ctx[:, b * LANES : (b + 1) * LANES]
        mine = pltpu.make_async_copy(gctx.at[me, m], do_out.at[me, m], local.at[2 + m])
        mine.start()
        own.append(mine)
        for b in unit:
            sent.append(pushes.start(gctx.at[b, m], do_out.at[me, m], {"seq": base + b}))

    for m in range(micro):
        send_sums(m)
        if m + 1 < micro:
            send_direct(m + 1)
        if m + 2 < micro:
            send_diagonal(m + 2)
        if m > 0:
            compute(m - 1)
    compute(micro - 1)
    rest = width // (copies * UNIT)
    out_term = dot_tn(ctx_ref[...], gbranch[...]).astype(BF16)
    router_term = dot_tn(normed_ref[...], glogs[...]).astype(BF16)
    for a in range(copies):
        for b in range(UNIT):
            at = (a * UNIT + b) * rest
            term[a, b, :, :width] = out_term[at : at + rest]
            term[a, b, :, width:] = router_term[at : at + rest]
    turned = [
        pushes.start(term.at[:, 2 * j + 1 - core], twin_term.at[j], {"seq": twin})
        for j in range(4)
    ]
    for j, copy in enumerate(turned):
        copy.wait_recv()
        summed = term[:, 2 * j + core].astype(F32) + twin_term[j].astype(F32)
        pre_ref[j] = summed.astype(BF16)
    for group in [first] + diagonal + direct + sums:
        for copy in group:
            copy.wait_send()
    for copy in turned:
        copy.wait_send()
    for copy in own[2:] + sent:
        copy.wait()


def return_tokens(
    dx, gg, mixed, normed, dz, chosen, heads, w_out, context, own_out, back_out, micro, copies, collective
):
    any_spec = pl.BlockSpec(memory_space=pl.ANY)
    like = jax.ShapeDtypeStruct
    count, width = mixed.shape
    ctx_shape = (UNIT, micro, count // micro, LANES)
    pre_shape = (4, copies, width // (copies * UNIT), width + LANES)
    pushes = 3 + 6 * micro + (UNIT - 1) * micro + 4
    piece = (micro, count // micro // 2, width)

    def fixed(i):
        return (0, 0)

    late = Late(
        [
            (2, mixed.shape, F32, None),
            (3, normed.shape, BF16, None),
            (4, dz.shape, BF16, None),
            (5, chosen.shape, BF16, None),
            (6, (width, LANES), BF16, small_view),
            (7, w_out.shape, BF16, None),
            (8, context.shape, BF16, None),
            (9, (1, count, width), BF16, lambda ref: ref.at[pl.ds(0, 1)]),
            (10, back_out.shape, BF16, None),
        ]
    )

    return pl.pallas_call(
        late.wrap(functools.partial(return_kernel, micro, copies), 11),
        grid=(1,),
        in_specs=late.specs(11),
        out_specs=[
            any_spec,
            pl.BlockSpec((count, width), fixed),
            pl.BlockSpec(pre_shape, lambda i: (0, 0, 0, 0)),
            pl.BlockSpec((count, width), fixed),
        ],
        out_shape=[
            like(ctx_shape, BF16),
            like((count, width), F32),
            like(pre_shape, BF16),
            like((count, width), BF16),
        ],
        scratch_shapes=[
            pltpu.VMEM((4, count, width), BF16),
            pltpu.VMEM((count, width), BF16),
            pltpu.VMEM((count, width), BF16),
            pltpu.VMEM(piece, BF16),
            pltpu.VMEM(piece, BF16),
            pltpu.VMEM(piece, BF16),
            pltpu.VMEM(piece, BF16),
            pltpu.VMEM((4, E, count), F32),
            pltpu.VMEM(ctx_shape, BF16),
            pltpu.VMEM((count, width), BF16),
            pltpu.VMEM((count, LANES), BF16),
            pltpu.VMEM((copies, UNIT) + pre_shape[2:], BF16),
            pltpu.VMEM(pre_shape, BF16),
            pltpu.SemaphoreType.DMA((pushes,)),
            pltpu.SemaphoreType.DMA((pushes,)),
            pltpu.SemaphoreType.DMA((2 + micro,)),
        ]
        + late.scratch(),
        compiler_params=params(collective_id=collective, has_side_effects=True),
        cost_estimate=cost(4.0 * count * width * width, 1.2e8),
    )(dx, gg, mixed, normed, dz, chosen, heads, w_out, context, own_out, back_out)


def unpack_grads_kernel(
    ex0, ex1, head_ref, out_ref, gate_w, up_w, query_w, key_w, value_w, router_w, attn_ref, ffn_ref,
    gattn, gquery, gkey, gvalue, gout, gffn, grouter, ggate, gup, gdown,
):
    part, hidden = gate_w.shape[1:]
    half = part // 2
    width = gout.shape[1]
    ffn = jnp.zeros((part, hidden), F32)
    for n, source in enumerate((ex0, ex1)):
        for b in range(UNIT):
            e = 2 * b + n
            gate = source[b, :part].astype(F32)
            up = source[b, part : 2 * part].astype(F32)
            ggate[e] = gate
            gup[e] = up
            ffn = ffn + gate * gate_w[e].astype(F32) + up * up_w[e].astype(F32)
            for c in range(2):
                start = 2 * part + c * half
                gdown[e, :, c * hidden : (c + 1) * hidden] = source[b, start : start + half].astype(
                    F32
                )
    router = out_ref[:, width:].T[:E]
    grouter[...] = router
    gout[...] = out_ref[:, :width]
    low = lane_iota((part, LANES)) < HD
    attn = jnp.zeros((part, LANES), F32)
    for pair in range(UNIT // 2):
        lanes = slice(pair * LANES, (pair + 1) * LANES)
        even = head_ref[2 * pair, :, LANES:].astype(F32)
        odd = head_ref[2 * pair + 1, :, LANES:].astype(F32)
        key = jnp.where(low, even, pltpu.roll(odd, HD, 1))
        value = jnp.where(low, pltpu.roll(even, HD, 1), odd)
        gkey[:, lanes] = key
        gvalue[:, lanes] = value
        attn = attn + key * key_w[:, lanes].astype(F32) + value * value_w[:, lanes].astype(F32)
    for b in range(UNIT):
        lanes = slice(b * LANES, (b + 1) * LANES)
        query = head_ref[b, :, :LANES].astype(F32)
        gquery[:, lanes] = query
        attn = attn + query * query_w[:, lanes].astype(F32)

    def as_row(column):
        return jnp.broadcast_to(column, (part, LANES)).T[:1]

    attn = jnp.sum(attn, axis=1, keepdims=True)
    ffn = jnp.sum(ffn, axis=1, keepdims=True)
    gattn[...] = as_row(attn) / attn_ref[...].astype(F32)
    routed = jnp.sum(router * router_w[...].astype(F32), axis=0, keepdims=True)
    gffn[...] = (as_row(ffn) + routed) / ffn_ref[...].astype(F32)


def shards(
    copies, tokens, segments, routes, cotangent, norm_attn, w_query, w_key, w_value, w_out, norm_ffn,
    w_router, w_gate, w_up, w_down, rows,
):
    micro, local_len, width = tokens.shape
    length = segments.shape[1]
    count = micro * local_len
    unit_len = UNIT * local_len
    part = w_query.shape[0]
    hidden = w_gate.shape[2]
    seq_size = copies * UNIT
    seq = lax.axis_index("seq")
    row = lax.axis_index("row")
    unit = seq // UNIT
    me = seq % UNIT
    unit_groups = None
    copy_groups = None
    if copies > 1:
        unit_groups = [[a * UNIT + b for b in range(UNIT)] for a in range(copies)]
        copy_groups = [[a * UNIT + b for a in range(copies)] for b in range(UNIT)]

    def exchange(x):
        return lax.all_to_all(x, "seq", 0, 0, tiled=True, axis_index_groups=unit_groups)

    def flip(x, k):
        return lax.ppermute(x, "seq", [(s, s ^ k) for s in range(seq_size)])

    flat_tokens = tokens.reshape(count, width)

    def wait_for(x, *others):
        return lax.optimization_barrier((x,) + others)[0]

    if copies == 1:
        inputs = [
            w_gate, w_up, w_down, w_query, w_key, w_value, w_router.T, norm_attn[None],
            norm_ffn[None],
        ]
    else:
        small = jnp.concatenate(
            [w_router.T, norm_attn[None], norm_ffn[None], jnp.zeros((LANES - 2 - E, part), BF16)], axis=0
        ).T
        head_part = jnp.concatenate(
            [
                w_query.reshape(part, UNIT, 2 * HD),
                w_key.reshape(part, UNIT, HD),
                w_value.reshape(part, UNIT, HD),
                jnp.broadcast_to(small[:, None], (part, UNIT, LANES)),
            ],
            axis=2,
        ).transpose(1, 0, 2)

        down_halves = w_down.reshape(E, -1, 2, hidden).transpose(0, 2, 1, 3).reshape(E, part, hidden)
        packed_part = jnp.concatenate([w_gate, w_up, down_halves], axis=1)
        packed_part = packed_part.reshape(UNIT, E // UNIT, 3 * part, hidden).transpose(1, 0, 2, 3)
        inputs = [packed_part, head_part]
    *packed_mine, heads_all, w_out_rows = begin(rows, part, hidden, inputs, w_out)

    if copies > 1:
        heads_all = lax.all_gather(heads_all, "seq", axis=0, axis_index_groups=copy_groups)
        w_out_rows = lax.all_gather(w_out_rows, "seq", axis=0, axis_index_groups=copy_groups)
    w_out_all = w_out_rows.reshape(H * HD, width)
    heads_all = heads_all.reshape(width, 4 * HD + LANES)

    def gather_packed(x):
        x = lax.all_gather(x, "row", axis=0)
        if copies > 1:
            x = lax.all_gather(x, "seq", axis=0, axis_index_groups=copy_groups)
            x = x.transpose(0, 2, 1, 3, 4).reshape(-1, 3 * part, hidden)
            halves = x[:, 2 * part :].reshape(-1, 2, part // 2, hidden).transpose(0, 2, 1, 3)
            return pack(
                x[:, :part].reshape(width, hidden),
                x[:, part : 2 * part].reshape(width, hidden),
                halves.reshape(hidden, width),
            )
        return x

    def pack(gate, up, down):
        gate = gate.reshape(UNIT, PIECES, ROWS_IN, hidden)
        up = up.reshape(UNIT, PIECES, ROWS_IN, hidden)
        down = down.reshape(UNIT, PIECES, ROWS_OUT, 2, hidden).transpose(0, 1, 3, 2, 4)
        down = down.reshape(UNIT, PIECES, ROWS_IN, hidden)
        return jnp.concatenate([gate, up, down], axis=2).transpose(1, 0, 2, 3)

    def repack(x):
        x = x.transpose(1, 0, 2, 3)
        gate = x[:, :, :ROWS_IN].reshape(copies, UNIT, rows, part, hidden)
        up = x[:, :, ROWS_IN : 2 * ROWS_IN].reshape(copies, UNIT, rows, part, hidden)
        down = x[:, :, 2 * ROWS_IN :].reshape(UNIT, PIECES, 2, ROWS_OUT, hidden)
        down = down.transpose(0, 1, 3, 2, 4).reshape(copies, UNIT, rows, part // 2, 2, hidden)
        down = down.transpose(0, 1, 2, 4, 3, 5).reshape(copies, UNIT, rows, part, hidden)
        return jnp.concatenate([gate, up, down], axis=3).transpose(2, 0, 1, 3, 4)

    own_first = gather_packed(packed_mine[0])
    if copies > 1:
        whole_second = gather_packed(jnp.concatenate(packed_mine[1:], axis=1))
        own_second = (whole_second[:, :, : 2 * ROWS_IN], whole_second[:, :, 2 * ROWS_IN :])
    else:
        own_second = tuple(gather_packed(x) for x in packed_mine[1:])

    (tok_all,) = unit_gather([wait_for(flat_tokens, w_out_all)], 1)
    tok_all = tok_all.reshape(UNIT, micro, local_len, width)

    chosen = jnp.any(
        routes.reshape(count, TOPK).T[:, None, :] == jnp.arange(E, dtype=jnp.int32)[None, :, None],
        axis=0,
    ).astype(BF16)
    dz_own = cotangent.reshape(count, width)

    frequency = BASE ** (-2.0 * np.arange(HD // 2) / HD)
    angles = np.arange(length)[:, None].astype(np.float32) * frequency[None].astype(np.float32)
    key_cos = jnp.asarray(np.tile(np.cos(angles), (1, 4)).astype(np.float32))
    key_sin = np.concatenate([-np.sin(angles), np.sin(angles)] * 2, axis=1)
    key_sin = jnp.asarray(key_sin.astype(np.float32))
    places = jnp.asarray(np.arange(unit_len, dtype=np.int32))
    cosine, sine = key_cos, key_sin
    if copies > 1:
        places = unit * unit_len + places
        cosine = lax.dynamic_slice_in_dim(key_cos, unit * unit_len, unit_len, 0)
        sine = lax.dynamic_slice_in_dim(key_sin, unit * unit_len, unit_len, 0)

    def by_row4(m):
        return (0, m, 0, 0)

    def by_row3(m):
        return (m, 0, 0)

    def fixed(*_):
        return (0, 0)

    def zeros3(*_):
        return (0, 0, 0)

    def zeros4(*_):
        return (0, 0, 0, 0)

    def small_block(*_):
        return (0, 2)

    seg_keys = segments.astype(F32).reshape(micro, 1, length)
    seg_queries = seg_keys
    if copies > 1:
        seg_queries = lax.dynamic_slice_in_dim(seg_keys, unit * unit_len, unit_len, 2)
    skip = copies == 1
    place_row = places[None]
    attention_flops = 4.0 * micro * unit_len * length * 2 * LANES
    attention_specs = [
        pl.BlockSpec((1, unit_len, LANES), by_row3),
        pl.BlockSpec((1, length, LANES), by_row3),
        pl.BlockSpec((1, 1, unit_len), by_row3),
        pl.BlockSpec((1, 1, length), by_row3),
        pl.BlockSpec((1, unit_len), fixed),
    ]
    if copies == 1:
        normed_all, q_all, kv_all, ctx_heads, lse, dz_all, chosen_all = pl.pallas_call(
            attend_kernel,
            grid=(micro,),
            in_specs=[
                pl.BlockSpec((UNIT, 1, local_len, width), by_row4),
                pl.BlockSpec((width, LANES), small_block),
                pl.BlockSpec((width, 4 * HD), fixed),
                pl.BlockSpec((unit_len, LANES), fixed),
                pl.BlockSpec((unit_len, LANES), fixed),
            ]
            + attention_specs[2:]
            + [pl.BlockSpec(memory_space=pl.ANY)] * 2,
            out_specs=[
                pl.BlockSpec((UNIT, 1, local_len, width), by_row4),
                pl.BlockSpec((1, unit_len, LANES), by_row3),
                pl.BlockSpec((1, unit_len, LANES), by_row3),
                pl.BlockSpec((UNIT, 1, local_len, LANES), by_row4),
                pl.BlockSpec((1, 2, unit_len), by_row3),
                pl.BlockSpec(memory_space=pl.ANY),
                pl.BlockSpec(memory_space=pl.ANY),
            ],
            out_shape=[
                jax.ShapeDtypeStruct((UNIT, micro, local_len, width), BF16),
                jax.ShapeDtypeStruct((micro, unit_len, LANES), BF16),
                jax.ShapeDtypeStruct((micro, unit_len, LANES), BF16),
                jax.ShapeDtypeStruct((UNIT, micro, local_len, LANES), BF16),
                jax.ShapeDtypeStruct((micro, 2, unit_len), F32),
                jax.ShapeDtypeStruct((4, count, width), BF16),
                jax.ShapeDtypeStruct((E, 4 * count), BF16),
            ],
            scratch_shapes=[
                pltpu.VMEM((count, width), BF16),
                pltpu.VMEM((E, count), BF16),
                pltpu.SemaphoreType.DMA((9,)),
                pltpu.SemaphoreType.DMA((9,)),
                pltpu.SemaphoreType.DMA((2, 2)),
            ],
            compiler_params=params(collective_id=8, has_side_effects=True),
            cost_estimate=cost(attention_flops, 4e6),
        )(
            tok_all, heads_all, heads_all, cosine, sine, seg_queries, seg_keys, place_row, dz_own,
            chosen,
        )
    else:
        normed_all, q_all, kv_own = pl.pallas_call(
            project_kernel,
            grid=(micro,),
            in_specs=[
                pl.BlockSpec((UNIT, 1, local_len, width), by_row4),
                pl.BlockSpec((width, LANES), small_block),
                pl.BlockSpec((width, 4 * HD), fixed),
                pl.BlockSpec((unit_len, LANES), fixed),
                pl.BlockSpec((unit_len, LANES), fixed),
            ],
            out_specs=[
                pl.BlockSpec((UNIT, 1, local_len, width), by_row4),
                pl.BlockSpec((1, unit_len, LANES), by_row3),
                pl.BlockSpec((1, unit_len, LANES), by_row3),
            ],
            out_shape=[
                jax.ShapeDtypeStruct((UNIT, micro, local_len, width), BF16),
                jax.ShapeDtypeStruct((micro, unit_len, LANES), BF16),
                jax.ShapeDtypeStruct((micro, unit_len, LANES), BF16),
            ],
            compiler_params=params(),
            cost_estimate=cost(2.0 * UNIT * count * width * 4 * HD, 1.5e7),
        )(tok_all, heads_all, heads_all, cosine, sine)
        kv_all = lax.all_gather(kv_own, "seq", axis=1, tiled=True, axis_index_groups=copy_groups)
        ctx_heads, lse = pl.pallas_call(
            functools.partial(attention_kernel, skip),
            grid=(micro,),
            in_specs=attention_specs,
            out_specs=[
                pl.BlockSpec((UNIT, 1, local_len, LANES), by_row4),
                pl.BlockSpec((1, 2, unit_len), by_row3),
            ],
            out_shape=[
                jax.ShapeDtypeStruct((UNIT, micro, local_len, LANES), BF16),
                jax.ShapeDtypeStruct((micro, 2, unit_len), F32),
            ],
            compiler_params=params(),
            cost_estimate=cost(attention_flops, 4e6),
        )(q_all, kv_all, seg_queries, seg_keys, place_row)
        dz_all = jnp.stack([dz_own] + [flip(dz_own, k) for k in (2, 4, 6)])
        chosen_all = jnp.concatenate([chosen] + [flip(chosen, k) for k in (2, 4, 6)], axis=1)

    x_all, sib_first, mixed, normed_ffn, context = bridge(
        ctx_heads, own_first, w_out_all, flat_tokens, heads_all, 2
    )
    x_all = x_all.reshape(4 * count, width)
    dz_all = dz_all.reshape(4 * count, width)
    out_part, dx_part, gg_part, gates_all, total_first, w_heads = run_experts(
        "both", x_all, dz_all, chosen_all, (sib_first, own_first),
        router=heads_all,
    )

    def finish_expert(total):
        if copies > 1:
            total = repack(total)
            total = lax.psum_scatter(total, "row", scatter_dimension=0)
            total = lax.psum_scatter(
                total, "seq", scatter_dimension=0, axis_index_groups=copy_groups
            )
        else:
            total = lax.psum_scatter(total, "row", scatter_dimension=0)
        return total

    reduced_first = finish_expert(total_first)
    out_part, gate_acts, up_acts, *sib_second = run_experts(
        "forward", x_all, None, None, own_second, gates=gates_all, carried=out_part
    )
    out_split = out_part.reshape(4, count, width)
    dx_part, gg_part, total_second, out_back = run_experts(
        "backward", x_all, dz_all, None, (*sib_second, *own_second), gates=gates_all,
        carried=(dx_part, gg_part), acts=(gate_acts, up_acts), pushed=out_split,
    )
    reduced_second = finish_expert(total_second)
    do_heads, gmixed, out_pre, block_out = return_tokens(
        dx_part.reshape(4, count, width), gg_part, mixed, normed_ffn, dz_own, chosen, heads_all,
        w_out_all, context, out_split, out_back, micro, copies, 3,
    )
    if copies > 1:
        out_pre = lax.psum_scatter(
            out_pre, "seq", scatter_dimension=1, axis_index_groups=copy_groups
        )
    out_pre = out_pre.reshape(4, rows, part, width + LANES)
    graw, head_term, out_in, exchanged = pl.pallas_call(
        functools.partial(attention_back_kernel, skip),
        grid=(micro,),
        in_specs=attention_specs
        + [
            pl.BlockSpec((1, 2, unit_len), by_row3),
            pl.BlockSpec((UNIT, 1, local_len, LANES), by_row4),
            pl.BlockSpec((unit_len, LANES), fixed),
            pl.BlockSpec((unit_len, LANES), fixed),
            pl.BlockSpec((length, LANES), fixed),
            pl.BlockSpec((length, LANES), fixed),
            pl.BlockSpec((UNIT, 1, local_len, width), by_row4),
            pl.BlockSpec(memory_space=pl.ANY),
            pl.BlockSpec(memory_space=pl.ANY),
        ],
        out_specs=[
            pl.BlockSpec((seq_size, 1, local_len, 2 * LANES), by_row4),
            pl.BlockSpec((PIECES, UNIT, ROWS_IN, 2 * LANES), zeros4),
            pl.BlockSpec(memory_space=pl.ANY),
            pl.BlockSpec(memory_space=pl.ANY),
        ],
        out_shape=[
            jax.ShapeDtypeStruct((seq_size, micro, local_len, 2 * LANES), BF16),
            jax.ShapeDtypeStruct((PIECES, UNIT, ROWS_IN, 2 * LANES), BF16),
            jax.ShapeDtypeStruct((3,) + out_pre.shape[1:], BF16),
            jax.ShapeDtypeStruct(reduced_first.shape, BF16),
        ],
        scratch_shapes=[
            pltpu.VMEM((length, LANES), F32),
            pltpu.VMEM((length, LANES), F32),
            pltpu.VMEM((width, 2 * LANES), F32),
            pltpu.VMEM(reduced_first.shape[1:], BF16),
            pltpu.SemaphoreType.DMA((UNIT + 2,)),
            pltpu.SemaphoreType.DMA((UNIT + 2,)),
            pltpu.SemaphoreType.DMA((2,)),
        ],
        compiler_params=params(collective_id=7, has_side_effects=True),
        cost_estimate=cost(2.5 * attention_flops, 8e6),
    )(
        q_all, kv_all, seg_queries, seg_keys, place_row, lse, do_heads,
        cosine, sine, key_cos, key_sin, normed_all, out_pre, reduced_first,
    )
    if copies > 1:
        graw_kv = lax.psum_scatter(
            graw[..., LANES:], "seq", scatter_dimension=0, tiled=True,
            axis_index_groups=copy_groups,
        )
        graw = jnp.concatenate([graw[:UNIT, ..., :LANES], graw_kv], axis=3)
        head_term = jnp.einsum(
            "nd,nh->dh",
            normed_all.reshape(UNIT * count, width),
            graw.reshape(UNIT * count, 2 * LANES),
            preferred_element_type=F32,
        ).astype(BF16)
        head_term = head_term.reshape(copies, UNIT, rows, part, 2 * LANES)
        head_term = lax.psum_scatter(
            head_term, "seq", scatter_dimension=0, axis_index_groups=copy_groups
        ).transpose(1, 0, 2, 3)
    head_grad, exchanged_second, out_grad, grad_input = finish(
        rows, graw, head_term, reduced_second, out_pre, out_in, w_heads, flat_tokens, heads_all,
        gmixed, 4,
    )
    if copies == 1:
        like = jax.ShapeDtypeStruct
        (
            grad_norm_attn, grad_query, grad_key, grad_value, grad_out, grad_norm_ffn, grad_router,
            grad_gate, grad_up, grad_down,
        ) = pl.pallas_call(
            unpack_grads_kernel,
            out_shape=[
                like((1, part), F32), like(w_query.shape, F32), like(w_key.shape, F32),
                like(w_value.shape, F32), like(w_out.shape, F32), like((1, part), F32),
                like(w_router.shape[::-1], F32), like(w_gate.shape, F32), like(w_up.shape, F32),
                like(w_down.shape, F32),
            ],
            compiler_params=params(),
            cost_estimate=cost(1, 1e7),
        )(
            exchanged, exchanged_second, head_grad, out_grad, w_gate, w_up, w_query, w_key, w_value,
            w_router.T, norm_attn[None], norm_ffn[None],
        )
        grad_router = grad_router.T
        grad_norm_attn = grad_norm_attn.reshape(part)
        grad_norm_ffn = grad_norm_ffn.reshape(part)
    else:
        finished = [exchanged, exchanged_second]
        finished = jnp.stack(finished, axis=1).reshape(E, 3 * part, hidden).astype(F32)
        grad_gate = finished[:, :part]
        grad_up = finished[:, part : 2 * part]
        grad_down = finished[:, 2 * part :].reshape(E, 2, -1, hidden).transpose(0, 2, 1, 3)
        grad_down = grad_down.reshape(E, -1, width)
        head_grad = head_grad.astype(F32)
        grad_query = head_grad[:, :, :LANES].transpose(1, 0, 2).reshape(part, H * HD)
        grad_key = head_grad[:, :, LANES : LANES + HD].transpose(1, 0, 2).reshape(part, KVH * HD)
        grad_value = head_grad[:, :, LANES + HD :].transpose(1, 0, 2).reshape(part, KVH * HD)
        grad_out = out_grad[:, :width]
        grad_router = out_grad[:, width : width + E]

        attn_weights = jnp.concatenate([w_query, w_key, w_value], axis=1).astype(F32)
        attn_grads = jnp.concatenate([grad_query, grad_key, grad_value], axis=1)
        grad_norm_attn = jnp.sum(attn_weights * attn_grads, axis=1) / norm_attn.astype(F32)
        grad_norm_ffn = (
            jnp.sum(w_gate.astype(F32) * grad_gate, axis=(0, 2))
            + jnp.sum(w_up.astype(F32) * grad_up, axis=(0, 2))
            + jnp.sum(w_router.astype(F32) * grad_router, axis=1)
        ) / norm_ffn.astype(F32)
    return (
        block_out.reshape(tokens.shape),
        grad_input.reshape(tokens.shape),
        grad_norm_attn,
        grad_query,
        grad_key,
        grad_value,
        grad_out,
        grad_norm_ffn,
        grad_router,
        grad_gate,
        grad_up,
        grad_down,
    )


def solution(mesh):
    both = ("seq", "row")
    body = functools.partial(shards, mesh.shape["seq"] // UNIT, rows=mesh.shape["row"])
    return jax.shard_map(
        body,
        mesh=mesh,
        in_specs=(
            P("row", "seq", None),
            P("row", None),
            P("row", "seq", None),
            P("row", "seq", None),
            P(both),
            P(both, None),
            P(both, None),
            P(both, None),
            P(both, None),
            P(both),
            P(both, None),
            P(None, both, None),
            P(None, both, None),
            P(None, both, None),
        ),
        out_specs=(
            P("row", "seq", None),
            P("row", "seq", None),
            P(both),
            P(both, None),
            P(both, None),
            P(both, None),
            P(both, None),
            P(both),
            P(both, None),
            P(None, both, None),
            P(None, both, None),
            P(None, both, None),
        ),
        check_vma=False,
    )
```

```python
import functools

import jax
import jax.numpy as jnp
import numpy as np
from jax import lax
from jax.experimental import pallas as pl
from jax.experimental.pallas import tpu as pltpu
from jax.sharding import PartitionSpec as P

H = 16
KVH = 8
TOPK = 8
HD = 64
E = 16
UNIT = 8
LANES = 128
QBLOCK = 256
PIECES = 4
ROWS_IN = 32
ROWS_OUT = 16

EPS = 1e-05
BASE = 10000.0
NEGATIVE = -1e30
F32 = jnp.float32
BF16 = jnp.bfloat16
VMEM_LIMIT = 60 * 1024 * 1024


def dot_nn(left, right):
    return lax.dot_general(left, right, (((1,), (0,)), ((), ())), preferred_element_type=F32)


def dot_nt(left, right):
    return lax.dot_general(left, right, (((1,), (1,)), ((), ())), preferred_element_type=F32)


def dot_tn(left, right):
    return lax.dot_general(left, right, (((0,), (0,)), ((), ())), preferred_element_type=F32)


def params(**kw):
    return pltpu.CompilerParams(vmem_limit_bytes=VMEM_LIMIT, **kw)


def cost(flops, nbytes):
    return pl.CostEstimate(flops=int(flops), bytes_accessed=int(nbytes), transcendentals=0)


def neighbours(seq):
    core = seq % 2
    chip = (seq // 2) % 4
    base = seq - seq % UNIT

    def at(other, same=True):
        return base + 2 * other + (core if same else 1 - core)

    across = chip + 1 - 2 * (chip % 2)
    along = (chip + 2) % 4
    return at(across), at(along), at(3 - chip), at(chip, False)


def greet(targets):
    barrier = pltpu.get_barrier_semaphore()
    for target in targets:
        pl.semaphore_signal(
            barrier, inc=1, device_id=target, device_id_type=pl.DeviceIdType.MESH
        )
    pl.semaphore_wait(barrier, len(targets))


class Pushes:
    def __init__(self, send, recv):
        self.send, self.recv, self.used = send, recv, 0

    def start(self, source, target, device):
        copy = self.make(source, target, device)
        copy.start()
        return copy

    def make(self, source, target, device):
        n = self.used
        self.used += 1
        return pltpu.make_async_remote_copy(
            src_ref=source,
            dst_ref=target,
            send_sem=self.send.at[n],
            recv_sem=self.recv.at[n],
            device_id=device,
            device_id_type=pl.DeviceIdType.MESH,
        )


class Late:
    def __init__(self, places):
        self.places = places

    def specs(self, count):
        return [pl.BlockSpec(memory_space=pl.ANY)] * count

    def scratch(self):
        buffers = [pltpu.VMEM(shape, kind) for _, shape, kind, _ in self.places]
        return buffers + [pltpu.SemaphoreType.DMA((len(self.places),))]

    def wrap(self, kernel, count):
        def wrapped(*refs):
            extra = len(self.places) + 1
            ins, rest = list(refs[:count]), refs[count:-extra]
            *buffers, sems = refs[-extra:]
            copies = []
            for n, (place, _, _, view) in enumerate(self.places):
                source = ins[place] if view is None else view(ins[place])
                copies.append(pltpu.make_async_copy(source, buffers[n], sems.at[n]))
                copies[n].start()
                ins[place] = buffers[n]

            def ready():
                for copy in copies:
                    copy.wait()

            kernel(ready, *ins, *rest)

        return wrapped


def small_view(ref):
    return ref.at[:, pl.ds(2 * LANES, LANES)]


class Bounce:
    def __init__(self, source, middle, target, sems, start=True):
        self.inward = pltpu.make_async_copy(source, middle, sems.at[0])
        self.outward = pltpu.make_async_copy(middle, target, sems.at[1])
        if start:
            self.inward.start()

    def turn(self):
        self.inward.wait()
        self.outward.start()

    def wait(self):
        self.outward.wait()


def pack_kernel_inputs(
    gate_ref, up_ref, down_ref, query_ref, key_ref, value_ref, router_ref, attn_ref, ffn_ref,
    packed, head_ref, gains,
):
    part, hidden = gate_ref.shape[1:]
    half = part // 2
    for n in range(2):
        for b in range(UNIT):
            e = 2 * b + n
            packed[n, b, :part] = gate_ref[e]
            packed[n, b, part : 2 * part] = up_ref[e]
            for c in range(2):
                start = 2 * part + c * half
                packed[n, b, start : start + half] = down_ref[e, :, c * hidden : (c + 1) * hidden]
    gains[...] = jnp.zeros_like(gains)
    gains[:E, :part] = router_ref[...].astype(F32)
    gains[E : E + 1, :part] = attn_ref[...].astype(F32)
    gains[E + 1 : E + 2, :part] = ffn_ref[...].astype(F32)
    small = gains[...].T[:part].astype(BF16)
    low = lane_iota((part, LANES)) < HD
    for pair in range(UNIT // 2):
        lanes = slice(pair * LANES, (pair + 1) * LANES)
        key = key_ref[:, lanes].astype(F32)
        value = value_ref[:, lanes].astype(F32)
        even = jnp.where(low, key, pltpu.roll(value, HD, 1)).astype(BF16)
        odd = jnp.where(low, pltpu.roll(key, HD, 1), value).astype(BF16)
        for b, mixed in ((2 * pair, even), (2 * pair + 1, odd)):
            head_ref[b, :, :LANES] = query_ref[:, b * LANES : (b + 1) * LANES]
            head_ref[b, :, LANES : 2 * LANES] = mixed
            head_ref[b, :, 2 * LANES :] = small


def begin_kernel(rows, raw, *refs):
    inputs, refs = refs[:raw], refs[raw:]
    wout_ref, mine0, mine1, mine2, head_all, wout_all, wout_mid, *refs = refs
    if raw > 2:
        head_mine, packed, head_ref, gains, send, recv, local = refs
    else:
        (packed, head_ref), (head_mine, send, recv, local) = inputs, refs
    seq, row = lax.axis_index("seq"), lax.axis_index("row")
    me = seq % UNIT
    base = seq - me
    unit = [(me + k) % UNIT for k in range(1, UNIT)]
    column = [(row + k) % rows for k in range(1, rows)]
    greet([{"seq": base + b} for b in unit] + [{"row": r} for r in column])
    pushes = Pushes(send, recv)
    outs = [pushes.start(wout_ref, wout_mid.at[row], {"row": r}) for r in column]
    kept = pltpu.make_async_copy(wout_ref, wout_mid.at[row], local.at[4])
    kept.start()
    if raw > 2:
        pack_kernel_inputs(*inputs, packed, head_ref, gains)
    inner = mine1.shape[1]
    upper, lower = pl.ds(0, inner), pl.ds(inner, mine2.shape[1])
    first = pltpu.make_async_copy(head_ref.at[me], head_mine.at[me], local.at[0])
    own = [
        pltpu.make_async_copy(packed.at[0, me], mine0.at[me], local.at[1]),
        pltpu.make_async_copy(packed.at[1, me, upper], mine1.at[me], local.at[2]),
        pltpu.make_async_copy(packed.at[1, me, lower], mine2.at[me], local.at[3]),
    ]
    first.start()
    heads = [pushes.start(head_ref.at[b], head_mine.at[me], {"seq": base + b}) for b in unit]
    others = []
    for source, target in (
        (lambda b: packed.at[0, b], mine0),
        (lambda b: packed.at[1, b, upper], mine1),
        (lambda b: packed.at[1, b, lower], mine2),
    ):
        others += [pushes.start(source(b), target.at[me], {"seq": base + b}) for b in unit]
    for copy in own:
        copy.start()
    first.wait()
    for copy in heads:
        copy.wait_recv()
    last = pltpu.make_async_copy(head_mine, head_all.at[:, row], local.at[5])
    last.start()
    others += [pushes.start(head_mine, head_all.at[:, row], {"row": r}) for r in column]
    kept.wait()
    for copy in outs:
        copy.wait_recv()
    own.append(pltpu.make_async_copy(wout_mid, wout_all.at[me], local.at[6]))
    own[-1].start()
    across, along, _, twin = neighbours(seq)
    a, b, d = across - base, along - base, 6 - me + 2 * (me % 2)
    half = rows // 2
    top, low = pl.ds(0, half), pl.ds(half, rows - half)

    def own_part(part, device):
        return pushes.start(wout_mid.at[part], wout_all.at[me, part], {"seq": device})

    def passed(slot, part, device):
        view = wout_all.at[slot, part]
        others.append(pushes.start(view, view, {"seq": device}))
        return others[-1]

    xa, yb, xb, ya = (
        own_part(top, across), own_part(low, along), own_part(low, across), own_part(top, along)
    )
    others += [own_part(top, twin), own_part(low, twin)]
    xa.wait_recv()
    da = passed(a, top, along)
    passed(a, top, twin)
    yb.wait_recv()
    db = passed(b, low, across)
    passed(b, low, twin)
    xb.wait_recv()
    passed(a, low, twin)
    ya.wait_recv()
    passed(b, top, twin)
    da.wait_recv()
    passed(d, top, twin)
    db.wait_recv()
    passed(d, low, twin)
    others = [copy for copy in others if copy is not da and copy is not db]
    for copy in heads + outs + [xa, yb, xb, ya, da, db]:
        copy.wait_send()
    for copy in own + [last]:
        copy.wait()
    for copy in others:
        copy.wait()


def begin(rows, part, hidden, inputs, w_out):
    any_spec = pl.BlockSpec(memory_space=pl.ANY)
    vmem_spec = pl.BlockSpec(memory_space=pltpu.VMEM)
    count = 4 * (UNIT - 1) + 2 * (rows - 1) + 14
    like = jax.ShapeDtypeStruct
    deep, inner = 3 * part, 2 * part
    head_shape = (UNIT, part, 4 * HD + LANES)
    built = [
        pltpu.VMEM((2, UNIT, deep, hidden), BF16),
        pltpu.VMEM(head_shape, BF16),
        pltpu.VMEM((LANES, LANES), F32),
    ]
    return pl.pallas_call(
        functools.partial(begin_kernel, rows, len(inputs)),
        in_specs=[vmem_spec] * (len(inputs) + 1),
        out_specs=[any_spec] * 5,
        out_shape=[
            like((UNIT, deep, hidden), BF16),
            like((UNIT, inner, hidden), BF16),
            like((UNIT, deep - inner, hidden), BF16),
            like((UNIT, rows) + head_shape[1:], BF16),
            like((UNIT, rows) + w_out.shape, BF16),
        ],
        scratch_shapes=[pltpu.VMEM((rows,) + w_out.shape, BF16), pltpu.VMEM(head_shape, BF16)]
        + (built if len(inputs) > 2 else [])
        + [
            pltpu.SemaphoreType.DMA((count,)),
            pltpu.SemaphoreType.DMA((count,)),
            pltpu.SemaphoreType.DMA((7,)),
        ],
        compiler_params=params(collective_id=0, has_side_effects=True),
        cost_estimate=cost(1, 2e7),
    )(*inputs, w_out)


def unit_gather_kernel(sources, *refs):
    ins, outs = refs[:sources], refs[sources : 2 * sources]
    middles = refs[2 * sources : 3 * sources]
    send, recv, local = refs[3 * sources :]
    seq = lax.axis_index("seq")
    me = seq % UNIT
    base = seq - me
    across, along, _, twin = neighbours(seq)
    a, b, t = across - base, along - base, twin - base
    d = UNIT - 1 - me + 2 * (me % 2) - 1
    greet([{"seq": across}, {"seq": along}, {"seq": twin}])
    pushes = Pushes(send, recv)
    own, done, stage = [], [], []
    for n, (source, target) in enumerate(zip(ins, outs)):
        half = source.shape[0] // 2
        halves = [pl.ds(0, half), pl.ds(half, half)]
        own.append(Bounce(source, middles[n], target.at[me], local.at[n]))

        def part(device, h, source=source, target=target, halves=halves):
            return pushes.start(
                source.at[halves[h]], target.at[me, halves[h]], {"seq": device}
            )

        xa, yb = part(across, 0), part(along, 1)
        xb, ya = part(across, 1), part(along, 0)
        done.append(pushes.start(source, target.at[me], {"seq": twin}))
        stage.append((target, halves, xa, yb, xb, ya))
    for copy in own:
        copy.turn()
    for target, halves, xa, yb, xb, ya in stage:

        def pass_on(slot, h, device, target=target, halves=halves):
            view = target.at[slot, halves[h]]
            return pushes.start(view, view, {"seq": device})

        xa.wait_recv()
        da = pass_on(a, 0, along)
        done.append(pass_on(a, 0, twin))
        yb.wait_recv()
        db = pass_on(b, 1, across)
        done.append(pass_on(b, 1, twin))
        xb.wait_recv()
        done.append(pass_on(a, 1, twin))
        ya.wait_recv()
        done.append(pass_on(b, 0, twin))
        da.wait_recv()
        done.append(pass_on(d, 0, twin))
        db.wait_recv()
        done.append(pass_on(d, 1, twin))
        for copy in (xa, yb, xb, ya, da, db):
            copy.wait_send()
    for copy in own + done:
        copy.wait()


def unit_gather(sources, collective):
    any_spec = pl.BlockSpec(memory_space=pl.ANY)
    n = len(sources)
    return pl.pallas_call(
        functools.partial(unit_gather_kernel, n),
        in_specs=[any_spec] * n,
        out_specs=[any_spec] * n,
        out_shape=[jax.ShapeDtypeStruct((UNIT,) + x.shape, x.dtype) for x in sources],
        scratch_shapes=[pltpu.VMEM(x.shape, x.dtype) for x in sources]
        + [
            pltpu.SemaphoreType.DMA((13 * n,)),
            pltpu.SemaphoreType.DMA((13 * n,)),
            pltpu.SemaphoreType.DMA((n, 2)),
        ],
        compiler_params=params(collective_id=collective, has_side_effects=True),
        cost_estimate=cost(1, 8e7),
    )(*sources)


def bridge_kernel(
    micro, ready, ctx_ref, weights, w_ref, tok_ref, small_ref,
    target, flipped, mixed_ref, normed_ref, ctx_out,
    ctx_in, send, recv, local,
):
    seq = lax.axis_index("seq")
    me = seq % UNIT
    base = seq - me
    unit = [(me + k) % UNIT for k in range(1, UNIT)]
    across, along, _, twin = neighbours(seq)
    greet([{"seq": base + b} for b in unit])
    pushes = Pushes(send, recv)
    arrivals = [
        [pushes.start(ctx_ref.at[b, m], ctx_in.at[me, m], {"seq": base + b}) for b in unit]
        for m in range(micro)
    ]
    mine = pltpu.make_async_copy(ctx_ref.at[me], ctx_in.at[me], local.at[0])
    mine.start()
    turned = pushes.start(weights, flipped, {"seq": twin})
    count, width = tok_ref.shape
    step = count // micro
    half = step // 2
    ready()
    gain = gain_row(small_ref[...], E + 1)
    mine.wait()
    sent = []

    def forward(m):
        top, low = pl.ds(m * step, half), pl.ds(m * step + half, half)
        xa, yb, xb, ya = sent[m]
        xa.wait_recv()
        da = pushes.start(target.at[1, top], target.at[3, top], {"seq": along})
        yb.wait_recv()
        db = pushes.start(target.at[2, low], target.at[3, low], {"seq": across})
        sent[m] = (xa, yb, xb, ya, da, db)

    for m in range(micro):
        here = slice(m * step, (m + 1) * step)
        for copy in arrivals[m]:
            copy.wait_recv()
        for b in range(UNIT):
            ctx_out[here, b * LANES : (b + 1) * LANES] = ctx_in[b, m]
        mixed = tok_ref[here].astype(F32) + dot_nn(ctx_out[here], w_ref[...])
        mixed_ref[here] = mixed
        inverse = lax.rsqrt(jnp.mean(mixed * mixed, axis=-1, keepdims=True) + EPS)
        normed_ref[here] = (mixed * inverse * gain).astype(BF16)
        top, low = pl.ds(m * step, half), pl.ds(m * step + half, half)
        sent.append(
            (
                pushes.start(normed_ref.at[top], target.at[1, top], {"seq": across}),
                pushes.start(normed_ref.at[low], target.at[2, low], {"seq": along}),
                pushes.start(normed_ref.at[low], target.at[1, low], {"seq": across}),
                pushes.start(normed_ref.at[top], target.at[2, top], {"seq": along}),
            )
        )
        if m > 0:
            forward(m - 1)
    last = pltpu.make_async_copy(normed_ref, target.at[0], local.at[1])
    last.start()
    forward(micro - 1)
    for group in sent:
        for copy in group[2:]:
            copy.wait_recv()
        for copy in group:
            copy.wait_send()
    for group in arrivals:
        for copy in group:
            copy.wait_send()
    turned.wait()
    last.wait()


def bridge(ctx_heads, weights, w_out, tokens, heads, collective):
    any_spec = pl.BlockSpec(memory_space=pl.ANY)
    like = jax.ShapeDtypeStruct
    count, width = tokens.shape
    micro = ctx_heads.shape[1]
    pushes = (UNIT - 1) * micro + 6 * micro + 1

    def fixed(i):
        return (0, 0)

    late = Late(
        [
            (2, w_out.shape, BF16, None),
            (3, tokens.shape, BF16, None),
            (4, (width, LANES), BF16, small_view),
        ]
    )

    return pl.pallas_call(
        late.wrap(functools.partial(bridge_kernel, micro), 5),
        grid=(1,),
        in_specs=late.specs(5),
        out_specs=[any_spec] * 2 + [pl.BlockSpec((count, width), fixed)] * 3,
        out_shape=[
            like((4, count, width), BF16),
            like(weights.shape, BF16),
            like((count, width), F32),
            like((count, width), BF16),
            like((count, H * HD), BF16),
        ],
        scratch_shapes=[
            pltpu.VMEM(ctx_heads.shape, BF16),
            pltpu.SemaphoreType.DMA((pushes,)),
            pltpu.SemaphoreType.DMA((pushes,)),
            pltpu.SemaphoreType.DMA((2,)),
        ]
        + late.scratch(),
        compiler_params=params(collective_id=collective, has_side_effects=True),
        cost_estimate=cost(2.0 * count * width * width, 8e7),
    )(ctx_heads, weights, w_out, tokens, heads)


def finish_kernel(
    rows, ready, graw_ref, head_ref, red_ref, pre_ref, out_ref, w_ref, own_ref, tok_ref, small_ref, gmixed_ref,
    head_fin, red_out, out_fin, gin_ref,
    head_col, head_sum, out_sum, out_col, raw_in, red_own, send, recv, local,
):
    seq, row = lax.axis_index("seq"), lax.axis_index("row")
    me = seq % UNIT
    base = seq - me
    unit = [(me + k) % UNIT for k in range(1, UNIT)]
    senders = [(me + UNIT - k) % UNIT for k in range(1, UNIT)]
    column = [(row + k) % rows for k in range(1, rows)]
    greet([{"seq": base + b} for b in unit] + [{"row": r} for r in column])
    pushes = Pushes(send, recv)
    first = pltpu.make_async_copy(head_ref.at[row], head_col.at[row], local.at[0, 0])
    first.start()
    second = pltpu.make_async_copy(graw_ref.at[me], raw_in.at[me], local.at[1, 0])
    second.start()
    heads = [pushes.start(head_ref.at[r], head_col.at[row], {"row": r}) for r in column]
    raws = [pushes.start(graw_ref.at[b], raw_in.at[me], {"seq": base + b}) for b in unit]
    others = [pushes.start(red_ref.at[b], red_out.at[me], {"seq": base + b}) for b in unit]
    bounce = Bounce(red_ref.at[me], red_own, red_out.at[me], local.at[4])
    ready()
    total = pre_ref[me // 2].astype(F32)
    for n in range(3):
        total = total + out_ref[n].astype(F32)
    out_sum[...] = total.astype(BF16)
    bounce.turn()
    third = pltpu.make_async_copy(out_sum.at[row], out_col.at[row], local.at[2, 0])
    third.start()
    outs = [pushes.start(out_sum.at[r], out_col.at[row], {"row": r}) for r in column]
    first.wait()
    for copy in heads:
        copy.wait_recv()
    total = head_col[0].astype(F32)
    for r in range(1, rows):
        total = total + head_col[r].astype(F32)
    head_sum[...] = total.astype(BF16)
    fourth = pltpu.make_async_copy(head_sum.at[me], head_fin.at[me], local.at[3, 0])
    fourth.start()
    others += [pushes.start(head_sum.at[b], head_fin.at[me], {"seq": base + b}) for b in unit]
    count, width = tok_ref.shape
    second.wait()
    acc = dot_nt(raw_in[me].reshape(count, 2 * LANES), own_ref[...])
    for b, copy in zip(senders, raws):
        copy.wait_recv()
        acc = acc + dot_nt(raw_in[b].reshape(count, 2 * LANES), w_ref[b])
    v = tok_ref[...].astype(F32)
    inverse = lax.rsqrt(jnp.mean(v * v, axis=-1, keepdims=True) + EPS)
    scaled = acc * gain_row(small_ref[...], E)
    mean = jnp.mean(scaled * v, axis=-1, keepdims=True)
    grad = gmixed_ref[...] + scaled * inverse - v * (inverse * inverse * inverse * mean)
    gin_ref[...] = grad.astype(BF16)
    third.wait()
    for copy in outs:
        copy.wait_recv()
    total = out_col[0].astype(F32)
    for r in range(1, rows):
        total = total + out_col[r].astype(F32)
    out_fin[...] = total
    for copy in heads + outs + raws:
        copy.wait_send()
    fourth.wait()
    bounce.wait()
    for copy in others:
        copy.wait()


def finish(
    rows, graw, head_term, reduced, pre, out_in, w_heads, tokens, heads, gmixed, collective
):
    any_spec = pl.BlockSpec(memory_space=pl.ANY)
    like = jax.ShapeDtypeStruct
    pushes = 3 * (UNIT - 1) + 2 * (rows - 1)
    count, width = tokens.shape

    def fixed(i):
        return (0, 0)

    late = Late(
        [
            (3, pre.shape, BF16, None),
            (4, out_in.shape, BF16, None),
            (5, w_heads.shape, BF16, None),
            (6, (width, 4 * HD), BF16, lambda ref: ref.at[:, pl.ds(0, 4 * HD)]),
            (7, tokens.shape, BF16, None),
            (8, (width, LANES), BF16, small_view),
            (9, gmixed.shape, F32, None),
        ]
    )

    return pl.pallas_call(
        late.wrap(functools.partial(finish_kernel, rows), 10),
        grid=(1,),
        in_specs=late.specs(10),
        out_specs=[
            any_spec,
            any_spec,
            pl.BlockSpec(pre.shape[2:], fixed),
            pl.BlockSpec(tokens.shape, fixed),
        ],
        out_shape=[
            like(head_term.shape[1:], BF16),
            like(reduced.shape, BF16),
            like(pre.shape[2:], F32),
            like(tokens.shape, BF16),
        ],
        scratch_shapes=[
            pltpu.VMEM(head_term.shape, BF16),
            pltpu.VMEM(head_term.shape[1:], BF16),
            pltpu.VMEM(pre.shape[1:], BF16),
            pltpu.VMEM(pre.shape[1:], BF16),
            pltpu.VMEM(graw.shape, BF16),
            pltpu.VMEM(reduced.shape[1:], BF16),
            pltpu.SemaphoreType.DMA((pushes,)),
            pltpu.SemaphoreType.DMA((pushes,)),
            pltpu.SemaphoreType.DMA((5, 2)),
        ]
        + late.scratch(),
        compiler_params=params(collective_id=collective, has_side_effects=True),
        cost_estimate=cost(4.0 * count * width * width, 6e7),
    )(graw, head_term, reduced, pre, out_in, w_heads, heads, tokens, heads, gmixed)


def lane_iota(shape):
    return lax.broadcasted_iota(jnp.int32, shape, len(shape) - 1)


def turn(u, cosine, sine):
    low_half = lane_iota(u.shape) % HD < HD // 2
    partner = jnp.where(
        low_half, pltpu.roll(u, LANES - HD // 2, u.ndim - 1), pltpu.roll(u, HD // 2, u.ndim - 1)
    )
    return u * cosine + partner * sine


def value_tables(cosine, sine):
    low = lane_iota(cosine.shape) < HD
    return jnp.where(low, cosine, 1.0), jnp.where(low, sine, 0.0)


def gain_row(small, lane):
    return small.astype(F32).T[lane : lane + 1]


def project_kernel(tok_ref, small_ref, w_ref, cos_ref, sin_ref, normed_ref, q_ref, kv_ref):
    count = q_ref.shape[1]
    width = w_ref.shape[0]
    x = tok_ref[...].reshape(count, width).astype(F32)
    inverse = lax.rsqrt(jnp.mean(x * x, axis=-1, keepdims=True) + EPS)
    normed = (x * inverse * gain_row(small_ref[...], E)).astype(BF16)
    normed_ref[...] = normed.reshape(normed_ref.shape)
    raw = dot_nn(normed, w_ref[...])
    cosine, sine = cos_ref[...], sin_ref[...]
    q = turn(raw[:, :LANES], cosine, sine).astype(BF16)
    q_ref[0] = (q.astype(F32) * HD**-0.5).astype(BF16)
    kv_ref[0] = turn(raw[:, LANES:], *value_tables(cosine, sine)).astype(BF16)


def pair_keys(kv):
    kv = kv.astype(F32)
    rolled = pltpu.roll(kv, HD, 1)
    low = lane_iota(kv.shape) < HD
    return jnp.where(low, kv, rolled), jnp.where(low, rolled, kv)


def bias_block(seg_col, seg_row, q_places, first, length):
    key_places = lax.broadcasted_iota(jnp.int32, (length, q_places.shape[1]), 0)
    allowed = (seg_col[:length] == seg_row) & (key_places <= q_places)
    return jnp.where(allowed, 0.0, NEGATIVE)


def attention_kernel(skip, q_ref, kv_ref, segq_ref, segk_ref, place_ref, ctx_ref, lse_ref):
    length = kv_ref.shape[1]
    queries = q_ref.shape[1]
    kk, vv = pair_keys(kv_ref[0])
    v_t = vv.T.astype(BF16)[:HD]
    kk = kk.astype(BF16)
    seg_col = jnp.broadcast_to(segk_ref[0], (8, length)).T[:, :1]
    for block in range(queries // QBLOCK):
        here = slice(block * QBLOCK, (block + 1) * QBLOCK)
        keys = (block + 1) * QBLOCK if skip else length
        bias = bias_block(seg_col, segq_ref[0][:, here], place_ref[:, here], 0, keys)
        q = q_ref[0, here, :]
        low = lane_iota(q.shape) < HD
        parts = []
        for head in range(2):
            mine = jnp.where(low == (head == 0), q, jnp.zeros_like(q))
            scores = dot_nt(kk[:keys], mine) + bias
            top = jnp.max(scores, axis=0, keepdims=True)
            weight = jnp.exp(scores - top)
            total = jnp.sum(weight, axis=0, keepdims=True)
            prob = (weight * (1.0 / total)).astype(BF16)
            parts.append(dot_nn(v_t[:, :keys], prob))
            lse_ref[0, head : head + 1, here] = top + jnp.log(total)
        ctx = jnp.concatenate(parts, axis=0).T.astype(BF16)
        per = QBLOCK // LANES
        ctx_ref[block * per : (block + 1) * per, 0] = ctx.reshape(per, LANES, LANES)


def attend_kernel(
    tok_ref, small_ref, w_ref, cos_ref, sin_ref, segq_ref, segk_ref, place_ref, z_ref, c_ref,
    normed_ref, q_ref, kv_ref, ctx_ref, lse_ref, z_all, c_all,
    z_middle, c_middle, send, recv, local,
):
    m = pl.program_id(0)
    across, along, far, _ = neighbours(lax.axis_index("seq"))
    pushes = Pushes(send, recv)
    count = z_ref.shape[0]
    half = count // 2
    top, low = pl.ds(0, half), pl.ds(half, half)
    first = [
        pushes.make(z_ref.at[top], z_all.at[1, top], {"seq": across}),
        pushes.make(z_ref.at[low], z_all.at[2, low], {"seq": along}),
        pushes.make(z_ref.at[low], z_all.at[1, low], {"seq": across}),
        pushes.make(z_ref.at[top], z_all.at[2, top], {"seq": along}),
    ]
    for n, peer in enumerate((across, along, far)):
        place = pl.ds((n + 1) * count, count)
        first.append(pushes.make(c_ref, c_all.at[:, place], {"seq": peer}))
    second = [
        pushes.make(z_all.at[1, top], z_all.at[3, top], {"seq": along}),
        pushes.make(z_all.at[2, low], z_all.at[3, low], {"seq": across}),
    ]
    bounces = [
        Bounce(z_ref, z_middle, z_all.at[0], local.at[0], False),
        Bounce(c_ref, c_middle, c_all.at[:, pl.ds(0, count)], local.at[1], False),
    ]

    @pl.when(m == 0)
    def _():
        greet([{"seq": across}, {"seq": along}, {"seq": far}])
        for copy in first[:2] + first[4:]:
            copy.start()
        for copy in bounces:
            copy.inward.start()
        for copy in bounces:
            copy.turn()

    project_kernel(tok_ref, small_ref, w_ref, cos_ref, sin_ref, normed_ref, q_ref, kv_ref)

    @pl.when(m == 1)
    def _():
        for copy, onward in zip(first, second):
            copy.wait_recv()
            onward.start()

    attention_kernel(True, q_ref, kv_ref, segq_ref, segk_ref, place_ref, ctx_ref, lse_ref)

    @pl.when(m == 0)
    def _():
        for copy in first[2:4]:
            copy.start()

    @pl.when(m == pl.num_programs(0) - 1)
    def _():
        for copy in first[2:] + second:
            copy.wait_recv()
        for copy in first + second:
            copy.wait_send()
        for copy in bounces:
            copy.wait()


def attention_back_kernel(
    skip, q_ref, kv_ref, segq_ref, segk_ref, place_ref, lse_ref, do_ref, cosq_ref, sinq_ref,
    cosk_ref, sink_ref, normed_ref, pre_ref, red_ref, graw_ref, term_ref, pre_in, red_out,
    dk_acc, dv_acc, term_acc, red_own, send, recv, local,
):
    seq = lax.axis_index("seq")
    me = seq % UNIT
    base = seq - me
    unit = [(me + k) % UNIT for k in range(1, UNIT)]
    pushes = Pushes(send, recv)
    sides = []
    for n, peer in enumerate(neighbours(seq)[:3]):
        sides.append(pushes.make(pre_ref.at[(peer - base) // 2], pre_in.at[n], {"seq": peer}))
    for b in unit:
        sides.append(pushes.make(red_ref.at[b], red_out.at[me], {"seq": base + b}))
    bounce = Bounce(red_ref.at[me], red_own, red_out.at[me], local, False)
    m = pl.program_id(0)

    @pl.when(m == 0)
    def _():
        greet([{"seq": base + b} for b in unit])
        bounce.inward.start()
        for copy in sides:
            copy.start()
        bounce.turn()

    length = kv_ref.shape[1]
    queries = q_ref.shape[1]
    kk, vv = pair_keys(kv_ref[0])
    k_t = kk.T.astype(BF16)[:HD]
    kk = kk.astype(BF16)
    vv = vv.astype(BF16)
    seg_col = jnp.broadcast_to(segk_ref[0], (8, length)).T[:, :1]
    dk_acc[...] = jnp.zeros_like(dk_acc)
    dv_acc[...] = jnp.zeros_like(dv_acc)
    per = QBLOCK // LANES
    for block in range(queries // QBLOCK):
        here = slice(block * QBLOCK, (block + 1) * QBLOCK)
        keys = (block + 1) * QBLOCK if skip else length
        bias = bias_block(seg_col, segq_ref[0][:, here], place_ref[:, here], 0, keys)
        q = q_ref[0, here, :]
        do = do_ref[block * per : (block + 1) * per, 0].reshape(QBLOCK, LANES)
        low = lane_iota(q.shape) < HD
        parts = []
        for head in range(2):
            pick = low == (head == 0)
            mine = jnp.where(pick, q, jnp.zeros_like(q))
            mine_do = jnp.where(pick, do, jnp.zeros_like(do))
            scores = dot_nt(kk[:keys], mine) + bias
            weight = jnp.exp(scores - lse_ref[0, head : head + 1, here])
            product = dot_nt(vv[:keys], mine_do)
            delta = jnp.sum(weight * product, axis=0, keepdims=True)
            grad_scores = (weight * (product - delta)).astype(BF16)
            dv_acc[:keys] += dot_nn(weight.astype(BF16), mine_do)
            dk_acc[:keys] += dot_nn(grad_scores, mine)
            parts.append(dot_nn(k_t[:, :keys], grad_scores))
        dq = jnp.concatenate(parts, axis=0).T * HD**-0.5
        dq = turn(dq, cosq_ref[here, :], -sinq_ref[here, :]).astype(BF16)
        graw_ref[block * per : (block + 1) * per, 0, :, :LANES] = dq.reshape(per, LANES, LANES)
    dk = dk_acc[...]
    dv = dv_acc[...]
    dk = dk + pltpu.roll(dk, HD, 1)
    dv = dv + pltpu.roll(dv, HD, 1)
    gkv = jnp.where(lane_iota(dk.shape) < HD, dk, dv)
    key_cos, key_sin = value_tables(cosk_ref[...], sink_ref[...])
    gkv = turn(gkv, key_cos, -key_sin).astype(BF16)
    graw_ref[:, 0, :, LANES:] = gkv.reshape(length // LANES, LANES, LANES)
    if skip:
        normed_t = normed_ref[...].reshape(queries, -1).T
        term = dot_nn(normed_t, graw_ref[...].reshape(queries, 2 * LANES))
        @pl.when(m == 0)
        def _():
            term_acc[...] = term

        @pl.when(m > 0)
        def _():
            term_acc[...] += term

        @pl.when(m == pl.num_programs(0) - 1)
        def _():
            for b in range(UNIT):
                for r in range(PIECES):
                    at = (b * PIECES + r) * ROWS_IN
                    term_ref[r, b] = term_acc[at : at + ROWS_IN].astype(BF16)

    @pl.when(m == pl.num_programs(0) - 1)
    def _():
        for copy in sides:
            copy.wait()
        bounce.wait()


def spread(rows):
    rest = jnp.zeros((LANES - E, rows.shape[1]), F32)
    return jnp.concatenate([rows.astype(F32), rest], axis=0).T


def soft_gates(normed, router, chosen):
    logits = jnp.where(chosen > 0, dot_nn(normed, router), NEGATIVE)
    top = jnp.max(logits, axis=-1, keepdims=True)
    weight = jnp.where(chosen > 0, jnp.exp(logits - top), 0.0)
    return weight / jnp.sum(weight, axis=-1, keepdims=True)


def unpack(inner_ref, down_ref, first, wg, wu, wd):
    half = wg.shape[1]
    for r in range(PIECES):
        for b in range(UNIT):
            at = (b * PIECES + r) * ROWS_IN
            low = (b * PIECES + r) * ROWS_OUT
            wg[at : at + ROWS_IN] = inner_ref[r, b, :ROWS_IN]
            wu[at : at + ROWS_IN] = inner_ref[r, b, ROWS_IN : 2 * ROWS_IN]
            for c in range(2):
                start = first + c * ROWS_OUT
                wd[low : low + ROWS_OUT, c * half : (c + 1) * half] = down_ref[
                    r, b, start : start + ROWS_OUT
                ]


def load_weights(now, later, first, fetches, wg, wu, wd, greeted):
    e, t = pl.program_id(0), pl.program_id(1)

    @pl.when((t == 0) & (e == 0))
    def _():
        for copy in fetches:
            copy.start()
        greet([{"seq": peer} for peer in greeted])
        unpack(*now, first, wg, wu, wd)

    @pl.when((t == 0) & (e == 1))
    def _():
        for copy in fetches:
            copy.wait()
        unpack(*later, first, wg, wu, wd)


def twin_push(source, target, send, recv):
    twin = neighbours(lax.axis_index("seq"))[3]
    return pltpu.make_async_remote_copy(
        src_ref=source,
        dst_ref=target,
        send_sem=send,
        recv_sem=recv,
        device_id={"seq": twin},
        device_id_type=pl.DeviceIdType.MESH,
    )


def collect_terms(x, dz, grad_gate, grad_up, gated, ag, au, ad, stage, total, dw, sems):
    e, t = pl.program_id(0), pl.program_id(1)
    last_t = pl.num_programs(1) - 1
    half = ag.shape[1]

    @pl.when(t == 0)
    def _():
        ag[...] = dot_tn(x, grad_gate)
        au[...] = dot_tn(x, grad_up)
        ad[...] = dot_tn(gated, dz)

    @pl.when((t > 0) & (t < last_t))
    def _():
        ag[...] += dot_tn(x, grad_gate)
        au[...] += dot_tn(x, grad_up)
        ad[...] += dot_tn(gated, dz)

    send, recv, local = sems
    push = twin_push(stage, total, send.at[0], recv.at[0])
    out = pltpu.make_async_copy(stage, dw, local.at[1])

    def store(write):
        for place, acc, grad in ((0, ag, grad_gate), (ROWS_IN, au, grad_up)):
            final = acc[...] + dot_tn(x, grad)
            for r in range(PIECES):
                for b in range(UNIT):
                    at = (b * PIECES + r) * ROWS_IN
                    write(r, b, place, final[at : at + ROWS_IN])
        final = ad[...] + dot_tn(gated, dz)
        for r in range(PIECES):
            for b in range(UNIT):
                low = (b * PIECES + r) * ROWS_OUT
                for c in range(2):
                    start = 2 * ROWS_IN + c * ROWS_OUT
                    write(r, b, start, final[low : low + ROWS_OUT, c * half : (c + 1) * half])

    @pl.when((t == last_t) & (e == 0))
    def _():
        def write(r, b, place, value):
            stage[r, b, place : place + value.shape[0]] = value.astype(BF16)

        store(write)
        push.start()

    @pl.when((t == last_t) & (e == 1))
    def _():
        push.wait()

        def write(r, b, place, value):
            here = slice(place, place + value.shape[0])
            stage[r, b, here] = (value + total[r, b, here].astype(F32)).astype(BF16)

        store(write)
        out.start()
        out.wait()


def sigmoid(v):
    return 0.5 + 0.5 * jnp.tanh(0.5 * v)


def grads_of(gate_act, up_act, back, gate):
    sig = sigmoid(gate_act)
    silu = gate_act * sig
    hidden = silu * up_act
    grad_hidden = back * gate
    grad_gate = (grad_hidden * up_act * (sig + silu * (1.0 - sig))).astype(BF16)
    grad_up = (grad_hidden * silu).astype(BF16)
    return hidden, grad_gate, grad_up


def expert_id(twin, index):
    me = lax.axis_index("seq") % UNIT
    return 2 * (me + twin * (1 - 2 * (me % 2))) + index


def pick_gate(gates, gid):
    mine = lane_iota(gates.shape) == gid
    return mine, jnp.sum(jnp.where(mine, gates, 0.0), axis=1, keepdims=True)


def gate_terms(mine, hidden, back):
    terms = jnp.where(mine, jnp.sum(hidden * back, axis=1, keepdims=True), 0.0)
    return terms.T[:E]


def both_kernel(
    x_ref, dz_ref, chosen_ref, wr_ref, w0_ref, w1_hbm, heads_ref,
    out_ref, dx_ref, gg_ref, gates_ref, dw, w_heads,
    wg, wu, wd, gates_s, ag, au, ad, oacc, dxacc, ggacc, w1_ref, stage, total,
    send, recv, local,
):
    e, t = pl.program_id(0), pl.program_id(1)
    tile, width = out_ref.shape
    rows = pl.ds(pl.multiple_of(t * tile, tile), tile)
    x = x_ref[...]
    dz = dz_ref[...]
    last_t = pl.num_programs(1) - 1
    across, along, _, twin = neighbours(lax.axis_index("seq"))
    fetch = pltpu.make_async_copy(w1_hbm, w1_ref, local.at[0])
    packed = (w0_ref, w0_ref)
    load_weights(
        packed, (w1_ref, w1_ref), 2 * ROWS_IN, [fetch], wg, wu, wd, (across, along, twin)
    )

    me = lax.axis_index("seq") % UNIT
    base = lax.axis_index("seq") - me
    a, b, d = across - base, along - base, 6 - me + 2 * (me % 2)
    half = heads_ref.shape[0] // 2
    top, low = pl.ds(0, half), pl.ds(half, half)
    lanes = pl.ds(0, w_heads.shape[2])
    pushes = Pushes(send, recv)
    pushes.used = 1

    def own_part(part, device):
        return pushes.make(heads_ref.at[part, lanes], w_heads.at[me, part], {"seq": device})

    def passed(slot, part, device):
        view = w_heads.at[slot, part]
        return pushes.make(view, view, {"seq": device})

    hop1 = [own_part(top, across), own_part(low, along), own_part(low, across), own_part(top, along)]
    hop1 += [own_part(top, twin), own_part(low, twin)]
    hop2 = [passed(a, top, along), passed(b, low, across), passed(a, top, twin), passed(b, low, twin)]
    hop3 = [passed(a, low, twin), passed(b, top, twin)]
    hop4 = [passed(d, top, twin), passed(d, low, twin)]
    events = (
        (0, 0, (), hop1),
        (0, last_t, hop1[:2], hop2),
        (1, 0, hop1[2:4], hop3),
        (1, 1, hop2[:2], hop4),
    )
    for at_e, at_t, arrived, onward in events:

        @pl.when((e == at_e) & (t == at_t))
        def _(arrived=arrived, onward=onward):
            for copy in arrived:
                copy.wait_recv()
            for copy in onward:
                copy.start()

    @pl.when(e == 0)
    def _():
        gates_s[rows, :] = soft_gates(x, wr_ref[...], spread(chosen_ref[...]))

    mine, gate = pick_gate(gates_s[rows, :], expert_id(1 - e, 0))
    gate_act = dot_nn(x, wg[...])
    up_act = dot_nn(x, wu[...])
    back = dot_nt(dz, wd[...])
    hidden, grad_gate, grad_up = grads_of(gate_act, up_act, back, gate)
    ggterm = gate_terms(mine, hidden, back)
    gated = (hidden * gate).astype(BF16)
    out = dot_nn(gated, wd[...])
    dx = dot_nt(grad_gate, wg[...]) + dot_nt(grad_up, wu[...])

    @pl.when(e == 0)
    def _():
        oacc[rows, :] = out
        dxacc[rows, :] = dx
        ggacc[t] = ggterm

    @pl.when(e == 1)
    def _():
        out_ref[...] = (oacc[rows, :] + out).astype(BF16)
        dx_ref[...] = (dxacc[rows, :] + dx).astype(BF16)
        gg_ref[...] = ggacc[t] + ggterm
        gates_ref[...] = gates_s[rows, :]

    sems = (send, recv, local)
    collect_terms(x, dz, grad_gate, grad_up, gated, ag, au, ad, stage, total, dw, sems)

    @pl.when((e == 1) & (t == last_t))
    def _():
        for copy in hop1[4:] + hop2[2:] + hop3 + hop4:
            copy.wait_recv()
        for copy in hop1 + hop2 + hop3 + hop4:
            copy.wait_send()


def forward_kernel(
    x_ref, gates_ref, inner_ref, down_ref, inner_hbm, down_hbm, oin_ref,
    out_ref, gact_ref, uact_ref, inner_twin, down_twin,
    wg, wu, wd, oacc, inner_next, down_next, send, recv, local,
):
    e, t = pl.program_id(0), pl.program_id(1)
    tile = out_ref.shape[0]
    rows = pl.ds(pl.multiple_of(t * tile, tile), tile)
    x = x_ref[...]
    last_t = pl.num_programs(1) - 1
    turned = [
        twin_push(inner_hbm, inner_next, send.at[0], recv.at[0]),
        twin_push(down_hbm, down_next, send.at[1], recv.at[1]),
    ]
    keeps = [
        pltpu.make_async_copy(inner_next, inner_twin, local.at[0]),
        pltpu.make_async_copy(down_next, down_twin, local.at[1]),
    ]

    @pl.when((e == 0) & (t == 0))
    def _():
        greet([{"seq": neighbours(lax.axis_index("seq"))[3]}])
        for copy in turned:
            copy.start()
        unpack(inner_ref, down_ref, 0, wg, wu, wd)

    @pl.when((e == 1) & (t == 0))
    def _():
        for copy in turned:
            copy.wait()
        for copy in keeps:
            copy.start()
        unpack(inner_next, down_next, 0, wg, wu, wd)

    _, gate = pick_gate(gates_ref[...], expert_id(e, 1))
    gate_act = dot_nn(x, wg[...])
    up_act = dot_nn(x, wu[...])
    gact_ref[0] = gate_act.astype(BF16)
    uact_ref[0] = up_act.astype(BF16)
    gated = (gate_act * sigmoid(gate_act) * up_act * gate).astype(BF16)
    out = dot_nn(gated, wd[...])

    @pl.when(e == 0)
    def _():
        oacc[rows, :] = oin_ref[...].astype(F32) + out

    @pl.when(e == 1)
    def _():
        out_ref[...] = (oacc[rows, :] + out).astype(BF16)

    @pl.when((e == 1) & (t == last_t))
    def _():
        for copy in keeps:
            copy.wait()


def backward_kernel(
    x_ref, dz_ref, gates_ref, gact_ref, uact_ref, inner_ref, down_ref,
    inner_hbm, down_hbm, dxin_ref, ggin_ref,
    out_hbm, dx_ref, gg_ref, dw, out_in,
    wg, wu, wd, ag, au, ad, dxacc, ggacc, inner_next, down_next, stage, total,
    diag_x, diag_y, own_x, own_y, send, recv, local,
):
    e, t = pl.program_id(0), pl.program_id(1)
    tile, width = dx_ref.shape
    rows = pl.ds(pl.multiple_of(t * tile, tile), tile)
    x = x_ref[...]
    dz = dz_ref[...]
    fetches = [
        pltpu.make_async_copy(inner_hbm, inner_next, local.at[0]),
        pltpu.make_async_copy(down_hbm, down_next, local.at[4]),
    ]
    load_weights(
        (inner_ref, down_ref), (inner_next, down_next), 0, fetches, wg, wu, wd,
        neighbours(lax.axis_index("seq")),
    )
    across, along, _, _ = neighbours(lax.axis_index("seq"))
    pushes = Pushes(send, recv)
    pushes.used = 1
    half = own_x.shape[0]
    top, low = pl.ds(0, half), pl.ds(half, half)
    first = [
        pushes.make(out_hbm.at[3, top], diag_x, {"seq": across}),
        pushes.make(out_hbm.at[3, low], diag_y, {"seq": along}),
        pushes.make(out_hbm.at[1, top], out_in.at[0, top], {"seq": across}),
        pushes.make(out_hbm.at[2, low], out_in.at[1, low], {"seq": along}),
    ]
    second = [
        pushes.make(own_x, out_in.at[0, low], {"seq": across}),
        pushes.make(own_y, out_in.at[1, top], {"seq": along}),
    ]
    loads = [
        pltpu.make_async_copy(out_hbm.at[1, low], own_x, local.at[2]),
        pltpu.make_async_copy(out_hbm.at[2, top], own_y, local.at[3]),
    ]

    @pl.when((e == 0) & (t == 0))
    def _():
        for copy in first[:2] + loads:
            copy.start()

    @pl.when((e == 0) & (t == 1))
    def _():
        for copy in first[2:]:
            copy.start()

    mine, gate = pick_gate(gates_ref[...], expert_id(1 - e, 1))
    back = dot_nt(dz, wd[...])
    hidden, grad_gate, grad_up = grads_of(
        gact_ref[0].astype(F32), uact_ref[0].astype(F32), back, gate
    )
    ggterm = gate_terms(mine, hidden, back)
    gated = (hidden * gate).astype(BF16)
    dx = dot_nt(grad_gate, wg[...]) + dot_nt(grad_up, wu[...])

    @pl.when(e == 0)
    def _():
        dxacc[rows, :] = dxin_ref[...].astype(F32) + dx
        ggacc[t] = ggin_ref[...] + ggterm

    @pl.when(e == 1)
    def _():
        dx_ref[...] = (dxacc[rows, :] + dx).astype(BF16)
        gg_ref[...] = ggacc[t] + ggterm

    sems = (send, recv, local)
    collect_terms(x, dz, grad_gate, grad_up, gated, ag, au, ad, stage, total, dw, sems)

    @pl.when((e == 0) & (t == pl.num_programs(1) - 1))
    def _():
        for copy in loads:
            copy.wait()
        first[0].wait_recv()
        first[1].wait_recv()
        own_x[...] = (own_x[...].astype(F32) + diag_y[...].astype(F32)).astype(BF16)
        own_y[...] = (own_y[...].astype(F32) + diag_x[...].astype(F32)).astype(BF16)
        for copy in second:
            copy.start()

    @pl.when((e == 1) & (t == pl.num_programs(1) - 1))
    def _():
        first[0].wait_send()
        first[1].wait_send()
        for copy in first[2:] + second:
            copy.wait()


def run_experts(which, x, dz, chosen, weights, router=None, gates=None, carried=None, acts=None, pushed=None):
    tokens, width = x.shape
    hidden = weights[0].shape[3]
    packed_shape = (PIECES, UNIT, 3 * ROWS_IN, hidden)
    inner_shape = (PIECES, UNIT, 2 * ROWS_IN, hidden)
    down_shape = (PIECES, UNIT, ROWS_IN, hidden)
    tiles = 2 if which == "forward" else 3
    tile = tokens // tiles
    like = jax.ShapeDtypeStruct
    any_spec = pl.BlockSpec(memory_space=pl.ANY)
    once = pl.Buffered(1)

    def by_token(e, t):
        return (t, 0)

    def at_end(e, t):
        return (jnp.where(e == 1, t, 0), 0)

    def at_start(e, t):
        return (jnp.where(e == 0, t, tiles - 1), 0)

    def lanes_end(e, t):
        return (0, jnp.where(e == 1, t, 0))

    def lanes_start(e, t):
        return (0, jnp.where(e == 0, t, tiles - 1))

    def acts_map(e, t):
        return (e, t, 0)

    x_spec = pl.BlockSpec((tile, width), by_token)
    gates_spec = pl.BlockSpec((tile, LANES), by_token)

    def weight_spec(shape):
        return pl.BlockSpec(shape, lambda e, t: (0, 0, 0, 0), pipeline_mode=once)

    acts_spec = pl.BlockSpec((1, tile, hidden), acts_map)
    acts_back = pl.BlockSpec((1, tile, hidden), lambda e, t: (1 - e, t, 0))
    token_end = pl.BlockSpec((tile, width), at_end)
    token_start = pl.BlockSpec((tile, width), at_start)
    packed_like = like(packed_shape, BF16)
    pair_like = [like(inner_shape, BF16), like(down_shape, BF16)]
    pair_vmem = [pltpu.VMEM(inner_shape, BF16), pltpu.VMEM(down_shape, BF16)]
    pair_specs = [weight_spec(inner_shape), weight_spec(down_shape), any_spec, any_spec]
    token_like = like((tokens, width), BF16)
    gg_like = like((E, tokens), F32)
    acts_like = like((2, tokens, hidden), BF16)
    unpacked = [
        pltpu.VMEM((width, hidden), BF16),
        pltpu.VMEM((width, hidden), BF16),
        pltpu.VMEM((hidden, width), BF16),
    ]
    terms = [
        pltpu.VMEM((width, hidden), F32),
        pltpu.VMEM((width, hidden), F32),
        pltpu.VMEM((hidden, width), F32),
    ]
    acc = pltpu.VMEM((tokens, width), F32)
    gg_acc = pltpu.VMEM((tiles, E, tile), F32)
    second = pltpu.VMEM(packed_shape, BF16)
    stage = pltpu.VMEM(packed_shape, BF16)
    sem, sems = pltpu.SemaphoreType.DMA, pltpu.SemaphoreType.DMA((2,))
    flops = 4.0 * tokens * width * hidden
    if which == "both":
        return pl.pallas_call(
            both_kernel,
            grid=(2, tiles),
            in_specs=[
                x_spec, x_spec, pl.BlockSpec((E, tile), lambda e, t: (0, t)),
                pl.BlockSpec((width, LANES), lambda e, t: (0, 2), pipeline_mode=once),
                weight_spec(packed_shape), any_spec, any_spec,
            ],
            out_specs=[
                token_end, token_end, pl.BlockSpec((E, tile), lanes_end),
                pl.BlockSpec((tile, LANES), at_end), any_spec, any_spec,
            ],
            out_shape=[
                token_like, token_like, gg_like, like((tokens, LANES), F32),
                packed_like, like((UNIT, width, 4 * HD), BF16),
            ],
            scratch_shapes=unpacked
            + [pltpu.VMEM((tokens, LANES), F32)]
            + terms
            + [acc, acc, gg_acc, second, stage, stage]
            + [pltpu.SemaphoreType.DMA((15,)), pltpu.SemaphoreType.DMA((15,)), sems],
            compiler_params=params(collective_id=5, has_side_effects=True),
            cost_estimate=cost(1, 1e5),
        )(x, dz, chosen, router, *weights, router)
    if which == "forward":
        return pl.pallas_call(
            forward_kernel,
            grid=(2, tiles),
            in_specs=[x_spec, gates_spec] + pair_specs + [token_start],
            out_specs=[token_end, acts_spec, acts_spec, any_spec, any_spec],
            out_shape=[token_like, acts_like, acts_like] + pair_like,
            scratch_shapes=unpacked + [acc] + pair_vmem + [sems, sems, sems],
            compiler_params=params(collective_id=9, has_side_effects=True),
            cost_estimate=cost(3 * flops, 2e7),
        )(x, gates, *weights, *weights, carried)
    return pl.pallas_call(
        backward_kernel,
        grid=(2, tiles),
        in_specs=[
            x_spec, x_spec, gates_spec, acts_back, acts_back, *pair_specs,
            token_start, pl.BlockSpec((E, tile), lanes_start), any_spec,
        ],
        out_specs=[token_end, pl.BlockSpec((E, tile), lanes_end), any_spec, any_spec],
        out_shape=[
            token_like, gg_like, packed_like, like((2,) + pushed.shape[1:], BF16),
        ],
        scratch_shapes=unpacked + terms + [acc, gg_acc]
        + pair_vmem
        + [stage, stage]
        + [pltpu.VMEM((pushed.shape[1] // 2, width), BF16)] * 4
        + [pltpu.SemaphoreType.DMA((7,)), pltpu.SemaphoreType.DMA((7,))]
        + [pltpu.SemaphoreType.DMA((5,))],
        compiler_params=params(collective_id=6, has_side_effects=True),
        cost_estimate=cost(6 * flops, 2e7),
    )(x, dz, gates, acts[0], acts[1], *weights, carried[0], carried[1], pushed)


def return_kernel(
    micro, copies, ready, dx_ref, gg_ref, mixed_ref, normed_ref, dz_ref, chosen_ref, small_ref, w_ref,
    ctx_ref, own_out, back_out, do_out, gmixed_ref, pre_ref, block_ref,
    mine_dx, from_x, from_y, diag_x, diag_y, sum_x, sum_y, gparts, gctx, gbranch, glogs, term, twin_term, send, recv, local,
):
    seq = lax.axis_index("seq")
    me = seq % UNIT
    core = me % 2
    base = seq - me
    unit = [(me + k) % UNIT for k in range(1, UNIT)]
    *peers, twin = neighbours(seq)
    greet([{"seq": base + b} for b in unit])
    pushes = Pushes(send, recv)
    count, width = mixed_ref.shape
    step = count // micro
    half = step // 2
    chunks = [pl.ds(m * step, step) for m in range(micro)]
    tops = [pl.ds(m * step, half) for m in range(micro)]
    lows = [pl.ds(m * step + half, half) for m in range(micro)]
    across, along = peers[:2]
    own = [
        pltpu.make_async_copy(dx_ref, mine_dx, local.at[0]),
        pltpu.make_async_copy(gg_ref.at[:, pl.ds(0, count)], gparts.at[0], local.at[1]),
    ]
    for copy in own:
        copy.start()
    diagonal, direct, sums = [], [], []

    def send_diagonal(m):
        diagonal.append(
            (
                pushes.start(dx_ref.at[3, tops[m]], diag_x.at[m], {"seq": across}),
                pushes.start(dx_ref.at[3, lows[m]], diag_y.at[m], {"seq": along}),
            )
        )

    def send_direct(m):
        direct.append(
            (
                pushes.start(dx_ref.at[1, tops[m]], from_x.at[tops[m]], {"seq": across}),
                pushes.start(dx_ref.at[2, lows[m]], from_y.at[lows[m]], {"seq": along}),
            )
        )

    def send_sums(m):
        for copy in diagonal[m]:
            copy.wait_recv()
        own_y = mine_dx[2, tops[m]].astype(F32) + diag_x[m].astype(F32)
        own_x = mine_dx[1, lows[m]].astype(F32) + diag_y[m].astype(F32)
        sum_y[m] = own_y.astype(BF16)
        sum_x[m] = own_x.astype(BF16)
        sums.append(
            (
                pushes.start(sum_y.at[m], from_y.at[tops[m]], {"seq": along}),
                pushes.start(sum_x.at[m], from_x.at[lows[m]], {"seq": across}),
            )
        )

    send_diagonal(0)
    first = []
    for n in (2, 0, 1):
        part = gg_ref.at[:, pl.ds((n + 1) * count, count)]
        first.append(pushes.start(part, gparts.at[n + 1], {"seq": peers[n]}))
    send_direct(0)
    if micro > 1:
        send_diagonal(1)
    ready()
    small = small_ref[...]
    gain = gain_row(small, E + 1)
    gates = soft_gates(normed_ref[...], small, spread(chosen_ref[...]))
    block = mixed_ref[...] + own_out[0].astype(F32) + back_out[0].astype(F32)
    block_ref[...] = (block + back_out[1].astype(F32)).astype(BF16)
    for copy in own:
        copy.wait()
    for copy in first:
        copy.wait_recv()
    grad_gates = gparts[0] + gparts[1] + gparts[2] + gparts[3]
    grad_gates = spread(grad_gates)
    centre = jnp.sum(gates * grad_gates, axis=-1, keepdims=True)
    glogs[...] = (gates * (grad_gates - centre)).astype(BF16)
    sent = []

    def compute(m):
        here = chunks[m]
        for copy in direct[m] + sums[m]:
            copy.wait_recv()
        dy = mine_dx[0, here].astype(F32) + from_x[here].astype(F32) + from_y[here].astype(F32)
        dy = dy + dot_nt(glogs[here], small)
        v = mixed_ref[here]
        inverse = lax.rsqrt(jnp.mean(v * v, axis=-1, keepdims=True) + EPS)
        scaled = dy * gain
        mean = jnp.mean(scaled * v, axis=-1, keepdims=True)
        gmixed = dz_ref[here].astype(F32) + scaled * inverse
        gmixed = gmixed - v * (inverse * inverse * inverse * mean)
        gmixed_ref[here] = gmixed
        branch = gmixed.astype(BF16)
        gbranch[here] = branch
        grad_ctx = dot_nt(branch, w_ref[...]).astype(BF16)
        for b in range(UNIT):
            gctx[b, m] = grad_ctx[:, b * LANES : (b + 1) * LANES]
        mine = pltpu.make_async_copy(gctx.at[me, m], do_out.at[me, m], local.at[2 + m])
        mine.start()
        own.append(mine)
        for b in unit:
            sent.append(pushes.start(gctx.at[b, m], do_out.at[me, m], {"seq": base + b}))

    for m in range(micro):
        send_sums(m)
        if m + 1 < micro:
            send_direct(m + 1)
        if m + 2 < micro:
            send_diagonal(m + 2)
        if m > 0:
            compute(m - 1)
    compute(micro - 1)
    rest = width // (copies * UNIT)
    out_term = dot_tn(ctx_ref[...], gbranch[...]).astype(BF16)
    router_term = dot_tn(normed_ref[...], glogs[...]).astype(BF16)
    for a in range(copies):
        for b in range(UNIT):
            at = (a * UNIT + b) * rest
            term[a, b, :, :width] = out_term[at : at + rest]
            term[a, b, :, width:] = router_term[at : at + rest]
    turned = [
        pushes.start(term.at[:, 2 * j + 1 - core], twin_term.at[j], {"seq": twin})
        for j in range(4)
    ]
    for j, copy in enumerate(turned):
        copy.wait_recv()
        summed = term[:, 2 * j + core].astype(F32) + twin_term[j].astype(F32)
        pre_ref[j] = summed.astype(BF16)
    for group in [first] + diagonal + direct + sums:
        for copy in group:
            copy.wait_send()
    for copy in turned:
        copy.wait_send()
    for copy in own[2:] + sent:
        copy.wait()


def return_tokens(
    dx, gg, mixed, normed, dz, chosen, heads, w_out, context, own_out, back_out, micro, copies, collective
):
    any_spec = pl.BlockSpec(memory_space=pl.ANY)
    like = jax.ShapeDtypeStruct
    count, width = mixed.shape
    ctx_shape = (UNIT, micro, count // micro, LANES)
    pre_shape = (4, copies, width // (copies * UNIT), width + LANES)
    pushes = 3 + 6 * micro + (UNIT - 1) * micro + 4
    piece = (micro, count // micro // 2, width)

    def fixed(i):
        return (0, 0)

    late = Late(
        [
            (2, mixed.shape, F32, None),
            (3, normed.shape, BF16, None),
            (4, dz.shape, BF16, None),
            (5, chosen.shape, BF16, None),
            (6, (width, LANES), BF16, small_view),
            (7, w_out.shape, BF16, None),
            (8, context.shape, BF16, None),
            (9, (1, count, width), BF16, lambda ref: ref.at[pl.ds(0, 1)]),
            (10, back_out.shape, BF16, None),
        ]
    )

    return pl.pallas_call(
        late.wrap(functools.partial(return_kernel, micro, copies), 11),
        grid=(1,),
        in_specs=late.specs(11),
        out_specs=[
            any_spec,
            pl.BlockSpec((count, width), fixed),
            pl.BlockSpec(pre_shape, lambda i: (0, 0, 0, 0)),
            pl.BlockSpec((count, width), fixed),
        ],
        out_shape=[
            like(ctx_shape, BF16),
            like((count, width), F32),
            like(pre_shape, BF16),
            like((count, width), BF16),
        ],
        scratch_shapes=[
            pltpu.VMEM((4, count, width), BF16),
            pltpu.VMEM((count, width), BF16),
            pltpu.VMEM((count, width), BF16),
            pltpu.VMEM(piece, BF16),
            pltpu.VMEM(piece, BF16),
            pltpu.VMEM(piece, BF16),
            pltpu.VMEM(piece, BF16),
            pltpu.VMEM((4, E, count), F32),
            pltpu.VMEM(ctx_shape, BF16),
            pltpu.VMEM((count, width), BF16),
            pltpu.VMEM((count, LANES), BF16),
            pltpu.VMEM((copies, UNIT) + pre_shape[2:], BF16),
            pltpu.VMEM(pre_shape, BF16),
            pltpu.SemaphoreType.DMA((pushes,)),
            pltpu.SemaphoreType.DMA((pushes,)),
            pltpu.SemaphoreType.DMA((2 + micro,)),
        ]
        + late.scratch(),
        compiler_params=params(collective_id=collective, has_side_effects=True),
        cost_estimate=cost(4.0 * count * width * width, 1.2e8),
    )(dx, gg, mixed, normed, dz, chosen, heads, w_out, context, own_out, back_out)


def unpack_grads_kernel(
    ex0, ex1, head_ref, out_ref, gate_w, up_w, query_w, key_w, value_w, router_w, attn_ref, ffn_ref,
    gattn, gquery, gkey, gvalue, gout, gffn, grouter, ggate, gup, gdown,
):
    part, hidden = gate_w.shape[1:]
    half = part // 2
    width = gout.shape[1]
    ffn = jnp.zeros((part, hidden), F32)
    for n, source in enumerate((ex0, ex1)):
        for b in range(UNIT):
            e = 2 * b + n
            gate = source[b, :part].astype(F32)
            up = source[b, part : 2 * part].astype(F32)
            ggate[e] = gate
            gup[e] = up
            ffn = ffn + gate * gate_w[e].astype(F32) + up * up_w[e].astype(F32)
            for c in range(2):
                start = 2 * part + c * half
                gdown[e, :, c * hidden : (c + 1) * hidden] = source[b, start : start + half].astype(
                    F32
                )
    router = out_ref[:, width:].T[:E]
    grouter[...] = router
    gout[...] = out_ref[:, :width]
    low = lane_iota((part, LANES)) < HD
    attn = jnp.zeros((part, LANES), F32)
    for pair in range(UNIT // 2):
        lanes = slice(pair * LANES, (pair + 1) * LANES)
        even = head_ref[2 * pair, :, LANES:].astype(F32)
        odd = head_ref[2 * pair + 1, :, LANES:].astype(F32)
        key = jnp.where(low, even, pltpu.roll(odd, HD, 1))
        value = jnp.where(low, pltpu.roll(even, HD, 1), odd)
        gkey[:, lanes] = key
        gvalue[:, lanes] = value
        attn = attn + key * key_w[:, lanes].astype(F32) + value * value_w[:, lanes].astype(F32)
    for b in range(UNIT):
        lanes = slice(b * LANES, (b + 1) * LANES)
        query = head_ref[b, :, :LANES].astype(F32)
        gquery[:, lanes] = query
        attn = attn + query * query_w[:, lanes].astype(F32)

    def as_row(column):
        return jnp.broadcast_to(column, (part, LANES)).T[:1]

    attn = jnp.sum(attn, axis=1, keepdims=True)
    ffn = jnp.sum(ffn, axis=1, keepdims=True)
    gattn[...] = as_row(attn) / attn_ref[...].astype(F32)
    routed = jnp.sum(router * router_w[...].astype(F32), axis=0, keepdims=True)
    gffn[...] = (as_row(ffn) + routed) / ffn_ref[...].astype(F32)


def shards(
    copies, tokens, segments, routes, cotangent, norm_attn, w_query, w_key, w_value, w_out, norm_ffn,
    w_router, w_gate, w_up, w_down, rows,
):
    micro, local_len, width = tokens.shape
    length = segments.shape[1]
    count = micro * local_len
    unit_len = UNIT * local_len
    part = w_query.shape[0]
    hidden = w_gate.shape[2]
    seq_size = copies * UNIT
    seq = lax.axis_index("seq")
    row = lax.axis_index("row")
    unit = seq // UNIT
    me = seq % UNIT
    unit_groups = None
    copy_groups = None
    if copies > 1:
        unit_groups = [[a * UNIT + b for b in range(UNIT)] for a in range(copies)]
        copy_groups = [[a * UNIT + b for a in range(copies)] for b in range(UNIT)]

    def exchange(x):
        return lax.all_to_all(x, "seq", 0, 0, tiled=True, axis_index_groups=unit_groups)

    def flip(x, k):
        return lax.ppermute(x, "seq", [(s, s ^ k) for s in range(seq_size)])

    flat_tokens = tokens.reshape(count, width)

    def wait_for(x, *others):
        return lax.optimization_barrier((x,) + others)[0]

    if copies == 1:
        inputs = [
            w_gate, w_up, w_down, w_query, w_key, w_value, w_router.T, norm_attn[None],
            norm_ffn[None],
        ]
    else:
        small = jnp.concatenate(
            [w_router.T, norm_attn[None], norm_ffn[None], jnp.zeros((LANES - 2 - E, part), BF16)], axis=0
        ).T
        head_part = jnp.concatenate(
            [
                w_query.reshape(part, UNIT, 2 * HD),
                w_key.reshape(part, UNIT, HD),
                w_value.reshape(part, UNIT, HD),
                jnp.broadcast_to(small[:, None], (part, UNIT, LANES)),
            ],
            axis=2,
        ).transpose(1, 0, 2)

        down_halves = w_down.reshape(E, -1, 2, hidden).transpose(0, 2, 1, 3).reshape(E, part, hidden)
        packed_part = jnp.concatenate([w_gate, w_up, down_halves], axis=1)
        packed_part = packed_part.reshape(UNIT, E // UNIT, 3 * part, hidden).transpose(1, 0, 2, 3)
        inputs = [packed_part, head_part]
    *packed_mine, heads_all, w_out_rows = begin(rows, part, hidden, inputs, w_out)

    if copies > 1:
        heads_all = lax.all_gather(heads_all, "seq", axis=0, axis_index_groups=copy_groups)
        w_out_rows = lax.all_gather(w_out_rows, "seq", axis=0, axis_index_groups=copy_groups)
    w_out_all = w_out_rows.reshape(H * HD, width)
    heads_all = heads_all.reshape(width, 4 * HD + LANES)

    def gather_packed(x):
        x = lax.all_gather(x, "row", axis=0)
        if copies > 1:
            x = lax.all_gather(x, "seq", axis=0, axis_index_groups=copy_groups)
            x = x.transpose(0, 2, 1, 3, 4).reshape(-1, 3 * part, hidden)
            halves = x[:, 2 * part :].reshape(-1, 2, part // 2, hidden).transpose(0, 2, 1, 3)
            return pack(
                x[:, :part].reshape(width, hidden),
                x[:, part : 2 * part].reshape(width, hidden),
                halves.reshape(hidden, width),
            )
        return x

    def pack(gate, up, down):
        gate = gate.reshape(UNIT, PIECES, ROWS_IN, hidden)
        up = up.reshape(UNIT, PIECES, ROWS_IN, hidden)
        down = down.reshape(UNIT, PIECES, ROWS_OUT, 2, hidden).transpose(0, 1, 3, 2, 4)
        down = down.reshape(UNIT, PIECES, ROWS_IN, hidden)
        return jnp.concatenate([gate, up, down], axis=2).transpose(1, 0, 2, 3)

    def repack(x):
        x = x.transpose(1, 0, 2, 3)
        gate = x[:, :, :ROWS_IN].reshape(copies, UNIT, rows, part, hidden)
        up = x[:, :, ROWS_IN : 2 * ROWS_IN].reshape(copies, UNIT, rows, part, hidden)
        down = x[:, :, 2 * ROWS_IN :].reshape(UNIT, PIECES, 2, ROWS_OUT, hidden)
        down = down.transpose(0, 1, 3, 2, 4).reshape(copies, UNIT, rows, part // 2, 2, hidden)
        down = down.transpose(0, 1, 2, 4, 3, 5).reshape(copies, UNIT, rows, part, hidden)
        return jnp.concatenate([gate, up, down], axis=3).transpose(2, 0, 1, 3, 4)

    own_first = gather_packed(packed_mine[0])
    if copies > 1:
        whole_second = gather_packed(jnp.concatenate(packed_mine[1:], axis=1))
        own_second = (whole_second[:, :, : 2 * ROWS_IN], whole_second[:, :, 2 * ROWS_IN :])
    else:
        own_second = tuple(gather_packed(x) for x in packed_mine[1:])

    (tok_all,) = unit_gather([wait_for(flat_tokens, w_out_all)], 1)
    tok_all = tok_all.reshape(UNIT, micro, local_len, width)

    chosen = jnp.any(
        routes.reshape(count, TOPK).T[:, None, :] == jnp.arange(E, dtype=jnp.int32)[None, :, None],
        axis=0,
    ).astype(BF16)
    dz_own = cotangent.reshape(count, width)

    frequency = BASE ** (-2.0 * np.arange(HD // 2) / HD)
    angles = np.arange(length)[:, None].astype(np.float32) * frequency[None].astype(np.float32)
    key_cos = jnp.asarray(np.tile(np.cos(angles), (1, 4)).astype(np.float32))
    key_sin = np.concatenate([-np.sin(angles), np.sin(angles)] * 2, axis=1)
    key_sin = jnp.asarray(key_sin.astype(np.float32))
    places = jnp.asarray(np.arange(unit_len, dtype=np.int32))
    cosine, sine = key_cos, key_sin
    if copies > 1:
        places = unit * unit_len + places
        cosine = lax.dynamic_slice_in_dim(key_cos, unit * unit_len, unit_len, 0)
        sine = lax.dynamic_slice_in_dim(key_sin, unit * unit_len, unit_len, 0)

    def by_row4(m):
        return (0, m, 0, 0)

    def by_row3(m):
        return (m, 0, 0)

    def fixed(*_):
        return (0, 0)

    def zeros3(*_):
        return (0, 0, 0)

    def zeros4(*_):
        return (0, 0, 0, 0)

    def small_block(*_):
        return (0, 2)

    seg_keys = segments.astype(F32).reshape(micro, 1, length)
    seg_queries = seg_keys
    if copies > 1:
        seg_queries = lax.dynamic_slice_in_dim(seg_keys, unit * unit_len, unit_len, 2)
    skip = copies == 1
    place_row = places[None]
    attention_flops = 4.0 * micro * unit_len * length * 2 * LANES
    attention_specs = [
        pl.BlockSpec((1, unit_len, LANES), by_row3),
        pl.BlockSpec((1, length, LANES), by_row3),
        pl.BlockSpec((1, 1, unit_len), by_row3),
        pl.BlockSpec((1, 1, length), by_row3),
        pl.BlockSpec((1, unit_len), fixed),
    ]
    if copies == 1:
        normed_all, q_all, kv_all, ctx_heads, lse, dz_all, chosen_all = pl.pallas_call(
            attend_kernel,
            grid=(micro,),
            in_specs=[
                pl.BlockSpec((UNIT, 1, local_len, width), by_row4),
                pl.BlockSpec((width, LANES), small_block),
                pl.BlockSpec((width, 4 * HD), fixed),
                pl.BlockSpec((unit_len, LANES), fixed),
                pl.BlockSpec((unit_len, LANES), fixed),
            ]
            + attention_specs[2:]
            + [pl.BlockSpec(memory_space=pl.ANY)] * 2,
            out_specs=[
                pl.BlockSpec((UNIT, 1, local_len, width), by_row4),
                pl.BlockSpec((1, unit_len, LANES), by_row3),
                pl.BlockSpec((1, unit_len, LANES), by_row3),
                pl.BlockSpec((UNIT, 1, local_len, LANES), by_row4),
                pl.BlockSpec((1, 2, unit_len), by_row3),
                pl.BlockSpec(memory_space=pl.ANY),
                pl.BlockSpec(memory_space=pl.ANY),
            ],
            out_shape=[
                jax.ShapeDtypeStruct((UNIT, micro, local_len, width), BF16),
                jax.ShapeDtypeStruct((micro, unit_len, LANES), BF16),
                jax.ShapeDtypeStruct((micro, unit_len, LANES), BF16),
                jax.ShapeDtypeStruct((UNIT, micro, local_len, LANES), BF16),
                jax.ShapeDtypeStruct((micro, 2, unit_len), F32),
                jax.ShapeDtypeStruct((4, count, width), BF16),
                jax.ShapeDtypeStruct((E, 4 * count), BF16),
            ],
            scratch_shapes=[
                pltpu.VMEM((count, width), BF16),
                pltpu.VMEM((E, count), BF16),
                pltpu.SemaphoreType.DMA((9,)),
                pltpu.SemaphoreType.DMA((9,)),
                pltpu.SemaphoreType.DMA((2, 2)),
            ],
            compiler_params=params(collective_id=8, has_side_effects=True),
            cost_estimate=cost(attention_flops, 4e6),
        )(
            tok_all, heads_all, heads_all, cosine, sine, seg_queries, seg_keys, place_row, dz_own,
            chosen,
        )
    else:
        normed_all, q_all, kv_own = pl.pallas_call(
            project_kernel,
            grid=(micro,),
            in_specs=[
                pl.BlockSpec((UNIT, 1, local_len, width), by_row4),
                pl.BlockSpec((width, LANES), small_block),
                pl.BlockSpec((width, 4 * HD), fixed),
                pl.BlockSpec((unit_len, LANES), fixed),
                pl.BlockSpec((unit_len, LANES), fixed),
            ],
            out_specs=[
                pl.BlockSpec((UNIT, 1, local_len, width), by_row4),
                pl.BlockSpec((1, unit_len, LANES), by_row3),
                pl.BlockSpec((1, unit_len, LANES), by_row3),
            ],
            out_shape=[
                jax.ShapeDtypeStruct((UNIT, micro, local_len, width), BF16),
                jax.ShapeDtypeStruct((micro, unit_len, LANES), BF16),
                jax.ShapeDtypeStruct((micro, unit_len, LANES), BF16),
            ],
            compiler_params=params(),
            cost_estimate=cost(2.0 * UNIT * count * width * 4 * HD, 1.5e7),
        )(tok_all, heads_all, heads_all, cosine, sine)
        kv_all = lax.all_gather(kv_own, "seq", axis=1, tiled=True, axis_index_groups=copy_groups)
        ctx_heads, lse = pl.pallas_call(
            functools.partial(attention_kernel, skip),
            grid=(micro,),
            in_specs=attention_specs,
            out_specs=[
                pl.BlockSpec((UNIT, 1, local_len, LANES), by_row4),
                pl.BlockSpec((1, 2, unit_len), by_row3),
            ],
            out_shape=[
                jax.ShapeDtypeStruct((UNIT, micro, local_len, LANES), BF16),
                jax.ShapeDtypeStruct((micro, 2, unit_len), F32),
            ],
            compiler_params=params(),
            cost_estimate=cost(attention_flops, 4e6),
        )(q_all, kv_all, seg_queries, seg_keys, place_row)
        dz_all = jnp.stack([dz_own] + [flip(dz_own, k) for k in (2, 4, 6)])
        chosen_all = jnp.concatenate([chosen] + [flip(chosen, k) for k in (2, 4, 6)], axis=1)

    x_all, sib_first, mixed, normed_ffn, context = bridge(
        ctx_heads, own_first, w_out_all, flat_tokens, heads_all, 2
    )
    x_all = x_all.reshape(4 * count, width)
    dz_all = dz_all.reshape(4 * count, width)
    out_part, dx_part, gg_part, gates_all, total_first, w_heads = run_experts(
        "both", x_all, dz_all, chosen_all, (sib_first, own_first),
        router=heads_all,
    )

    def finish_expert(total):
        if copies > 1:
            total = repack(total)
            total = lax.psum_scatter(total, "row", scatter_dimension=0)
            total = lax.psum_scatter(
                total, "seq", scatter_dimension=0, axis_index_groups=copy_groups
            )
        else:
            total = lax.psum_scatter(total, "row", scatter_dimension=0)
        return total

    reduced_first = finish_expert(total_first)
    out_part, gate_acts, up_acts, *sib_second = run_experts(
        "forward", x_all, None, None, own_second, gates=gates_all, carried=out_part
    )
    out_split = out_part.reshape(4, count, width)
    dx_part, gg_part, total_second, out_back = run_experts(
        "backward", x_all, dz_all, None, (*sib_second, *own_second), gates=gates_all,
        carried=(dx_part, gg_part), acts=(gate_acts, up_acts), pushed=out_split,
    )
    reduced_second = finish_expert(total_second)
    do_heads, gmixed, out_pre, block_out = return_tokens(
        dx_part.reshape(4, count, width), gg_part, mixed, normed_ffn, dz_own, chosen, heads_all,
        w_out_all, context, out_split, out_back, micro, copies, 3,
    )
    if copies > 1:
        out_pre = lax.psum_scatter(
            out_pre, "seq", scatter_dimension=1, axis_index_groups=copy_groups
        )
    out_pre = out_pre.reshape(4, rows, part, width + LANES)
    graw, head_term, out_in, exchanged = pl.pallas_call(
        functools.partial(attention_back_kernel, skip),
        grid=(micro,),
        in_specs=attention_specs
        + [
            pl.BlockSpec((1, 2, unit_len), by_row3),
            pl.BlockSpec((UNIT, 1, local_len, LANES), by_row4),
            pl.BlockSpec((unit_len, LANES), fixed),
            pl.BlockSpec((unit_len, LANES), fixed),
            pl.BlockSpec((length, LANES), fixed),
            pl.BlockSpec((length, LANES), fixed),
            pl.BlockSpec((UNIT, 1, local_len, width), by_row4),
            pl.BlockSpec(memory_space=pl.ANY),
            pl.BlockSpec(memory_space=pl.ANY),
        ],
        out_specs=[
            pl.BlockSpec((seq_size, 1, local_len, 2 * LANES), by_row4),
            pl.BlockSpec((PIECES, UNIT, ROWS_IN, 2 * LANES), zeros4),
            pl.BlockSpec(memory_space=pl.ANY),
            pl.BlockSpec(memory_space=pl.ANY),
        ],
        out_shape=[
            jax.ShapeDtypeStruct((seq_size, micro, local_len, 2 * LANES), BF16),
            jax.ShapeDtypeStruct((PIECES, UNIT, ROWS_IN, 2 * LANES), BF16),
            jax.ShapeDtypeStruct((3,) + out_pre.shape[1:], BF16),
            jax.ShapeDtypeStruct(reduced_first.shape, BF16),
        ],
        scratch_shapes=[
            pltpu.VMEM((length, LANES), F32),
            pltpu.VMEM((length, LANES), F32),
            pltpu.VMEM((width, 2 * LANES), F32),
            pltpu.VMEM(reduced_first.shape[1:], BF16),
            pltpu.SemaphoreType.DMA((UNIT + 2,)),
            pltpu.SemaphoreType.DMA((UNIT + 2,)),
            pltpu.SemaphoreType.DMA((2,)),
        ],
        compiler_params=params(collective_id=7, has_side_effects=True),
        cost_estimate=cost(2.5 * attention_flops, 8e6),
    )(
        q_all, kv_all, seg_queries, seg_keys, place_row, lse, do_heads,
        cosine, sine, key_cos, key_sin, normed_all, out_pre, reduced_first,
    )
    if copies > 1:
        graw_kv = lax.psum_scatter(
            graw[..., LANES:], "seq", scatter_dimension=0, tiled=True,
            axis_index_groups=copy_groups,
        )
        graw = jnp.concatenate([graw[:UNIT, ..., :LANES], graw_kv], axis=3)
        head_term = jnp.einsum(
            "nd,nh->dh",
            normed_all.reshape(UNIT * count, width),
            graw.reshape(UNIT * count, 2 * LANES),
            preferred_element_type=F32,
        ).astype(BF16)
        head_term = head_term.reshape(copies, UNIT, rows, part, 2 * LANES)
        head_term = lax.psum_scatter(
            head_term, "seq", scatter_dimension=0, axis_index_groups=copy_groups
        ).transpose(1, 0, 2, 3)
    head_grad, exchanged_second, out_grad, grad_input = finish(
        rows, graw, head_term, reduced_second, out_pre, out_in, w_heads, flat_tokens, heads_all,
        gmixed, 4,
    )
    if copies == 1:
        like = jax.ShapeDtypeStruct
        (
            grad_norm_attn, grad_query, grad_key, grad_value, grad_out, grad_norm_ffn, grad_router,
            grad_gate, grad_up, grad_down,
        ) = pl.pallas_call(
            unpack_grads_kernel,
            out_shape=[
                like((1, part), F32), like(w_query.shape, F32), like(w_key.shape, F32),
                like(w_value.shape, F32), like(w_out.shape, F32), like((1, part), F32),
                like(w_router.shape[::-1], F32), like(w_gate.shape, F32), like(w_up.shape, F32),
                like(w_down.shape, F32),
            ],
            compiler_params=params(),
            cost_estimate=cost(1, 1e7),
        )(
            exchanged, exchanged_second, head_grad, out_grad, w_gate, w_up, w_query, w_key, w_value,
            w_router.T, norm_attn[None], norm_ffn[None],
        )
        grad_router = grad_router.T
        grad_norm_attn = grad_norm_attn.reshape(part)
        grad_norm_ffn = grad_norm_ffn.reshape(part)
    else:
        finished = [exchanged, exchanged_second]
        finished = jnp.stack(finished, axis=1).reshape(E, 3 * part, hidden).astype(F32)
        grad_gate = finished[:, :part]
        grad_up = finished[:, part : 2 * part]
        grad_down = finished[:, 2 * part :].reshape(E, 2, -1, hidden).transpose(0, 2, 1, 3)
        grad_down = grad_down.reshape(E, -1, width)
        head_grad = head_grad.astype(F32)
        grad_query = head_grad[:, :, :LANES].transpose(1, 0, 2).reshape(part, H * HD)
        grad_key = head_grad[:, :, LANES : LANES + HD].transpose(1, 0, 2).reshape(part, KVH * HD)
        grad_value = head_grad[:, :, LANES + HD :].transpose(1, 0, 2).reshape(part, KVH * HD)
        grad_out = out_grad[:, :width]
        grad_router = out_grad[:, width : width + E]

        attn_weights = jnp.concatenate([w_query, w_key, w_value], axis=1).astype(F32)
        attn_grads = jnp.concatenate([grad_query, grad_key, grad_value], axis=1)
        grad_norm_attn = jnp.sum(attn_weights * attn_grads, axis=1) / norm_attn.astype(F32)
        grad_norm_ffn = (
            jnp.sum(w_gate.astype(F32) * grad_gate, axis=(0, 2))
            + jnp.sum(w_up.astype(F32) * grad_up, axis=(0, 2))
            + jnp.sum(w_router.astype(F32) * grad_router, axis=1)
        ) / norm_ffn.astype(F32)
    return (
        block_out.reshape(tokens.shape),
        grad_input.reshape(tokens.shape),
        grad_norm_attn,
        grad_query,
        grad_key,
        grad_value,
        grad_out,
        grad_norm_ffn,
        grad_router,
        grad_gate,
        grad_up,
        grad_down,
    )


def solution(mesh):
    both = ("seq", "row")
    body = functools.partial(shards, mesh.shape["seq"] // UNIT, rows=mesh.shape["row"])
    return jax.shard_map(
        body,
        mesh=mesh,
        in_specs=(
            P("row", "seq", None),
            P("row", None),
            P("row", "seq", None),
            P("row", "seq", None),
            P(both),
            P(both, None),
            P(both, None),
            P(both, None),
            P(both, None),
            P(both),
            P(both, None),
            P(None, both, None),
            P(None, both, None),
            P(None, both, None),
        ),
        out_specs=(
            P("row", "seq", None),
            P("row", "seq", None),
            P(both),
            P(both, None),
            P(both, None),
            P(both, None),
            P(both, None),
            P(both),
            P(both, None),
            P(None, both, None),
            P(None, both, None),
            P(None, both, None),
        ),
        check_vma=False,
    )
```
